32 devices in a mesh: seq: 8 (over y, x, core), fsdp: 4 (over z).
Axes of the slice: x: 2, y: 2, z: 4, core: 2. Of those that a mesh axis runs over, the one named last changes fastest.
Arguments:
- tokens: bfloat16 [4, 4096, 1600], P('fsdp', 'seq'), may hold values from -6 to 6
- ln1_gain: bfloat16 [1600], P('fsdp'), may hold values from 0.099609375 to 1.8984375
- ln1_bias: bfloat16 [1600], P('fsdp'), may hold values from -1.75 to 1.75
- qkv_weight: bfloat16 [1600, 4800], P('fsdp', 'seq'), may hold values from -0.15625 to 0.15625
- qv_bias: bfloat16 [3200], P('fsdp'), may hold values from -3 to 3
- out_weight: bfloat16 [1600, 1600], P('fsdp', 'seq'), may hold values from -2.5 to 2.5
- out_bias: bfloat16 [1600], P('fsdp'), may hold values from -1.75 to 1.75
- ln2_gain: bfloat16 [1600], P('fsdp'), may hold values from 0.099609375 to 1.8984375
- ln2_bias: bfloat16 [1600], P('fsdp'), may hold values from -1.75 to 1.75
- fc_weight: bfloat16 [1600, 6400], P('fsdp', 'seq'), may hold values from -0.15625 to 0.15625
- fc_bias: bfloat16 [6400], P('fsdp'), may hold values from -3 to 3
- proj_weight: bfloat16 [6400, 1600], P('fsdp', 'seq'), may hold values from -0.078125 to 0.078125
- proj_bias: bfloat16 [1600], P('fsdp'), may hold values from -1.75 to 1.75
- seg_lengths: int32 [4, 6], P('fsdp'), may hold values from 1 to 512, 2304 in all within a row
- parents: int32 [4, 6], P('fsdp'), may hold values from 0 to 2, as said below
- cotangent: bfloat16 [4, 4096, 1600], P('fsdp', 'seq'), may hold values from -6 to 6
Outputs:
- output: bfloat16 [4, 4096, 1600], P('fsdp', 'seq')
- input_grad: bfloat16 [4, 4096, 1600], P('fsdp', 'seq')
- ln1_gain_grad: float32 [1600], P('fsdp')
- ln1_bias_grad: float32 [1600], P('fsdp')
- qkv_weight_grad: float32 [1600, 4800], P('fsdp', 'seq')
- qv_bias_grad: float32 [3200], P('fsdp')
- out_weight_grad: float32 [1600, 1600], P('fsdp', 'seq')
- out_bias_grad: float32 [1600], P('fsdp')
- ln2_gain_grad: float32 [1600], P('fsdp')
- ln2_bias_grad: float32 [1600], P('fsdp')
- fc_weight_grad: float32 [1600, 6400], P('fsdp', 'seq')
- fc_bias_grad: float32 [6400], P('fsdp')
- proj_weight_grad: float32 [6400, 1600], P('fsdp', 'seq')
- proj_bias_grad: float32 [1600], P('fsdp')
The draws below stay inside these ranges and needn't reach their ends.
Inputs may be any that keep to these rules, and one draw needn't show every extreme that they name: `seg_lengths`: valid tokens of each branch and leaf segment of a tree, in slot order; each row sums to 2304. `parents`: in each tree the first 2 entries are 0 (branches hang from the trunk); each of the other 4 entries names a branch segment 1 to 2, and each branch is named by exactly two of them.
All inputs are finite; a program needn't handle non-finite values.
Results may differ from the reference program's by a relative error of at most 0.018.
Values may be sent and summed in bfloat16 or wider, within the bound.
A program may use at most 448 MiB of HBM per device.

```python
import math
import jax
import jax.numpy as jnp
import numpy as np
from jax import lax

D = 1600
HEADS = 25
HEAD = 64
FF = 6400
BLOCK = 512
SLOTS = 8
TRUNK_SLOTS = 2
BRANCHES = 2
TREE = 4096
GROUPS = 4


def draw_parents(key, part):
    tree_keys = jax.random.split(jax.random.fold_in(key, 17), GROUPS)

    def one_tree(tree_key):
        owners = jnp.repeat(jnp.arange(BRANCHES, dtype=jnp.int32), 2)
        mixed = jax.random.permutation(tree_key, owners)
        return jnp.concatenate([jnp.zeros((BRANCHES,), jnp.int32), mixed + 1])
    return jax.vmap(one_tree)(tree_keys)


def block_scale(stream_key, dims, pieces, low, top_value):
    loudness = 1.0
    for axis_at, blocks in pieces:
        steps = jax.random.uniform(jax.random.fold_in(jax.random.fold_in(stream_key, 6), axis_at), (blocks,), jnp.float32, low / len(pieces), top_value / len(pieces))
        loudness = loudness * jnp.repeat(jnp.exp(steps), dims[axis_at] // blocks).reshape((-1,) + (1,) * (len(dims) - 1 - axis_at))
    return loudness


def length_profile(number_of, total, most, slope):
    portions = [(1 << 20) // math.isqrt(rank ** slope) + 1 for rank in range(2, number_of + 1)]
    spare, counts = total - most - (number_of - 1), [1] * (number_of - 1)
    while spare > 0:
        candidates = [i for i in range(number_of - 1) if counts[i] < most]
        whole, remaining = sum([portions[i] for i in candidates]), spare
        for i in candidates:
            extra = min(most - counts[i], max(1, remaining * portions[i] // whole), spare)
            counts[i] = counts[i] + extra
            spare = spare - extra
    return np.array([most] + counts)


def ragged(rng, number_of, total, reach, skew):
    if number_of == 2:
        one = jax.random.randint(rng, (), max(1, total - reach), min(reach, total - 1) + 1)
        return jnp.stack([one, total - one])
    tallies = jnp.asarray(length_profile(number_of, total, reach, skew), jnp.int32)
    couples = (number_of - 1) // 2
    source_of, taker = tallies[1:1 + 2 * couples:2], tallies[2:2 + 2 * couples:2]
    margin = jnp.minimum(source_of - 1, reach - taker)
    passed = jax.random.randint(jax.random.fold_in(rng, 1), (couples,), 0, 1 << 20) % (margin + 1)
    tallies = tallies.at[1:1 + 2 * couples:2].set(source_of - passed).at[2:2 + 2 * couples:2].set(taker + passed)
    return tallies[jax.random.permutation(jax.random.fold_in(rng, 2), number_of)]


def noise(key, dims, width, bound, cuts=(), kind=jnp.bfloat16):
    entries = jax.random.normal(key, dims, jnp.float32) * width
    if len(cuts) > 0:
        entries = block_scale(key, dims, cuts, -0.22, 0.18) * entries
    return jnp.clip(entries, min=-bound, max=bound).astype(kind)


def setup_inputs(seed: int = 0) -> dict:
    key_of = jax.random.split(jax.random.key(seed), 17)
    return {
        "tokens": noise(key_of[0], (GROUPS, TREE, D), 1.0, 6.0, ((0, 4), (1, 8))),
        "ln1_gain": jnp.clip(1.0 + 0.18 * jax.random.normal(key_of[1], (D,), jnp.float32), 0.099609375, 1.8984375).astype(jnp.bfloat16),
        "ln1_bias": noise(key_of[2], (D,), 0.3, 1.75, ((0, 4),)),
        "qkv_weight": noise(key_of[3], (D, 3 * D), D ** -0.5, 0.15625, ((0, 4), (1, 8))),
        "qv_bias": noise(key_of[4], (2 * D,), 0.5, 3.0, ((0, 4),)),
        "out_weight": noise(key_of[5], (D, D), (max(D // 256, 2)) ** -0.5, 2.5, ((0, 4), (1, 8))),
        "out_bias": noise(key_of[6], (D,), 0.3, 1.75, ((0, 4),)),
        "ln2_gain": jnp.clip(1.0 + 0.18 * jax.random.normal(key_of[7], (D,), jnp.float32), 0.099609375, 1.8984375).astype(jnp.bfloat16),
        "ln2_bias": noise(key_of[8], (D,), 0.3, 1.75, ((0, 4),)),
        "fc_weight": noise(key_of[9], (D, FF), D ** -0.5, 0.15625, ((0, 4), (1, 8))),
        "fc_bias": noise(key_of[10], (FF,), 0.5, 3.0, ((0, 4),)),
        "proj_weight": noise(key_of[11], (FF, D), FF ** -0.5, 0.078125, ((0, 4), (1, 8))),
        "proj_bias": noise(key_of[12], (D,), 0.3, 1.75, ((0, 4),)),
        "seg_lengths": jax.vmap(lambda own: ragged(own, 3 * BRANCHES, 9 * BRANCHES * BLOCK // 4, BLOCK, 0))(jax.random.split(key_of[13], GROUPS)).reshape((GROUPS, 3 * BRANCHES)).astype(jnp.int32),
        "parents": draw_parents(jax.random.fold_in(key_of[16], 71), 0),
        "cotangent": noise(key_of[15], (GROUPS, TREE, D), 1.0, 6.0, ((0, 4), (1, 8))),
    }


@jax.custom_vjp
def low(v):
    return lax.optimization_barrier(v.astype(jnp.bfloat16)).astype(jnp.float32)

@jax.custom_vjp
def low_back(v):
    return v

def low_keep(v):
    return (low(v), None)

def low_pass(kept, grad):
    return (grad,)

def back_keep(v):
    return (v, None)

def back_low(kept, grad):
    return (low(grad),)
low.defvjp(low_keep, low_pass)
low_back.defvjp(back_keep, back_low)
highest = lax.Precision.HIGHEST

def layer_norm(values, gain, shift):
    centred = values - lax.optimization_barrier(jnp.mean(values, -1, keepdims=True))
    spread = lax.optimization_barrier(jnp.mean(centred * centred, -1, keepdims=True))
    return centred * lax.rsqrt(spread + 1e-05) * gain + shift

def segment_of(slot):
    return jnp.where(slot < TRUNK_SLOTS, 0, slot - TRUNK_SLOTS + 1)

def tree_forward(params, inputs):
    tokens, lengths, parents = inputs
    gain_one, shift_one, qkv_weight, qv_bias, out_weight, out_bias, gain_two, shift_two, fc_weight, fc_bias, proj_weight, proj_bias = params
    normed_one = low(layer_norm(tokens, gain_one, shift_one))
    bias_three = jnp.concatenate([qv_bias[:D], jnp.zeros((D,), jnp.float32), qv_bias[D:]])
    projected = low(low_back(jnp.dot(normed_one, qkv_weight, precision=highest) + bias_three))
    queries = projected[:, :D].reshape(TREE, HEADS, HEAD)
    keys_all = projected[:, D:2 * D].reshape(TREE, HEADS, HEAD)
    values_all = projected[:, 2 * D:].reshape(TREE, HEADS, HEAD)
    seg_len = jnp.concatenate([jnp.full((1,), TRUNK_SLOTS * BLOCK, jnp.int32), lengths])
    parent_full = jnp.concatenate([jnp.zeros((1,), jnp.int32), parents])
    key_pos = jnp.arange(TREE, dtype=jnp.int32)
    key_seg = segment_of(key_pos // BLOCK)
    key_off = key_pos % BLOCK
    key_open = key_off < seg_len[key_seg]

    def attend(slot):
        query_block = lax.dynamic_slice_in_dim(queries, slot * BLOCK, BLOCK, 0)
        own_seg = segment_of(slot)
        above = parent_full[own_seg]
        offsets = jnp.arange(BLOCK, dtype=jnp.int32)[:, None]
        trunk_open = (key_seg == 0)[None, :] & (key_pos[None, :] <= slot * BLOCK + offsets)
        other_open = (key_seg == 0)[None, :] | (key_seg == own_seg)[None, :] & (key_off[None, :] <= offsets) & key_open[None, :] | (key_seg == above)[None, :] & key_open[None, :]
        allowed = jnp.where(own_seg == 0, trunk_open, other_open)
        raw = jnp.einsum('qhd,khd->hqk', query_block, keys_all, precision=highest)
        scores = low_back(raw) * 0.125
        weights = jnp.where(allowed[None], jnp.exp(scores), 0.0)
        totals = lax.optimization_barrier(jnp.sum(weights, -1))
        summed = low_back(jnp.einsum('hqk,khd->qhd', low(weights), values_all, precision=highest))
        return (summed / totals.T[:, :, None]).reshape(BLOCK, D)
    attended = lax.map(jax.checkpoint(attend), jnp.arange(SLOTS, dtype=jnp.int32)).reshape(TREE, D)
    branch = low_back(jnp.dot(low(attended), out_weight, precision=highest) + out_bias)
    middle = tokens + branch
    normed_two = low(layer_norm(middle, gain_two, shift_two))
    pre = low_back(jnp.dot(normed_two, fc_weight, precision=highest) + fc_bias)
    act = low(jax.nn.gelu(pre, approximate=True))
    return middle + jnp.dot(act, proj_weight, precision=highest) + proj_bias

def reference(tokens, ln1_gain, ln1_bias, qkv_weight, qv_bias, out_weight, out_bias, ln2_gain, ln2_bias, fc_weight, fc_bias, proj_weight, proj_bias, seg_lengths, parents, cotangent):
    params = (ln1_gain.astype(jnp.float32), ln1_bias.astype(jnp.float32), qkv_weight.astype(jnp.float32), qv_bias.astype(jnp.float32), out_weight.astype(jnp.float32), out_bias.astype(jnp.float32), ln2_gain.astype(jnp.float32), ln2_bias.astype(jnp.float32), fc_weight.astype(jnp.float32), fc_bias.astype(jnp.float32), proj_weight.astype(jnp.float32), proj_bias.astype(jnp.float32))
    tree_step = jax.checkpoint(tree_forward)

    def forward(inputs, weights):
        return lax.map(lambda item: tree_step(weights, item), (inputs, seg_lengths, parents))
    output, backward = jax.vjp(forward, tokens.astype(jnp.float32), params)
    grad_tokens, grads = backward(cotangent.astype(jnp.float32))
    return (output.astype(jnp.bfloat16), grad_tokens.astype(jnp.bfloat16), grads[0], grads[1], grads[2], grads[3], grads[4], grads[5], grads[6], grads[7], grads[8], grads[9], grads[10], grads[11])
```

```python
import functools
import math

import jax
import jax.numpy as jnp
from jax import lax
from jax.experimental import pallas as pl
from jax.experimental.pallas import tpu as pltpu
from jax.sharding import PartitionSpec as P

MESH = pl.DeviceIdType.MESH
HEADS = 25


def route_bits(n):
    bits = []
    b = 2
    while b < n:
        bits.append(b)
        b *= 2
    return bits


def flip(a, b):
    return jnp.where(lax.rem(lax.div(a, b), 2) == 0, a + b, a - b)


def place(me, r, n):
    if isinstance(r, int):
        for b in [1] + route_bits(n):
            if r & b:
                me = flip(me, b)
        return me
    for b in [1] + route_bits(n):
        me = jnp.where(lax.rem(lax.div(r, b), 2) == 0, me, flip(me, b))
    return me


def pick(table, q):
    value = jnp.int32(table[0])
    for i, entry in enumerate(table[1:]):
        value = jnp.where(q == i + 1, jnp.int32(entry), value)
    return value


def greet(ids):
    barrier = pltpu.get_barrier_semaphore()
    for i in ids:
        pl.semaphore_signal(barrier, inc=1, device_id=i, device_id_type=MESH)
    pl.semaphore_wait(barrier, len(ids))


def remote(src, dst, send, recv, device):
    return pltpu.make_async_remote_copy(
        src_ref=src, dst_ref=dst, send_sem=send, recv_sem=recv, device_id=device, device_id_type=MESH
    )


def arrival_order(n):
    bits = route_bits(n)
    orders = [bits, bits[::-1]]
    lists = []
    for order in orders:
        held, phases = [0], [-1]
        for i, b in enumerate(order):
            fresh = [h ^ b for h in held]
            held, phases = held + fresh, phases + [i] * len(fresh)
        lists.append(list(zip(held, phases)))
    entries = []
    for i in range(n // 2):
        for odd in (0, 1):
            for half in (0, 1):
                k, phase = lists[half][i]
                entries.append((half, k ^ odd, phase, odd))
    return orders, entries


def gather_kernel(n, h, body, n_const, n_out, relative, *refs):
    x_ref = refs[0]
    consts = refs[1 : 1 + n_const]
    all_ref = refs[1 + n_const]
    outs = refs[2 + n_const : 2 + n_const + n_out]
    held = refs[2 + n_const + n_out]
    stages = refs[3 + n_const + n_out : 3 + n_const + 2 * n_out]
    send, recv, keep, store = refs[3 + n_const + 2 * n_out :]
    me = lax.axis_index("seq")
    orders, entries = arrival_order(n)
    bits = orders[0]
    nb = len(bits)

    def device(b):
        return {"seq": flip(me, b)}

    def spot(half, k):
        return 2 * (k if relative else place(me, k, n)) + half

    def ship(half, k, b):
        at = spot(half, k)
        src = x_ref.at[pl.ds(half * h, h)] if isinstance(k, int) and k == 0 else held.at[at]
        lane = 0 if b == 1 else 1 + bits.index(b)
        to = k ^ b if isinstance(k, int) else place(k, b, n)
        dst = 2 * to + half if relative else at
        return remote(src, held.at[dst], send.at[half, lane, k], recv.at[half, to], device(b))

    greet([device(b) for b in [1] + bits])
    for i in range(nb):
        for half in (0, 1):
            ship(half, 0, orders[half][i]).start()
    for half in (0, 1):
        ship(half, 0, 1).start()

    def output(o, q, at):
        slot = lax.rem(q, 2)
        return pltpu.make_async_copy(stages[o].at[slot], outs[o].at[at], store.at[o, slot])

    def entry(q, at, value):
        results = body(value, *consts)
        for o in range(n_out):

            @pl.when(q >= 2)
            def _(o=o):
                output(o, q, at).wait()

            stages[o][lax.rem(q, 2)] = results[o]
            output(o, q, at).start()

    def step(q, carry):
        half = pick([e[0] for e in entries], q)
        k = pick([e[1] for e in entries], q)
        phase = pick([e[2] for e in entries], q)
        odd = pick([e[3] for e in entries], q)
        at = spot(half, k)

        @pl.when(k == 0)
        def _():
            held[at] = x_ref[pl.ds(pl.multiple_of(half * h, h), h)]

        @pl.when(k != 0)
        def _():
            remote(held.at[at], held.at[at], send.at[0, 0, 0], recv.at[half, k], device(1)).wait_recv()

        for side in (0, 1):
            for i in range(nb):

                @pl.when((half == side) & (odd == 0) & (k != 0) & (phase < i))
                def _(side=side, i=i):
                    ship(side, k, orders[side][i]).start()

            @pl.when((half == side) & (odd == 0) & (k != 0))
            def _(side=side):
                ship(side, k, 1).start()

        pltpu.make_async_copy(held.at[at], all_ref.at[at], keep.at[q]).start()
        if n_out:
            entry(q, at, held[at])
        return carry

    lax.fori_loop(0, 2 * n, step, 0)
    for q, (half, k, phase, odd) in enumerate(entries):
        at = spot(half, k)
        pltpu.make_async_copy(held.at[at], all_ref.at[at], keep.at[q]).wait()
        if q >= 2 * n - 2:
            for o in range(n_out):
                output(o, jnp.int32(q), at).wait()
        if not odd:
            for i in range(nb):
                if phase < i:
                    ship(half, k, orders[half][i]).wait_send()
            ship(half, k, 1).wait_send()


def seq_gather(x, n, ident, name, body=None, consts=(), outs=(), relative=False):
    rows, cols = x.shape
    h = rows // 2
    nb = len(route_bits(n))
    shapes = [jax.ShapeDtypeStruct((2 * n, h, c), d) for c, d in outs]
    vmem = pl.BlockSpec(memory_space=pltpu.VMEM)
    hbm = pl.BlockSpec(memory_space=pl.ANY)
    out = pl.pallas_call(
        functools.partial(gather_kernel, n, h, body, len(consts), len(outs), relative),
        out_shape=[jax.ShapeDtypeStruct((2 * n, h, cols), x.dtype)] + shapes,
        in_specs=[vmem] * (1 + len(consts)),
        out_specs=[hbm] * (1 + len(outs)),
        scratch_shapes=[pltpu.VMEM((2 * n, h, cols), x.dtype)]
        + [pltpu.VMEM((2, h, c), d) for c, d in outs]
        + [
            pltpu.SemaphoreType.DMA((2, nb + 1, n)),
            pltpu.SemaphoreType.DMA((2, n)),
            pltpu.SemaphoreType.DMA((2 * n,)),
            pltpu.SemaphoreType.DMA((max(len(outs), 1), 2)),
        ],
        compiler_params=pltpu.CompilerParams(
            collective_id=ident, has_side_effects=True, vmem_limit_bytes=60 << 20
        ),
        cost_estimate=pl.CostEstimate(
            flops=0, bytes_accessed=34 * n * rows * cols, transcendentals=0
        ),
        name=name,
    )(x, *consts)
    return [o.reshape(2 * n * h, o.shape[2]) for o in out]


def scatter_order(n):
    bits = route_bits(n)
    orders = [bits, bits[::-1]]
    lists = [
        sorted(range(0, n, 2), key=lambda k: [-int(bool(k & b)) for b in order]) for order in orders
    ]
    return orders, [(half, lists[half][i]) for i in range(n // 2) for half in (0, 1)]


def scatter_kernel(n, h, body, n_in, n_const, n_out, modes, *refs):
    ins = refs[:n_in]
    consts = refs[n_in : n_in + n_const]
    at = n_in + n_const
    sum_ref = refs[at]
    outs = refs[at + 1 : at + 1 + n_out]
    at += 1 + n_out
    give, pair, own, far, total = refs[at : at + 5]
    at += 5
    loads = refs[at : at + n_in]
    stages = refs[at + n_in : at + n_in + n_out]
    pair_send, pair_recv, far_send, far_recv, load, store, done = refs[at + n_in + n_out :]
    me = lax.axis_index("seq")
    orders, entries = scatter_order(n)
    bits = orders[0]
    slots = give.shape[0]
    index = {e: j for j, e in enumerate(entries)}

    def device(b):
        return {"seq": flip(me, b)}

    def phase_of(half, k):
        for i, b in enumerate(orders[half]):
            if k & b:
                return i
        return len(bits)

    landing = {}
    for half in (0, 1):
        for i, b in enumerate(orders[half]):
            for k in range(0, n, 2):
                if phase_of(half, k) == i:
                    landing[half, i, k ^ b] = len(landing)

    halves = [e[0] for e in entries]
    ks = [e[1] for e in entries]

    def spot(q, relative):
        j = lax.div(q, 2)
        k = pick(ks, j)
        k = jnp.where(lax.rem(q, 2) == 0, flip(k, 1), k)
        return 2 * (k if relative else place(me, k, n)) + pick(halves, j)

    def fetch(q):
        slot = lax.rem(q, 2)
        return [
            pltpu.make_async_copy(ins[i].at[spot(q, modes[0][i])], loads[i].at[slot], load.at[i, slot])
            for i in range(n_in)
        ]

    def output(o, q):
        slot = lax.rem(q, 2)
        return pltpu.make_async_copy(stages[o].at[slot], outs[o].at[spot(q, modes[1][o])], store.at[o, slot])

    def hand(j):
        slot = lax.rem(j, slots)
        return remote(give.at[slot], pair.at[j], pair_send.at[j], pair_recv.at[j], device(1))

    def launch(half, k):
        i = phase_of(half, k)
        b = orders[half][i]
        to = landing[half, i, k ^ b]
        return remote(own.at[index[half, k]], far.at[to], far_send.at[to], far_recv.at[to], device(b))

    def join(j):
        hand(j).wait_recv()
        own[j] = (own[j].astype(jnp.float32) + pair[j].astype(jnp.float32)).astype(own.dtype)
        for e, (half, k) in enumerate(entries):
            if phase_of(half, k) == 0:

                @pl.when(j == e)
                def _(half=half, k=k):
                    launch(half, k).start()

    for c in fetch(jnp.int32(0)):
        c.start()
    greet([device(b) for b in [1] + bits])

    def step(q, carry):
        j = lax.div(q, 2)
        slot = lax.rem(q, 2)

        @pl.when(q + 1 < 2 * n)
        def _():
            for c in fetch(q + 1):
                c.start()

        for c in fetch(q):
            c.wait()
        part, *results = body(*[r[slot] for r in loads], *consts)
        for o in range(n_out):

            @pl.when(q >= 2)
            def _(o=o):
                output(o, q).wait()

            stages[o][slot] = results[o]
            output(o, q).start()

        @pl.when(slot == 0)
        def _():
            @pl.when(j >= slots)
            def _():
                hand(j - slots).wait_send()

            give[lax.rem(j, slots)] = part.astype(give.dtype)
            hand(j).start()

        @pl.when(slot == 1)
        def _():
            own[j] = part.astype(own.dtype)

            @pl.when(j >= 1)
            def _():
                join(j - 1)

        return carry

    lax.fori_loop(0, 2 * n, step, 0)
    join(jnp.int32(n - 1))
    for i in range(len(bits)):
        for half in (0, 1):
            order = orders[half]
            for k in [k for hh, k in entries if hh == half and phase_of(half, k) > i]:
                to = landing[half, i, k]
                remote(far.at[to], far.at[to], far_send.at[to], far_recv.at[to], device(1)).wait_recv()
                j = index[half, k]
                rows = pl.ds(half * h, h)
                if i == len(bits) - 1:
                    total[rows] = own[j].astype(jnp.float32) + far[to].astype(jnp.float32)
                    pltpu.make_async_copy(total.at[rows], sum_ref.at[rows], done.at[half]).start()
                else:
                    own[j] = (own[j].astype(jnp.float32) + far[to].astype(jnp.float32)).astype(own.dtype)
                    if phase_of(half, k) == i + 1:
                        launch(half, k).start()
    for half in (0, 1):
        rows = pl.ds(half * h, h)
        pltpu.make_async_copy(total.at[rows], sum_ref.at[rows], done.at[half]).wait()
    for q in (2 * n - 2, 2 * n - 1):
        for o in range(n_out):
            output(o, jnp.int32(q)).wait()
    for j in range(max(n - slots, 0), n):
        hand(jnp.int32(j)).wait_send()
    for half, k in entries:
        if phase_of(half, k) < len(bits):
            launch(half, k).wait_send()


def seq_scatter(n, cols, ident, name, body, ins, consts, outs=(), modes=None):
    h = ins[0].shape[0] // (2 * n)
    low = jnp.bfloat16
    slots = min(4, n)
    split = [a.reshape(2 * n, h, a.shape[1]) for a in ins]
    vmem = pl.BlockSpec(memory_space=pltpu.VMEM)
    hbm = pl.BlockSpec(memory_space=pl.ANY)
    reach = n - 2
    out = pl.pallas_call(
        functools.partial(scatter_kernel, n, h, body, len(ins), len(consts), len(outs), modes or ([0] * len(ins), [0] * len(outs))),
        out_shape=[jax.ShapeDtypeStruct((2 * h, cols), jnp.float32)]
        + [jax.ShapeDtypeStruct((2 * n, h, c), d) for c, d in outs],
        in_specs=[hbm] * len(ins) + [vmem] * len(consts),
        out_specs=[hbm] * (1 + len(outs)),
        scratch_shapes=[
            pltpu.VMEM((slots, h, cols), low),
            pltpu.VMEM((n, h, cols), low),
            pltpu.VMEM((n, h, cols), low),
            pltpu.VMEM((reach, h, cols), low),
            pltpu.VMEM((2 * h, cols), jnp.float32),
        ]
        + [pltpu.VMEM((2, h, a.shape[2]), a.dtype) for a in split]
        + [pltpu.VMEM((2, h, c), d) for c, d in outs]
        + [
            pltpu.SemaphoreType.DMA((n,)),
            pltpu.SemaphoreType.DMA((n,)),
            pltpu.SemaphoreType.DMA((reach,)),
            pltpu.SemaphoreType.DMA((reach,)),
            pltpu.SemaphoreType.DMA((len(ins), 2)),
            pltpu.SemaphoreType.DMA((max(len(outs), 1), 2)),
            pltpu.SemaphoreType.DMA((2,)),
        ],
        compiler_params=pltpu.CompilerParams(
            collective_id=ident, has_side_effects=True, vmem_limit_bytes=60 << 20
        ),
        cost_estimate=pl.CostEstimate(flops=0, bytes_accessed=68 * n * h * cols, transcendentals=0),
        name=name,
    )(*split, *consts)
    return [out[0]] + [o.reshape(2 * n * h, o.shape[2]) for o in out[1:]]


def exchange_kernel(n, nf, h, w_ref, p_ref, c_ref, v_ref, w_all, p_all, c_all, v_all, send, recv, p_send, p_recv, c_send, c_recv, v_send, v_recv, local):
    me = lax.axis_index("seq")
    f = lax.axis_index("fsdp")
    bits = route_bits(n)
    orders = [bits, bits[::-1]]
    group = n // nf

    def device(r):
        return {"seq": place(me, r, n)}

    def rows(half):
        return pl.ds(0, h) if half == 0 else pl.ds(h, w_ref.shape[0] - h)

    planes = [{"fsdp": lax.rem(f + d, nf)} for d in range(1, nf)]
    greet([device(r) for r in range(1, n)] + planes)
    started = []

    def ship(half, r, b):
        owner = place(me, r, n)
        src = w_ref if r == 0 else w_all.at[owner]
        c = remote(
            src.at[rows(half)],
            w_all.at[owner].at[rows(half)],
            send.at[half, r, 0 if b == 1 else 1 + bits.index(b)],
            recv.at[half, r ^ b],
            device(b),
        )
        c.start()
        started.append(c)

    def arrive(half, k):
        dst = w_all.at[place(me, k, n)].at[rows(half)]
        remote(dst, dst, send.at[half, 0, 0], recv.at[half, k], device(1)).wait_recv()

    for d in range(1, nf):
        c = remote(v_ref, v_all.at[f], v_send.at[d - 1], v_recv.at[d - 1], planes[d - 1])
        c.start()
        started.append(c)
    for i in range(len(bits)):
        for half in (0, 1):
            ship(half, 0, orders[half][i])
    for half in (0, 1):
        ship(half, 0, 1)
    mine = [
        pltpu.make_async_copy(w_ref, w_all.at[me], local.at[0]),
        pltpu.make_async_copy(p_ref.at[me], p_all.at[me], local.at[1]),
        pltpu.make_async_copy(v_ref, v_all.at[f], local.at[2]),
    ]
    for c in mine:
        c.start()
    for i in range(len(bits)):
        for half in (0, 1):
            order = orders[half]
            had = [0]
            for b in order[:i]:
                had = had + [k ^ b for k in had]
            for k0 in had:
                k = k0 ^ order[i]
                arrive(half, k)
                for b in order[i + 1 :]:
                    ship(half, k, b)
                ship(half, k, 1)
        if i == 0:
            for r in range(1, n):
                c = remote(p_ref.at[place(me, r, n)], p_all.at[me], p_send.at[r - 1], p_recv.at[r - 1], device(r))
                c.start()
                started.append(c)
            for i2 in range(nf):
                to = lax.rem(me, group) * nf + i2
                slot = lax.div(me, group)

                @pl.when(to != me)
                def _(i2=i2, to=to, slot=slot):
                    remote(c_ref.at[i2], c_all.at[slot], c_send.at[i2], c_recv.at[slot], {"seq": to}).start()

                @pl.when(to == me)
                def _(i2=i2, slot=slot):
                    pltpu.make_async_copy(c_ref.at[i2], c_all.at[slot], local.at[3]).start()

    for half in (0, 1):
        for k in range(1, n, 2):
            arrive(half, k)
    for r in range(1, n):
        dst = p_all.at[place(me, r, n)]
        remote(dst, dst, p_send.at[0], p_recv.at[r - 1], device(r)).wait_recv()
    for p in range(nf):
        source = p * group + lax.div(me, nf)

        @pl.when(source != me)
        def _(p=p):
            remote(c_all.at[p], c_all.at[p], c_send.at[0], c_recv.at[p], device(1)).wait_recv()

        @pl.when(source == me)
        def _(p=p):
            pltpu.make_async_copy(c_all.at[p], c_all.at[p], local.at[3]).wait()

    for d in range(1, nf):
        dst = v_all.at[lax.rem(f + nf - d, nf)]
        remote(dst, dst, v_send.at[0], v_recv.at[d - 1], planes[0]).wait_recv()
    for c in mine:
        c.wait()
    for i2 in range(nf):
        to = lax.rem(me, group) * nf + i2

        @pl.when(to != me)
        def _(i2=i2):
            remote(c_ref.at[i2], c_ref.at[i2], c_send.at[i2], c_recv.at[0], device(1)).wait_send()

    for c in started:
        c.wait_send()


def exchange(w, p, c, v, n, nf, ident):
    rows, cols = w.shape
    h = (rows // 2 + 7) // 8 * 8
    nb = len(route_bits(n))
    hbm = pl.BlockSpec(memory_space=pl.ANY)
    dma = pltpu.SemaphoreType.DMA
    return pl.pallas_call(
        functools.partial(exchange_kernel, n, nf, h),
        out_shape=[
            jax.ShapeDtypeStruct((n, rows, cols), w.dtype),
            jax.ShapeDtypeStruct(p.shape, p.dtype),
            jax.ShapeDtypeStruct(c.shape, c.dtype),
            jax.ShapeDtypeStruct((nf,) + v.shape, v.dtype),
        ],
        in_specs=[hbm] * 4,
        out_specs=[hbm] * 4,
        scratch_shapes=[
            dma((2, n, nb + 1)),
            dma((2, n)),
            dma((n - 1,)),
            dma((n - 1,)),
            dma((nf,)),
            dma((nf,)),
            dma((nf - 1,)),
            dma((nf - 1,)),
            dma((4,)),
        ],
        compiler_params=pltpu.CompilerParams(collective_id=ident, has_side_effects=True),
        cost_estimate=pl.CostEstimate(flops=0, bytes_accessed=60 << 20, transcendentals=0),
        name="exchange",
    )(w, p, c, v)


def swap_kernel(n, wide, to_heads, x_ref, o_ref, send, recv, local):
    me = lax.axis_index("seq")

    def lanes(i):
        return pl.ds(pl.multiple_of(i * wide, 128), wide)

    def source(i):
        return x_ref.at[:, lanes(i)] if to_heads else x_ref.at[i]

    def target(i):
        return o_ref.at[i] if to_heads else o_ref.at[:, lanes(i)]

    greet([{"seq": place(me, r, n)} for r in range(1, n)])
    copies = []
    for r in range(n - 1, 0, -1):
        to = place(me, r, n)
        c = remote(source(to), target(me), send.at[r - 1], recv.at[r - 1], {"seq": to})
        c.start()
        copies.append(c)
    mine = pltpu.make_async_copy(source(me), target(me), local)
    mine.start()
    for r in range(1, n):
        dst = target(place(me, r, n))
        remote(dst, dst, send.at[0], recv.at[r - 1], {"seq": place(me, r, n)}).wait_recv()
    mine.wait()
    for c in copies:
        c.wait_send()


def swap(x, n, wide, to_heads, ident):
    rows = x.shape[0] if to_heads else x.shape[1]
    hbm = pl.BlockSpec(memory_space=pl.ANY)
    shape = (n, rows, wide) if to_heads else (rows, n * wide)
    return pl.pallas_call(
        functools.partial(swap_kernel, n, wide, to_heads),
        out_shape=jax.ShapeDtypeStruct(shape, x.dtype),
        in_specs=[hbm],
        out_specs=hbm,
        scratch_shapes=[
            pltpu.SemaphoreType.DMA((n - 1,)),
            pltpu.SemaphoreType.DMA((n - 1,)),
            pltpu.SemaphoreType.DMA,
        ],
        compiler_params=pltpu.CompilerParams(collective_id=ident, has_side_effects=True),
        cost_estimate=pl.CostEstimate(flops=0, bytes_accessed=40 << 20, transcendentals=0),
        name="to_heads" if to_heads else "to_tokens",
    )(x)


HEAD=64
SCALE=0.125*math.log2(math.e)

def block_table(lengths, parents, slots, trunk, block):
    branches=lengths.shape[0]//3
    rows=[]
    for t in range(slots):
        if t<trunk:
            keys=[(c,0 if c==t else block,block) for c in range(t+1)]
        else:
            m=t-trunk
            keys=[(c,block,block) for c in range(trunk)]
            if m>=branches:
                keys.append((trunk-1+parents[m],block,jnp.sum(jnp.where(jnp.arange(lengths.shape[0])==parents[m]-1,lengths,0))))
            keys.append((t,0,lengths[m]))
        for i,(c,shift,count) in enumerate(keys):
            masked=jnp.where(jnp.logical_or(shift==0,count<block),1,0)
            rows.append(jnp.stack([jnp.asarray(v,jnp.int32) for v in (t,c,shift,count,masked,int(i==0),int(i==len(keys)-1))]))
    return jnp.stack(rows,1)

def lane_half(shape):
    return lax.broadcasted_iota(jnp.int32,shape,len(shape)-1)<HEAD

def nt(a,b):
    return lax.dot_general(a,b,(((1,),(1,)),((),())),preferred_element_type=jnp.float32)

def mm(a,b):
    return jnp.dot(a,b,preferred_element_type=jnp.float32)

def attend_kernel(width, block, tab, qkv, low, att, tot, acc):
    p=pl.program_id(0)
    qs,ks,shift,count,masked=tab[0,p],tab[1,p],tab[2,p],tab[3,p],tab[4,p]
    first,last=tab[5,p],tab[6,p]
    qrow=pl.ds(pl.multiple_of(qs*block,block),block)
    krow=pl.ds(pl.multiple_of(ks*block,block),block)
    left=lane_half((block,2*HEAD))
    @pl.when(first==1)
    def _(): acc[...]=jnp.zeros_like(acc)
    def step(mask):
        for j in range(width//(2*HEAD)):
            q=qkv[qrow,j*2*HEAD:(j+1)*2*HEAD]
            k=qkv[krow,width+j*2*HEAD:width+(j+1)*2*HEAD]
            v=qkv[krow,2*width+j*2*HEAD:2*width+(j+1)*2*HEAD]
            for h in range(2):
                here=left if h==0 else jnp.logical_not(left)
                s=nt(jnp.where(here,q,0),k)
                e=jnp.exp2(s*SCALE)
                if mask is not None: e=jnp.where(mask,e,0.0)
                acc[2*j+h]+=mm(e.astype(jnp.bfloat16),jnp.where(here,v,1))
    @pl.when(masked==0)
    def _(): step(None)
    @pl.when(masked==1)
    def _():
        row=lax.broadcasted_iota(jnp.int32,(block,block),0)
        col=lax.broadcasted_iota(jnp.int32,(block,block),1)
        step((col<=row+shift)&(col<count))
    @pl.when(last==1)
    def _():
        for j in range(width//(2*HEAD)):
            a,b=acc[2*j],acc[2*j+1]
            total=jnp.where(left,pltpu.roll(a,HEAD,1),pltpu.roll(b,HEAD,1))
            value=jnp.where(left,a,b)/total
            lanes=slice(j*2*HEAD,(j+1)*2*HEAD)
            low[:,lanes]=value.astype(jnp.bfloat16)
            att[:,lanes]=value
            tot[:,lanes]=total

def attend(table, qkv, block):
    rows,width=qkv.shape[0],qkv.shape[1]//3
    steps=table.shape[1]
    by_q=lambda p,t:(t[0,p],0)
    heads=width//HEAD
    return pl.pallas_call(functools.partial(attend_kernel,width,block),
        out_shape=(jax.ShapeDtypeStruct((rows,width),jnp.bfloat16),jax.ShapeDtypeStruct((rows,width),jnp.float32),jax.ShapeDtypeStruct((rows,width),jnp.float32)),
        grid_spec=pltpu.PrefetchScalarGridSpec(num_scalar_prefetch=1,grid=(steps,),
            in_specs=[pl.BlockSpec((rows,3*width),lambda p,t:(0,0),pipeline_mode=pl.Buffered(1))],
            out_specs=[pl.BlockSpec((block,width),by_q)]*3,
            scratch_shapes=[pltpu.VMEM((heads,block,2*HEAD),jnp.float32)]),
        compiler_params=pltpu.CompilerParams(dimension_semantics=("arbitrary",),vmem_limit_bytes=50<<20),
        cost_estimate=pl.CostEstimate(flops=4*steps*heads*block*block*4*HEAD,bytes_accessed=rows*width*16,transcendentals=steps*heads*block*block),
        name="attend")(table,qkv)

def attend_back_kernel(width, block, tab, qkv, kt, datt, att, tot, out, dk, dv, dqt, aug):
    p=pl.program_id(0)
    qs,ks,shift,count,masked=tab[0,p],tab[1,p],tab[2,p],tab[3,p],tab[4,p]
    first,last=tab[5,p],tab[6,p]
    qrow=pl.ds(pl.multiple_of(qs*block,block),block)
    krow=pl.ds(pl.multiple_of(ks*block,block),block)
    left=lane_half((block,2*HEAD))
    lane=lax.broadcasted_iota(jnp.int32,(block,2*HEAD),1)
    pairs=width//(2*HEAD)
    @pl.when(p==0)
    def _():
        dk[...]=jnp.zeros_like(dk)
        dv[...]=jnp.zeros_like(dv)
    @pl.when(first==1)
    def _():
        dqt[...]=jnp.zeros_like(dqt)
        for j in range(pairs):
            lanes=slice(j*2*HEAD,(j+1)*2*HEAD)
            d=datt[:,lanes].astype(jnp.float32)
            total=tot[:,lanes]
            low=(d/total).astype(jnp.bfloat16)
            prod=d*att[:,lanes]/total
            for h in range(2):
                here=left if h==0 else jnp.logical_not(left)
                delta=-jnp.sum(jnp.where(here,prod,0.0),1,keepdims=True)
                hi=delta.astype(jnp.bfloat16).astype(jnp.float32)
                mid=(delta-hi).astype(jnp.bfloat16).astype(jnp.float32)
                rest=delta-hi-mid
                at=HEAD*(1-h)
                extra=jnp.where(lane==at,hi,jnp.where(lane==at+1,mid,jnp.where(lane==at+2,rest,0.0)))
                aug[2*j+h]=jnp.where(here,low.astype(jnp.float32),extra).astype(jnp.bfloat16)
    def step(mask):
        for j in range(pairs):
            q=qkv[qrow,j*2*HEAD:(j+1)*2*HEAD]
            k=qkv[krow,width+j*2*HEAD:width+(j+1)*2*HEAD]
            v=qkv[krow,2*width+j*2*HEAD:2*width+(j+1)*2*HEAD]
            lanes=slice(j*2*HEAD,(j+1)*2*HEAD)
            dvs,dks=[],[]
            for h in range(2):
                here=left if h==0 else jnp.logical_not(left)
                qh=jnp.where(here,q,0)
                e=jnp.exp2(nt(k,qh)*SCALE)
                if mask is not None: e=jnp.where(mask,e,0.0)
                dod=aug[2*j+h]
                ds=(e*nt(jnp.where(here,v*0.125,0.125).astype(jnp.bfloat16),dod)).astype(jnp.bfloat16)
                dvs.append(mm(e.astype(jnp.bfloat16),dod))
                dks.append(mm(ds,qh))
                at=j*2*HEAD+h*HEAD
                dqt[at:at+HEAD]+=mm(kt[at:at+HEAD,krow],ds)
            dv[krow,lanes]+=jnp.where(left,dvs[0],dvs[1])
            dk[krow,lanes]+=dks[0]+dks[1]
    @pl.when(masked==0)
    def _(): step(None)
    @pl.when(masked==1)
    def _():
        col=lax.broadcasted_iota(jnp.int32,(block,block),0)
        row=lax.broadcasted_iota(jnp.int32,(block,block),1)
        step((col<=row+shift)&(col<count))
    @pl.when(last==1)
    def _():
        out[qrow,0:width]=dqt[...].T.astype(jnp.bfloat16)
    @pl.when(p==pl.num_programs(0)-1)
    def _():
        out[:,width:2*width]=dk[...].astype(jnp.bfloat16)
        out[:,2*width:]=dv[...].astype(jnp.bfloat16)

def attend_back(table, qkv, datt, att, tot, block):
    rows,width=qkv.shape[0],qkv.shape[1]//3
    steps=table.shape[1]
    by_q=lambda p,t:(t[0,p],0)
    heads=width//HEAD
    kt=qkv[:,width:2*width].T
    whole=lambda s:pl.BlockSpec(s,lambda p,t:(0,0),pipeline_mode=pl.Buffered(1))
    return pl.pallas_call(functools.partial(attend_back_kernel,width,block),
        out_shape=jax.ShapeDtypeStruct((rows,3*width),jnp.bfloat16),
        grid_spec=pltpu.PrefetchScalarGridSpec(num_scalar_prefetch=1,grid=(steps,),
            in_specs=[whole((rows,3*width)),whole((width,rows))]+[pl.BlockSpec((block,width),by_q)]*3,
            out_specs=whole((rows,3*width)),
            scratch_shapes=[pltpu.VMEM((rows,width),jnp.float32),pltpu.VMEM((rows,width),jnp.float32),pltpu.VMEM((width,block),jnp.float32),pltpu.VMEM((heads,block,2*HEAD),jnp.bfloat16)]),
        compiler_params=pltpu.CompilerParams(dimension_semantics=("arbitrary",),vmem_limit_bytes=60<<20),
        cost_estimate=pl.CostEstimate(flops=10*steps*heads*block*block*2*HEAD,bytes_accessed=rows*width*32,transcendentals=steps*heads*block*block),
        name="attend_back")(table,qkv,kt,datt,att,tot)


def layer_norm(values, gain, shift):
    centred = values - jnp.mean(values, -1, keepdims=True)
    spread = jnp.mean(centred * centred, -1, keepdims=True)
    return centred * lax.rsqrt(spread + 1e-05) * gain + shift


def contract_rows(left, right):
    return lax.dot_general(
        left, right, (((0,), (0,)), ((), ())), preferred_element_type=jnp.float32
    )


def contract_cols(left, right):
    return lax.dot_general(
        left, right, (((1,), (1,)), ((), ())), preferred_element_type=jnp.float32
    )


def sum_kernel(n, nf, v_ref, o_ref, planes, sums, send_z, recv_z, send_s, recv_s):
    s = lax.axis_index("seq")
    f = lax.axis_index("fsdp")
    others = [{"fsdp": lax.rem(f + d, nf)} for d in range(1, nf)]
    peers = [{"seq": lax.rem(s + d, n)} for d in range(1, n)]
    greet(others + peers)
    copies = []
    for d in range(1, nf):
        c = pltpu.make_async_remote_copy(
            src_ref=v_ref.at[lax.rem(f + d, nf)],
            dst_ref=planes.at[d - 1],
            send_sem=send_z.at[d - 1],
            recv_sem=recv_z.at[d - 1],
            device_id=others[d - 1],
            device_id_type=MESH,
        )
        c.start()
        copies.append(c)
    total = v_ref[f]
    for d, c in enumerate(copies):
        c.wait_recv()
        total = total + planes[d]
    sums[0] = total
    spread = []
    for d in range(1, n):
        c = pltpu.make_async_remote_copy(
            src_ref=sums.at[0],
            dst_ref=sums.at[d],
            send_sem=send_s.at[d - 1],
            recv_sem=recv_s.at[d - 1],
            device_id=peers[d - 1],
            device_id_type=MESH,
        )
        c.start()
        spread.append(c)
    for d, c in enumerate(spread):
        c.wait_recv()
        total = total + sums[d + 1]
    o_ref[...] = total
    for c in copies + spread:
        c.wait_send()


def sum_vectors(blocks, n, nf):
    k = blocks.shape[1]
    rows = -(-k // 1024) * 8
    padded = jnp.pad(blocks, ((0, 0), (0, rows * 128 - k))).reshape(nf, rows, 128)
    out = pl.pallas_call(
        functools.partial(sum_kernel, n, nf),
        out_shape=jax.ShapeDtypeStruct((rows, 128), jnp.float32),
        in_specs=[pl.BlockSpec(memory_space=pltpu.VMEM)],
        out_specs=pl.BlockSpec(memory_space=pltpu.VMEM),
        scratch_shapes=[
            pltpu.VMEM((nf - 1, rows, 128), jnp.float32),
            pltpu.VMEM((n, rows, 128), jnp.float32),
            pltpu.SemaphoreType.DMA((nf - 1,)),
            pltpu.SemaphoreType.DMA((nf - 1,)),
            pltpu.SemaphoreType.DMA((n - 1,)),
            pltpu.SemaphoreType.DMA((n - 1,)),
        ],
        compiler_params=pltpu.CompilerParams(collective_id=7, has_side_effects=True),
        name="sum_vectors",
    )(padded)
    return out.reshape(-1)[:k]


def local(
    tokens,
    ln1_gain,
    ln1_bias,
    qkv_weight,
    qv_bias,
    out_weight,
    out_bias,
    ln2_gain,
    ln2_bias,
    fc_weight,
    fc_bias,
    proj_weight,
    proj_bias,
    seg_lengths,
    parents,
    cotangent,
):
    n = lax.axis_size("seq")
    nf = lax.axis_size("fsdp")
    s = lax.axis_index("seq")
    f = lax.axis_index("fsdp")
    trunk = n // 4
    block, width = tokens.shape[1], tokens.shape[2]
    rows = width // nf
    hidden = fc_weight.shape[1] * n
    piece = hidden // (n * nf)
    group = n // nf
    wide = 2 * HEAD * (-(-HEADS // (2 * n)))
    low = jnp.bfloat16
    wider = jnp.float32

    vectors = [ln1_gain, ln1_bias, qv_bias, out_bias, ln2_gain, ln2_bias, fc_bias, proj_bias]
    sizes = [v.shape[0] for v in vectors]
    joined = jnp.concatenate(vectors)
    joined = jnp.pad(joined, (0, -joined.shape[0] % 2048)).reshape(-1, 128)
    qkv_cols = qkv_weight.shape[1]
    turned = jnp.pad(qkv_weight.T, ((0, 0 if qkv_cols % 8 == 0 else -qkv_cols % 16), (0, 0)))
    out_turned = lax.all_gather(out_weight, "fsdp", axis=0, tiled=True).T
    turned, proj_blocks, fc_blocks, joined = exchange(
        turned,
        proj_weight.reshape(n, piece, width // n),
        fc_weight.reshape(rows, nf, piece).transpose(1, 0, 2),
        joined,
        n,
        nf,
        0,
    )
    joined = joined.reshape(nf, -1)
    whole = []
    at = 0
    for size in sizes:
        whole.append(joined[:, at : at + size].reshape(-1).astype(wider))
        at += size
    gain_one, shift_one, bias_qv, bias_out, gain_two, shift_two, bias_fc, bias_proj = whole
    bias_three = jnp.stack([bias_qv[:width], jnp.zeros((width,), wider), bias_qv[width:]])
    bias_three = jnp.pad(bias_three, ((0, 0), (0, n * wide - width)))
    bias_mine = lax.dynamic_slice_in_dim(bias_three, s * wide, wide, 1).reshape(-1)
    bias_hidden = lax.dynamic_index_in_dim(bias_fc.reshape(nf, n, piece), s, 1, False)
    bias_hidden = bias_hidden.reshape(1, -1)

    turned = turned[:, :qkv_cols].reshape(3, width, rows)
    turned = jnp.pad(turned, ((0, 0), (0, n * wide - width), (0, 0)))
    turned = lax.dynamic_slice_in_dim(turned, s * wide, wide, 1)
    qkv_rows = turned.transpose(2, 0, 1).reshape(rows, 3 * wide)
    qkv_mine = lax.all_gather(qkv_rows, "fsdp", axis=0, tiled=True)
    out_turned = lax.all_gather(out_turned, "seq", axis=0, tiled=True)
    fc_rows = fc_blocks.transpose(1, 0, 2).reshape(rows, nf * piece)
    fc_mine = lax.all_gather(fc_rows, "fsdp", axis=0, tiled=True)
    proj_rows = proj_blocks.transpose(1, 0, 2).reshape(piece, width)
    proj_mine = lax.all_gather(proj_rows, "fsdp", axis=0, tiled=True)

    table = block_table(seg_lengths[0], parents[0], n, trunk, block)

    resid = tokens[0].astype(wider)
    (normed_one,) = seq_gather(
        layer_norm(resid, gain_one, shift_one).astype(low), n, 1, "gather_one"
    )
    projected = (
        jnp.dot(normed_one, qkv_mine, preferred_element_type=wider) + bias_mine
    ).astype(low)

    upstream = cotangent[0].astype(wider)
    sent, normed_one = lax.optimization_barrier((cotangent[0], normed_one))
    pieces = {}
    bits = route_bits(n)
    for half, order in enumerate([bits, bits[::-1]]):
        held = {0: sent[half * block // 2 : (half + 1) * block // 2]}
        for b in order:
            pairs = [(i, i ^ b) for i in range(n)]
            held.update({k ^ b: lax.ppermute(v, "seq", pairs) for k, v in held.items()})
        pairs = [(i, i ^ 1) for i in range(n)]
        held.update({k ^ 1: lax.ppermute(v, "seq", pairs) for k, v in held.items()})
        pieces.update({2 * k + half: v for k, v in held.items()})
    upstream_all = jnp.concatenate([pieces[i] for i in range(2 * n)])

    attended_low, attended, totals = attend(table, projected, block)
    attended_mine = swap(attended_low.reshape(n, block, wide), n, wide, False, 2)[:, :width]
    middle = resid + contract_cols(attended_mine, out_turned) + bias_out
    normed_two = layer_norm(middle, gain_two, shift_two).astype(low)
    ff = nf * piece

    def expand(value, weight, bias):
        pre = mm(value, weight[...]) + bias[...]
        bend = math.sqrt(2 / math.pi)
        inner = jnp.tanh(bend * (pre + 0.044715 * (pre * pre * pre)))
        act = 0.5 * pre * (1 + inner)
        slope = 0.5 * (1 + inner) + 0.5 * pre * (1 - inner * inner) * (
            bend * (1 + 3 * 0.044715 * (pre * pre))
        )
        return act.astype(low), slope.astype(low)

    normed_two, hidden_act, hidden_slope = seq_gather(
        normed_two, n, 3, "gather_two", expand, (fc_mine, bias_hidden), ((ff, low), (ff, low)), True
    )

    def shrink(up, act, slope, proj, fc):
        mixed = mm(act, proj[...])
        grad = (nt(up, proj[...]) * slope.astype(wider)).astype(low)
        return nt(grad, fc[...]), grad, mixed.astype(low)

    grad_normed_two, grad_pre, mixed = seq_scatter(
        n,
        width,
        4,
        "scatter_two",
        shrink,
        (upstream_all, hidden_act, hidden_slope),
        (proj_mine, fc_mine),
        ((ff, low), (width, low)),
        ((1, 1, 1), (1, 0)),
    )
    unused_two, norm_two_back = jax.vjp(layer_norm, middle, gain_two, shift_two)
    grad_middle_norm, grad_gain_two, grad_shift_two = norm_two_back(grad_normed_two)
    grad_middle = upstream + grad_middle_norm
    grad_branch = grad_middle.astype(low)
    grad_attended = jnp.dot(grad_branch, out_turned, preferred_element_type=wider).astype(low)
    grad_attended = jnp.pad(grad_attended, ((0, 0), (0, n * wide - width)))
    grad_attended = swap(grad_attended, n, wide, True, 5).reshape(n * block, wide)
    mixed, grad_attended = lax.optimization_barrier((mixed, grad_attended))
    mixed = lax.psum_scatter(mixed, "seq", scatter_dimension=0, tiled=True).astype(wider)
    output = (middle + mixed + bias_proj).astype(low)[None]
    grad_projected = attend_back(table, projected, grad_attended, attended, totals, block)
    grad_qkv = contract_rows(normed_one, grad_projected).astype(low)
    (grad_normed_one,) = seq_scatter(
        n, width, 6, "scatter_one", lambda g, w: (nt(g, w[...]),), (grad_projected,), (qkv_mine,)
    )
    unused_one, norm_one_back = jax.vjp(layer_norm, resid, gain_one, shift_one)
    grad_resid_norm, grad_gain_one, grad_shift_one = norm_one_back(grad_normed_one)
    input_grad = (grad_middle + grad_resid_norm).astype(low)[None]

    grad_proj = contract_rows(hidden_act, upstream_all).astype(low)
    grad_fc = contract_rows(normed_two, grad_pre).astype(low)
    grad_out = contract_rows(grad_branch, attended_mine).astype(low)
    proj_part = lax.psum_scatter(grad_proj, "fsdp", scatter_dimension=0, tiled=True)
    proj_out = lax.all_to_all(proj_part, "seq", 1, 0, tiled=True).astype(wider)
    fc_part = lax.psum_scatter(grad_fc, "fsdp", scatter_dimension=0, tiled=True)
    fc_part = fc_part.reshape(rows, nf, piece).transpose(1, 0, 2)
    fc_part = lax.all_to_all(jnp.repeat(fc_part, group, axis=0), "seq", 0, 0, tiled=True)
    fc_part = lax.dynamic_index_in_dim(
        fc_part.reshape(group, nf, rows, piece), lax.rem(s, group), 0, False
    )
    fc_out = fc_part.transpose(1, 0, 2).reshape(rows, nf * piece).astype(wider)
    out_part = lax.psum_scatter(grad_out, "seq", scatter_dimension=0, tiled=True).T
    out_out = lax.psum_scatter(out_part, "fsdp", scatter_dimension=0, tiled=True).astype(wider)
    qkv_part = lax.psum_scatter(grad_qkv, "fsdp", scatter_dimension=0, tiled=True)
    qkv_part = lax.all_gather(qkv_part.reshape(rows, 3, wide), "seq", axis=2, tiled=True)
    qkv_part = qkv_part[:, :, :width].reshape(rows, 3 * width)
    qkv_out = lax.dynamic_slice_in_dim(qkv_part, s * qkv_cols, qkv_cols, 1).astype(wider)

    column_sums = jnp.sum(grad_projected.astype(wider), 0).reshape(3, wide)
    placed = lax.dynamic_update_slice_in_dim(
        jnp.zeros((3, n * wide), wider), column_sums, s * wide, 1
    )[:, :width]
    grad_qv = jnp.concatenate([placed[0], placed[2]])
    hidden_sums = jnp.sum(grad_pre.astype(wider), 0).reshape(nf, 1, piece)
    grad_fc_bias = lax.dynamic_update_slice_in_dim(
        jnp.zeros((nf, n, piece), wider), hidden_sums, s, 1
    )
    parts = [
        grad_gain_one,
        grad_shift_one,
        grad_qv,
        jnp.sum(grad_branch.astype(wider), 0),
        grad_gain_two,
        grad_shift_two,
        grad_fc_bias,
        jnp.sum(upstream, 0),
    ]
    summed = sum_vectors(jnp.concatenate([p.reshape(nf, -1) for p in parts], 1), n, nf)
    vector_out = []
    at = 0
    for size in sizes:
        vector_out.append(summed[at : at + size])
        at += size
    return (
        output,
        input_grad,
        vector_out[0],
        vector_out[1],
        qkv_out,
        vector_out[2],
        out_out,
        vector_out[3],
        vector_out[4],
        vector_out[5],
        fc_out,
        vector_out[6],
        proj_out,
        vector_out[7],
    )


def solution(mesh):
    in_specs = (
        P("fsdp", "seq", None),
        P("fsdp"),
        P("fsdp"),
        P("fsdp", "seq"),
        P("fsdp"),
        P("fsdp", "seq"),
        P("fsdp"),
        P("fsdp"),
        P("fsdp"),
        P("fsdp", "seq"),
        P("fsdp"),
        P("fsdp", "seq"),
        P("fsdp"),
        P("fsdp", None),
        P("fsdp", None),
        P("fsdp", "seq", None),
    )
    out_specs = (
        P("fsdp", "seq", None),
        P("fsdp", "seq", None),
        P("fsdp"),
        P("fsdp"),
        P("fsdp", "seq"),
        P("fsdp"),
        P("fsdp", "seq"),
        P("fsdp"),
        P("fsdp"),
        P("fsdp"),
        P("fsdp", "seq"),
        P("fsdp"),
        P("fsdp", "seq"),
        P("fsdp"),
    )
    return jax.shard_map(local, mesh=mesh, in_specs=in_specs, out_specs=out_specs, check_vma=False)
```

```python
import functools
import math

import jax
import jax.numpy as jnp
import numpy as np
from jax import lax
from jax.experimental import pallas as pl
from jax.experimental.layout import Layout, with_layout_constraint
from jax.experimental.pallas import tpu as pltpu
from jax.sharding import PartitionSpec as P

MESH = pl.DeviceIdType.MESH
HEADS = 25
SMALL = pl.CostEstimate(flops=0, bytes_accessed=1 << 20, transcendentals=0)


def route_bits(n):
    bits = []
    b = 2
    while b < n:
        bits.append(b)
        b *= 2
    return bits


def flip(a, b):
    return jnp.where(lax.rem(lax.div(a, b), 2) == 0, a + b, a - b)


def place(me, r, n):
    if isinstance(r, int):
        for b in [1] + route_bits(n):
            if r & b:
                me = flip(me, b)
        return me
    for b in [1] + route_bits(n):
        me = jnp.where(lax.rem(lax.div(r, b), 2) == 0, me, flip(me, b))
    return me


def pick(table, q):
    value = jnp.int32(table[0])
    for i, entry in enumerate(table[1:]):
        value = jnp.where(q == i + 1, jnp.int32(entry), value)
    return value


def greet(ids):
    barrier = pltpu.get_barrier_semaphore()
    for i in ids:
        pl.semaphore_signal(barrier, inc=1, device_id=i, device_id_type=MESH)
    pl.semaphore_wait(barrier, len(ids))


def remote(src, dst, send, recv, device):
    return pltpu.make_async_remote_copy(
        src_ref=src, dst_ref=dst, send_sem=send, recv_sem=recv, device_id=device, device_id_type=MESH
    )


class Blocks:
    def __init__(self, axis, size, same, source, target, send, recv, local):
        self.axis, self.size, self.same = axis, size, same
        self.source, self.target = source, target
        self.send, self.recv, self.local = send, recv, local
        self.me = lax.axis_index(axis)

    @staticmethod
    def scratch(size):
        dma = pltpu.SemaphoreType.DMA
        return [dma((size - 1,)), dma((size - 1,)), dma]

    def peers(self):
        return [{self.axis: lax.rem(self.me + d, self.size)} for d in range(1, self.size)]

    def copy(self, d):
        to = lax.rem(self.me + d, self.size)
        src = self.source if self.same else self.source.at[to]
        return remote(src, self.target.at[self.me], self.send.at[d - 1], self.recv.at[d - 1], {self.axis: to})

    def own(self):
        src = self.source if self.same else self.source.at[self.me]
        return pltpu.make_async_copy(src, self.target.at[self.me], self.local)

    def start(self):
        for d in range(1, self.size):
            self.copy(d).start()
        self.own().start()

    def finish(self):
        for d in range(1, self.size):
            dst = self.target.at[lax.rem(self.me + self.size - d, self.size)]
            remote(dst, dst, self.send.at[d - 1], self.recv.at[d - 1], {self.axis: self.me}).wait_recv()
        self.own().wait()
        for d in range(1, self.size):
            self.copy(d).wait_send()


def blocks_shape(x, size, same):
    return jax.ShapeDtypeStruct(((size,) + x.shape) if same else x.shape, x.dtype)


def arrival_order(n):
    bits = route_bits(n)
    orders = [bits, bits[::-1]]
    lists = []
    for order in orders:
        held, phases = [0], [-1]
        for i, b in enumerate(order):
            fresh = [h ^ b for h in held]
            held, phases = held + fresh, phases + [i] * len(fresh)
        lists.append(list(zip(held, phases)))
    entries = []
    for i in range(n // 2):
        for odd in (0, 1):
            for half in (0, 1):
                k, phase = lists[half][i]
                entries.append((half, k ^ odd, phase, odd))
    return orders, entries


def gather_kernel(n, h, body, n_const, n_out, relative, modes, nf, same, second, *refs):
    if second:
        at = 1 + n_const
        out = at + 1 + min(nf, 1) + 1 + n_out
        w_ref, w_all = refs[at], refs[out]
        w_send, w_recv, w_keep = refs[-3:]
        refs = refs[:at] + refs[at + 1 : out] + refs[out + 1 : -3]
        w_half = w_ref.shape[1] // 2
    refs, rider = split_rider(refs, nf, same, 1 + n_const, 1 + n_out)
    x_ref = refs[0]
    consts = refs[1 : 1 + n_const]
    all_ref = refs[1 + n_const]
    outs = refs[2 + n_const : 2 + n_const + n_out]
    held = refs[2 + n_const + n_out]
    stages = refs[3 + n_const + n_out : 3 + n_const + 2 * n_out]
    send, recv, keep, store = refs[3 + n_const + 2 * n_out :]
    me = lax.axis_index("seq")
    orders, entries = arrival_order(n)
    bits = orders[0]
    nb = len(bits)

    def device(b):
        return {"seq": flip(me, b)}

    def spot(half, k):
        return 2 * (k if relative else place(me, k, n)) + half

    def ship(half, k, b):
        at = spot(half, k)
        src = x_ref.at[pl.ds(half * h, h)] if isinstance(k, int) and k == 0 else held.at[at]
        lane = 0 if b == 1 else 1 + bits.index(b)
        to = k ^ b if isinstance(k, int) else place(k, b, n)
        dst = 2 * to + half if relative else at
        first = remote(src, held.at[dst], send.at[half, lane, k], recv.at[half, to], device(b))
        if not second:
            return [first]
        owner = place(me, k, n)
        lanes = pl.ds(half * w_half, w_half)
        src = w_ref if isinstance(k, int) and k == 0 else w_all.at[owner]
        other = remote(
            src.at[:, lanes], w_all.at[owner].at[:, lanes], w_send.at[half, lane, k], w_recv.at[half, to], device(b)
        )
        return [first, other]

    def each(copies, act):
        for c in copies:
            act(c)

    def w_arrive(half, k):
        dst = w_all.at[place(me, k, n)].at[:, pl.ds(0, w_half)]
        remote(dst, dst, w_send.at[0, 0, 0], w_recv.at[half, k], device(1)).wait_recv()

    greet([device(b) for b in [1] + bits] + (rider.peers() if nf else []))
    for i in range(nb):
        for half in (0, 1):
            each(ship(half, 0, orders[half][i]), lambda c: c.start())
    for half in (0, 1):
        each(ship(half, 0, 1), lambda c: c.start())
    if second:
        pltpu.make_async_copy(w_ref, w_all.at[me], w_keep).start()
    if nf:
        rider.start()

    def output(o, q, at):
        slot = lax.rem(q, 2)
        return pltpu.make_async_copy(stages[o].at[slot], outs[o].at[at], store.at[o, slot])

    def entry(q, at, value):
        results = body(value, *consts)
        for o in range(n_out):

            @pl.when(q >= 2)
            def _(o=o):
                output(o, q, at[modes[o]]).wait()

            stages[o][lax.rem(q, 2)] = results[o]
            output(o, q, at[modes[o]]).start()

    def step(q, carry):
        half = pick([e[0] for e in entries], q)
        k = pick([e[1] for e in entries], q)
        phase = pick([e[2] for e in entries], q)
        odd = pick([e[3] for e in entries], q)
        at = spot(half, k)

        @pl.when(k == 0)
        def _():
            held[at] = x_ref[pl.ds(pl.multiple_of(half * h, h), h)]

        @pl.when(k != 0)
        def _():
            remote(held.at[at], held.at[at], send.at[0, 0, 0], recv.at[half, k], device(1)).wait_recv()
            if second:
                w_arrive(half, k)

        for side in (0, 1):
            for i in range(nb):

                @pl.when((half == side) & (odd == 0) & (k != 0) & (phase < i))
                def _(side=side, i=i):
                    each(ship(side, k, orders[side][i]), lambda c: c.start())

            @pl.when((half == side) & (odd == 0) & (k != 0))
            def _(side=side):
                each(ship(side, k, 1), lambda c: c.start())

        pltpu.make_async_copy(held.at[at], all_ref.at[at], keep.at[q]).start()
        if n_out:
            entry(q, (2 * place(me, k, n) + half, 2 * k + half), held[at])
        return carry

    lax.fori_loop(0, 2 * n, step, 0)
    for q, (half, k, phase, odd) in enumerate(entries):
        at = spot(half, k)
        pltpu.make_async_copy(held.at[at], all_ref.at[at], keep.at[q]).wait()
        if q >= 2 * n - 2:
            for o in range(n_out):
                output(o, jnp.int32(q), at).wait()
        if not odd:
            for i in range(nb):
                if phase < i:
                    each(ship(half, k, orders[half][i]), lambda c: c.wait_send())
            each(ship(half, k, 1), lambda c: c.wait_send())
    if second:
        pltpu.make_async_copy(w_ref, w_all.at[me], w_keep).wait()
    if nf:
        rider.finish()


def split_rider(refs, nf, same, n_in, n_out):
    if not nf:
        return refs, None
    source = refs[n_in]
    target = refs[n_in + 1 + n_out]
    rider = Blocks("fsdp", nf, same, source, target, *refs[-3:])
    return refs[:n_in] + refs[n_in + 1 : n_in + 1 + n_out] + refs[n_in + 2 + n_out : -3], rider


def rider_parts(rider):
    if rider is None:
        return [], [], [], [], 0, False
    x, same, nf = rider
    hbm = [pl.BlockSpec(memory_space=pl.ANY)]
    return [x], hbm, [blocks_shape(x, nf, same)], Blocks.scratch(nf), nf, same


def seq_gather(x, n, ident, name, body=None, consts=(), outs=(), relative=False, modes=None, rider=None, second=None):
    rows, cols = x.shape
    h = rows // 2
    nb = len(route_bits(n))
    shapes = [jax.ShapeDtypeStruct((2 * n, h, c), d) for c, d in outs]
    vmem = pl.BlockSpec(memory_space=pltpu.VMEM)
    hbm = pl.BlockSpec(memory_space=pl.ANY)
    more, spec, shape, scratch, nf, same = rider_parts(rider)
    also = [] if second is None else [second]
    out = pl.pallas_call(
        functools.partial(
            gather_kernel, n, h, body, len(consts), len(outs), relative, modes, nf, same, second is not None
        ),
        out_shape=[jax.ShapeDtypeStruct((2 * n, h, cols), x.dtype)]
        + shapes
        + [jax.ShapeDtypeStruct((n,) + w.shape, w.dtype) for w in also]
        + shape,
        in_specs=[vmem] * (1 + len(consts)) + [hbm] * len(also) + spec,
        out_specs=[hbm] * (1 + len(outs)) + [hbm] * len(also) + spec,
        scratch_shapes=[pltpu.VMEM((2 * n, h, cols), x.dtype)]
        + [pltpu.VMEM((2, h, c), d) for c, d in outs]
        + [
            pltpu.SemaphoreType.DMA((2, nb + 1, n)),
            pltpu.SemaphoreType.DMA((2, n)),
            pltpu.SemaphoreType.DMA((2 * n,)),
            pltpu.SemaphoreType.DMA((max(len(outs), 1), 2)),
        ]
        + scratch
        + [
            pltpu.SemaphoreType.DMA((2, nb + 1, n)),
            pltpu.SemaphoreType.DMA((2, n)),
            pltpu.SemaphoreType.DMA,
        ]
        * len(also),
        compiler_params=pltpu.CompilerParams(
            collective_id=ident, has_side_effects=True, vmem_limit_bytes=60 << 20
        ),
        cost_estimate=SMALL,
        name=name,
    )(x, *consts, *also, *more)
    return [o.reshape(2 * n * h, o.shape[2]) for o in out[: 1 + len(outs)]] + list(out[1 + len(outs) :])


class Side:
    def __init__(self, count, product, refs):
        self.count, self.product = count, product
        self.a, self.b, self.grad, self.made, self.acc, self.abuf, self.bbuf, self.mbuf, self.load, self.store = refs

    def fetch(self, i):
        slot = lax.rem(i, 2)
        return [
            pltpu.make_async_copy(self.a.at[i], self.abuf.at[slot], self.load.at[0, slot]),
            pltpu.make_async_copy(self.b.at[i], self.bbuf.at[slot], self.load.at[1, slot]),
        ]

    def output(self, i):
        slot = lax.rem(i, 2)
        return pltpu.make_async_copy(self.mbuf.at[slot], self.made.at[i], self.store.at[slot])

    def begin(self):
        self.acc[...] = jnp.zeros_like(self.acc)
        for c in self.fetch(jnp.int32(0)):
            c.start()

    def run(self, first, last):
        def step(i, carry):
            @pl.when(i + 1 < self.count)
            def _():
                for c in self.fetch(i + 1):
                    c.start()

            for c in self.fetch(i):
                c.wait()
            slot = lax.rem(i, 2)
            a, b = self.abuf[slot], self.bbuf[slot]
            self.acc[...] += lax.dot_general(
                a, b, (((0,), (0,)), ((), ())), preferred_element_type=jnp.float32
            )
            if self.product is not None:

                @pl.when(i >= 2)
                def _():
                    self.output(i).wait()

                self.mbuf[slot] = self.product(a)
                self.output(i).start()
            return carry

        lax.fori_loop(first, last, step, 0)

    def end(self):
        self.grad[...] = self.acc[...].astype(self.grad.dtype)
        if self.product is not None:
            for i in (self.count - 2, self.count - 1):
                self.output(jnp.int32(i)).wait()


def side_parts(side, count):
    if side is None:
        return [], [], [], [], []
    a, b, product, made = side
    h = a.shape[0] // count
    low = jnp.bfloat16
    made = made or 128
    hbm = pl.BlockSpec(memory_space=pl.ANY)
    vmem = pl.BlockSpec(memory_space=pltpu.VMEM)
    dma = pltpu.SemaphoreType.DMA
    return (
        [x.reshape(count, h, x.shape[1]) for x in (a, b)],
        [
            jax.ShapeDtypeStruct((a.shape[1], b.shape[1]), low),
            jax.ShapeDtypeStruct((count, h, made), low),
        ],
        [hbm, hbm],
        [vmem, hbm],
        [
            pltpu.VMEM((a.shape[1], b.shape[1]), jnp.float32),
            pltpu.VMEM((2, h, a.shape[1]), low),
            pltpu.VMEM((2, h, b.shape[1]), low),
            pltpu.VMEM((2, h, made), low),
            dma((2, 2)),
            dma((2,)),
        ],
    )


def scatter_order(n):
    bits = route_bits(n)
    orders = [bits, bits[::-1]]
    lists = [
        sorted(range(0, n, 2), key=lambda k: [-int(bool(k & b)) for b in order]) for order in orders
    ]
    return orders, [(half, lists[half][i]) for i in range(n // 2) for half in (0, 1)]


def scatter_kernel(n, h, body, n_in, n_const, n_out, modes, nf, same, product, *refs):
    side = None
    if product is not False:
        at = n_in + n_const
        out = at + 2 + min(nf, 1) + 1 + n_out
        extra = refs[at : at + 2] + refs[out : out + 2] + refs[-6:]
        refs = refs[:at] + refs[at + 2 : out] + refs[out + 2 : -6]
        consts = refs[n_in : n_in + n_const]
        make = None if product is None else lambda a: product(a, *consts)
        side = Side(2 * n, make, extra)
    refs, rider = split_rider(refs, nf, same, n_in + n_const, 1 + n_out)
    ins = refs[:n_in]
    consts = refs[n_in : n_in + n_const]
    at = n_in + n_const
    sum_ref = refs[at]
    outs = refs[at + 1 : at + 1 + n_out]
    at += 1 + n_out
    give, pair, own, far, total = refs[at : at + 5]
    at += 5
    loads = refs[at : at + n_in]
    stages = refs[at + n_in : at + n_in + n_out]
    pair_send, pair_recv, far_send, far_recv, load, store, done = refs[at + n_in + n_out :]
    me = lax.axis_index("seq")
    orders, entries = scatter_order(n)
    bits = orders[0]
    slots = give.shape[0]
    index = {e: j for j, e in enumerate(entries)}

    def device(b):
        return {"seq": flip(me, b)}

    def phase_of(half, k):
        for i, b in enumerate(orders[half]):
            if k & b:
                return i
        return len(bits)

    landing = {}
    for half in (0, 1):
        for i, b in enumerate(orders[half]):
            for k in range(0, n, 2):
                if phase_of(half, k) == i:
                    landing[half, i, k ^ b] = len(landing)

    halves = [e[0] for e in entries]
    ks = [e[1] for e in entries]

    def spot(q, relative):
        j = lax.div(q, 2)
        k = pick(ks, j)
        k = jnp.where(lax.rem(q, 2) == 0, flip(k, 1), k)
        return 2 * (k if relative else place(me, k, n)) + pick(halves, j)

    def fetch(q):
        slot = lax.rem(q, 2)
        return [
            pltpu.make_async_copy(ins[i].at[spot(q, modes[0][i])], loads[i].at[slot], load.at[i, slot])
            for i in range(n_in)
        ]

    def output(o, q):
        slot = lax.rem(q, 2)
        return pltpu.make_async_copy(stages[o].at[slot], outs[o].at[spot(q, modes[1][o])], store.at[o, slot])

    def hand(j):
        slot = lax.rem(j, slots)
        return remote(give.at[slot], pair.at[j], pair_send.at[j], pair_recv.at[j], device(1))

    def launch(half, k):
        i = phase_of(half, k)
        b = orders[half][i]
        to = landing[half, i, k ^ b]
        return remote(own.at[index[half, k]], far.at[to], far_send.at[to], far_recv.at[to], device(b))

    def join(j):
        hand(j).wait_recv()
        own[j] = (own[j].astype(jnp.float32) + pair[j].astype(jnp.float32)).astype(own.dtype)
        for e, (half, k) in enumerate(entries):
            if phase_of(half, k) == 0:

                @pl.when(j == e)
                def _(half=half, k=k):
                    launch(half, k).start()

    for c in fetch(jnp.int32(0)):
        c.start()
    greet([device(b) for b in [1] + bits] + (rider.peers() if nf else []))
    if nf:
        rider.start()

    def step(q, carry):
        j = lax.div(q, 2)
        slot = lax.rem(q, 2)

        @pl.when(q + 1 < 2 * n)
        def _():
            for c in fetch(q + 1):
                c.start()

        for c in fetch(q):
            c.wait()
        part, *results = body(*[r[slot] for r in loads], *consts)
        for o in range(n_out):

            @pl.when(q >= 2)
            def _(o=o):
                output(o, q).wait()

            stages[o][slot] = results[o]
            output(o, q).start()

        @pl.when(slot == 0)
        def _():
            @pl.when(j >= slots)
            def _():
                hand(j - slots).wait_send()

            give[lax.rem(j, slots)] = part.astype(give.dtype)
            hand(j).start()

        @pl.when(slot == 1)
        def _():
            own[j] = part.astype(own.dtype)

            @pl.when(j >= 1)
            def _():
                join(j - 1)

        return carry

    lax.fori_loop(0, 2 * n, step, 0)
    if side:
        side.begin()
    join(jnp.int32(n - 1))
    first = n // 2
    cuts = [0, first] + [first + (2 * n - first) * i // (len(bits) - 1) for i in range(1, len(bits))]
    for i in range(len(bits)):
        if side:
            side.run(cuts[i], cuts[i + 1])
        for half in (0, 1):
            order = orders[half]
            for k in [k for hh, k in entries if hh == half and phase_of(half, k) > i]:
                to = landing[half, i, k]
                remote(far.at[to], far.at[to], far_send.at[to], far_recv.at[to], device(1)).wait_recv()
                j = index[half, k]
                rows = pl.ds(half * h, h)
                if i == len(bits) - 1:
                    total[rows] = own[j].astype(jnp.float32) + far[to].astype(jnp.float32)
                    pltpu.make_async_copy(total.at[rows], sum_ref.at[rows], done.at[half]).start()
                else:
                    own[j] = (own[j].astype(jnp.float32) + far[to].astype(jnp.float32)).astype(own.dtype)
                    if phase_of(half, k) == i + 1:
                        launch(half, k).start()
    for half in (0, 1):
        rows = pl.ds(half * h, h)
        pltpu.make_async_copy(total.at[rows], sum_ref.at[rows], done.at[half]).wait()
    for q in (2 * n - 2, 2 * n - 1):
        for o in range(n_out):
            output(o, jnp.int32(q)).wait()
    for j in range(max(n - slots, 0), n):
        hand(jnp.int32(j)).wait_send()
    for half, k in entries:
        if phase_of(half, k) < len(bits):
            launch(half, k).wait_send()
    if nf:
        rider.finish()
    if side:
        side.end()


def seq_scatter(n, cols, ident, name, body, ins, consts, outs=(), modes=None, rider=None, side=None):
    h = ins[0].shape[0] // (2 * n)
    low = jnp.bfloat16
    slots = min(4, n)
    split = [a.reshape(2 * n, h, a.shape[1]) for a in ins]
    vmem = pl.BlockSpec(memory_space=pltpu.VMEM)
    hbm = pl.BlockSpec(memory_space=pl.ANY)
    reach = n - 2
    modes = modes or ([0] * len(ins), [0] * len(outs))
    more, spec, shape, scratch, nf, same = rider_parts(rider)
    s_ins, s_shapes, s_in_specs, s_out_specs, s_scratch = side_parts(side, 2 * n)
    product = False if side is None else side[2]
    out = pl.pallas_call(
        functools.partial(
            scatter_kernel, n, h, body, len(ins), len(consts), len(outs), modes, nf, same, product
        ),
        out_shape=[jax.ShapeDtypeStruct((2 * h, cols), jnp.float32)]
        + [jax.ShapeDtypeStruct((2 * n, h, c), d) for c, d in outs]
        + s_shapes
        + shape,
        in_specs=[hbm] * len(ins) + [vmem] * len(consts) + s_in_specs + spec,
        out_specs=[hbm] * (1 + len(outs)) + s_out_specs + spec,
        scratch_shapes=[
            pltpu.VMEM((slots, h, cols), low),
            pltpu.VMEM((n, h, cols), low),
            pltpu.VMEM((n, h, cols), low),
            pltpu.VMEM((reach, h, cols), low),
            pltpu.VMEM((2 * h, cols), jnp.float32),
        ]
        + [pltpu.VMEM((2, h, a.shape[2]), a.dtype) for a in split]
        + [pltpu.VMEM((2, h, c), d) for c, d in outs]
        + [
            pltpu.SemaphoreType.DMA((n,)),
            pltpu.SemaphoreType.DMA((n,)),
            pltpu.SemaphoreType.DMA((reach,)),
            pltpu.SemaphoreType.DMA((reach,)),
            pltpu.SemaphoreType.DMA((len(ins), 2)),
            pltpu.SemaphoreType.DMA((max(len(outs), 1), 2)),
            pltpu.SemaphoreType.DMA((2,)),
        ]
        + scratch
        + s_scratch,
        compiler_params=pltpu.CompilerParams(
            collective_id=ident, has_side_effects=True, vmem_limit_bytes=60 << 20
        ),
        cost_estimate=SMALL,
        name=name,
    )(*split, *consts, *s_ins, *more)
    many = 1 + len(outs)
    sides = [] if side is None else [out[many], out[many + 1].reshape(2 * n * h, -1)]
    more = list(out[many + len(sides) :])
    return [out[0]] + [o.reshape(2 * n * h, o.shape[2]) for o in out[1:many]] + sides + more


class Rows:
    def __init__(self, n, held, width, wide, back):
        moves = []
        for to in range(n):
            for third in range(3):
                at, end = third * width + to * wide, third * width + min((to + 1) * wide, width)
                row = third * wide
                while at < end:
                    source = at // held
                    count = min(end, (source + 1) * held) - at
                    moves.append((source, at - source * held, to, row, count))
                    at, row = at + count, row + count
        self.n = n
        self.moves = [(c, d, a, b, e) if back else (a, b, c, d, e) for a, b, c, d, e in moves]
        self.out = [[m for m in self.moves if m[0] == i] for i in range(n)]
        self.into = [[m for m in self.moves if m[2] == i] for i in range(n)]
        self.most = max(len(v) for v in self.out + self.into)

    def scratch(self):
        dma = pltpu.SemaphoreType.DMA
        return [dma((self.most,)), dma((self.most,)), dma((self.most,))]

    def bind(self, source, target, send, recv, local):
        self.source, self.target, self.send, self.recv, self.local = source, target, send, recv, local
        return self

    def copy(self, i, m):
        src = self.source.at[pl.ds(m[1], m[4])]
        dst = self.target.at[pl.ds(m[3], m[4])]
        if m[0] == m[2]:
            return pltpu.make_async_copy(src, dst, self.local.at[i])
        return remote(src, dst, self.send.at[i], self.recv.at[self.into[m[2]].index(m)], {"seq": m[2]})

    def start(self):
        me = lax.axis_index("seq")
        for s in range(self.n):

            @pl.when(me == s)
            def _(s=s):
                for i, m in enumerate(self.out[s]):
                    self.copy(i, m).start()

    def finish(self):
        me = lax.axis_index("seq")
        for s in range(self.n):

            @pl.when(me == s)
            def _(s=s):
                for i, m in enumerate(self.into[s]):
                    if m[0] != s:
                        dst = self.target.at[pl.ds(m[3], m[4])]
                        remote(dst, dst, self.send.at[0], self.recv.at[i], {"seq": s}).wait_recv()
                for i, m in enumerate(self.out[s]):
                    if m[0] == m[2]:
                        self.copy(i, m).wait()
                    else:
                        self.copy(i, m).wait_send()


class Units:
    def __init__(self, n, nf, back, source, target, send, recv, local):
        self.n, self.nf, self.back = n, nf, back
        self.source, self.target, self.send, self.recv, self.local = source, target, send, recv, local
        self.me = lax.axis_index("seq")

    @staticmethod
    def scratch(nf):
        dma = pltpu.SemaphoreType.DMA
        return [dma((nf,)), dma((nf,)), dma]

    def ends(self, i):
        group = self.n // self.nf
        if self.back:
            return i * group + lax.div(self.me, self.nf), lax.rem(self.me, self.nf)
        return lax.rem(self.me, group) * self.nf + i, lax.div(self.me, group)

    def comes(self, i):
        group = self.n // self.nf
        if self.back:
            return lax.rem(self.me, group) * self.nf + i
        return i * group + lax.div(self.me, self.nf)

    def each(self, i, there, here):
        to, slot = self.ends(i)

        @pl.when(to != self.me)
        def _():
            there(remote(self.source.at[i], self.target.at[slot], self.send.at[i], self.recv.at[slot], {"seq": to}))

        @pl.when(to == self.me)
        def _():
            here(pltpu.make_async_copy(self.source.at[i], self.target.at[slot], self.local))

    def start(self):
        for i in range(self.nf):
            self.each(i, lambda c: c.start(), lambda c: c.start())

    def finish(self):
        for i in range(self.nf):
            source = self.comes(i)

            @pl.when(source != self.me)
            def _(i=i):
                dst = self.target.at[i]
                remote(dst, dst, self.send.at[0], self.recv.at[i], {"seq": self.me}).wait_recv()

        for i in range(self.nf):
            self.each(i, lambda c: c.wait_send(), lambda c: c.wait())


def all_peers(n, nf):
    me, f = lax.axis_index("seq"), lax.axis_index("fsdp")
    return [{"seq": place(me, r, n)} for r in range(1, n)] + [
        {"fsdp": lax.rem(f + d, nf)} for d in range(1, nf)
    ]


def exchange_kernel(n, nf, rows, count, *refs):
    ins, outs, sems = refs[: 4 + count], refs[4 + count : 8 + 2 * count], list(refs[8 + 2 * count :])
    take = lambda k: [sems.pop(0) for _ in range(k)]
    parts = []
    if rows is not None:
        parts.append(rows.bind(ins[0], outs[0], *take(3)))
    vectors = [Blocks("fsdp", nf, True, ins[4 + i], outs[4 + i], *take(3)) for i in range(count)]
    later = [
        Blocks("fsdp", nf, True, ins[3], outs[3], *take(3)),
        Units(n, nf, False, ins[2], outs[2], *take(3)),
        Blocks("seq", n, False, ins[1], outs[1], *take(3)),
    ]
    parts = vectors + parts + later
    greet(all_peers(n, nf))
    for p in parts:
        p.start()
    for p in parts:
        p.finish()


def exchange(w, p, c, o, vectors, n, nf, rows, wide, ident):
    hbm = pl.BlockSpec(memory_space=pl.ANY)
    count = len(vectors)
    out = pl.pallas_call(
        functools.partial(exchange_kernel, n, nf, rows, count),
        out_shape=[
            jax.ShapeDtypeStruct((3 * wide, w.shape[1]) if rows is not None else w.shape, w.dtype),
            blocks_shape(p, n, False),
            blocks_shape(c, nf, False),
            blocks_shape(o, nf, True),
        ]
        + [blocks_shape(v, nf, True) for v in vectors],
        in_specs=[hbm] * (4 + count),
        out_specs=[hbm] * (4 + count),
        scratch_shapes=(rows.scratch() if rows is not None else [])
        + sum([Blocks.scratch(nf) for _ in vectors], [])
        + Blocks.scratch(nf)
        + Units.scratch(nf)
        + Blocks.scratch(n),
        compiler_params=pltpu.CompilerParams(collective_id=ident, has_side_effects=True),
        cost_estimate=SMALL,
        name="exchange",
    )(w, p, c, o, *vectors)
    return out[0], out[1], out[2], out[3], out[4:]


def to_tokens_kernel(n, wide, x_ref, o_ref, send, recv, local):
    me = lax.axis_index("seq")

    def target(i):
        return o_ref.at[:, pl.ds(pl.multiple_of(i * wide, 128), wide)]

    greet([{"seq": place(me, r, n)} for r in range(1, n)])
    copies = []
    for r in range(n - 1, 0, -1):
        to = place(me, r, n)
        c = remote(x_ref.at[to], target(me), send.at[r - 1], recv.at[r - 1], {"seq": to})
        c.start()
        copies.append(c)
    mine = pltpu.make_async_copy(x_ref.at[me], target(me), local)
    mine.start()
    for r in range(1, n):
        dst = target(place(me, r, n))
        remote(dst, dst, send.at[0], recv.at[r - 1], {"seq": place(me, r, n)}).wait_recv()
    mine.wait()
    for c in copies:
        c.wait_send()


def to_tokens(x, n, wide, ident):
    rows = x.shape[1]
    hbm = pl.BlockSpec(memory_space=pl.ANY)
    return pl.pallas_call(
        functools.partial(to_tokens_kernel, n, wide),
        out_shape=jax.ShapeDtypeStruct((rows, n * wide), x.dtype),
        in_specs=[hbm],
        out_specs=hbm,
        scratch_shapes=Blocks.scratch(n),
        compiler_params=pltpu.CompilerParams(collective_id=ident, has_side_effects=True),
        cost_estimate=SMALL,
        name="to_tokens",
    )(x)


def to_heads_kernel(n, wide, x_ref, w_ref, a_ref, b_ref, o_ref, g_ref, m_ref, made, send, recv, local, *extra):
    me = lax.axis_index("seq")
    side = Side(2 * n, None, (a_ref, b_ref, g_ref, m_ref) + extra)
    side.begin()
    greet([{"seq": place(me, r, n)} for r in range(1, n)])

    def copy(r):
        to = place(me, r, n)
        return remote(made.at[r], o_ref.at[me], send.at[r - 1], recv.at[r - 1], {"seq": to})

    def mine():
        return pltpu.make_async_copy(made.at[0], o_ref.at[me], local)

    def step(i, carry):
        r = n - 1 - i
        lanes = pl.ds(pl.multiple_of(place(me, r, n) * wide, 128), wide)
        made[r] = mm(x_ref[...], w_ref[:, lanes]).astype(made.dtype)

        @pl.when(r > 0)
        def _():
            copy(r).start()

        return carry

    lax.fori_loop(0, n, step, 0)
    mine().start()
    side.run(0, 2 * n)
    for r in range(1, n):
        dst = o_ref.at[place(me, r, n)]
        remote(dst, dst, send.at[0], recv.at[r - 1], {"seq": me}).wait_recv()
    mine().wait()
    for r in range(1, n):
        copy(r).wait_send()
    side.end()


def to_heads(x, w, n, wide, ident, a, b):
    rows = x.shape[0]
    vmem = pl.BlockSpec(memory_space=pltpu.VMEM)
    hbm = pl.BlockSpec(memory_space=pl.ANY)
    s_ins, s_shapes, s_in_specs, s_out_specs, s_scratch = side_parts((a, b, None, 0), 2 * n)
    out = pl.pallas_call(
        functools.partial(to_heads_kernel, n, wide),
        out_shape=[jax.ShapeDtypeStruct((n, rows, wide), x.dtype)] + s_shapes,
        in_specs=[vmem, vmem] + s_in_specs,
        out_specs=[hbm] + s_out_specs,
        scratch_shapes=[pltpu.VMEM((n, rows, wide), x.dtype)] + Blocks.scratch(n) + s_scratch,
        compiler_params=pltpu.CompilerParams(
            collective_id=ident, has_side_effects=True, vmem_limit_bytes=60 << 20
        ),
        cost_estimate=SMALL,
        name="to_heads",
    )(x, w, *s_ins)
    return out[0], out[1]


def project_kernel(x_ref, w_ref, b_ref, o_ref):
    o_ref[...] = (mm(x_ref[...], w_ref[...]) + b_ref[...]).astype(o_ref.dtype)


def project(x, w, bias, tile):
    rows, cols = x.shape[0], w.shape[1]
    still = lambda shape: pl.BlockSpec(shape, lambda i: (0, 0), pipeline_mode=pl.Buffered(1))
    return pl.pallas_call(
        project_kernel,
        out_shape=jax.ShapeDtypeStruct((rows, cols), x.dtype),
        grid=(rows // tile,),
        in_specs=[pl.BlockSpec((tile, x.shape[1]), lambda i: (i, 0)), still(w.shape), still((1, cols))],
        out_specs=pl.BlockSpec((tile, cols), lambda i: (i, 0)),
        compiler_params=pltpu.CompilerParams(vmem_limit_bytes=40 << 20),
        cost_estimate=SMALL,
        name="project",
    )(x, w, bias)


def contract_kernel(a_ref, b_ref, ready, o_ref, acc):
    i = pl.program_id(0)
    part = lax.dot_general(
        a_ref[...], b_ref[...], (((0,), (0,)), ((), ())), preferred_element_type=jnp.float32
    )

    @pl.when(i == 0)
    def _():
        acc[...] = part

    @pl.when(i > 0)
    def _():
        acc[...] += part

    @pl.when(i == pl.num_programs(0) - 1)
    def _():
        o_ref[...] = acc[...].astype(o_ref.dtype)


def contract(a, b, ready, tile):
    rows = a.shape[0]
    shape = (a.shape[1], b.shape[1])
    still = lambda s: pl.BlockSpec(s, lambda i: (0,) * len(s), pipeline_mode=pl.Buffered(1))
    return pl.pallas_call(
        contract_kernel,
        out_shape=jax.ShapeDtypeStruct(shape, a.dtype),
        grid=(rows // tile,),
        in_specs=[
            pl.BlockSpec((tile, shape[0]), lambda i: (i, 0)),
            pl.BlockSpec((tile, shape[1]), lambda i: (i, 0)),
            still(ready.shape),
        ],
        out_specs=still(shape),
        scratch_shapes=[pltpu.VMEM(shape, jnp.float32)],
        compiler_params=pltpu.CompilerParams(
            dimension_semantics=("arbitrary",), vmem_limit_bytes=40 << 20
        ),
        cost_estimate=SMALL,
        name="contract",
    )(a, b, ready)


def give_back_kernel(
    n, nf, rows, v_ref, w_ref, p_ref, c_ref, o_ref, v_out, w_out, p_out, c_out, o_out, planes, sums, *sems
):
    s = lax.axis_index("seq")
    f = lax.axis_index("fsdp")
    sems = list(sems)
    take = lambda k: [sems.pop(0) for _ in range(k)]
    send_z, recv_z, send_s, recv_s = take(4)
    parts = []
    if rows is not None:
        parts.append(rows.bind(w_ref, w_out, *take(3)))
    parts.append(Units(n, nf, True, c_ref, c_out, *take(3)))
    parts.append(Blocks("seq", n, False, p_ref, p_out, *take(3)))
    parts.append(Blocks("fsdp", nf, False, o_ref, o_out, *take(3)))
    others = [{"fsdp": lax.rem(f + d, nf)} for d in range(1, nf)]
    peers = [{"seq": place(s, r, n)} for r in range(1, n)]
    greet(peers + others)
    copies = []
    for d in range(1, nf):
        c = remote(v_ref.at[lax.rem(f + d, nf)], planes.at[d - 1], send_z.at[d - 1], recv_z.at[d - 1], others[d - 1])
        c.start()
        copies.append(c)
    for p in parts[:1]:
        p.start()
    total = v_ref[f]
    for d, c in enumerate(copies):
        c.wait_recv()
        total = total + planes[d]
    sums[0] = total
    spread = []
    for r in range(1, n):
        c = remote(sums.at[0], sums.at[r], send_s.at[r - 1], recv_s.at[r - 1], peers[r - 1])
        c.start()
        spread.append(c)
    for p in parts[1:]:
        p.start()
    for r, c in enumerate(spread):
        c.wait_recv()
        total = total + sums[r + 1]
    v_out[...] = total
    for p in parts:
        p.finish()
    for c in copies + spread:
        c.wait_send()


def give_back(vectors, w, held, p, c, o, n, nf, rows, ident):
    k = vectors.shape[1]
    tiles = -(-k // 1024) * 8
    padded = jnp.pad(vectors, ((0, 0), (0, tiles * 128 - k))).reshape(nf, tiles, 128)
    vmem = pl.BlockSpec(memory_space=pltpu.VMEM)
    hbm = pl.BlockSpec(memory_space=pl.ANY)
    dma = pltpu.SemaphoreType.DMA
    out = pl.pallas_call(
        functools.partial(give_back_kernel, n, nf, rows),
        out_shape=[
            jax.ShapeDtypeStruct((tiles, 128), jnp.float32),
            jax.ShapeDtypeStruct((held, w.shape[1]), w.dtype),
            blocks_shape(p, n, False),
            blocks_shape(c, nf, False),
            blocks_shape(o, nf, False),
        ],
        in_specs=[vmem, hbm, hbm, hbm, hbm],
        out_specs=[vmem, hbm, hbm, hbm, hbm],
        scratch_shapes=[
            pltpu.VMEM((nf - 1, tiles, 128), jnp.float32),
            pltpu.VMEM((n, tiles, 128), jnp.float32),
            dma((nf - 1,)),
            dma((nf - 1,)),
            dma((n - 1,)),
            dma((n - 1,)),
        ]
        + (rows.scratch() if rows is not None else [])
        + Units.scratch(nf)
        + Blocks.scratch(n)
        + Blocks.scratch(nf),
        compiler_params=pltpu.CompilerParams(collective_id=ident, has_side_effects=True),
        cost_estimate=SMALL,
        name="give_back",
    )(padded, w, p, c, o)
    return out[0].reshape(-1)[:k], out[1], out[2], out[3], out[4]


HEAD=64
SCALE=0.125*math.log2(math.e)

def block_table(lengths, parents, slots, trunk, block):
    count=lengths.shape[0]
    branches=count//3
    fixed,owner,child=[],[],[]
    for t in range(slots):
        m=t-trunk
        if t<trunk:
            keys=[(c,0 if c==t else block,-1,-1) for c in range(t+1)]
        else:
            keys=[(c,block,-1,-1) for c in range(trunk)]
            if m>=branches:
                keys.append((trunk-1,block,-1,m))
            keys.append((t,0,m,-1))
        for i,(c,shift,own,leaf) in enumerate(keys):
            fixed.append((t,c,shift,int(i==0),int(i==len(keys)-1)))
            owner.append(own)
            child.append(leaf)
    fixed=np.array(fixed,np.int32).T
    segments=np.arange(count)
    own=np.array(owner)[None,:]==segments[:,None]
    leaf=np.array(child)[None,:]==segments[:,None]
    above=jnp.sum(jnp.where(leaf,parents[:,None],0),0)
    source=own|(segments[:,None]+1==above[None,:])
    closed=(np.array(owner)<0)&(np.array(child)<0)
    reach=jnp.where(closed,block,jnp.sum(jnp.where(source,lengths[:,None],0),0))
    masked=jnp.where((fixed[2]==0)|(reach<block),1,0)
    return jnp.stack([fixed[0],fixed[1]+above,fixed[2],reach,masked,fixed[3],fixed[4]]).astype(jnp.int32)

def lane_half(shape):
    return lax.broadcasted_iota(jnp.int32,shape,len(shape)-1)<HEAD

def nt(a,b):
    return lax.dot_general(a,b,(((1,),(1,)),((),())),preferred_element_type=jnp.float32)

def mm(a,b):
    return jnp.dot(a,b,preferred_element_type=jnp.float32)

def attend_kernel(width, block, tab, qkv, low, att, tot, acc):
    p=pl.program_id(0)
    qs,ks,shift,count,masked=tab[0,p],tab[1,p],tab[2,p],tab[3,p],tab[4,p]
    first,last=tab[5,p],tab[6,p]
    qrow=pl.ds(pl.multiple_of(qs*block,block),block)
    krow=pl.ds(pl.multiple_of(ks*block,block),block)
    left=lane_half((block,2*HEAD))
    @pl.when(first==1)
    def _(): acc[...]=jnp.zeros_like(acc)
    def step(mask):
        for j in range(width//(2*HEAD)):
            q=qkv[qrow,j*2*HEAD:(j+1)*2*HEAD]
            k=qkv[krow,width+j*2*HEAD:width+(j+1)*2*HEAD]
            v=qkv[krow,2*width+j*2*HEAD:2*width+(j+1)*2*HEAD]
            for h in range(2):
                here=left if h==0 else jnp.logical_not(left)
                s=nt(jnp.where(here,q,0),k)
                e=jnp.exp2(s*SCALE)
                if mask is not None: e=jnp.where(mask,e,0.0)
                acc[2*j+h]+=mm(e.astype(jnp.bfloat16),jnp.where(here,v,1))
    @pl.when(masked==0)
    def _(): step(None)
    @pl.when(masked==1)
    def _():
        row=lax.broadcasted_iota(jnp.int32,(block,block),0)
        col=lax.broadcasted_iota(jnp.int32,(block,block),1)
        step((col<=row+shift)&(col<count))
    @pl.when(last==1)
    def _():
        for j in range(width//(2*HEAD)):
            a,b=acc[2*j],acc[2*j+1]
            total=jnp.where(left,pltpu.roll(a,HEAD,1),pltpu.roll(b,HEAD,1))
            value=jnp.where(left,a,b)/total
            lanes=slice(j*2*HEAD,(j+1)*2*HEAD)
            low[:,lanes]=value.astype(jnp.bfloat16)
            att[:,lanes]=value
            tot[:,lanes]=total

def attend(table, qkv, block):
    rows,width=qkv.shape[0],qkv.shape[1]//3
    steps=table.shape[1]
    by_q=lambda p,t:(t[0,p],0)
    heads=width//HEAD
    return pl.pallas_call(functools.partial(attend_kernel,width,block),
        out_shape=(jax.ShapeDtypeStruct((rows,width),jnp.bfloat16),jax.ShapeDtypeStruct((rows,width),jnp.float32),jax.ShapeDtypeStruct((rows,width),jnp.float32)),
        grid_spec=pltpu.PrefetchScalarGridSpec(num_scalar_prefetch=1,grid=(steps,),
            in_specs=[pl.BlockSpec((rows,3*width),lambda p,t:(0,0),pipeline_mode=pl.Buffered(1))],
            out_specs=[pl.BlockSpec((block,width),by_q)]*3,
            scratch_shapes=[pltpu.VMEM((heads,block,2*HEAD),jnp.float32)]),
        compiler_params=pltpu.CompilerParams(dimension_semantics=("arbitrary",),vmem_limit_bytes=50<<20),
        cost_estimate=SMALL,
        name="attend")(table,qkv)

def attend_back_kernel(width, block, tab, qkv, kt, datt, att, tot, out, dk, dv, dqt, aug):
    p=pl.program_id(0)
    qs,ks,shift,count,masked=tab[0,p],tab[1,p],tab[2,p],tab[3,p],tab[4,p]
    first,last=tab[5,p],tab[6,p]
    qrow=pl.ds(pl.multiple_of(qs*block,block),block)
    krow=pl.ds(pl.multiple_of(ks*block,block),block)
    left=lane_half((block,2*HEAD))
    lane=lax.broadcasted_iota(jnp.int32,(block,2*HEAD),1)
    pairs=width//(2*HEAD)
    @pl.when(p==0)
    def _():
        dk[...]=jnp.zeros_like(dk)
        dv[...]=jnp.zeros_like(dv)
    @pl.when(first==1)
    def _():
        dqt[...]=jnp.zeros_like(dqt)
        for j in range(pairs):
            lanes=slice(j*2*HEAD,(j+1)*2*HEAD)
            d=datt[:,lanes].astype(jnp.float32)
            total=tot[:,lanes]
            low=(d/total).astype(jnp.bfloat16)
            prod=d*att[:,lanes]/total
            for h in range(2):
                here=left if h==0 else jnp.logical_not(left)
                delta=-jnp.sum(jnp.where(here,prod,0.0),1,keepdims=True)
                hi=delta.astype(jnp.bfloat16).astype(jnp.float32)
                mid=(delta-hi).astype(jnp.bfloat16).astype(jnp.float32)
                rest=delta-hi-mid
                at=HEAD*(1-h)
                extra=jnp.where(lane==at,hi,jnp.where(lane==at+1,mid,jnp.where(lane==at+2,rest,0.0)))
                aug[2*j+h]=jnp.where(here,low.astype(jnp.float32),extra).astype(jnp.bfloat16)
    def step(mask):
        for j in range(pairs):
            q=qkv[qrow,j*2*HEAD:(j+1)*2*HEAD]
            k=qkv[krow,width+j*2*HEAD:width+(j+1)*2*HEAD]
            v=qkv[krow,2*width+j*2*HEAD:2*width+(j+1)*2*HEAD]
            lanes=slice(j*2*HEAD,(j+1)*2*HEAD)
            dvs,dks=[],[]
            for h in range(2):
                here=left if h==0 else jnp.logical_not(left)
                qh=jnp.where(here,q,0)
                e=jnp.exp2(nt(k,qh)*SCALE)
                if mask is not None: e=jnp.where(mask,e,0.0)
                dod=aug[2*j+h]
                ds=(e*nt(jnp.where(here,v*0.125,0.125).astype(jnp.bfloat16),dod)).astype(jnp.bfloat16)
                dvs.append(mm(e.astype(jnp.bfloat16),dod))
                dks.append(mm(ds,qh))
                at=j*2*HEAD+h*HEAD
                dqt[at:at+HEAD]+=mm(kt[at:at+HEAD,krow],ds)
            dv[krow,lanes]+=jnp.where(left,dvs[0],dvs[1])
            dk[krow,lanes]+=dks[0]+dks[1]
    @pl.when(masked==0)
    def _(): step(None)
    @pl.when(masked==1)
    def _():
        col=lax.broadcasted_iota(jnp.int32,(block,block),0)
        row=lax.broadcasted_iota(jnp.int32,(block,block),1)
        step((col<=row+shift)&(col<count))
    @pl.when(last==1)
    def _():
        out[qrow,0:width]=dqt[...].T.astype(jnp.bfloat16)
    @pl.when(p==pl.num_programs(0)-1)
    def _():
        out[:,width:2*width]=dk[...].astype(jnp.bfloat16)
        out[:,2*width:]=dv[...].astype(jnp.bfloat16)

def attend_back(table, qkv, datt, att, tot, block):
    rows,width=qkv.shape[0],qkv.shape[1]//3
    steps=table.shape[1]
    by_q=lambda p,t:(t[0,p],0)
    heads=width//HEAD
    kt=qkv[:,width:2*width].T
    whole=lambda s:pl.BlockSpec(s,lambda p,t:(0,0),pipeline_mode=pl.Buffered(1))
    return pl.pallas_call(functools.partial(attend_back_kernel,width,block),
        out_shape=jax.ShapeDtypeStruct((rows,3*width),jnp.bfloat16),
        grid_spec=pltpu.PrefetchScalarGridSpec(num_scalar_prefetch=1,grid=(steps,),
            in_specs=[whole((rows,3*width)),whole((width,rows))]+[pl.BlockSpec((block,width),by_q)]*3,
            out_specs=whole((rows,3*width)),
            scratch_shapes=[pltpu.VMEM((rows,width),jnp.float32),pltpu.VMEM((rows,width),jnp.float32),pltpu.VMEM((width,block),jnp.float32),pltpu.VMEM((heads,block,2*HEAD),jnp.bfloat16)]),
        compiler_params=pltpu.CompilerParams(dimension_semantics=("arbitrary",),vmem_limit_bytes=60<<20),
        cost_estimate=SMALL,
        name="attend_back")(table,qkv,kt,datt,att,tot)


def layer_norm(values, gain, shift):
    centred = values - jnp.mean(values, -1, keepdims=True)
    spread = jnp.mean(centred * centred, -1, keepdims=True)
    return centred * lax.rsqrt(spread + 1e-05) * gain + shift


def contract_rows(left, right):
    return lax.dot_general(
        left, right, (((0,), (0,)), ((), ())), preferred_element_type=jnp.float32
    )


def contract_cols(left, right):
    return lax.dot_general(
        left, right, (((1,), (1,)), ((), ())), preferred_element_type=jnp.float32
    )


def after(value, other):
    return value + (other[(0,) * other.ndim] * 0).astype(value.dtype)


def row_major(x):
    return with_layout_constraint(x, Layout(major_to_minor=tuple(range(x.ndim))))


def local(
    tokens,
    ln1_gain,
    ln1_bias,
    qkv_weight,
    qv_bias,
    out_weight,
    out_bias,
    ln2_gain,
    ln2_bias,
    fc_weight,
    fc_bias,
    proj_weight,
    proj_bias,
    seg_lengths,
    parents,
    cotangent,
):
    n = lax.axis_size("seq")
    nf = lax.axis_size("fsdp")
    s = lax.axis_index("seq")
    f = lax.axis_index("fsdp")
    trunk = n // 4
    block, width = tokens.shape[1], tokens.shape[2]
    rows = width // nf
    hidden = fc_weight.shape[1] * n
    piece = hidden // (n * nf)
    group = n // nf
    wide = 2 * HEAD * (-(-HEADS // (2 * n)))
    low = jnp.bfloat16
    wider = jnp.float32

    vectors = [ln1_gain, ln1_bias, qv_bias, out_bias, ln2_gain, ln2_bias, fc_bias, proj_bias]
    sizes = [v.shape[0] for v in vectors]
    qkv_cols = qkv_weight.shape[1]
    even = qkv_cols % 8 == 0
    forth = Rows(n, qkv_cols, width, wide, False) if even else None
    back = Rows(n, qkv_cols, width, wide, True) if even else None
    turned, proj_blocks, fc_blocks, out_blocks, gathered = exchange(
        qkv_weight.T,
        proj_weight.reshape(n, piece, width // n),
        fc_weight.reshape(rows, nf, piece).transpose(1, 0, 2),
        out_weight,
        [v.reshape(1, -1) for v in vectors],
        n,
        nf,
        forth,
        wide,
        0,
    )
    whole = [v.reshape(-1).astype(wider) for v in gathered]
    gain_one, shift_one, bias_qv, bias_out, gain_two, shift_two, bias_fc, bias_proj = whole
    bias_three = jnp.stack([bias_qv[:width], jnp.zeros((width,), wider), bias_qv[width:]])
    bias_three = jnp.pad(bias_three, ((0, 0), (0, n * wide - width)))
    bias_mine = lax.dynamic_slice_in_dim(bias_three, s * wide, wide, 1).reshape(1, -1)
    bias_hidden = lax.dynamic_index_in_dim(bias_fc.reshape(nf, n, piece), s, 1, False)
    bias_hidden = bias_hidden.reshape(1, -1)

    if even:
        turned = turned.reshape(3, wide, rows)
        kept = lax.broadcasted_iota(jnp.int32, turned.shape, 1) + s * wide < width
        turned = jnp.where(kept, turned, 0).reshape(3 * wide, rows)
    else:
        turned = lax.all_gather(qkv_weight.T, "seq", axis=0, tiled=True).reshape(3, width, rows)
        turned = jnp.pad(turned, ((0, 0), (0, n * wide - width), (0, 0)))
        turned = lax.dynamic_slice_in_dim(turned, s * wide, wide, 1).reshape(3 * wide, rows)
    table = block_table(seg_lengths[0], parents[0], n, trunk, block)

    resid = tokens[0].astype(wider)
    out_turned = jnp.pad(out_blocks.reshape(width, width // n).T, ((0, 0), (0, n * wide - width)))
    normed_one, out_turned, qkv_mine = seq_gather(
        layer_norm(resid, gain_one, shift_one).astype(low),
        n,
        1,
        "gather_one",
        rider=(turned.T, True, nf),
        second=out_turned,
    )
    out_turned = out_turned.reshape(width, n * wide)
    qkv_mine = qkv_mine.reshape(width, 3 * wide)
    fc_rows = fc_blocks.transpose(1, 0, 2).reshape(rows, nf * piece)
    fc_mine = lax.all_gather(fc_rows, "fsdp", axis=0, tiled=True)

    upstream = cotangent[0].astype(wider)
    projected = project(normed_one, qkv_mine, bias_mine, block // 2)
    sent = row_major(after(after(cotangent[0], fc_mine), projected))
    upstream_all = row_major(lax.all_gather(sent, "seq", axis=0, tiled=True))
    table = after(table, sent)
    attended_low, attended, totals = attend(table, projected, block)
    proj_rows = proj_blocks.transpose(1, 0, 2).reshape(piece, width)
    proj_mine = lax.all_gather(after(proj_rows, attended_low), "fsdp", axis=0, tiled=True)
    attended_mine = to_tokens(attended_low.reshape(n, block, wide), n, wide, 2)
    middle = after(resid, upstream_all) + contract_cols(attended_mine, out_turned) + bias_out
    normed_two = layer_norm(middle, gain_two, shift_two).astype(low)
    ff = nf * piece

    def expand(value, fc, bias):
        pre = mm(value, fc[...]) + bias[...]
        bend = math.sqrt(2 / math.pi)
        square = pre * pre
        inner = jnp.tanh(pre * (bend + bend * 0.044715 * square))
        half = 0.5 + 0.5 * inner
        act = (pre * half).astype(low)
        slope = half + 0.5 * pre * (1 - inner * inner) * (bend + 3 * bend * 0.044715 * square)
        return act, slope.astype(low)

    normed_two, hidden_act, hidden_slope = seq_gather(
        normed_two,
        n,
        3,
        "gather_two",
        expand,
        (fc_mine, bias_hidden),
        ((ff, low), (ff, low)),
        modes=(0, 0),
    )

    def shrink(up, slope, proj, fc):
        grad = (nt(up, proj[...]) * slope.astype(wider)).astype(low)
        return nt(grad, fc[...]), grad

    grad_normed_two, grad_pre, grad_proj, mixed = seq_scatter(
        n,
        width,
        4,
        "scatter_two",
        shrink,
        (upstream_all, hidden_slope),
        (proj_mine, fc_mine),
        ((ff, low),),
        side=(hidden_act, upstream_all, lambda a, proj, fc: mm(a, proj[...]).astype(low), width),
    )
    mixed = lax.psum_scatter(mixed, "seq", scatter_dimension=0, tiled=True).astype(wider)
    proj_part = lax.psum_scatter(
        grad_proj.reshape(nf, piece, width), "fsdp", scatter_dimension=0, tiled=False
    )
    unused_two, norm_two_back = jax.vjp(layer_norm, middle, gain_two, shift_two)
    grad_middle_norm, grad_gain_two, grad_shift_two = norm_two_back(grad_normed_two)
    grad_middle = upstream + grad_middle_norm
    grad_branch = grad_middle.astype(low)
    grad_attended, grad_fc = to_heads(
        grad_branch, out_turned, n, wide, 5, normed_two, grad_pre
    )
    grad_attended = grad_attended.reshape(n * block, wide)
    fc_part = lax.psum_scatter(grad_fc, "fsdp", scatter_dimension=0, tiled=True)
    grad_projected = attend_back(table, projected, grad_attended, attended, totals, block)
    output = (after(middle, grad_projected) + mixed + bias_proj).astype(low)[None]
    ready = output[0, :8, :128].astype(wider)
    grad_qkv = contract(normed_one, grad_projected, ready, block)
    grad_normed_one, qkv_parts = seq_scatter(
        n,
        width,
        6,
        "scatter_one",
        lambda g, w: (nt(g, w[...]),),
        (grad_projected,),
        (qkv_mine,),
        rider=(grad_qkv.reshape(nf, rows, 3 * wide), False, nf),
    )
    unused_one, norm_one_back = jax.vjp(layer_norm, resid, gain_one, shift_one)
    grad_resid_norm, grad_gain_one, grad_shift_one = norm_one_back(grad_normed_one)
    input_grad = (grad_middle + grad_resid_norm).astype(low)[None]

    proj_part = after(proj_part, grad_normed_one).reshape(piece, n, width // n).transpose(1, 0, 2)
    fc_part = after(fc_part, grad_normed_one).reshape(rows, nf, piece).transpose(1, 0, 2)
    grad_out = contract_rows(
        after(grad_branch, grad_attended), attended_mine[:, :width]
    ).astype(low)
    out_part = lax.psum_scatter(grad_out, "seq", scatter_dimension=0, tiled=True).T
    out_part = after(out_part, grad_normed_one).reshape(nf, rows, width // n)
    qkv_part = jnp.sum(qkv_parts.astype(wider), 0).astype(low).T

    column_sums = jnp.sum(grad_projected.astype(wider), 0).reshape(3, wide)
    placed = lax.dynamic_update_slice_in_dim(
        jnp.zeros((3, n * wide), wider), column_sums, s * wide, 1
    )[:, :width]
    grad_qv = jnp.concatenate([placed[0], placed[2]])
    hidden_sums = jnp.sum(grad_pre.astype(wider), 0).reshape(nf, 1, piece)
    grad_fc_bias = lax.dynamic_update_slice_in_dim(
        jnp.zeros((nf, n, piece), wider), hidden_sums, s, 1
    )
    parts = [
        grad_gain_one,
        grad_shift_one,
        grad_qv,
        jnp.sum(grad_branch.astype(wider), 0),
        grad_gain_two,
        grad_shift_two,
        grad_fc_bias,
        jnp.sum(upstream, 0),
    ]
    summed, qkv_out, proj_out, fc_out, out_out = give_back(
        jnp.concatenate([p.reshape(nf, -1) for p in parts], 1),
        qkv_part,
        qkv_cols,
        proj_part,
        fc_part,
        out_part,
        n,
        nf,
        back,
        7,
    )
    if not even:
        qkv_part = qkv_part.reshape(3, wide, rows)
        qkv_out = lax.all_gather(qkv_part, "seq", axis=1, tiled=True)[:, :width]
        qkv_out = qkv_out.reshape(3 * width, rows)
        qkv_out = lax.dynamic_slice_in_dim(qkv_out, s * qkv_cols, qkv_cols, 0)
    out_out = jnp.sum(out_out.astype(wider), 0)
    qkv_out = qkv_out.T.astype(wider)
    proj_out = proj_out.reshape(n * piece, width // n).astype(wider)
    fc_out = fc_out.transpose(1, 0, 2).reshape(rows, nf * piece).astype(wider)
    vector_out = []
    at = 0
    for size in sizes:
        vector_out.append(summed[at : at + size])
        at += size
    return (
        output,
        input_grad,
        vector_out[0],
        vector_out[1],
        qkv_out,
        vector_out[2],
        out_out,
        vector_out[3],
        vector_out[4],
        vector_out[5],
        fc_out,
        vector_out[6],
        proj_out,
        vector_out[7],
    )


def solution(mesh):
    in_specs = (
        P("fsdp", "seq", None),
        P("fsdp"),
        P("fsdp"),
        P("fsdp", "seq"),
        P("fsdp"),
        P("fsdp", "seq"),
        P("fsdp"),
        P("fsdp"),
        P("fsdp"),
        P("fsdp", "seq"),
        P("fsdp"),
        P("fsdp", "seq"),
        P("fsdp"),
        P("fsdp", None),
        P("fsdp", None),
        P("fsdp", "seq", None),
    )
    out_specs = (
        P("fsdp", "seq", None),
        P("fsdp", "seq", None),
        P("fsdp"),
        P("fsdp"),
        P("fsdp", "seq"),
        P("fsdp"),
        P("fsdp", "seq"),
        P("fsdp"),
        P("fsdp"),
        P("fsdp"),
        P("fsdp", "seq"),
        P("fsdp"),
        P("fsdp", "seq"),
        P("fsdp"),
    )
    return jax.shard_map(local, mesh=mesh, in_specs=in_specs, out_specs=out_specs, check_vma=False)
```

```python
import functools
import math

import jax
import jax.numpy as jnp
import numpy as np
from jax import lax
from jax.experimental import pallas as pl
from jax.experimental.layout import Layout, with_layout_constraint
from jax.experimental.pallas import tpu as pltpu
from jax.sharding import PartitionSpec as P

MESH = pl.DeviceIdType.MESH
HEADS = 25
SMALL = pl.CostEstimate(flops=0, bytes_accessed=1 << 20, transcendentals=0)


def route_bits(n):
    bits = []
    b = 2
    while b < n:
        bits.append(b)
        b *= 2
    return bits


def flip(a, b):
    return jnp.where(lax.rem(lax.div(a, b), 2) == 0, a + b, a - b)


def place(me, r, n):
    if isinstance(r, int):
        for b in [1] + route_bits(n):
            if r & b:
                me = flip(me, b)
        return me
    for b in [1] + route_bits(n):
        me = jnp.where(lax.rem(lax.div(r, b), 2) == 0, me, flip(me, b))
    return me


def pick(table, q):
    value = jnp.int32(table[0])
    for i, entry in enumerate(table[1:]):
        value = jnp.where(q == i + 1, jnp.int32(entry), value)
    return value


def greet(ids):
    barrier = pltpu.get_barrier_semaphore()
    for i in ids:
        pl.semaphore_signal(barrier, inc=1, device_id=i, device_id_type=MESH)
    pl.semaphore_wait(barrier, len(ids))


def remote(src, dst, send, recv, device):
    return pltpu.make_async_remote_copy(
        src_ref=src, dst_ref=dst, send_sem=send, recv_sem=recv, device_id=device, device_id_type=MESH
    )


class Blocks:
    def __init__(self, axis, size, same, source, target, send, recv, local):
        self.axis, self.size, self.same = axis, size, same
        self.source, self.target = source, target
        self.send, self.recv, self.local = send, recv, local
        self.me = lax.axis_index(axis)

    @staticmethod
    def scratch(size):
        dma = pltpu.SemaphoreType.DMA
        return [dma((size - 1,)), dma((size - 1,)), dma]

    def peers(self):
        return [{self.axis: lax.rem(self.me + d, self.size)} for d in range(1, self.size)]

    def copy(self, d):
        to = lax.rem(self.me + d, self.size)
        src = self.source if self.same else self.source.at[to]
        return remote(src, self.target.at[self.me], self.send.at[d - 1], self.recv.at[d - 1], {self.axis: to})

    def own(self):
        src = self.source if self.same else self.source.at[self.me]
        return pltpu.make_async_copy(src, self.target.at[self.me], self.local)

    def start(self):
        for d in range(1, self.size):
            self.copy(d).start()
        self.own().start()

    def finish(self):
        for d in range(1, self.size):
            dst = self.target.at[lax.rem(self.me + self.size - d, self.size)]
            remote(dst, dst, self.send.at[d - 1], self.recv.at[d - 1], {self.axis: self.me}).wait_recv()
        self.own().wait()
        for d in range(1, self.size):
            self.copy(d).wait_send()


class Spread:
    def __init__(self, n, source, target, send, recv, local):
        self.n, self.source, self.target = n, source, target
        self.send, self.recv, self.local = send, recv, local
        self.me = lax.axis_index("seq")
        self.bits = route_bits(n)
        self.orders = [self.bits, self.bits[::-1]]
        self.h = source.shape[0] // 2

    @staticmethod
    def scratch(n):
        dma = pltpu.SemaphoreType.DMA
        return [dma((2, len(route_bits(n)) + 1, n)), dma((2, n)), dma]

    def device(self, b):
        return {"seq": flip(self.me, b)}

    def peers(self):
        return [self.device(b) for b in [1] + self.bits]

    def rows(self, half):
        return pl.ds(half * self.h, self.h)

    def ship(self, half, k, b):
        owner = place(self.me, k, self.n)
        src = self.source if k == 0 else self.target.at[owner]
        lane = 0 if b == 1 else 1 + self.bits.index(b)
        return remote(
            src.at[self.rows(half)],
            self.target.at[owner].at[self.rows(half)],
            self.send.at[half, lane, k],
            self.recv.at[half, k ^ b],
            self.device(b),
        )

    def arrive(self, half, k):
        dst = self.target.at[place(self.me, k, self.n)].at[self.rows(half)]
        remote(dst, dst, self.send.at[half, 0, 0], self.recv.at[half, k], self.device(1)).wait_recv()

    def own(self):
        return pltpu.make_async_copy(self.source, self.target.at[self.me], self.local)

    def fresh(self, half, i):
        had = [0]
        for b in self.orders[half][:i]:
            had = had + [k ^ b for k in had]
        return [k ^ self.orders[half][i] for k in had]

    def start(self):
        for i in range(len(self.bits)):
            for half in (0, 1):
                self.ship(half, 0, self.orders[half][i]).start()
        for half in (0, 1):
            self.ship(half, 0, 1).start()
        self.own().start()

    def phase(self, i):
        for half in (0, 1):
            for k in self.fresh(half, i):
                self.arrive(half, k)
                for b in self.orders[half][i + 1 :] + [1]:
                    self.ship(half, k, b).start()

    def finish(self):
        for half in (0, 1):
            for k in range(1, self.n, 2):
                self.arrive(half, k)
        self.own().wait()
        for half in (0, 1):
            for b in self.orders[half] + [1]:
                self.ship(half, 0, b).wait_send()
            for i in range(len(self.bits)):
                for k in self.fresh(half, i):
                    for b in self.orders[half][i + 1 :] + [1]:
                        self.ship(half, k, b).wait_send()


def blocks_shape(x, size, same):
    return jax.ShapeDtypeStruct(((size,) + x.shape) if same else x.shape, x.dtype)


def arrival_order(n):
    bits = route_bits(n)
    orders = [bits, bits[::-1]]
    lists = []
    for order in orders:
        held, phases = [0], [-1]
        for i, b in enumerate(order):
            fresh = [h ^ b for h in held]
            held, phases = held + fresh, phases + [i] * len(fresh)
        lists.append(list(zip(held, phases)))
    entries = []
    for i in range(n // 2):
        for odd in (0, 1):
            for half in (0, 1):
                k, phase = lists[half][i]
                entries.append((half, k ^ odd, phase, odd))
    return orders, entries


def gather_kernel(n, h, body, n_const, n_out, relative, modes, nf, same, second, *refs):
    if second:
        at = 1 + n_const
        out = at + 1 + min(nf, 1) + 1 + n_out
        w_ref, w_all = refs[at], refs[out]
        w_send, w_recv, w_keep = refs[-3:]
        refs = refs[:at] + refs[at + 1 : out] + refs[out + 1 : -3]
        w_half = w_ref.shape[1] // 2
    refs, rider = split_rider(refs, nf, same, 1 + n_const, 1 + n_out)
    x_ref = refs[0]
    consts = refs[1 : 1 + n_const]
    all_ref = refs[1 + n_const]
    outs = refs[2 + n_const : 2 + n_const + n_out]
    held = refs[2 + n_const + n_out]
    stages = refs[3 + n_const + n_out : 3 + n_const + 2 * n_out]
    send, recv, keep, store = refs[3 + n_const + 2 * n_out :]
    me = lax.axis_index("seq")
    orders, entries = arrival_order(n)
    bits = orders[0]
    nb = len(bits)

    def device(b):
        return {"seq": flip(me, b)}

    def spot(half, k):
        return 2 * (k if relative else place(me, k, n)) + half

    def ship(half, k, b):
        at = spot(half, k)
        src = x_ref.at[pl.ds(half * h, h)] if isinstance(k, int) and k == 0 else held.at[at]
        lane = 0 if b == 1 else 1 + bits.index(b)
        to = k ^ b if isinstance(k, int) else place(k, b, n)
        dst = 2 * to + half if relative else at
        first = remote(src, held.at[dst], send.at[half, lane, k], recv.at[half, to], device(b))
        if not second:
            return [first]
        owner = place(me, k, n)
        lanes = pl.ds(half * w_half, w_half)
        src = w_ref if isinstance(k, int) and k == 0 else w_all.at[owner]
        other = remote(
            src.at[:, lanes], w_all.at[owner].at[:, lanes], w_send.at[half, lane, k], w_recv.at[half, to], device(b)
        )
        return [first, other]

    def each(copies, act):
        for c in copies:
            act(c)

    def w_arrive(half, k):
        dst = w_all.at[place(me, k, n)].at[:, pl.ds(0, w_half)]
        remote(dst, dst, w_send.at[0, 0, 0], w_recv.at[half, k], device(1)).wait_recv()

    greet([device(b) for b in [1] + bits] + (rider.peers() if nf else []))
    for i in range(nb):
        for half in (0, 1):
            each(ship(half, 0, orders[half][i]), lambda c: c.start())
    for half in (0, 1):
        each(ship(half, 0, 1), lambda c: c.start())
    if second:
        pltpu.make_async_copy(w_ref, w_all.at[me], w_keep).start()
    if nf:
        rider.start()

    def output(o, q, at):
        slot = lax.rem(q, 2)
        return pltpu.make_async_copy(stages[o].at[slot], outs[o].at[at], store.at[o, slot])

    def entry(q, at, value):
        results = body(value, *consts)
        for o in range(n_out):

            @pl.when(q >= 2)
            def _(o=o):
                output(o, q, at[modes[o]]).wait()

            stages[o][lax.rem(q, 2)] = results[o]
            output(o, q, at[modes[o]]).start()

    def step(q, carry):
        half = pick([e[0] for e in entries], q)
        k = pick([e[1] for e in entries], q)
        phase = pick([e[2] for e in entries], q)
        odd = pick([e[3] for e in entries], q)
        at = spot(half, k)

        @pl.when(k == 0)
        def _():
            held[at] = x_ref[pl.ds(pl.multiple_of(half * h, h), h)]

        @pl.when(k != 0)
        def _():
            remote(held.at[at], held.at[at], send.at[0, 0, 0], recv.at[half, k], device(1)).wait_recv()
            if second:
                w_arrive(half, k)

        for side in (0, 1):
            for i in range(nb):

                @pl.when((half == side) & (odd == 0) & (k != 0) & (phase < i))
                def _(side=side, i=i):
                    each(ship(side, k, orders[side][i]), lambda c: c.start())

            @pl.when((half == side) & (odd == 0) & (k != 0))
            def _(side=side):
                each(ship(side, k, 1), lambda c: c.start())

        pltpu.make_async_copy(held.at[at], all_ref.at[at], keep.at[q]).start()
        if n_out:
            entry(q, (2 * place(me, k, n) + half, 2 * k + half), held[at])
        return carry

    lax.fori_loop(0, 2 * n, step, 0)
    for q, (half, k, phase, odd) in enumerate(entries):
        at = spot(half, k)
        pltpu.make_async_copy(held.at[at], all_ref.at[at], keep.at[q]).wait()
        if q >= 2 * n - 2:
            for o in range(n_out):
                output(o, jnp.int32(q), at).wait()
        if not odd:
            for i in range(nb):
                if phase < i:
                    each(ship(half, k, orders[half][i]), lambda c: c.wait_send())
            each(ship(half, k, 1), lambda c: c.wait_send())
    if second:
        pltpu.make_async_copy(w_ref, w_all.at[me], w_keep).wait()
    if nf:
        rider.finish()


def split_rider(refs, nf, same, n_in, n_out):
    if not nf:
        return refs, None
    source = refs[n_in]
    target = refs[n_in + 1 + n_out]
    rider = Blocks("fsdp", nf, same, source, target, *refs[-3:])
    return refs[:n_in] + refs[n_in + 1 : n_in + 1 + n_out] + refs[n_in + 2 + n_out : -3], rider


def rider_parts(rider):
    if rider is None:
        return [], [], [], [], 0, False
    x, same, nf = rider
    hbm = [pl.BlockSpec(memory_space=pl.ANY)]
    return [x], hbm, [blocks_shape(x, nf, same)], Blocks.scratch(nf), nf, same


def seq_gather(x, n, ident, name, body=None, consts=(), outs=(), relative=False, modes=None, rider=None, second=None):
    rows, cols = x.shape
    h = rows // 2
    nb = len(route_bits(n))
    shapes = [jax.ShapeDtypeStruct((2 * n, h, c), d) for c, d in outs]
    vmem = pl.BlockSpec(memory_space=pltpu.VMEM)
    hbm = pl.BlockSpec(memory_space=pl.ANY)
    more, spec, shape, scratch, nf, same = rider_parts(rider)
    also = [] if second is None else [second]
    out = pl.pallas_call(
        functools.partial(
            gather_kernel, n, h, body, len(consts), len(outs), relative, modes, nf, same, second is not None
        ),
        out_shape=[jax.ShapeDtypeStruct((2 * n, h, cols), x.dtype)]
        + shapes
        + [jax.ShapeDtypeStruct((n,) + w.shape, w.dtype) for w in also]
        + shape,
        in_specs=[vmem] * (1 + len(consts)) + [hbm] * len(also) + spec,
        out_specs=[hbm] * (1 + len(outs)) + [hbm] * len(also) + spec,
        scratch_shapes=[pltpu.VMEM((2 * n, h, cols), x.dtype)]
        + [pltpu.VMEM((2, h, c), d) for c, d in outs]
        + [
            pltpu.SemaphoreType.DMA((2, nb + 1, n)),
            pltpu.SemaphoreType.DMA((2, n)),
            pltpu.SemaphoreType.DMA((2 * n,)),
            pltpu.SemaphoreType.DMA((max(len(outs), 1), 2)),
        ]
        + scratch
        + [
            pltpu.SemaphoreType.DMA((2, nb + 1, n)),
            pltpu.SemaphoreType.DMA((2, n)),
            pltpu.SemaphoreType.DMA,
        ]
        * len(also),
        compiler_params=pltpu.CompilerParams(
            collective_id=ident, has_side_effects=True, vmem_limit_bytes=60 << 20
        ),
        cost_estimate=SMALL,
        name=name,
    )(x, *consts, *also, *more)
    return [o.reshape(2 * n * h, o.shape[2]) for o in out[: 1 + len(outs)]] + list(out[1 + len(outs) :])


class Side:
    def __init__(self, count, refs):
        self.count = count
        self.a, self.b, self.grad, self.sums, self.acc, self.abuf, self.bbuf, self.load = refs

    def fetch(self, i):
        slot = lax.rem(i, 2)
        return [
            pltpu.make_async_copy(self.a.at[i], self.abuf.at[slot], self.load.at[0, slot]),
            pltpu.make_async_copy(self.b.at[i], self.bbuf.at[slot], self.load.at[1, slot]),
        ]

    def begin(self):
        self.acc[...] = jnp.zeros_like(self.acc)
        self.sums[...] = jnp.zeros_like(self.sums)
        for c in self.fetch(jnp.int32(0)):
            c.start()

    def run(self, first, last):
        def step(i, carry):
            @pl.when(i + 1 < self.count)
            def _():
                for c in self.fetch(i + 1):
                    c.start()

            for c in self.fetch(i):
                c.wait()
            slot = lax.rem(i, 2)
            a, b = self.abuf[slot], self.bbuf[slot]
            self.acc[...] += lax.dot_general(
                a, b, (((0,), (0,)), ((), ())), preferred_element_type=jnp.float32
            )
            self.sums[...] += jnp.sum(b.astype(jnp.float32), 0, keepdims=True)
            return carry

        lax.fori_loop(first, last, step, 0)

    def end(self):
        self.grad[...] = self.acc[...].astype(self.grad.dtype)


def side_parts(side, count):
    if side is None:
        return [], [], [], [], []
    a, b = side
    h = a.shape[0] // count
    low = jnp.bfloat16
    hbm = pl.BlockSpec(memory_space=pl.ANY)
    vmem = pl.BlockSpec(memory_space=pltpu.VMEM)
    return (
        [x.reshape(count, h, x.shape[1]) for x in (a, b)],
        [
            jax.ShapeDtypeStruct((a.shape[1], b.shape[1]), low),
            jax.ShapeDtypeStruct((1, b.shape[1]), jnp.float32),
        ],
        [hbm, hbm],
        [vmem, vmem],
        [
            pltpu.VMEM((a.shape[1], b.shape[1]), jnp.float32),
            pltpu.VMEM((2, h, a.shape[1]), low),
            pltpu.VMEM((2, h, b.shape[1]), low),
            pltpu.SemaphoreType.DMA((2, 2)),
        ],
    )


def scatter_order(n):
    bits = route_bits(n)
    orders = [bits, bits[::-1]]
    lists = [
        sorted(range(0, n, 2), key=lambda k: [-int(bool(k & b)) for b in order]) for order in orders
    ]
    return orders, [(half, lists[half][i]) for i in range(n // 2) for half in (0, 1)]


def scatter_kernel(n, h, body, n_in, n_const, n_out, modes, nf, same, has_side, carried, *refs):
    if carried:
        out = n_in + n_const + 2 * has_side + min(nf, 1) + 2 + n_out + 2 * has_side + min(nf, 1)
        refs = refs[1:out] + refs[out + 1 :]
    side = None
    if has_side:
        at = n_in + n_const
        out = at + 2 + min(nf, 1) + 1 + n_out
        extra = refs[at : at + 2] + refs[out : out + 2] + refs[-4:]
        refs = refs[:at] + refs[at + 2 : out] + refs[out + 2 : -4]
        side = Side(2 * n, extra)
    refs, rider = split_rider(refs, nf, same, n_in + n_const, 1 + n_out)
    ins = refs[:n_in]
    consts = refs[n_in : n_in + n_const]
    at = n_in + n_const
    sum_ref = refs[at]
    outs = refs[at + 1 : at + 1 + n_out]
    at += 1 + n_out
    give, pair, own, far, total = refs[at : at + 5]
    at += 5
    loads = refs[at : at + n_in]
    stages = refs[at + n_in : at + n_in + n_out]
    pair_send, pair_recv, far_send, far_recv, load, store, done = refs[at + n_in + n_out :]
    me = lax.axis_index("seq")
    orders, entries = scatter_order(n)
    bits = orders[0]
    slots = give.shape[0]
    index = {e: j for j, e in enumerate(entries)}

    def device(b):
        return {"seq": flip(me, b)}

    def phase_of(half, k):
        for i, b in enumerate(orders[half]):
            if k & b:
                return i
        return len(bits)

    landing = {}
    for half in (0, 1):
        for i, b in enumerate(orders[half]):
            for k in range(0, n, 2):
                if phase_of(half, k) == i:
                    landing[half, i, k ^ b] = len(landing)

    halves = [e[0] for e in entries]
    ks = [e[1] for e in entries]

    def spot(q, relative):
        j = lax.div(q, 2)
        k = pick(ks, j)
        k = jnp.where(lax.rem(q, 2) == 0, flip(k, 1), k)
        return 2 * (k if relative else place(me, k, n)) + pick(halves, j)

    def fetch(q):
        slot = lax.rem(q, 2)
        return [
            pltpu.make_async_copy(ins[i].at[spot(q, modes[0][i])], loads[i].at[slot], load.at[i, slot])
            for i in range(n_in)
        ]

    def output(o, q):
        slot = lax.rem(q, 2)
        return pltpu.make_async_copy(stages[o].at[slot], outs[o].at[spot(q, modes[1][o])], store.at[o, slot])

    def hand(j):
        slot = lax.rem(j, slots)
        return remote(give.at[slot], pair.at[j], pair_send.at[j], pair_recv.at[j], device(1))

    def launch(half, k):
        i = phase_of(half, k)
        b = orders[half][i]
        to = landing[half, i, k ^ b]
        return remote(own.at[index[half, k]], far.at[to], far_send.at[to], far_recv.at[to], device(b))

    def join(j):
        hand(j).wait_recv()
        own[j] = (own[j].astype(jnp.float32) + pair[j].astype(jnp.float32)).astype(own.dtype)
        for e, (half, k) in enumerate(entries):
            if phase_of(half, k) == 0:

                @pl.when(j == e)
                def _(half=half, k=k):
                    launch(half, k).start()

    for c in fetch(jnp.int32(0)):
        c.start()
    greet([device(b) for b in [1] + bits] + (rider.peers() if nf else []))
    if nf:
        rider.start()

    def step(q, carry):
        j = lax.div(q, 2)
        slot = lax.rem(q, 2)

        @pl.when(q + 1 < 2 * n)
        def _():
            for c in fetch(q + 1):
                c.start()

        for c in fetch(q):
            c.wait()
        part, *results = body(*[r[slot] for r in loads], *consts)
        for o in range(n_out):

            @pl.when(q >= 2)
            def _(o=o):
                output(o, q).wait()

            stages[o][slot] = results[o]
            output(o, q).start()

        @pl.when(slot == 0)
        def _():
            @pl.when(j >= slots)
            def _():
                hand(j - slots).wait_send()

            give[lax.rem(j, slots)] = part.astype(give.dtype)
            hand(j).start()

        @pl.when(slot == 1)
        def _():
            own[j] = part.astype(own.dtype)

            @pl.when(j >= 1)
            def _():
                join(j - 1)

        return carry

    lax.fori_loop(0, 2 * n, step, 0)
    if side:
        side.begin()
    join(jnp.int32(n - 1))
    first = n // 2
    cuts = [0, first] + [first + (2 * n - first) * i // (len(bits) - 1) for i in range(1, len(bits))]
    for i in range(len(bits)):
        if side:
            side.run(cuts[i], cuts[i + 1])
        for half in (0, 1):
            order = orders[half]
            for k in [k for hh, k in entries if hh == half and phase_of(half, k) > i]:
                to = landing[half, i, k]
                remote(far.at[to], far.at[to], far_send.at[to], far_recv.at[to], device(1)).wait_recv()
                j = index[half, k]
                rows = pl.ds(half * h, h)
                if i == len(bits) - 1:
                    total[rows] = own[j].astype(jnp.float32) + far[to].astype(jnp.float32)
                    pltpu.make_async_copy(total.at[rows], sum_ref.at[rows], done.at[half]).start()
                else:
                    own[j] = (own[j].astype(jnp.float32) + far[to].astype(jnp.float32)).astype(own.dtype)
                    if phase_of(half, k) == i + 1:
                        launch(half, k).start()
    for half in (0, 1):
        rows = pl.ds(half * h, h)
        pltpu.make_async_copy(total.at[rows], sum_ref.at[rows], done.at[half]).wait()
    for q in (2 * n - 2, 2 * n - 1):
        for o in range(n_out):
            output(o, jnp.int32(q)).wait()
    for j in range(max(n - slots, 0), n):
        hand(jnp.int32(j)).wait_send()
    for half, k in entries:
        if phase_of(half, k) < len(bits):
            launch(half, k).wait_send()
    if nf:
        rider.finish()
    if side:
        side.end()


def seq_scatter(n, cols, ident, name, body, ins, consts, outs=(), modes=None, rider=None, side=None, carry=None):
    h = ins[0].shape[0] // (2 * n)
    low = jnp.bfloat16
    slots = min(4, n)
    split = [a.reshape(2 * n, h, a.shape[1]) for a in ins]
    vmem = pl.BlockSpec(memory_space=pltpu.VMEM)
    hbm = pl.BlockSpec(memory_space=pl.ANY)
    reach = n - 2
    modes = modes or ([0] * len(ins), [0] * len(outs))
    more, spec, shape, scratch, nf, same = rider_parts(rider)
    s_ins, s_shapes, s_in_specs, s_out_specs, s_scratch = side_parts(side, 2 * n)
    carries = [] if carry is None else [carry]
    out = pl.pallas_call(
        functools.partial(
            scatter_kernel, n, h, body, len(ins), len(consts), len(outs), modes, nf, same, int(side is not None), carry is not None
        ),
        out_shape=[jax.ShapeDtypeStruct((2 * h, cols), jnp.float32)]
        + [jax.ShapeDtypeStruct((2 * n, h, c), d) for c, d in outs]
        + s_shapes
        + shape
        + [jax.ShapeDtypeStruct(x.shape, x.dtype) for x in carries],
        in_specs=[hbm] * (len(carries) + len(ins)) + [vmem] * len(consts) + s_in_specs + spec,
        out_specs=[hbm] * (1 + len(outs)) + s_out_specs + spec + [hbm] * len(carries),
        input_output_aliases={0: 1 + len(outs) + len(s_shapes) + len(shape)} if carries else {},
        scratch_shapes=[
            pltpu.VMEM((slots, h, cols), low),
            pltpu.VMEM((n, h, cols), low),
            pltpu.VMEM((n, h, cols), low),
            pltpu.VMEM((reach, h, cols), low),
            pltpu.VMEM((2 * h, cols), jnp.float32),
        ]
        + [pltpu.VMEM((2, h, a.shape[2]), a.dtype) for a in split]
        + [pltpu.VMEM((2, h, c), d) for c, d in outs]
        + [
            pltpu.SemaphoreType.DMA((n,)),
            pltpu.SemaphoreType.DMA((n,)),
            pltpu.SemaphoreType.DMA((reach,)),
            pltpu.SemaphoreType.DMA((reach,)),
            pltpu.SemaphoreType.DMA((len(ins), 2)),
            pltpu.SemaphoreType.DMA((max(len(outs), 1), 2)),
            pltpu.SemaphoreType.DMA((2,)),
        ]
        + scratch
        + s_scratch,
        compiler_params=pltpu.CompilerParams(
            collective_id=ident, has_side_effects=True, vmem_limit_bytes=60 << 20
        ),
        cost_estimate=SMALL,
        name=name,
    )(*carries, *split, *consts, *s_ins, *more)
    many = 1 + len(outs)
    sides = [] if side is None else list(out[many : many + 2])
    more = list(out[many + len(sides) :])
    return [out[0]] + [o.reshape(2 * n * h, o.shape[2]) for o in out[1:many]] + sides + more


class Rows:
    def __init__(self, n, held, width, wide, back):
        moves = []
        for to in range(n):
            for third in range(3):
                at, end = third * width + to * wide, third * width + min((to + 1) * wide, width)
                row = third * wide
                while at < end:
                    source = at // held
                    count = min(end, (source + 1) * held) - at
                    moves.append((source, at - source * held, to, row, count))
                    at, row = at + count, row + count
        self.n = n
        self.moves = [(c, d, a, b, e) if back else (a, b, c, d, e) for a, b, c, d, e in moves]
        self.out = [[m for m in self.moves if m[0] == i] for i in range(n)]
        self.into = [[m for m in self.moves if m[2] == i] for i in range(n)]
        self.most = max(len(v) for v in self.out + self.into)

    def scratch(self):
        dma = pltpu.SemaphoreType.DMA
        return [dma((self.most,)), dma((self.most,)), dma((self.most,))]

    def bind(self, source, target, send, recv, local):
        self.source, self.target, self.send, self.recv, self.local = source, target, send, recv, local
        return self

    def copy(self, i, m):
        src = self.source.at[pl.ds(m[1], m[4])]
        dst = self.target.at[pl.ds(m[3], m[4])]
        if m[0] == m[2]:
            return pltpu.make_async_copy(src, dst, self.local.at[i])
        return remote(src, dst, self.send.at[i], self.recv.at[self.into[m[2]].index(m)], {"seq": m[2]})

    def start(self):
        me = lax.axis_index("seq")
        for s in range(self.n):

            @pl.when(me == s)
            def _(s=s):
                for i, m in enumerate(self.out[s]):
                    self.copy(i, m).start()

    def finish(self):
        me = lax.axis_index("seq")
        for s in range(self.n):

            @pl.when(me == s)
            def _(s=s):
                for i, m in enumerate(self.into[s]):
                    if m[0] != s:
                        dst = self.target.at[pl.ds(m[3], m[4])]
                        remote(dst, dst, self.send.at[0], self.recv.at[i], {"seq": s}).wait_recv()
                for i, m in enumerate(self.out[s]):
                    if m[0] == m[2]:
                        self.copy(i, m).wait()
                    else:
                        self.copy(i, m).wait_send()


class Units:
    def __init__(self, n, nf, back, source, target, send, recv, local):
        self.n, self.nf, self.back = n, nf, back
        self.source, self.target, self.send, self.recv, self.local = source, target, send, recv, local
        self.me = lax.axis_index("seq")

    @staticmethod
    def scratch(nf):
        dma = pltpu.SemaphoreType.DMA
        return [dma((nf,)), dma((nf,)), dma]

    def ends(self, i):
        group = self.n // self.nf
        if self.back:
            return i * group + lax.div(self.me, self.nf), lax.rem(self.me, self.nf)
        return lax.rem(self.me, group) * self.nf + i, lax.div(self.me, group)

    def comes(self, i):
        group = self.n // self.nf
        if self.back:
            return lax.rem(self.me, group) * self.nf + i
        return i * group + lax.div(self.me, self.nf)

    def each(self, i, there, here):
        to, slot = self.ends(i)

        @pl.when(to != self.me)
        def _():
            there(remote(self.source.at[i], self.target.at[slot], self.send.at[i], self.recv.at[slot], {"seq": to}))

        @pl.when(to == self.me)
        def _():
            here(pltpu.make_async_copy(self.source.at[i], self.target.at[slot], self.local))

    def start(self):
        for i in range(self.nf):
            self.each(i, lambda c: c.start(), lambda c: c.start())

    def finish(self):
        for i in range(self.nf):
            source = self.comes(i)

            @pl.when(source != self.me)
            def _(i=i):
                dst = self.target.at[i]
                remote(dst, dst, self.send.at[0], self.recv.at[i], {"seq": self.me}).wait_recv()

        for i in range(self.nf):
            self.each(i, lambda c: c.wait_send(), lambda c: c.wait())


def all_peers(n, nf):
    me, f = lax.axis_index("seq"), lax.axis_index("fsdp")
    return [{"seq": place(me, r, n)} for r in range(1, n)] + [
        {"fsdp": lax.rem(f + d, nf)} for d in range(1, nf)
    ]


def exchange_kernel(n, nf, rows, count, *refs):
    ins, outs, sems = refs[: 4 + count], refs[4 + count : 8 + 2 * count], list(refs[8 + 2 * count :])
    take = lambda k: [sems.pop(0) for _ in range(k)]
    parts = []
    if rows is not None:
        parts.append(rows.bind(ins[0], outs[0], *take(3)))
    vectors = [Blocks("fsdp", nf, True, ins[4 + i], outs[4 + i], *take(3)) for i in range(count)]
    later = [
        Blocks("fsdp", nf, True, ins[3], outs[3], *take(3)),
        Units(n, nf, False, ins[2], outs[2], *take(3)),
        Blocks("seq", n, False, ins[1], outs[1], *take(3)),
    ]
    parts = vectors + parts + later
    greet(all_peers(n, nf))
    for p in parts:
        p.start()
    for p in parts:
        p.finish()


def exchange(w, p, c, o, vectors, n, nf, rows, wide, ident):
    hbm = pl.BlockSpec(memory_space=pl.ANY)
    count = len(vectors)
    out = pl.pallas_call(
        functools.partial(exchange_kernel, n, nf, rows, count),
        out_shape=[
            jax.ShapeDtypeStruct((3 * wide, w.shape[1]) if rows is not None else w.shape, w.dtype),
            blocks_shape(p, n, False),
            blocks_shape(c, nf, False),
            blocks_shape(o, nf, True),
        ]
        + [blocks_shape(v, nf, True) for v in vectors],
        in_specs=[hbm] * (4 + count),
        out_specs=[hbm] * (4 + count),
        scratch_shapes=(rows.scratch() if rows is not None else [])
        + sum([Blocks.scratch(nf) for _ in vectors], [])
        + Blocks.scratch(nf)
        + Units.scratch(nf)
        + Blocks.scratch(n),
        compiler_params=pltpu.CompilerParams(collective_id=ident, has_side_effects=True),
        cost_estimate=SMALL,
        name="exchange",
    )(w, p, c, o, *vectors)
    return out[0], out[1], out[2], out[3], out[4:]


def to_tokens_kernel(n, wide, x_ref, o_ref, send, recv, local):
    me = lax.axis_index("seq")

    def target(i):
        return o_ref.at[:, pl.ds(pl.multiple_of(i * wide, 128), wide)]

    greet([{"seq": place(me, r, n)} for r in range(1, n)])
    copies = []
    for r in range(n - 1, 0, -1):
        to = place(me, r, n)
        c = remote(x_ref.at[to], target(me), send.at[r - 1], recv.at[r - 1], {"seq": to})
        c.start()
        copies.append(c)
    mine = pltpu.make_async_copy(x_ref.at[me], target(me), local)
    mine.start()
    for r in range(1, n):
        dst = target(place(me, r, n))
        remote(dst, dst, send.at[0], recv.at[r - 1], {"seq": place(me, r, n)}).wait_recv()
    mine.wait()
    for c in copies:
        c.wait_send()


def to_tokens(x, n, wide, ident):
    rows = x.shape[1]
    hbm = pl.BlockSpec(memory_space=pl.ANY)
    return pl.pallas_call(
        functools.partial(to_tokens_kernel, n, wide),
        out_shape=jax.ShapeDtypeStruct((rows, n * wide), x.dtype),
        in_specs=[hbm],
        out_specs=hbm,
        scratch_shapes=Blocks.scratch(n),
        compiler_params=pltpu.CompilerParams(collective_id=ident, has_side_effects=True),
        cost_estimate=SMALL,
        name="to_tokens",
    )(x)


def to_heads_kernel(n, nf, wide, x_ref, w_ref, a_ref, b_ref, z_ref, o_ref, g_ref, m_ref, z_out, made, send, recv, local, *extra):
    me = lax.axis_index("seq")
    rider = Blocks("fsdp", nf, False, z_ref, z_out, *extra[-3:])
    extra = extra[:-3]
    side = Side(2 * n, (a_ref, b_ref, g_ref, m_ref) + extra)
    side.begin()
    greet([{"seq": place(me, r, n)} for r in range(1, n)] + rider.peers())
    rider.start()

    def copy(r):
        to = place(me, r, n)
        return remote(made.at[r], o_ref.at[me], send.at[r - 1], recv.at[r - 1], {"seq": to})

    def mine():
        return pltpu.make_async_copy(made.at[0], o_ref.at[me], local)

    def step(i, carry):
        r = n - 1 - i
        lanes = pl.ds(pl.multiple_of(place(me, r, n) * wide, 128), wide)
        made[r] = mm(x_ref[...], w_ref[:, lanes]).astype(made.dtype)

        @pl.when(r > 0)
        def _():
            copy(r).start()

        return carry

    lax.fori_loop(0, n, step, 0)
    mine().start()
    side.run(0, 2 * n)
    for r in range(1, n):
        dst = o_ref.at[place(me, r, n)]
        remote(dst, dst, send.at[0], recv.at[r - 1], {"seq": me}).wait_recv()
    mine().wait()
    for r in range(1, n):
        copy(r).wait_send()
    side.end()
    rider.finish()


def to_heads(x, w, n, nf, wide, ident, a, b, z):
    rows = x.shape[0]
    vmem = pl.BlockSpec(memory_space=pltpu.VMEM)
    hbm = pl.BlockSpec(memory_space=pl.ANY)
    s_ins, s_shapes, s_in_specs, s_out_specs, s_scratch = side_parts((a, b), 2 * n)
    out = pl.pallas_call(
        functools.partial(to_heads_kernel, n, nf, wide),
        out_shape=[jax.ShapeDtypeStruct((n, rows, wide), x.dtype)]
        + s_shapes
        + [blocks_shape(z, nf, False)],
        in_specs=[vmem, vmem] + s_in_specs + [hbm],
        out_specs=[hbm] + s_out_specs + [hbm],
        scratch_shapes=[pltpu.VMEM((n, rows, wide), x.dtype)]
        + Blocks.scratch(n)
        + s_scratch
        + Blocks.scratch(nf),
        compiler_params=pltpu.CompilerParams(
            collective_id=ident, has_side_effects=True, vmem_limit_bytes=60 << 20
        ),
        cost_estimate=SMALL,
        name="to_heads",
    )(x, w, *s_ins, z)
    return out


def contract_kernel(a_ref, b_ref, ready, o_ref, acc):
    i = pl.program_id(0)
    part = lax.dot_general(
        a_ref[...], b_ref[...], (((0,), (0,)), ((), ())), preferred_element_type=jnp.float32
    )

    @pl.when(i == 0)
    def _():
        acc[...] = part

    @pl.when(i > 0)
    def _():
        acc[...] += part

    @pl.when(i == pl.num_programs(0) - 1)
    def _():
        o_ref[...] = acc[...].astype(o_ref.dtype)


def contract(a, b, ready, tile):
    rows = a.shape[0]
    shape = (a.shape[1], b.shape[1])
    still = lambda s: pl.BlockSpec(s, lambda i: (0,) * len(s), pipeline_mode=pl.Buffered(1))
    return pl.pallas_call(
        contract_kernel,
        out_shape=jax.ShapeDtypeStruct(shape, a.dtype),
        grid=(rows // tile,),
        in_specs=[
            pl.BlockSpec((tile, shape[0]), lambda i: (i, 0)),
            pl.BlockSpec((tile, shape[1]), lambda i: (i, 0)),
            still(ready.shape),
        ],
        out_specs=still(shape),
        scratch_shapes=[pltpu.VMEM(shape, jnp.float32)],
        compiler_params=pltpu.CompilerParams(
            dimension_semantics=("arbitrary",), vmem_limit_bytes=40 << 20
        ),
        cost_estimate=SMALL,
        name="contract",
    )(a, b, ready)


def give_back_kernel(
    n, nf, rows, v_ref, w_ref, p_ref, c_ref, o_ref, v_out, w_out, p_out, c_out, o_out, planes, sums, *sems
):
    s = lax.axis_index("seq")
    f = lax.axis_index("fsdp")
    sems = list(sems)
    take = lambda k: [sems.pop(0) for _ in range(k)]
    send_z, recv_z, send_s, recv_s = take(4)
    parts = []
    if rows is not None:
        parts.append(rows.bind(w_ref, w_out, *take(3)))
    parts.append(Units(n, nf, True, c_ref, c_out, *take(3)))
    parts.append(Blocks("seq", n, False, p_ref, p_out, *take(3)))
    parts.append(Blocks("fsdp", nf, False, o_ref, o_out, *take(3)))
    others = [{"fsdp": lax.rem(f + d, nf)} for d in range(1, nf)]
    peers = [{"seq": place(s, r, n)} for r in range(1, n)]
    greet(peers + others)
    copies = []
    for d in range(1, nf):
        c = remote(v_ref.at[lax.rem(f + d, nf)], planes.at[d - 1], send_z.at[d - 1], recv_z.at[d - 1], others[d - 1])
        c.start()
        copies.append(c)
    for p in parts[:1]:
        p.start()
    total = v_ref[f]
    for d, c in enumerate(copies):
        c.wait_recv()
        total = total + planes[d]
    sums[0] = total
    spread = []
    for r in range(1, n):
        c = remote(sums.at[0], sums.at[r], send_s.at[r - 1], recv_s.at[r - 1], peers[r - 1])
        c.start()
        spread.append(c)
    for p in parts[1:]:
        p.start()
    for r, c in enumerate(spread):
        c.wait_recv()
        total = total + sums[r + 1]
    v_out[...] = total
    for p in parts:
        p.finish()
    for c in copies + spread:
        c.wait_send()


def give_back(vectors, w, held, p, c, o, n, nf, rows, ident):
    k = vectors.shape[1]
    tiles = -(-k // 1024) * 8
    padded = jnp.pad(vectors, ((0, 0), (0, tiles * 128 - k))).reshape(nf, tiles, 128)
    vmem = pl.BlockSpec(memory_space=pltpu.VMEM)
    hbm = pl.BlockSpec(memory_space=pl.ANY)
    dma = pltpu.SemaphoreType.DMA
    out = pl.pallas_call(
        functools.partial(give_back_kernel, n, nf, rows),
        out_shape=[
            jax.ShapeDtypeStruct((tiles, 128), jnp.float32),
            jax.ShapeDtypeStruct((held, w.shape[1]), w.dtype),
            blocks_shape(p, n, False),
            blocks_shape(c, nf, False),
            blocks_shape(o, nf, False),
        ],
        in_specs=[vmem, hbm, hbm, hbm, hbm],
        out_specs=[vmem, hbm, hbm, hbm, hbm],
        scratch_shapes=[
            pltpu.VMEM((nf - 1, tiles, 128), jnp.float32),
            pltpu.VMEM((n, tiles, 128), jnp.float32),
            dma((nf - 1,)),
            dma((nf - 1,)),
            dma((n - 1,)),
            dma((n - 1,)),
        ]
        + (rows.scratch() if rows is not None else [])
        + Units.scratch(nf)
        + Blocks.scratch(n)
        + Blocks.scratch(nf),
        compiler_params=pltpu.CompilerParams(collective_id=ident, has_side_effects=True),
        cost_estimate=SMALL,
        name="give_back",
    )(padded, w, p, c, o)
    return out[0].reshape(-1)[:k], out[1], out[2], out[3], out[4]


HEAD=64
SCALE=0.125*math.log2(math.e)


def block_pairs(slots, trunk):
    branches = (slots - trunk) // 3
    pairs = []
    for t in range(slots):
        m = t - trunk
        if t < trunk:
            keys = [(c, int(c == t), -1, -1) for c in range(t + 1)]
        else:
            keys = [(c, 0, -1, -1) for c in range(trunk)]
            if m >= branches:
                keys.append((trunk, 0, -1, m))
            keys.append((t, 1, m, -1))
        for i, (c, causal, own, leaf) in enumerate(keys):
            pairs.append((t, c, causal, own, leaf, int(i == 0), int(i == len(keys) - 1)))
    return pairs


def block_fields(p, slots, trunk):
    branches = (slots - trunk) // 3
    counts = [t + 1 for t in range(trunk)] + [trunk + 1] * branches
    counts += [trunk + 2] * (slots - trunk - branches)
    starts = [sum(counts[:t]) for t in range(slots)]
    t, begin, end = jnp.int32(0), jnp.int32(0), jnp.int32(counts[0])
    for i in range(1, slots):
        here = p >= starts[i]
        t = jnp.where(here, i, t)
        begin = jnp.where(here, starts[i], begin)
        end = jnp.where(here, starts[i] + counts[i], end)
    i = p - begin
    last = p == end - 1
    leaf = (t >= trunk + branches) & (i == trunk)
    key = jnp.where((t >= trunk) & last, t, i)
    return t, key, last, leaf, i == 0, last


def block_values(lengths, parents, pairs, block):
    count = lengths.shape[0]
    segments = np.arange(count)
    own = np.array([p[3] for p in pairs])[None, :] == segments[:, None]
    leaf = np.array([p[4] for p in pairs])[None, :] == segments[:, None]
    above = jnp.sum(jnp.where(leaf, parents[:, None], 0), 0)
    source = own | (segments[:, None] + 1 == above[None, :])
    closed = np.array([p[3] < 0 and p[4] < 0 for p in pairs])
    reach = jnp.where(closed, block, jnp.sum(jnp.where(source, lengths[:, None], 0), 0))
    return jnp.stack([jnp.maximum(above - 1, 0), reach]).astype(jnp.int32)


def lane_half(shape):
    return lax.broadcasted_iota(jnp.int32, shape, len(shape) - 1) < HEAD


def nt(a, b):
    return lax.dot_general(a, b, (((1,), (1,)), ((), ())), preferred_element_type=jnp.float32)


def mm(a, b):
    return jnp.dot(a, b, preferred_element_type=jnp.float32)


def attend_kernel(width, block, trunk, n, values, x_ref, w_ref, b_ref, c_ref, qkv, low, att, tot, kt, c_all, acc, xbuf, xsem, *sems):
    p = pl.program_id(0)
    slot, key, causal, leaf, first, last = block_fields(p, n, trunk)
    rows = lambda slot: pl.ds(pl.multiple_of(slot * block, block), block)
    qrow = rows(slot)
    above = values[0, p]
    reach = values[1, p]
    branches = (n - trunk) // 3
    left = lane_half((block, 2 * HEAD))
    spread = Spread(n, c_ref, c_all, *sems)

    def fetch(i):
        slot = lax.rem(i, 2)
        return pltpu.make_async_copy(x_ref.at[i], xbuf.at[slot], xsem.at[slot])

    @pl.when(p == 0)
    def _():
        fetch(jnp.int32(0)).start()
        greet(spread.peers())
        spread.start()

        def step(i, carry):
            @pl.when(i + 1 < n)
            def _():
                fetch(i + 1).start()

            fetch(i).wait()
            made = (mm(xbuf[lax.rem(i, 2)], w_ref[...]) + b_ref[...]).astype(qkv.dtype)
            qkv[rows(i)] = made
            kt[:, rows(i)] = made[:, width : 2 * width].T
            return carry

        lax.fori_loop(0, n, step, 0)
        for i in range(len(spread.bits) - 1):
            spread.phase(i)

    @pl.when(first)
    def _():
        acc[...] = jnp.zeros_like(acc)

    def keyed(mask, read):
        got = read(rows(key))
        if mask is not None:
            for b in range(1, branches):
                got = jnp.where(leaf & (above == b), read(pl.ds((trunk + b) * block, block)), got)
        return got

    def step(mask):
        for j in range(width // (2 * HEAD)):
            lanes = slice(j * 2 * HEAD, (j + 1) * 2 * HEAD)
            q = qkv[qrow, lanes]
            k = keyed(mask, lambda at: qkv[at, width + j * 2 * HEAD : width + (j + 1) * 2 * HEAD])
            v = keyed(mask, lambda at: qkv[at, 2 * width + j * 2 * HEAD : 2 * width + (j + 1) * 2 * HEAD])
            for h in range(2):
                here = left if h == 0 else jnp.logical_not(left)
                s = nt(jnp.where(here, q, 0), k)
                e = jnp.exp2(s * SCALE)
                if mask is not None:
                    e = jnp.where(mask, e, 0.0)
                acc[2 * j + h] += mm(e.astype(jnp.bfloat16), jnp.where(here, v, 1))

    closes = causal | leaf
    shift = jnp.where(causal, 0, block)

    @pl.when(jnp.logical_not(closes))
    def _():
        step(None)

    @pl.when(closes)
    def _():
        row = lax.broadcasted_iota(jnp.int32, (block, block), 0)
        col = lax.broadcasted_iota(jnp.int32, (block, block), 1)
        step((col <= row + shift) & (col < reach))

    @pl.when(last)
    def _():
        for j in range(width // (2 * HEAD)):
            a, b = acc[2 * j], acc[2 * j + 1]
            total = jnp.where(left, pltpu.roll(a, HEAD, 1), pltpu.roll(b, HEAD, 1))
            value = jnp.where(left, a, b) / total
            lanes = slice(j * 2 * HEAD, (j + 1) * 2 * HEAD)
            low[:, lanes] = value.astype(jnp.bfloat16)
            att[:, lanes] = value
            tot[:, lanes] = total

    @pl.when(p == pl.num_programs(0) - 1)
    def _():
        spread.phase(len(spread.bits) - 1)
        spread.finish()


def attend(values, pairs, x, w, bias, block, trunk, sent, n, ident):
    rows, width = x.shape[0], w.shape[1] // 3
    by_q = lambda p: (block_fields(p, n, trunk)[0], 0)
    heads = width // HEAD
    once = lambda s: pl.BlockSpec(s, lambda p: (0,) * len(s), pipeline_mode=pl.Buffered(1))
    hbm = pl.BlockSpec(memory_space=pl.ANY)
    out = pl.pallas_call(
        functools.partial(attend_kernel, width, block, trunk, n),
        grid=(len(pairs),),
        out_shape=(
            jax.ShapeDtypeStruct((rows, 3 * width), x.dtype),
            jax.ShapeDtypeStruct((rows, width), x.dtype),
            jax.ShapeDtypeStruct((rows, width), jnp.float32),
            jax.ShapeDtypeStruct((rows, width), jnp.float32),
            jax.ShapeDtypeStruct((width, rows), x.dtype),
            jax.ShapeDtypeStruct((n,) + sent.shape, sent.dtype),
        ),
        in_specs=[pl.BlockSpec(memory_space=pltpu.SMEM), hbm, once(w.shape), once(bias.shape), hbm],
        out_specs=[once((rows, 3 * width))]
        + [pl.BlockSpec((block, width), by_q)] * 3
        + [once((width, rows)), hbm],
        scratch_shapes=[
            pltpu.VMEM((heads, block, 2 * HEAD), jnp.float32),
            pltpu.VMEM((2, block, x.shape[1]), x.dtype),
            pltpu.SemaphoreType.DMA((2,)),
        ]
        + Spread.scratch(n),
        compiler_params=pltpu.CompilerParams(
            dimension_semantics=("arbitrary",),
            vmem_limit_bytes=60 << 20,
            collective_id=ident,
            has_side_effects=True,
        ),
        cost_estimate=SMALL,
        name="attend",
    )(values, x.reshape(n, block, x.shape[1]), w, bias, sent)
    return out[:5] + (out[5].reshape(n * sent.shape[0], sent.shape[1]),)


def attend_back_kernel(width, block, slots, trunk, branches, nf, count, *refs):
    values, qkv, kt, datt, att, tot = refs[:6]
    sources = refs[6 : 6 + count]
    out, sums = refs[6 + count : 8 + count]
    targets = refs[8 + count : 8 + 2 * count]
    dk, dv, dqt, aug = refs[8 + 2 * count : 12 + 2 * count]
    sems = refs[12 + 2 * count :]
    riders = [
        Blocks("fsdp", nf, False, sources[i], targets[i], *sems[3 * i : 3 * i + 3]) for i in range(count)
    ]
    p = pl.program_id(0)
    slot, key, causal, leaf, first, last = block_fields(p, slots, trunk)
    rows = lambda slot: pl.ds(pl.multiple_of(slot * block, block), block)
    above = values[0, p]
    reach = values[1, p]
    qrow = rows(slot)
    left = lane_half((block, 2 * HEAD))
    lane = lax.broadcasted_iota(jnp.int32, (block, 2 * HEAD), 1)
    columns = width // (2 * HEAD)

    @pl.when(p == 0)
    def _():
        greet(riders[0].peers())
        for r in riders:
            r.start()
        dk[...] = jnp.zeros_like(dk)
        dv[...] = jnp.zeros_like(dv)

    @pl.when(first)
    def _():
        dqt[...] = jnp.zeros_like(dqt)
        for j in range(columns):
            lanes = slice(j * 2 * HEAD, (j + 1) * 2 * HEAD)
            d = datt[:, lanes].astype(jnp.float32)
            total = tot[:, lanes]
            low = (d / total).astype(jnp.bfloat16)
            prod = d * att[:, lanes] / total
            for h in range(2):
                here = left if h == 0 else jnp.logical_not(left)
                delta = -jnp.sum(jnp.where(here, prod, 0.0), 1, keepdims=True)
                hi = delta.astype(jnp.bfloat16).astype(jnp.float32)
                mid = (delta - hi).astype(jnp.bfloat16).astype(jnp.float32)
                rest = delta - hi - mid
                at = HEAD * (1 - h)
                extra = jnp.where(
                    lane == at, hi, jnp.where(lane == at + 1, mid, jnp.where(lane == at + 2, rest, 0.0))
                )
                aug[2 * j + h] = jnp.where(here, low.astype(jnp.float32), extra).astype(jnp.bfloat16)

    def add(lanes, dks, dvs):
        @pl.when(jnp.logical_not(leaf))
        def _():
            at = rows(key)
            dk[at, lanes] += dks
            dv[at, lanes] += dvs

        @pl.when(leaf)
        def _():
            for b in range(branches):
                at = pl.ds((trunk + b) * block, block)
                dk[at, lanes] += jnp.where(above == b, dks, 0.0)
                dv[at, lanes] += jnp.where(above == b, dvs, 0.0)

    def keyed(mask, read):
        got = read(rows(key))
        if mask is not None:
            for b in range(1, branches):
                got = jnp.where(leaf & (above == b), read(pl.ds((trunk + b) * block, block)), got)
        return got

    def step(mask):
        for j in range(columns):
            lanes = slice(j * 2 * HEAD, (j + 1) * 2 * HEAD)
            q = qkv[qrow, lanes]
            k = keyed(mask, lambda at: qkv[at, width + j * 2 * HEAD : width + (j + 1) * 2 * HEAD])
            v = keyed(mask, lambda at: qkv[at, 2 * width + j * 2 * HEAD : 2 * width + (j + 1) * 2 * HEAD])
            dvs, dks = [], []
            for h in range(2):
                here = left if h == 0 else jnp.logical_not(left)
                qh = jnp.where(here, q, 0)
                e = jnp.exp2(nt(k, qh) * SCALE)
                if mask is not None:
                    e = jnp.where(mask, e, 0.0)
                dod = aug[2 * j + h]
                ds = (e * nt(jnp.where(here, v * 0.125, 0.125).astype(jnp.bfloat16), dod)).astype(
                    jnp.bfloat16
                )
                dvs.append(mm(e.astype(jnp.bfloat16), dod))
                dks.append(mm(ds, qh))
                at = j * 2 * HEAD + h * HEAD
                dqt[at : at + HEAD] += mm(keyed(mask, lambda i: kt[at : at + HEAD, i]), ds)
            add(lanes, dks[0] + dks[1], jnp.where(left, dvs[0], dvs[1]))

    closes = causal | leaf
    shift = jnp.where(causal, 0, block)

    @pl.when(jnp.logical_not(closes))
    def _():
        step(None)

    @pl.when(closes)
    def _():
        col = lax.broadcasted_iota(jnp.int32, (block, block), 0)
        row = lax.broadcasted_iota(jnp.int32, (block, block), 1)
        step((col <= row + shift) & (col < reach))

    @pl.when(last)
    def _():
        out[qrow, 0:width] = dqt[...].T.astype(jnp.bfloat16)

    @pl.when(p == pl.num_programs(0) - 1)
    def _():
        out[:, width : 2 * width] = dk[...].astype(jnp.bfloat16)
        out[:, 2 * width :] = dv[...].astype(jnp.bfloat16)
        for t in range(3):
            lanes = slice(t * width, (t + 1) * width)
            sums[:, lanes] = jnp.sum(out[:, lanes].astype(jnp.float32), 0, keepdims=True)
        for r in riders:
            r.finish()


def attend_back(values, pairs, qkv, kt, datt, att, tot, block, trunk, nf, riders, ident):
    rows, width = qkv.shape[0], qkv.shape[1] // 3
    by_q = lambda p: (block_fields(p, rows // block, trunk)[0], 0)
    heads = width // HEAD
    branches = (rows // block - trunk) // 3
    once = lambda s: pl.BlockSpec(s, lambda p: (0,) * len(s), pipeline_mode=pl.Buffered(1))
    hbm = pl.BlockSpec(memory_space=pl.ANY)
    out = pl.pallas_call(
        functools.partial(
            attend_back_kernel, width, block, rows // block, trunk, branches, nf, len(riders)
        ),
        grid=(len(pairs),),
        out_shape=[
            jax.ShapeDtypeStruct((rows, 3 * width), jnp.bfloat16),
            jax.ShapeDtypeStruct((1, 3 * width), jnp.float32),
        ]
        + [blocks_shape(r, nf, False) for r in riders],
        in_specs=[pl.BlockSpec(memory_space=pltpu.SMEM), once((rows, 3 * width)), once((width, rows))]
        + [pl.BlockSpec((block, width), by_q)] * 3
        + [hbm] * len(riders),
        out_specs=[once((rows, 3 * width)), once((1, 3 * width))] + [hbm] * len(riders),
        scratch_shapes=[
            pltpu.VMEM((rows, width), jnp.float32),
            pltpu.VMEM((rows, width), jnp.float32),
            pltpu.VMEM((width, block), jnp.float32),
            pltpu.VMEM((heads, block, 2 * HEAD), jnp.bfloat16),
        ]
        + sum([Blocks.scratch(nf) for _ in riders], []),
        compiler_params=pltpu.CompilerParams(
            dimension_semantics=("arbitrary",),
            vmem_limit_bytes=60 << 20,
            collective_id=ident,
            has_side_effects=True,
        ),
        cost_estimate=SMALL,
        name="attend_back",
    )(values, qkv, kt, datt, att, tot, *riders)
    return out[0], out[1], out[2:]


def layer_norm(values, gain, shift):
    centred = values - jnp.mean(values, -1, keepdims=True)
    spread = jnp.mean(centred * centred, -1, keepdims=True)
    return centred * lax.rsqrt(spread + 1e-05) * gain + shift


def contract_rows(left, right):
    return lax.dot_general(
        left, right, (((0,), (0,)), ((), ())), preferred_element_type=jnp.float32
    )


def contract_cols(left, right):
    return lax.dot_general(
        left, right, (((1,), (1,)), ((), ())), preferred_element_type=jnp.float32
    )


def after(value, other):
    return value + (other[(0,) * other.ndim] * 0).astype(value.dtype)


def row_major(x):
    return with_layout_constraint(x, Layout(major_to_minor=tuple(range(x.ndim))))


def local(
    tokens,
    ln1_gain,
    ln1_bias,
    qkv_weight,
    qv_bias,
    out_weight,
    out_bias,
    ln2_gain,
    ln2_bias,
    fc_weight,
    fc_bias,
    proj_weight,
    proj_bias,
    seg_lengths,
    parents,
    cotangent,
):
    n = lax.axis_size("seq")
    nf = lax.axis_size("fsdp")
    s = lax.axis_index("seq")
    f = lax.axis_index("fsdp")
    trunk = n // 4
    block, width = tokens.shape[1], tokens.shape[2]
    rows = width // nf
    hidden = fc_weight.shape[1] * n
    piece = hidden // (n * nf)
    group = n // nf
    wide = 2 * HEAD * (-(-HEADS // (2 * n)))
    low = jnp.bfloat16
    wider = jnp.float32

    vectors = [ln1_gain, ln1_bias, qv_bias, out_bias, ln2_gain, ln2_bias, fc_bias, proj_bias]
    sizes = [v.shape[0] for v in vectors]
    qkv_cols = qkv_weight.shape[1]
    even = qkv_cols % 8 == 0
    forth = Rows(n, qkv_cols, width, wide, False) if even else None
    back = Rows(n, qkv_cols, width, wide, True) if even else None
    turned, proj_blocks, fc_blocks, out_blocks, gathered = exchange(
        qkv_weight.T,
        proj_weight.reshape(n, piece, width // n),
        fc_weight.reshape(rows, nf, piece).transpose(1, 0, 2),
        out_weight,
        [v.reshape(1, -1) for v in vectors],
        n,
        nf,
        forth,
        wide,
        0,
    )
    whole = [v.reshape(-1).astype(wider) for v in gathered]
    gain_one, shift_one, bias_qv, bias_out, gain_two, shift_two, bias_fc, bias_proj = whole
    bias_three = jnp.stack([bias_qv[:width], jnp.zeros((width,), wider), bias_qv[width:]])
    bias_three = jnp.pad(bias_three, ((0, 0), (0, n * wide - width)))
    bias_mine = lax.dynamic_slice_in_dim(bias_three, s * wide, wide, 1).reshape(1, -1)
    bias_hidden = lax.dynamic_index_in_dim(bias_fc.reshape(nf, n, piece), s, 1, False)
    bias_hidden = bias_hidden.reshape(1, -1)

    if even:
        turned = turned.reshape(3, wide, rows)
        kept = lax.broadcasted_iota(jnp.int32, turned.shape, 1) + s * wide < width
        turned = jnp.where(kept, turned, 0).reshape(3 * wide, rows)
    else:
        turned = lax.all_gather(qkv_weight.T, "seq", axis=0, tiled=True).reshape(3, width, rows)
        turned = jnp.pad(turned, ((0, 0), (0, n * wide - width), (0, 0)))
        turned = lax.dynamic_slice_in_dim(turned, s * wide, wide, 1).reshape(3 * wide, rows)
    pairs = block_pairs(n, trunk)
    table = block_values(seg_lengths[0], parents[0], pairs, block)

    resid = tokens[0].astype(wider)
    out_turned = jnp.pad(out_blocks.reshape(width, width // n).T, ((0, 0), (0, n * wide - width)))
    normed_one, out_turned, qkv_mine = seq_gather(
        layer_norm(resid, gain_one, shift_one).astype(low),
        n,
        1,
        "gather_one",
        rider=(turned.T, True, nf),
        second=out_turned,
    )
    out_turned = out_turned.reshape(width, n * wide)
    qkv_mine = qkv_mine.reshape(width, 3 * wide)
    fc_rows = fc_blocks.transpose(1, 0, 2).reshape(rows, nf * piece)
    fc_mine = lax.all_gather(fc_rows, "fsdp", axis=0, tiled=True)

    upstream = cotangent[0].astype(wider)
    proj_rows = proj_blocks.transpose(1, 0, 2).reshape(piece, width)
    proj_mine = lax.all_gather(after(proj_rows, normed_one), "fsdp", axis=0, tiled=True)
    projected, attended_low, attended, totals, keys_turned, upstream_all = attend(
        table, pairs, normed_one, qkv_mine, bias_mine, block, trunk, cotangent[0], n, 8
    )
    attended_mine = to_tokens(attended_low.reshape(n, block, wide), n, wide, 2)
    middle = resid + contract_cols(attended_mine, out_turned) + bias_out
    normed_two = layer_norm(middle, gain_two, shift_two).astype(low)
    ff = nf * piece

    def expand(value, fc, bias, proj):
        pre = mm(value, fc[...]) + bias[...]
        bend = math.sqrt(2 / math.pi)
        square = pre * pre
        inner = jnp.tanh(pre * (bend + bend * 0.044715 * square))
        half = 0.5 + 0.5 * inner
        act = (pre * half).astype(low)
        slope = half + 0.5 * pre * (1 - inner * inner) * (bend + 3 * bend * 0.044715 * square)
        return act, slope.astype(low), mm(act, proj[...]).astype(low)

    normed_two, hidden_act, hidden_slope, mixed = seq_gather(
        normed_two,
        n,
        3,
        "gather_two",
        expand,
        (fc_mine, bias_hidden, proj_mine),
        ((ff, low), (ff, low), (width, low)),
        modes=(0, 0, 0),
    )

    def shrink(up, slope, proj, fc):
        grad = (nt(up, proj[...]) * slope.astype(wider)).astype(low)
        return nt(grad, fc[...]), grad

    grad_normed_two, grad_pre, grad_proj, unused_sums, mixed = seq_scatter(
        n,
        width,
        4,
        "scatter_two",
        shrink,
        (upstream_all, hidden_slope),
        (proj_mine, fc_mine),
        ((ff, low),),
        side=(hidden_act, upstream_all),
        carry=mixed,
    )
    mixed = lax.psum_scatter(mixed, "seq", scatter_dimension=0, tiled=True).astype(wider)
    grad_proj = grad_proj.reshape(nf, piece, width)
    cut = piece // 16 * 8
    unused_two, norm_two_back = jax.vjp(layer_norm, middle, gain_two, shift_two)
    grad_middle_norm, grad_gain_two, grad_shift_two = norm_two_back(grad_normed_two)
    grad_middle = upstream + grad_middle_norm
    grad_branch = grad_middle.astype(low)
    grad_attended, grad_fc, hidden_sums, proj_first = to_heads(
        grad_branch, out_turned, n, nf, wide, 5, normed_two, grad_pre, grad_proj[:, :cut]
    )
    grad_attended = grad_attended.reshape(n * block, wide)
    grad_projected, column_sums, (fc_parts, proj_second) = attend_back(
        table,
        pairs,
        projected,
        keys_turned,
        grad_attended,
        attended,
        totals,
        block,
        trunk,
        nf,
        (grad_fc.reshape(nf, rows, ff), grad_proj[:, cut:]),
        9,
    )
    output = (after(middle, grad_projected) + mixed + bias_proj).astype(low)[None]
    ready = output[0, :8, :128].astype(wider)
    grad_qkv = contract(normed_one, grad_projected, ready, block)
    grad_normed_one, qkv_parts = seq_scatter(
        n,
        width,
        6,
        "scatter_one",
        lambda g, w: (nt(g, w[...]),),
        (grad_projected,),
        (qkv_mine,),
        rider=(grad_qkv.reshape(nf, rows, 3 * wide), False, nf),
    )
    unused_one, norm_one_back = jax.vjp(layer_norm, resid, gain_one, shift_one)
    grad_resid_norm, grad_gain_one, grad_shift_one = norm_one_back(grad_normed_one)
    input_grad = (grad_middle + grad_resid_norm).astype(low)[None]

    proj_part = jnp.concatenate([proj_first, proj_second], 1)
    proj_part = jnp.sum(proj_part.astype(wider), 0).astype(low)
    proj_part = proj_part.reshape(piece, n, width // n).transpose(1, 0, 2)
    fc_part = jnp.sum(fc_parts.astype(wider), 0).astype(low)
    fc_part = fc_part.reshape(rows, nf, piece).transpose(1, 0, 2)
    grad_out = contract_rows(
        after(grad_branch, grad_attended), attended_mine[:, :width]
    ).astype(low)
    out_part = lax.psum_scatter(grad_out, "seq", scatter_dimension=0, tiled=True).T
    out_part = after(out_part, grad_normed_one).reshape(nf, rows, width // n)
    qkv_part = jnp.sum(qkv_parts.astype(wider), 0).astype(low).T

    column_sums = column_sums.reshape(3, wide)
    placed = lax.dynamic_update_slice_in_dim(
        jnp.zeros((3, n * wide), wider), column_sums, s * wide, 1
    )[:, :width]
    grad_qv = jnp.concatenate([placed[0], placed[2]])
    hidden_sums = hidden_sums.reshape(nf, 1, piece)
    grad_fc_bias = lax.dynamic_update_slice_in_dim(
        jnp.zeros((nf, n, piece), wider), hidden_sums, s, 1
    )
    parts = [
        grad_gain_one,
        grad_shift_one,
        grad_qv,
        jnp.sum(grad_branch.astype(wider), 0),
        grad_gain_two,
        grad_shift_two,
        grad_fc_bias,
        jnp.sum(upstream, 0),
    ]
    summed, qkv_out, proj_out, fc_out, out_out = give_back(
        jnp.concatenate([p.reshape(nf, -1) for p in parts], 1),
        qkv_part,
        qkv_cols,
        proj_part,
        fc_part,
        out_part,
        n,
        nf,
        back,
        7,
    )
    if not even:
        qkv_part = qkv_part.reshape(3, wide, rows)
        qkv_out = lax.all_gather(qkv_part, "seq", axis=1, tiled=True)[:, :width]
        qkv_out = qkv_out.reshape(3 * width, rows)
        qkv_out = lax.dynamic_slice_in_dim(qkv_out, s * qkv_cols, qkv_cols, 0)
    out_out = jnp.sum(out_out.astype(wider), 0)
    qkv_out = qkv_out.T.astype(wider)
    proj_out = proj_out.reshape(n * piece, width // n).astype(wider)
    fc_out = fc_out.transpose(1, 0, 2).reshape(rows, nf * piece).astype(wider)
    vector_out = []
    at = 0
    for size in sizes:
        vector_out.append(summed[at : at + size])
        at += size
    return (
        output,
        input_grad,
        vector_out[0],
        vector_out[1],
        qkv_out,
        vector_out[2],
        out_out,
        vector_out[3],
        vector_out[4],
        vector_out[5],
        fc_out,
        vector_out[6],
        proj_out,
        vector_out[7],
    )


def solution(mesh):
    in_specs = (
        P("fsdp", "seq", None),
        P("fsdp"),
        P("fsdp"),
        P("fsdp", "seq"),
        P("fsdp"),
        P("fsdp", "seq"),
        P("fsdp"),
        P("fsdp"),
        P("fsdp"),
        P("fsdp", "seq"),
        P("fsdp"),
        P("fsdp", "seq"),
        P("fsdp"),
        P("fsdp", None),
        P("fsdp", None),
        P("fsdp", "seq", None),
    )
    out_specs = (
        P("fsdp", "seq", None),
        P("fsdp", "seq", None),
        P("fsdp"),
        P("fsdp"),
        P("fsdp", "seq"),
        P("fsdp"),
        P("fsdp", "seq"),
        P("fsdp"),
        P("fsdp"),
        P("fsdp"),
        P("fsdp", "seq"),
        P("fsdp"),
        P("fsdp", "seq"),
        P("fsdp"),
    )
    return jax.shard_map(local, mesh=mesh, in_specs=in_specs, out_specs=out_specs, check_vma=False)
```

```python
import functools
import math

import jax
import jax.numpy as jnp
import numpy as np
from jax import lax
from jax.experimental import pallas as pl
from jax.experimental.layout import Layout, with_layout_constraint
from jax.experimental.pallas import tpu as pltpu
from jax.sharding import PartitionSpec as P

MESH = pl.DeviceIdType.MESH
HEADS = 25
SMALL = pl.CostEstimate(flops=0, bytes_accessed=1 << 20, transcendentals=0)


def route_bits(n):
    bits = []
    b = 2
    while b < n:
        bits.append(b)
        b *= 2
    return bits


def flip(a, b):
    return jnp.where(lax.rem(lax.div(a, b), 2) == 0, a + b, a - b)


def place(me, r, n):
    if isinstance(r, int):
        for b in [1] + route_bits(n):
            if r & b:
                me = flip(me, b)
        return me
    for b in [1] + route_bits(n):
        me = jnp.where(lax.rem(lax.div(r, b), 2) == 0, me, flip(me, b))
    return me


def pick(table, q):
    value = jnp.int32(table[0])
    for i, entry in enumerate(table[1:]):
        value = jnp.where(q == i + 1, jnp.int32(entry), value)
    return value


def greet(ids):
    barrier = pltpu.get_barrier_semaphore()
    for i in ids:
        pl.semaphore_signal(barrier, inc=1, device_id=i, device_id_type=MESH)
    pl.semaphore_wait(barrier, len(ids))


def remote(src, dst, send, recv, device):
    return pltpu.make_async_remote_copy(
        src_ref=src, dst_ref=dst, send_sem=send, recv_sem=recv, device_id=device, device_id_type=MESH
    )


class Blocks:
    def __init__(self, axis, size, same, source, target, send, recv, local):
        self.axis, self.size, self.same = axis, size, same
        self.source, self.target = source, target
        self.send, self.recv, self.local = send, recv, local
        self.me = lax.axis_index(axis)

    @staticmethod
    def scratch(size):
        dma = pltpu.SemaphoreType.DMA
        return [dma((size - 1,)), dma((size - 1,)), dma]

    def peers(self):
        return [{self.axis: lax.rem(self.me + d, self.size)} for d in range(1, self.size)]

    def copy(self, d):
        to = lax.rem(self.me + d, self.size)
        src = self.source if self.same else self.source.at[to]
        return remote(src, self.target.at[self.me], self.send.at[d - 1], self.recv.at[d - 1], {self.axis: to})

    def own(self):
        src = self.source if self.same else self.source.at[self.me]
        return pltpu.make_async_copy(src, self.target.at[self.me], self.local)

    def start(self):
        for d in range(1, self.size):
            self.copy(d).start()
        self.own().start()

    def finish(self):
        for d in range(1, self.size):
            dst = self.target.at[lax.rem(self.me + self.size - d, self.size)]
            remote(dst, dst, self.send.at[d - 1], self.recv.at[d - 1], {self.axis: self.me}).wait_recv()
        self.own().wait()
        for d in range(1, self.size):
            self.copy(d).wait_send()


class Spread:
    def __init__(self, n, source, target, send, recv, local):
        self.n, self.source, self.target = n, source, target
        self.send, self.recv, self.local = send, recv, local
        self.me = lax.axis_index("seq")
        self.bits = route_bits(n)
        self.orders = [self.bits, self.bits[::-1]]
        self.h = source.shape[0] // 2

    @staticmethod
    def scratch(n):
        dma = pltpu.SemaphoreType.DMA
        return [dma((2, len(route_bits(n)) + 1, n)), dma((2, n)), dma]

    def device(self, b):
        return {"seq": flip(self.me, b)}

    def peers(self):
        return [self.device(b) for b in [1] + self.bits]

    def rows(self, half):
        return pl.ds(half * self.h, self.h)

    def ship(self, half, k, b):
        owner = place(self.me, k, self.n)
        src = self.source if k == 0 else self.target.at[owner]
        lane = 0 if b == 1 else 1 + self.bits.index(b)
        return remote(
            src.at[self.rows(half)],
            self.target.at[owner].at[self.rows(half)],
            self.send.at[half, lane, k],
            self.recv.at[half, k ^ b],
            self.device(b),
        )

    def arrive(self, half, k):
        dst = self.target.at[place(self.me, k, self.n)].at[self.rows(half)]
        remote(dst, dst, self.send.at[half, 0, 0], self.recv.at[half, k], self.device(1)).wait_recv()

    def own(self):
        return pltpu.make_async_copy(self.source, self.target.at[self.me], self.local)

    def fresh(self, half, i):
        had = [0]
        for b in self.orders[half][:i]:
            had = had + [k ^ b for k in had]
        return [k ^ self.orders[half][i] for k in had]

    def start(self):
        for i in range(len(self.bits)):
            for half in (0, 1):
                self.ship(half, 0, self.orders[half][i]).start()
        for half in (0, 1):
            self.ship(half, 0, 1).start()
        self.own().start()

    def phase(self, i):
        for half in (0, 1):
            for k in self.fresh(half, i):
                self.arrive(half, k)
                for b in self.orders[half][i + 1 :] + [1]:
                    self.ship(half, k, b).start()

    def finish(self):
        for half in (0, 1):
            for k in range(1, self.n, 2):
                self.arrive(half, k)
        self.own().wait()
        for half in (0, 1):
            for b in self.orders[half] + [1]:
                self.ship(half, 0, b).wait_send()
            for i in range(len(self.bits)):
                for k in self.fresh(half, i):
                    for b in self.orders[half][i + 1 :] + [1]:
                        self.ship(half, k, b).wait_send()


class PlaneSum(Blocks):
    def __init__(self, size, source, low, target, send, recv, local):
        super().__init__("fsdp", size, False, source, target, send, recv, local)
        self.window = pl.ds(low, target.shape[1])

    @staticmethod
    def scratch(size, rows, cols):
        return [pltpu.VMEM((size, rows, cols), jnp.bfloat16)] + Blocks.scratch(size)

    def copy(self, d):
        to = lax.rem(self.me + d, self.size)
        src = self.source.at[to].at[self.window]
        return remote(src, self.target.at[self.me], self.send.at[d - 1], self.recv.at[d - 1], {self.axis: to})

    def own(self):
        src = self.source.at[self.me].at[self.window]
        return pltpu.make_async_copy(src, self.target.at[self.me], self.local)

    def store(self, out):
        total = self.target[0].astype(jnp.float32)
        for i in range(1, self.size):
            total = total + self.target[i].astype(jnp.float32)
        cols = out.shape[2]
        for i in range(out.shape[0]):
            out[i] = total[:, i * cols : (i + 1) * cols].astype(out.dtype)


def blocks_shape(x, size, same):
    return jax.ShapeDtypeStruct(((size,) + x.shape) if same else x.shape, x.dtype)


def arrival_order(n):
    bits = route_bits(n)
    orders = [bits, bits[::-1]]
    lists = []
    for order in orders:
        held, phases = [0], [-1]
        for i, b in enumerate(order):
            fresh = [h ^ b for h in held]
            held, phases = held + fresh, phases + [i] * len(fresh)
        lists.append(list(zip(held, phases)))
    entries = []
    for i in range(n // 2):
        for odd in (0, 1):
            for half in (0, 1):
                k, phase = lists[half][i]
                entries.append((half, k ^ odd, phase, odd))
    return orders, entries


def gather_kernel(n, h, body, n_const, n_out, relative, modes, nf, same, second, *refs):
    if second:
        at = 1 + n_const
        out = at + 1 + min(nf, 1) + 1 + n_out
        w_ref, w_all = refs[at], refs[out]
        w_send, w_recv, w_keep = refs[-3:]
        refs = refs[:at] + refs[at + 1 : out] + refs[out + 1 : -3]
        w_half = w_ref.shape[1] // 2
    refs, rider = split_rider(refs, nf, same, 1 + n_const, 1 + n_out)
    x_ref = refs[0]
    consts = refs[1 : 1 + n_const]
    all_ref = refs[1 + n_const]
    outs = refs[2 + n_const : 2 + n_const + n_out]
    held = refs[2 + n_const + n_out]
    stages = refs[3 + n_const + n_out : 3 + n_const + 2 * n_out]
    send, recv, keep, store = refs[3 + n_const + 2 * n_out :]
    me = lax.axis_index("seq")
    orders, entries = arrival_order(n)
    bits = orders[0]
    nb = len(bits)

    def device(b):
        return {"seq": flip(me, b)}

    def spot(half, k):
        return 2 * (k if relative else place(me, k, n)) + half

    def ship(half, k, b):
        at = spot(half, k)
        src = x_ref.at[pl.ds(half * h, h)] if isinstance(k, int) and k == 0 else held.at[at]
        lane = 0 if b == 1 else 1 + bits.index(b)
        to = k ^ b if isinstance(k, int) else place(k, b, n)
        dst = 2 * to + half if relative else at
        first = remote(src, held.at[dst], send.at[half, lane, k], recv.at[half, to], device(b))
        if not second:
            return [first]
        owner = place(me, k, n)
        lanes = pl.ds(half * w_half, w_half)
        src = w_ref if isinstance(k, int) and k == 0 else w_all.at[owner]
        other = remote(
            src.at[:, lanes], w_all.at[owner].at[:, lanes], w_send.at[half, lane, k], w_recv.at[half, to], device(b)
        )
        return [first, other]

    def each(copies, act):
        for c in copies:
            act(c)

    def w_arrive(half, k):
        dst = w_all.at[place(me, k, n)].at[:, pl.ds(0, w_half)]
        remote(dst, dst, w_send.at[0, 0, 0], w_recv.at[half, k], device(1)).wait_recv()

    greet([device(b) for b in [1] + bits] + (rider.peers() if nf else []))
    for i in range(nb):
        for half in (0, 1):
            each(ship(half, 0, orders[half][i]), lambda c: c.start())
    for half in (0, 1):
        each(ship(half, 0, 1), lambda c: c.start())
    if second:
        pltpu.make_async_copy(w_ref, w_all.at[me], w_keep).start()
    if nf:
        rider.start()

    def output(o, q, at):
        slot = lax.rem(q, 2)
        return pltpu.make_async_copy(stages[o].at[slot], outs[o].at[at], store.at[o, slot])

    def entry(q, at, value):
        results = body(value, *consts)
        for o in range(n_out):

            @pl.when(q >= 2)
            def _(o=o):
                output(o, q, at[modes[o]]).wait()

            stages[o][lax.rem(q, 2)] = results[o]
            output(o, q, at[modes[o]]).start()

    def step(q, carry):
        half = pick([e[0] for e in entries], q)
        k = pick([e[1] for e in entries], q)
        phase = pick([e[2] for e in entries], q)
        odd = pick([e[3] for e in entries], q)
        at = spot(half, k)

        @pl.when(k == 0)
        def _():
            held[at] = x_ref[pl.ds(pl.multiple_of(half * h, h), h)]

        @pl.when(k != 0)
        def _():
            remote(held.at[at], held.at[at], send.at[0, 0, 0], recv.at[half, k], device(1)).wait_recv()
            if second:
                w_arrive(half, k)

        for side in (0, 1):
            for i in range(nb):

                @pl.when((half == side) & (odd == 0) & (k != 0) & (phase < i))
                def _(side=side, i=i):
                    each(ship(side, k, orders[side][i]), lambda c: c.start())

            @pl.when((half == side) & (odd == 0) & (k != 0))
            def _(side=side):
                each(ship(side, k, 1), lambda c: c.start())

        pltpu.make_async_copy(held.at[at], all_ref.at[at], keep.at[q]).start()
        if n_out:
            entry(q, (2 * place(me, k, n) + half, 2 * k + half), held[at])
        return carry

    lax.fori_loop(0, 2 * n, step, 0)
    for q, (half, k, phase, odd) in enumerate(entries):
        at = spot(half, k)
        pltpu.make_async_copy(held.at[at], all_ref.at[at], keep.at[q]).wait()
        if q >= 2 * n - 2:
            for o in range(n_out):
                output(o, jnp.int32(q), at).wait()
        if not odd:
            for i in range(nb):
                if phase < i:
                    each(ship(half, k, orders[half][i]), lambda c: c.wait_send())
            each(ship(half, k, 1), lambda c: c.wait_send())
    if second:
        pltpu.make_async_copy(w_ref, w_all.at[me], w_keep).wait()
    if nf:
        rider.finish()


def split_rider(refs, nf, same, n_in, n_out):
    if not nf:
        return refs, None
    source = refs[n_in]
    target = refs[n_in + 1 + n_out]
    rider = Blocks("fsdp", nf, same, source, target, *refs[-3:])
    return refs[:n_in] + refs[n_in + 1 : n_in + 1 + n_out] + refs[n_in + 2 + n_out : -3], rider


def rider_parts(rider):
    if rider is None:
        return [], [], [], [], 0, False
    x, same, nf = rider
    hbm = [pl.BlockSpec(memory_space=pl.ANY)]
    return [x], hbm, [blocks_shape(x, nf, same)], Blocks.scratch(nf), nf, same


def seq_gather(x, n, ident, name, body=None, consts=(), outs=(), relative=False, modes=None, rider=None, second=None):
    rows, cols = x.shape
    h = rows // 2
    nb = len(route_bits(n))
    shapes = [jax.ShapeDtypeStruct((2 * n, h, c), d) for c, d in outs]
    vmem = pl.BlockSpec(memory_space=pltpu.VMEM)
    hbm = pl.BlockSpec(memory_space=pl.ANY)
    more, spec, shape, scratch, nf, same = rider_parts(rider)
    also = [] if second is None else [second]
    out = pl.pallas_call(
        functools.partial(
            gather_kernel, n, h, body, len(consts), len(outs), relative, modes, nf, same, second is not None
        ),
        out_shape=[jax.ShapeDtypeStruct((2 * n, h, cols), x.dtype)]
        + shapes
        + [jax.ShapeDtypeStruct((n,) + w.shape, w.dtype) for w in also]
        + shape,
        in_specs=[vmem] * (1 + len(consts)) + [hbm] * len(also) + spec,
        out_specs=[hbm] * (1 + len(outs)) + [hbm] * len(also) + spec,
        scratch_shapes=[pltpu.VMEM((2 * n, h, cols), x.dtype)]
        + [pltpu.VMEM((2, h, c), d) for c, d in outs]
        + [
            pltpu.SemaphoreType.DMA((2, nb + 1, n)),
            pltpu.SemaphoreType.DMA((2, n)),
            pltpu.SemaphoreType.DMA((2 * n,)),
            pltpu.SemaphoreType.DMA((max(len(outs), 1), 2)),
        ]
        + scratch
        + [
            pltpu.SemaphoreType.DMA((2, nb + 1, n)),
            pltpu.SemaphoreType.DMA((2, n)),
            pltpu.SemaphoreType.DMA,
        ]
        * len(also),
        compiler_params=pltpu.CompilerParams(
            collective_id=ident, has_side_effects=True, vmem_limit_bytes=60 << 20
        ),
        cost_estimate=SMALL,
        name=name,
    )(x, *consts, *also, *more)
    return [o.reshape(2 * n * h, o.shape[2]) for o in out[: 1 + len(outs)]] + list(out[1 + len(outs) :])


class Side:
    def __init__(self, count, refs):
        self.count = count
        self.a, self.b, self.grad, self.sums, self.acc, self.abuf, self.bbuf, self.load = refs

    def fetch(self, i):
        slot = lax.rem(i, 2)
        return [
            pltpu.make_async_copy(self.a.at[i], self.abuf.at[slot], self.load.at[0, slot]),
            pltpu.make_async_copy(self.b.at[i], self.bbuf.at[slot], self.load.at[1, slot]),
        ]

    def begin(self):
        self.acc[...] = jnp.zeros_like(self.acc)
        self.sums[...] = jnp.zeros_like(self.sums)
        for c in self.fetch(jnp.int32(0)):
            c.start()

    def run(self, first, last):
        def step(i, carry):
            @pl.when(i + 1 < self.count)
            def _():
                for c in self.fetch(i + 1):
                    c.start()

            for c in self.fetch(i):
                c.wait()
            slot = lax.rem(i, 2)
            a, b = self.abuf[slot], self.bbuf[slot]
            self.acc[...] += lax.dot_general(
                a, b, (((0,), (0,)), ((), ())), preferred_element_type=jnp.float32
            )
            self.sums[...] += jnp.sum(b.astype(jnp.float32), 0, keepdims=True)
            return carry

        lax.fori_loop(first, last, step, 0)

    def end(self):
        self.grad[...] = self.acc[...].astype(self.grad.dtype)


def side_parts(side, count):
    if side is None:
        return [], [], [], [], []
    a, b = side
    h = a.shape[0] // count
    low = jnp.bfloat16
    hbm = pl.BlockSpec(memory_space=pl.ANY)
    vmem = pl.BlockSpec(memory_space=pltpu.VMEM)
    return (
        [x.reshape(count, h, x.shape[1]) for x in (a, b)],
        [
            jax.ShapeDtypeStruct((a.shape[1], b.shape[1]), low),
            jax.ShapeDtypeStruct((1, b.shape[1]), jnp.float32),
        ],
        [hbm, hbm],
        [vmem, vmem],
        [
            pltpu.VMEM((a.shape[1], b.shape[1]), jnp.float32),
            pltpu.VMEM((2, h, a.shape[1]), low),
            pltpu.VMEM((2, h, b.shape[1]), low),
            pltpu.SemaphoreType.DMA((2, 2)),
        ],
    )


def scatter_order(n):
    bits = route_bits(n)
    orders = [bits, bits[::-1]]
    lists = [
        sorted(range(0, n, 2), key=lambda k: [-int(bool(k & b)) for b in order]) for order in orders
    ]
    return orders, [(half, lists[half][i]) for i in range(n // 2) for half in (0, 1)]


def scatter_kernel(n, h, body, n_in, n_const, n_out, modes, nf, same, has_side, has_norm, *refs):
    if has_norm:
        out = n_in + 3 + n_const + 2 * has_side + min(nf, 1)
        values, gain, joins = refs[:3]
        x_grad, g_grad, b_grad = refs[out], refs[out + 1], refs[out + 2]
        refs = refs[3:out] + (None,) + refs[out + 3 :]
    side = None
    if has_side:
        at = n_in + n_const
        out = at + 2 + min(nf, 1) + 1 + n_out
        extra = refs[at : at + 2] + refs[out : out + 2] + refs[-4:]
        refs = refs[:at] + refs[at + 2 : out] + refs[out + 2 : -4]
        side = Side(2 * n, extra)
    refs, rider = split_rider(refs, nf, same, n_in + n_const, 1 + n_out)
    ins = refs[:n_in]
    consts = refs[n_in : n_in + n_const]
    at = n_in + n_const
    sum_ref = refs[at]
    outs = refs[at + 1 : at + 1 + n_out]
    at += 1 + n_out
    give, pair, own, far, total = refs[at : at + 5]
    at += 5
    loads = refs[at : at + n_in]
    stages = refs[at + n_in : at + n_in + n_out]
    pair_send, pair_recv, far_send, far_recv, load, store, done = refs[at + n_in + n_out :]
    me = lax.axis_index("seq")
    orders, entries = scatter_order(n)
    bits = orders[0]
    slots = give.shape[0]
    index = {e: j for j, e in enumerate(entries)}

    def device(b):
        return {"seq": flip(me, b)}

    def phase_of(half, k):
        for i, b in enumerate(orders[half]):
            if k & b:
                return i
        return len(bits)

    landing = {}
    for half in (0, 1):
        for i, b in enumerate(orders[half]):
            for k in range(0, n, 2):
                if phase_of(half, k) == i:
                    landing[half, i, k ^ b] = len(landing)

    halves = [e[0] for e in entries]
    ks = [e[1] for e in entries]

    def spot(q, relative):
        j = lax.div(q, 2)
        k = pick(ks, j)
        k = jnp.where(lax.rem(q, 2) == 0, flip(k, 1), k)
        return 2 * (k if relative else place(me, k, n)) + pick(halves, j)

    def fetch(q):
        slot = lax.rem(q, 2)
        return [
            pltpu.make_async_copy(ins[i].at[spot(q, modes[0][i])], loads[i].at[slot], load.at[i, slot])
            for i in range(n_in)
        ]

    def output(o, q):
        slot = lax.rem(q, 2)
        return pltpu.make_async_copy(stages[o].at[slot], outs[o].at[spot(q, modes[1][o])], store.at[o, slot])

    def hand(j):
        slot = lax.rem(j, slots)
        return remote(give.at[slot], pair.at[j], pair_send.at[j], pair_recv.at[j], device(1))

    def launch(half, k):
        i = phase_of(half, k)
        b = orders[half][i]
        to = landing[half, i, k ^ b]
        return remote(own.at[index[half, k]], far.at[to], far_send.at[to], far_recv.at[to], device(b))

    def join(j):
        hand(j).wait_recv()
        own[j] = (own[j].astype(jnp.float32) + pair[j].astype(jnp.float32)).astype(own.dtype)
        for e, (half, k) in enumerate(entries):
            if phase_of(half, k) == 0:

                @pl.when(j == e)
                def _(half=half, k=k):
                    launch(half, k).start()

    for c in fetch(jnp.int32(0)):
        c.start()
    greet([device(b) for b in [1] + bits] + (rider.peers() if nf else []))
    if nf:
        rider.start()

    def step(q, carry):
        j = lax.div(q, 2)
        slot = lax.rem(q, 2)

        @pl.when(q + 1 < 2 * n)
        def _():
            for c in fetch(q + 1):
                c.start()

        for c in fetch(q):
            c.wait()
        part, *results = body(*[r[slot] for r in loads], *consts)
        for o in range(n_out):

            @pl.when(q >= 2)
            def _(o=o):
                output(o, q).wait()

            stages[o][slot] = results[o]
            output(o, q).start()

        @pl.when(slot == 0)
        def _():
            @pl.when(j >= slots)
            def _():
                hand(j - slots).wait_send()

            give[lax.rem(j, slots)] = part.astype(give.dtype)
            hand(j).start()

        @pl.when(slot == 1)
        def _():
            own[j] = part.astype(own.dtype)

            @pl.when(j >= 1)
            def _():
                join(j - 1)

        return carry

    lax.fori_loop(0, 2 * n, step, 0)
    if side:
        side.begin()
    join(jnp.int32(n - 1))
    first = n // 2
    cuts = [0, first] + [first + (2 * n - first) * i // (len(bits) - 1) for i in range(1, len(bits))]
    for i in range(len(bits)):
        if side:
            side.run(cuts[i], cuts[i + 1])
        for half in (0, 1):
            order = orders[half]
            for k in [k for hh, k in entries if hh == half and phase_of(half, k) > i]:
                to = landing[half, i, k]
                remote(far.at[to], far.at[to], far_send.at[to], far_recv.at[to], device(1)).wait_recv()
                j = index[half, k]
                rows = pl.ds(half * h, h)
                if i == len(bits) - 1:
                    total[rows] = own[j].astype(jnp.float32) + far[to].astype(jnp.float32)
                    if not has_norm:
                        pltpu.make_async_copy(total.at[rows], sum_ref.at[rows], done.at[half]).start()
                else:
                    own[j] = (own[j].astype(jnp.float32) + far[to].astype(jnp.float32)).astype(own.dtype)
                    if phase_of(half, k) == i + 1:
                        launch(half, k).start()
    if has_norm:
        g_grad[...] = jnp.zeros_like(g_grad)
        b_grad[...] = jnp.zeros_like(b_grad)

        def tile(i, carry):
            rows = pl.ds(pl.multiple_of(i * 64, 64), 64)
            x = values[rows].astype(jnp.float32)
            centred = x - jnp.mean(x, -1, keepdims=True)
            scale = lax.rsqrt(jnp.mean(centred * centred, -1, keepdims=True) + 1e-05)
            xhat = centred * scale
            grad = total[rows]
            g_grad[...] += jnp.sum(grad * xhat, 0, keepdims=True)
            b_grad[...] += jnp.sum(grad, 0, keepdims=True)
            e = gain[...] * grad
            inner = e - jnp.mean(e, -1, keepdims=True) - xhat * jnp.mean(e * xhat, -1, keepdims=True)
            x_grad[rows] = (joins[rows].astype(jnp.float32) + scale * inner).astype(x_grad.dtype)
            return carry

        lax.fori_loop(0, 2 * h // 64, tile, 0)
    for half in (0, 1) if not has_norm else ():
        rows = pl.ds(half * h, h)
        pltpu.make_async_copy(total.at[rows], sum_ref.at[rows], done.at[half]).wait()
    for q in (2 * n - 2, 2 * n - 1):
        for o in range(n_out):
            output(o, jnp.int32(q)).wait()
    for j in range(max(n - slots, 0), n):
        hand(jnp.int32(j)).wait_send()
    for half, k in entries:
        if phase_of(half, k) < len(bits):
            launch(half, k).wait_send()
    if nf:
        rider.finish()
    if side:
        side.end()


def seq_scatter(n, cols, ident, name, body, ins, consts, outs=(), modes=None, rider=None, side=None, norm=None):
    h = ins[0].shape[0] // (2 * n)
    low = jnp.bfloat16
    slots = min(4, n)
    split = [a.reshape(2 * n, h, a.shape[1]) for a in ins]
    vmem = pl.BlockSpec(memory_space=pltpu.VMEM)
    hbm = pl.BlockSpec(memory_space=pl.ANY)
    reach = n - 2
    modes = modes or ([0] * len(ins), [0] * len(outs))
    more, spec, shape, scratch, nf, same = rider_parts(rider)
    s_ins, s_shapes, s_in_specs, s_out_specs, s_scratch = side_parts(side, 2 * n)
    sums = [jax.ShapeDtypeStruct((2 * h, cols), jnp.float32)]
    norms = []
    if norm is not None:
        norms = list(norm[:3])
        line = jax.ShapeDtypeStruct((1, cols), jnp.float32)
        sums = [jax.ShapeDtypeStruct((2 * h, cols), norm[3]), line, line]
    out = pl.pallas_call(
        functools.partial(
            scatter_kernel, n, h, body, len(ins), len(consts), len(outs), modes, nf, same, int(side is not None), norm is not None
        ),
        out_shape=sums
        + [jax.ShapeDtypeStruct((2 * n, h, c), d) for c, d in outs]
        + s_shapes
        + shape,
        in_specs=[vmem] * len(norms) + [hbm] * len(ins) + [vmem] * len(consts) + s_in_specs + spec,
        out_specs=([vmem] * 3 if norms else [hbm]) + [hbm] * len(outs) + s_out_specs + spec,
        scratch_shapes=[
            pltpu.VMEM((slots, h, cols), low),
            pltpu.VMEM((n, h, cols), low),
            pltpu.VMEM((n, h, cols), low),
            pltpu.VMEM((reach, h, cols), low),
            pltpu.VMEM((2 * h, cols), jnp.float32),
        ]
        + [pltpu.VMEM((2, h, a.shape[2]), a.dtype) for a in split]
        + [pltpu.VMEM((2, h, c), d) for c, d in outs]
        + [
            pltpu.SemaphoreType.DMA((n,)),
            pltpu.SemaphoreType.DMA((n,)),
            pltpu.SemaphoreType.DMA((reach,)),
            pltpu.SemaphoreType.DMA((reach,)),
            pltpu.SemaphoreType.DMA((len(ins), 2)),
            pltpu.SemaphoreType.DMA((max(len(outs), 1), 2)),
            pltpu.SemaphoreType.DMA((2,)),
        ]
        + scratch
        + s_scratch,
        compiler_params=pltpu.CompilerParams(
            collective_id=ident, has_side_effects=True, vmem_limit_bytes=60 << 20
        ),
        cost_estimate=SMALL,
        name=name,
    )(*norms, *split, *consts, *s_ins, *more)
    lines = list(out[1:3]) if norms else []
    out = [out[0]] + list(out[1 + len(lines) :])
    many = 1 + len(outs)
    sides = [] if side is None else list(out[many : many + 2])
    more = list(out[many + len(sides) :])
    return [out[0]] + lines + [o.reshape(2 * n * h, o.shape[2]) for o in out[1:many]] + sides + more


class Rows:
    def __init__(self, n, held, width, wide, back):
        moves = []
        for to in range(n):
            for third in range(3):
                at, end = third * width + to * wide, third * width + min((to + 1) * wide, width)
                row = third * wide
                while at < end:
                    source = at // held
                    count = min(end, (source + 1) * held) - at
                    moves.append((source, at - source * held, to, row, count))
                    at, row = at + count, row + count
        self.n = n
        self.moves = [(c, d, a, b, e) if back else (a, b, c, d, e) for a, b, c, d, e in moves]
        self.out = [[m for m in self.moves if m[0] == i] for i in range(n)]
        self.into = [[m for m in self.moves if m[2] == i] for i in range(n)]
        self.most = max(len(v) for v in self.out + self.into)

    def scratch(self):
        dma = pltpu.SemaphoreType.DMA
        return [dma((self.most,)), dma((self.most,)), dma((self.most,))]

    def bind(self, source, target, send, recv, local):
        self.source, self.target, self.send, self.recv, self.local = source, target, send, recv, local
        return self

    def copy(self, i, m):
        src = self.source.at[pl.ds(m[1], m[4])]
        dst = self.target.at[pl.ds(m[3], m[4])]
        if m[0] == m[2]:
            return pltpu.make_async_copy(src, dst, self.local.at[i])
        return remote(src, dst, self.send.at[i], self.recv.at[self.into[m[2]].index(m)], {"seq": m[2]})

    def start(self):
        me = lax.axis_index("seq")
        for s in range(self.n):

            @pl.when(me == s)
            def _(s=s):
                for i, m in enumerate(self.out[s]):
                    self.copy(i, m).start()

    def finish(self):
        me = lax.axis_index("seq")
        for s in range(self.n):

            @pl.when(me == s)
            def _(s=s):
                for i, m in enumerate(self.into[s]):
                    if m[0] != s:
                        dst = self.target.at[pl.ds(m[3], m[4])]
                        remote(dst, dst, self.send.at[0], self.recv.at[i], {"seq": s}).wait_recv()
                for i, m in enumerate(self.out[s]):
                    if m[0] == m[2]:
                        self.copy(i, m).wait()
                    else:
                        self.copy(i, m).wait_send()


class Units:
    def __init__(self, n, nf, back, source, target, send, recv, local):
        self.n, self.nf, self.back = n, nf, back
        self.source, self.target, self.send, self.recv, self.local = source, target, send, recv, local
        self.me = lax.axis_index("seq")

    @staticmethod
    def scratch(nf):
        dma = pltpu.SemaphoreType.DMA
        return [dma((nf,)), dma((nf,)), dma]

    def ends(self, i):
        group = self.n // self.nf
        if self.back:
            return i * group + lax.div(self.me, self.nf), lax.rem(self.me, self.nf)
        return lax.rem(self.me, group) * self.nf + i, lax.div(self.me, group)

    def comes(self, i):
        group = self.n // self.nf
        if self.back:
            return lax.rem(self.me, group) * self.nf + i
        return i * group + lax.div(self.me, self.nf)

    def each(self, i, there, here):
        to, slot = self.ends(i)

        @pl.when(to != self.me)
        def _():
            there(remote(self.source.at[i], self.target.at[slot], self.send.at[i], self.recv.at[slot], {"seq": to}))

        @pl.when(to == self.me)
        def _():
            here(pltpu.make_async_copy(self.source.at[i], self.target.at[slot], self.local))

    def start(self):
        for i in range(self.nf):
            self.each(i, lambda c: c.start(), lambda c: c.start())

    def finish(self):
        for i in range(self.nf):
            source = self.comes(i)

            @pl.when(source != self.me)
            def _(i=i):
                dst = self.target.at[i]
                remote(dst, dst, self.send.at[0], self.recv.at[i], {"seq": self.me}).wait_recv()

        for i in range(self.nf):
            self.each(i, lambda c: c.wait_send(), lambda c: c.wait())


def all_peers(n, nf):
    me, f = lax.axis_index("seq"), lax.axis_index("fsdp")
    return [{"seq": place(me, r, n)} for r in range(1, n)] + [
        {"fsdp": lax.rem(f + d, nf)} for d in range(1, nf)
    ]


def exchange_kernel(n, nf, rows, count, *refs):
    ins, outs, sems = refs[: 4 + count], refs[4 + count : 8 + 2 * count], list(refs[8 + 2 * count :])
    take = lambda k: [sems.pop(0) for _ in range(k)]
    parts = []
    if rows is not None:
        parts.append(rows.bind(ins[0], outs[0], *take(3)))
    vectors = [Blocks("fsdp", nf, True, ins[4 + i], outs[4 + i], *take(3)) for i in range(count)]
    later = [
        Blocks("fsdp", nf, True, ins[3], outs[3], *take(3)),
        Units(n, nf, False, ins[2], outs[2], *take(3)),
        Blocks("seq", n, False, ins[1], outs[1], *take(3)),
    ]
    parts = vectors + parts + later
    greet(all_peers(n, nf))
    for p in parts:
        p.start()
    for p in parts:
        p.finish()


def exchange(w, p, c, o, vectors, n, nf, rows, wide, ident):
    hbm = pl.BlockSpec(memory_space=pl.ANY)
    count = len(vectors)
    out = pl.pallas_call(
        functools.partial(exchange_kernel, n, nf, rows, count),
        out_shape=[
            jax.ShapeDtypeStruct((3 * wide, w.shape[1]) if rows is not None else w.shape, w.dtype),
            blocks_shape(p, n, False),
            blocks_shape(c, nf, False),
            blocks_shape(o, nf, True),
        ]
        + [blocks_shape(v, nf, True) for v in vectors],
        in_specs=[hbm] * (4 + count),
        out_specs=[hbm] * (4 + count),
        scratch_shapes=(rows.scratch() if rows is not None else [])
        + sum([Blocks.scratch(nf) for _ in vectors], [])
        + Blocks.scratch(nf)
        + Units.scratch(nf)
        + Blocks.scratch(n),
        compiler_params=pltpu.CompilerParams(collective_id=ident, has_side_effects=True),
        cost_estimate=SMALL,
        name="exchange",
    )(w, p, c, o, *vectors)
    return out[0], out[1], out[2], out[3], out[4:]


def to_tokens_kernel(n, wide, x_ref, o_ref, send, recv, local):
    me = lax.axis_index("seq")

    def target(i):
        return o_ref.at[:, pl.ds(pl.multiple_of(i * wide, 128), wide)]

    greet([{"seq": place(me, r, n)} for r in range(1, n)])
    copies = []
    for r in range(n - 1, 0, -1):
        to = place(me, r, n)
        c = remote(x_ref.at[to], target(me), send.at[r - 1], recv.at[r - 1], {"seq": to})
        c.start()
        copies.append(c)
    mine = pltpu.make_async_copy(x_ref.at[me], target(me), local)
    mine.start()
    for r in range(1, n):
        dst = target(place(me, r, n))
        remote(dst, dst, send.at[0], recv.at[r - 1], {"seq": place(me, r, n)}).wait_recv()
    mine.wait()
    for c in copies:
        c.wait_send()


def to_tokens(x, n, wide, ident):
    rows = x.shape[1]
    hbm = pl.BlockSpec(memory_space=pl.ANY)
    return pl.pallas_call(
        functools.partial(to_tokens_kernel, n, wide),
        out_shape=jax.ShapeDtypeStruct((rows, n * wide), x.dtype),
        in_specs=[hbm],
        out_specs=hbm,
        scratch_shapes=Blocks.scratch(n),
        compiler_params=pltpu.CompilerParams(collective_id=ident, has_side_effects=True),
        cost_estimate=SMALL,
        name="to_tokens",
    )(x)


def to_heads_kernel(
    n, nf, wide, carried, x_ref, w_ref, t_ref, a_ref, b_ref, z_ref, o_ref, g_ref, m_ref, z_out, t_out, handed, made, *extra
):
    me = lax.axis_index("seq")
    send, recv, local = extra[:3]
    side = Side(2 * n, (a_ref, b_ref, g_ref, m_ref) + extra[3:7])
    planes = PlaneSum(nf, z_ref, 0, *extra[7:])
    side.begin()
    greet([{"seq": place(me, r, n)} for r in range(1, n)] + planes.peers())
    planes.start()

    def copy(r):
        to = place(me, r, n)
        return remote(made.at[r], o_ref.at[me], send.at[r - 1], recv.at[r - 1], {"seq": to})

    def mine():
        return pltpu.make_async_copy(made.at[0], o_ref.at[me], local)

    def step(i, carry):
        r = n - 1 - i
        lanes = pl.ds(pl.multiple_of(place(me, r, n) * wide, 128), wide)
        made[r] = mm(x_ref[...], w_ref[:, lanes]).astype(made.dtype)

        @pl.when(r > 0)
        def _():
            copy(r).start()

        return carry

    lax.fori_loop(0, n, step, 0)
    mine().start()
    side.run(0, 2 * n)
    cols = t_out.shape[0]
    for at in range(0, cols, 512):
        end = min(at + 512, cols)
        t_out[at:end] = lax.dot_general(
            x_ref[:, at:end], t_ref[...], (((0,), (0,)), ((), ())), preferred_element_type=jnp.float32
        ).astype(t_out.dtype)
    side.end()
    planes.finish()
    planes.store(z_out)
    for r in range(1, n):
        dst = o_ref.at[place(me, r, n)]
        remote(dst, dst, send.at[0], recv.at[r - 1], {"seq": me}).wait_recv()
    mine().wait()
    for r in range(1, n):
        copy(r).wait_send()


def to_heads(x, w, t, n, nf, wide, ident, a, b, z, count, carry):
    rows, cols = x.shape
    vmem = pl.BlockSpec(memory_space=pltpu.VMEM)
    hbm = pl.BlockSpec(memory_space=pl.ANY)
    s_ins, s_shapes, s_in_specs, s_out_specs, s_scratch = side_parts((a, b), 2 * n)
    return pl.pallas_call(
        functools.partial(to_heads_kernel, n, nf, wide),
        out_shape=[jax.ShapeDtypeStruct((n, rows, wide), x.dtype)]
        + s_shapes
        + [
            jax.ShapeDtypeStruct((n, count, z.shape[2] // n), z.dtype),
            jax.ShapeDtypeStruct((cols, t.shape[1]), x.dtype),
            jax.ShapeDtypeStruct(carry.shape, carry.dtype),
        ],
        in_specs=[hbm, vmem, vmem, vmem] + s_in_specs + [hbm],
        out_specs=[hbm] + s_out_specs + [vmem, vmem, hbm],
        input_output_aliases={0: 5},
        scratch_shapes=[pltpu.VMEM((n, rows, wide), x.dtype)]
        + Blocks.scratch(n)
        + s_scratch
        + PlaneSum.scratch(nf, count, z.shape[2]),
        compiler_params=pltpu.CompilerParams(
            collective_id=ident, has_side_effects=True, vmem_limit_bytes=60 << 20
        ),
        cost_estimate=SMALL,
        name="to_heads",
    )(carry, x, w, t, *s_ins, z)


def contract_kernel(a_ref, b_ref, ready, o_ref, acc):
    i = pl.program_id(0)
    part = lax.dot_general(
        a_ref[...], b_ref[...], (((0,), (0,)), ((), ())), preferred_element_type=jnp.float32
    )

    @pl.when(i == 0)
    def _():
        acc[...] = part

    @pl.when(i > 0)
    def _():
        acc[...] += part

    @pl.when(i == pl.num_programs(0) - 1)
    def _():
        o_ref[...] = acc[...].astype(o_ref.dtype)


def contract(a, b, ready, tile):
    rows = a.shape[0]
    shape = (a.shape[1], b.shape[1])
    still = lambda s: pl.BlockSpec(s, lambda i: (0,) * len(s), pipeline_mode=pl.Buffered(1))
    return pl.pallas_call(
        contract_kernel,
        out_shape=jax.ShapeDtypeStruct(shape, a.dtype),
        grid=(rows // tile,),
        in_specs=[
            pl.BlockSpec((tile, shape[0]), lambda i: (i, 0)),
            pl.BlockSpec((tile, shape[1]), lambda i: (i, 0)),
            still(ready.shape),
        ],
        out_specs=still(shape),
        scratch_shapes=[pltpu.VMEM(shape, jnp.float32)],
        compiler_params=pltpu.CompilerParams(
            dimension_semantics=("arbitrary",), vmem_limit_bytes=40 << 20
        ),
        cost_estimate=SMALL,
        name="contract",
    )(a, b, ready)


def give_back_kernel(
    n, nf, rows, v_ref, w_ref, p_ref, q_ref, c_ref, o_ref, v_out, w_out, p_out, q_out, c_out, o_out, planes, sums, *sems
):
    s = lax.axis_index("seq")
    f = lax.axis_index("fsdp")
    sems = list(sems)
    take = lambda k: [sems.pop(0) for _ in range(k)]
    send_z, recv_z, send_s, recv_s = take(4)
    parts = []
    if rows is not None:
        parts.append(rows.bind(w_ref, w_out, *take(3)))
    parts.append(Units(n, nf, True, c_ref, c_out, *take(3)))
    parts.append(Blocks("seq", n, False, p_ref, p_out, *take(3)))
    parts.append(Blocks("seq", n, False, q_ref, q_out, *take(3)))
    parts.append(Blocks("fsdp", nf, False, o_ref, o_out, *take(3)))
    others = [{"fsdp": lax.rem(f + d, nf)} for d in range(1, nf)]
    peers = [{"seq": place(s, r, n)} for r in range(1, n)]
    greet(peers + others)
    copies = []
    for d in range(1, nf):
        c = remote(v_ref.at[lax.rem(f + d, nf)], planes.at[d - 1], send_z.at[d - 1], recv_z.at[d - 1], others[d - 1])
        c.start()
        copies.append(c)
    for p in parts[:1]:
        p.start()
    total = v_ref[f]
    for d, c in enumerate(copies):
        c.wait_recv()
        total = total + planes[d]
    sums[0] = total
    spread = []
    for r in range(1, n):
        c = remote(sums.at[0], sums.at[r], send_s.at[r - 1], recv_s.at[r - 1], peers[r - 1])
        c.start()
        spread.append(c)
    for p in parts[1:]:
        p.start()
    for r, c in enumerate(spread):
        c.wait_recv()
        total = total + sums[r + 1]
    v_out[...] = total
    for p in parts:
        p.finish()
    for c in copies + spread:
        c.wait_send()


def give_back(vectors, w, held, p, q, c, o, n, nf, rows, ident):
    k = vectors.shape[1]
    tiles = -(-k // 1024) * 8
    padded = jnp.pad(vectors, ((0, 0), (0, tiles * 128 - k))).reshape(nf, tiles, 128)
    vmem = pl.BlockSpec(memory_space=pltpu.VMEM)
    hbm = pl.BlockSpec(memory_space=pl.ANY)
    dma = pltpu.SemaphoreType.DMA
    out = pl.pallas_call(
        functools.partial(give_back_kernel, n, nf, rows),
        out_shape=[
            jax.ShapeDtypeStruct((tiles, 128), jnp.float32),
            jax.ShapeDtypeStruct((held, w.shape[1]), w.dtype),
            blocks_shape(p, n, False),
            blocks_shape(q, n, False),
            blocks_shape(c, nf, False),
            blocks_shape(o, nf, False),
        ],
        in_specs=[vmem, hbm, hbm, hbm, hbm, hbm],
        out_specs=[vmem, hbm, hbm, hbm, hbm, hbm],
        scratch_shapes=[
            pltpu.VMEM((nf - 1, tiles, 128), jnp.float32),
            pltpu.VMEM((n, tiles, 128), jnp.float32),
            dma((nf - 1,)),
            dma((nf - 1,)),
            dma((n - 1,)),
            dma((n - 1,)),
        ]
        + (rows.scratch() if rows is not None else [])
        + Units.scratch(nf)
        + Blocks.scratch(n)
        + Blocks.scratch(n)
        + Blocks.scratch(nf),
        compiler_params=pltpu.CompilerParams(collective_id=ident, has_side_effects=True),
        cost_estimate=SMALL,
        name="give_back",
    )(padded, w, p, q, c, o)
    return (out[0].reshape(-1)[:k],) + tuple(out[1:])


HEAD=64
SCALE=0.125*math.log2(math.e)


def block_pairs(slots, trunk):
    branches = (slots - trunk) // 3
    pairs = []
    for t in range(slots):
        m = t - trunk
        if t < trunk:
            keys = [(c, int(c == t), -1, -1) for c in range(t + 1)]
        else:
            keys = [(c, 0, -1, -1) for c in range(trunk)]
            if m >= branches:
                keys.append((trunk, 0, -1, m))
            keys.append((t, 1, m, -1))
        for i, (c, causal, own, leaf) in enumerate(keys):
            pairs.append((t, c, causal, own, leaf, int(i == 0), int(i == len(keys) - 1)))
    return pairs


def block_fields(p, slots, trunk):
    branches = (slots - trunk) // 3
    counts = [t + 1 for t in range(trunk)] + [trunk + 1] * branches
    counts += [trunk + 2] * (slots - trunk - branches)
    starts = [sum(counts[:t]) for t in range(slots)]
    t, begin, end = jnp.int32(0), jnp.int32(0), jnp.int32(counts[0])
    for i in range(1, slots):
        here = p >= starts[i]
        t = jnp.where(here, i, t)
        begin = jnp.where(here, starts[i], begin)
        end = jnp.where(here, starts[i] + counts[i], end)
    i = p - begin
    last = p == end - 1
    leaf = (t >= trunk + branches) & (i == trunk)
    key = jnp.where((t >= trunk) & last, t, i)
    return t, key, last, leaf, i == 0, last


def block_values(lengths, parents, pairs, block):
    count = lengths.shape[0]
    segments = np.arange(count)
    own = np.array([p[3] for p in pairs])[None, :] == segments[:, None]
    leaf = np.array([p[4] for p in pairs])[None, :] == segments[:, None]
    above = jnp.sum(jnp.where(leaf, parents[:, None], 0), 0)
    source = own | (segments[:, None] + 1 == above[None, :])
    closed = np.array([p[3] < 0 and p[4] < 0 for p in pairs])
    reach = jnp.where(closed, block, jnp.sum(jnp.where(source, lengths[:, None], 0), 0))
    return jnp.stack([jnp.maximum(above - 1, 0), reach]).astype(jnp.int32)


def lane_half(shape):
    return lax.broadcasted_iota(jnp.int32, shape, len(shape) - 1) < HEAD


def nt(a, b):
    return lax.dot_general(a, b, (((1,), (1,)), ((), ())), preferred_element_type=jnp.float32)


def mm(a, b):
    return jnp.dot(a, b, preferred_element_type=jnp.float32)


def attend_kernel(width, block, trunk, n, values, x_ref, w_ref, b_ref, c_ref, qkv, low, att, tot, kt, c_all, acc, xbuf, xsem, *sems):
    p = pl.program_id(0)
    slot, key, causal, leaf, first, last = block_fields(p, n, trunk)
    rows = lambda slot: pl.ds(pl.multiple_of(slot * block, block), block)
    qrow = rows(slot)
    above = values[0, p]
    reach = values[1, p]
    branches = (n - trunk) // 3
    left = lane_half((block, 2 * HEAD))
    spread = Spread(n, c_ref, c_all, *sems)

    def fetch(i):
        slot = lax.rem(i, 2)
        return pltpu.make_async_copy(x_ref.at[i], xbuf.at[slot], xsem.at[slot])

    @pl.when(p == 0)
    def _():
        fetch(jnp.int32(0)).start()
        greet(spread.peers())
        spread.start()

        def step(i, carry):
            @pl.when(i + 1 < n)
            def _():
                fetch(i + 1).start()

            fetch(i).wait()
            made = (mm(xbuf[lax.rem(i, 2)], w_ref[...]) + b_ref[...]).astype(qkv.dtype)
            qkv[rows(i)] = made
            kt[:, rows(i)] = made[:, width : 2 * width].T
            return carry

        lax.fori_loop(0, n, step, 0)
        for i in range(len(spread.bits) - 1):
            spread.phase(i)

    @pl.when(first)
    def _():
        acc[...] = jnp.zeros_like(acc)

    def keyed(mask, read):
        got = read(rows(key))
        if mask is not None:
            for b in range(1, branches):
                got = jnp.where(leaf & (above == b), read(pl.ds((trunk + b) * block, block)), got)
        return got

    def step(mask):
        for j in range(width // (2 * HEAD)):
            lanes = slice(j * 2 * HEAD, (j + 1) * 2 * HEAD)
            q = qkv[qrow, lanes]
            k = keyed(mask, lambda at: qkv[at, width + j * 2 * HEAD : width + (j + 1) * 2 * HEAD])
            v = keyed(mask, lambda at: qkv[at, 2 * width + j * 2 * HEAD : 2 * width + (j + 1) * 2 * HEAD])
            for h in range(2):
                here = left if h == 0 else jnp.logical_not(left)
                s = nt(jnp.where(here, q, 0), k)
                e = jnp.exp2(s * SCALE)
                if mask is not None:
                    e = jnp.where(mask, e, 0.0)
                acc[2 * j + h] += mm(e.astype(jnp.bfloat16), jnp.where(here, v, 1))

    closes = causal | leaf
    shift = jnp.where(causal, 0, block)

    @pl.when(jnp.logical_not(closes))
    def _():
        step(None)

    @pl.when(closes)
    def _():
        row = lax.broadcasted_iota(jnp.int32, (block, block), 0)
        col = lax.broadcasted_iota(jnp.int32, (block, block), 1)
        step((col <= row + shift) & (col < reach))

    @pl.when(last)
    def _():
        for j in range(width // (2 * HEAD)):
            a, b = acc[2 * j], acc[2 * j + 1]
            total = jnp.where(left, pltpu.roll(a, HEAD, 1), pltpu.roll(b, HEAD, 1))
            value = jnp.where(left, a, b) / total
            lanes = slice(j * 2 * HEAD, (j + 1) * 2 * HEAD)
            low[:, lanes] = value.astype(jnp.bfloat16)
            att[:, lanes] = value
            tot[:, lanes] = total

    @pl.when(p == pl.num_programs(0) - 1)
    def _():
        spread.phase(len(spread.bits) - 1)
        spread.finish()


def attend(values, pairs, x, w, bias, block, trunk, sent, n, ident):
    rows, width = x.shape[0], w.shape[1] // 3
    by_q = lambda p: (block_fields(p, n, trunk)[0], 0)
    heads = width // HEAD
    once = lambda s: pl.BlockSpec(s, lambda p: (0,) * len(s), pipeline_mode=pl.Buffered(1))
    hbm = pl.BlockSpec(memory_space=pl.ANY)
    out = pl.pallas_call(
        functools.partial(attend_kernel, width, block, trunk, n),
        grid=(len(pairs),),
        out_shape=(
            jax.ShapeDtypeStruct((rows, 3 * width), x.dtype),
            jax.ShapeDtypeStruct((rows, width), x.dtype),
            jax.ShapeDtypeStruct((rows, width), jnp.float32),
            jax.ShapeDtypeStruct((rows, width), jnp.float32),
            jax.ShapeDtypeStruct((width, rows), x.dtype),
            jax.ShapeDtypeStruct((n,) + sent.shape, sent.dtype),
        ),
        in_specs=[pl.BlockSpec(memory_space=pltpu.SMEM), hbm, once(w.shape), once(bias.shape), hbm],
        out_specs=[once((rows, 3 * width))]
        + [pl.BlockSpec((block, width), by_q)] * 3
        + [once((width, rows)), hbm],
        scratch_shapes=[
            pltpu.VMEM((heads, block, 2 * HEAD), jnp.float32),
            pltpu.VMEM((2, block, x.shape[1]), x.dtype),
            pltpu.SemaphoreType.DMA((2,)),
        ]
        + Spread.scratch(n),
        compiler_params=pltpu.CompilerParams(
            dimension_semantics=("arbitrary",),
            vmem_limit_bytes=60 << 20,
            collective_id=ident,
            has_side_effects=True,
        ),
        cost_estimate=SMALL,
        name="attend",
    )(values, x.reshape(n, block, x.shape[1]), w, bias, sent)
    return out[:5] + (out[5].reshape(n * sent.shape[0], sent.shape[1]),)


def attend_back_kernel(width, block, slots, trunk, branches, nf, lows, *refs):
    count = len(lows)
    values, qkv, kt, datt, att, tot = refs[:6]
    sources = refs[6 : 6 + count]
    out, sums = refs[6 + count : 8 + count]
    parts = refs[8 + count : 8 + 2 * count]
    dk, dv, dqt, aug = refs[8 + 2 * count : 12 + 2 * count]
    rest = refs[12 + 2 * count :]
    riders = [PlaneSum(nf, sources[i], lows[i], *rest[4 * i : 4 * i + 4]) for i in range(count)]
    p = pl.program_id(0)
    slot, key, causal, leaf, first, last = block_fields(p, slots, trunk)
    rows = lambda slot: pl.ds(pl.multiple_of(slot * block, block), block)
    above = values[0, p]
    reach = values[1, p]
    qrow = rows(slot)
    left = lane_half((block, 2 * HEAD))
    lane = lax.broadcasted_iota(jnp.int32, (block, 2 * HEAD), 1)
    columns = width // (2 * HEAD)

    @pl.when(p == 0)
    def _():
        greet(riders[0].peers())
        for r in riders:
            r.start()
        dk[...] = jnp.zeros_like(dk)
        dv[...] = jnp.zeros_like(dv)

    @pl.when(first)
    def _():
        dqt[...] = jnp.zeros_like(dqt)
        for j in range(columns):
            lanes = slice(j * 2 * HEAD, (j + 1) * 2 * HEAD)
            d = datt[:, lanes].astype(jnp.float32)
            total = tot[:, lanes]
            low = (d / total).astype(jnp.bfloat16)
            prod = d * att[:, lanes] / total
            for h in range(2):
                here = left if h == 0 else jnp.logical_not(left)
                delta = -jnp.sum(jnp.where(here, prod, 0.0), 1, keepdims=True)
                hi = delta.astype(jnp.bfloat16).astype(jnp.float32)
                mid = (delta - hi).astype(jnp.bfloat16).astype(jnp.float32)
                rest = delta - hi - mid
                at = HEAD * (1 - h)
                extra = jnp.where(
                    lane == at, hi, jnp.where(lane == at + 1, mid, jnp.where(lane == at + 2, rest, 0.0))
                )
                aug[2 * j + h] = jnp.where(here, low.astype(jnp.float32), extra).astype(jnp.bfloat16)

    def add(lanes, dks, dvs):
        @pl.when(jnp.logical_not(leaf))
        def _():
            at = rows(key)
            dk[at, lanes] += dks
            dv[at, lanes] += dvs

        @pl.when(leaf)
        def _():
            for b in range(branches):
                at = pl.ds((trunk + b) * block, block)
                dk[at, lanes] += jnp.where(above == b, dks, 0.0)
                dv[at, lanes] += jnp.where(above == b, dvs, 0.0)

    def keyed(mask, read):
        got = read(rows(key))
        if mask is not None:
            for b in range(1, branches):
                got = jnp.where(leaf & (above == b), read(pl.ds((trunk + b) * block, block)), got)
        return got

    def step(mask):
        for j in range(columns):
            lanes = slice(j * 2 * HEAD, (j + 1) * 2 * HEAD)
            q = qkv[qrow, lanes]
            k = keyed(mask, lambda at: qkv[at, width + j * 2 * HEAD : width + (j + 1) * 2 * HEAD])
            v = keyed(mask, lambda at: qkv[at, 2 * width + j * 2 * HEAD : 2 * width + (j + 1) * 2 * HEAD])
            dvs, dks = [], []
            for h in range(2):
                here = left if h == 0 else jnp.logical_not(left)
                qh = jnp.where(here, q, 0)
                e = jnp.exp2(nt(k, qh) * SCALE)
                if mask is not None:
                    e = jnp.where(mask, e, 0.0)
                dod = aug[2 * j + h]
                ds = (e * nt(jnp.where(here, v * 0.125, 0.125).astype(jnp.bfloat16), dod)).astype(
                    jnp.bfloat16
                )
                dvs.append(mm(e.astype(jnp.bfloat16), dod))
                dks.append(mm(ds, qh))
                at = j * 2 * HEAD + h * HEAD
                dqt[at : at + HEAD] += mm(keyed(mask, lambda i: kt[at : at + HEAD, i]), ds)
            add(lanes, dks[0] + dks[1], jnp.where(left, dvs[0], dvs[1]))

    closes = causal | leaf
    shift = jnp.where(causal, 0, block)

    @pl.when(jnp.logical_not(closes))
    def _():
        step(None)

    @pl.when(closes)
    def _():
        col = lax.broadcasted_iota(jnp.int32, (block, block), 0)
        row = lax.broadcasted_iota(jnp.int32, (block, block), 1)
        step((col <= row + shift) & (col < reach))

    @pl.when(last)
    def _():
        out[qrow, 0:width] = dqt[...].T.astype(jnp.bfloat16)

    @pl.when(p == pl.num_programs(0) - 1)
    def _():
        out[:, width : 2 * width] = dk[...].astype(jnp.bfloat16)
        out[:, 2 * width :] = dv[...].astype(jnp.bfloat16)
        for t in range(3):
            lanes = slice(t * width, (t + 1) * width)
            sums[:, lanes] = jnp.sum(out[:, lanes].astype(jnp.float32), 0, keepdims=True)
        for r, made in zip(riders, parts):
            r.finish()
            r.store(made)


def attend_back(values, pairs, qkv, kt, datt, att, tot, block, trunk, nf, riders, ident):
    rows, width = qkv.shape[0], qkv.shape[1] // 3
    by_q = lambda p: (block_fields(p, rows // block, trunk)[0], 0)
    heads = width // HEAD
    branches = (rows // block - trunk) // 3
    made = [(k, z.shape[1] - at, z.shape[2] // k) for z, at, k in riders]
    once = lambda s: pl.BlockSpec(s, lambda p: (0,) * len(s), pipeline_mode=pl.Buffered(1))
    hbm = pl.BlockSpec(memory_space=pl.ANY)
    out = pl.pallas_call(
        functools.partial(
            attend_back_kernel, width, block, rows // block, trunk, branches, nf, [r[1] for r in riders]
        ),
        grid=(len(pairs),),
        out_shape=[
            jax.ShapeDtypeStruct((rows, 3 * width), jnp.bfloat16),
            jax.ShapeDtypeStruct((1, 3 * width), jnp.float32),
        ]
        + [jax.ShapeDtypeStruct(s, jnp.bfloat16) for s in made],
        in_specs=[pl.BlockSpec(memory_space=pltpu.SMEM), once((rows, 3 * width)), once((width, rows))]
        + [pl.BlockSpec((block, width), by_q)] * 3
        + [hbm] * len(riders),
        out_specs=[once((rows, 3 * width)), once((1, 3 * width))] + [once(s) for s in made],
        scratch_shapes=[
            pltpu.VMEM((rows, width), jnp.float32),
            pltpu.VMEM((rows, width), jnp.float32),
            pltpu.VMEM((width, block), jnp.float32),
            pltpu.VMEM((heads, block, 2 * HEAD), jnp.bfloat16),
        ]
        + sum([PlaneSum.scratch(nf, z.shape[1] - at, z.shape[2]) for z, at, k in riders], []),
        compiler_params=pltpu.CompilerParams(
            dimension_semantics=("arbitrary",),
            vmem_limit_bytes=60 << 20,
            collective_id=ident,
            has_side_effects=True,
        ),
        cost_estimate=SMALL,
        name="attend_back",
    )(values, qkv, kt, datt, att, tot, *[r[0] for r in riders])
    return out[0], out[1], out[2:]


def layer_norm(values, gain, shift):
    centred = values - jnp.mean(values, -1, keepdims=True)
    spread = jnp.mean(centred * centred, -1, keepdims=True)
    return centred * lax.rsqrt(spread + 1e-05) * gain + shift


def contract_rows(left, right):
    return lax.dot_general(
        left, right, (((0,), (0,)), ((), ())), preferred_element_type=jnp.float32
    )


def contract_cols(left, right):
    return lax.dot_general(
        left, right, (((1,), (1,)), ((), ())), preferred_element_type=jnp.float32
    )


def after(value, other):
    return value + (other[(0,) * other.ndim] * 0).astype(value.dtype)


def row_major(x):
    return with_layout_constraint(x, Layout(major_to_minor=tuple(range(x.ndim))))


def local(
    tokens,
    ln1_gain,
    ln1_bias,
    qkv_weight,
    qv_bias,
    out_weight,
    out_bias,
    ln2_gain,
    ln2_bias,
    fc_weight,
    fc_bias,
    proj_weight,
    proj_bias,
    seg_lengths,
    parents,
    cotangent,
):
    n = lax.axis_size("seq")
    nf = lax.axis_size("fsdp")
    s = lax.axis_index("seq")
    f = lax.axis_index("fsdp")
    trunk = n // 4
    block, width = tokens.shape[1], tokens.shape[2]
    rows = width // nf
    hidden = fc_weight.shape[1] * n
    piece = hidden // (n * nf)
    group = n // nf
    wide = 2 * HEAD * (-(-HEADS // (2 * n)))
    low = jnp.bfloat16
    wider = jnp.float32

    vectors = [ln1_gain, ln1_bias, qv_bias, out_bias, ln2_gain, ln2_bias, fc_bias, proj_bias]
    sizes = [v.shape[0] for v in vectors]
    qkv_cols = qkv_weight.shape[1]
    even = qkv_cols % 8 == 0
    forth = Rows(n, qkv_cols, width, wide, False) if even else None
    back = Rows(n, qkv_cols, width, wide, True) if even else None
    turned, proj_blocks, fc_blocks, out_blocks, gathered = exchange(
        qkv_weight.T,
        proj_weight.reshape(n, piece, width // n),
        fc_weight.reshape(rows, nf, piece).transpose(1, 0, 2),
        out_weight,
        [v.reshape(1, -1) for v in vectors],
        n,
        nf,
        forth,
        wide,
        0,
    )
    whole = [v.reshape(-1).astype(wider) for v in gathered]
    gain_one, shift_one, bias_qv, bias_out, gain_two, shift_two, bias_fc, bias_proj = whole
    bias_three = jnp.stack([bias_qv[:width], jnp.zeros((width,), wider), bias_qv[width:]])
    bias_three = jnp.pad(bias_three, ((0, 0), (0, n * wide - width)))
    bias_mine = lax.dynamic_slice_in_dim(bias_three, s * wide, wide, 1).reshape(1, -1)
    bias_hidden = lax.dynamic_index_in_dim(bias_fc.reshape(nf, n, piece), s, 1, False)
    bias_hidden = bias_hidden.reshape(1, -1)

    if even:
        turned = turned.reshape(3, wide, rows)
        kept = lax.broadcasted_iota(jnp.int32, turned.shape, 1) + s * wide < width
        turned = jnp.where(kept, turned, 0).reshape(3 * wide, rows)
    else:
        turned = lax.all_gather(qkv_weight.T, "seq", axis=0, tiled=True).reshape(3, width, rows)
        turned = jnp.pad(turned, ((0, 0), (0, n * wide - width), (0, 0)))
        turned = lax.dynamic_slice_in_dim(turned, s * wide, wide, 1).reshape(3 * wide, rows)
    pairs = block_pairs(n, trunk)
    table = block_values(seg_lengths[0], parents[0], pairs, block)

    resid = tokens[0].astype(wider)
    out_turned = jnp.pad(out_blocks.reshape(width, width // n).T, ((0, 0), (0, n * wide - width)))
    normed_one, out_turned, qkv_mine = seq_gather(
        layer_norm(resid, gain_one, shift_one).astype(low),
        n,
        1,
        "gather_one",
        rider=(turned.T, True, nf),
        second=out_turned,
    )
    out_turned = out_turned.reshape(width, n * wide)
    qkv_mine = qkv_mine.reshape(width, 3 * wide)
    fc_rows = fc_blocks.transpose(1, 0, 2).reshape(rows, nf * piece)
    fc_mine = lax.all_gather(fc_rows, "fsdp", axis=0, tiled=True)

    upstream = cotangent[0].astype(wider)
    proj_rows = proj_blocks.transpose(1, 0, 2).reshape(piece, width)
    proj_mine = lax.all_gather(after(proj_rows, normed_one), "fsdp", axis=0, tiled=True)
    projected, attended_low, attended, totals, keys_turned, upstream_all = attend(
        table, pairs, normed_one, qkv_mine, bias_mine, block, trunk, cotangent[0], n, 8
    )
    attended_mine = to_tokens(attended_low.reshape(n, block, wide), n, wide, 2)
    middle = resid + contract_cols(attended_mine, out_turned) + bias_out
    normed_two = layer_norm(middle, gain_two, shift_two).astype(low)
    ff = nf * piece

    def expand(value, fc, bias, proj):
        pre = mm(value, fc[...]) + bias[...]
        bend = math.sqrt(2 / math.pi)
        square = pre * pre
        inner = jnp.tanh(pre * (bend + bend * 0.044715 * square))
        half = 0.5 + 0.5 * inner
        act = (pre * half).astype(low)
        slope = half + 0.5 * pre * (1 - inner * inner) * (bend + 3 * bend * 0.044715 * square)
        return act, slope.astype(low), mm(act, proj[...]).astype(low)

    normed_two, hidden_act, hidden_slope, mixed = seq_gather(
        normed_two,
        n,
        3,
        "gather_two",
        expand,
        (fc_mine, bias_hidden, proj_mine),
        ((ff, low), (ff, low), (width, low)),
        modes=(0, 0, 0),
    )

    def shrink(up, slope, proj, fc):
        grad = (nt(up, proj[...]) * slope.astype(wider)).astype(low)
        return nt(grad, fc[...]), grad

    grad_normed_two, grad_pre, grad_proj, unused_sums = seq_scatter(
        n,
        width,
        4,
        "scatter_two",
        shrink,
        (upstream_all, hidden_slope),
        (proj_mine, fc_mine),
        ((ff, low),),
        side=(hidden_act, upstream_all),
    )
    grad_proj = grad_proj.reshape(nf, piece, width)
    cut = piece // 16 * 8
    unused_two, norm_two_back = jax.vjp(layer_norm, middle, gain_two, shift_two)
    grad_middle_norm, grad_gain_two, grad_shift_two = norm_two_back(grad_normed_two)
    grad_middle = upstream + grad_middle_norm
    grad_branch = grad_middle.astype(low)
    grad_attended, grad_fc, hidden_sums, proj_first, grad_out, mixed = to_heads(
        grad_branch,
        out_turned,
        attended_mine[:, :width],
        n,
        nf,
        wide,
        5,
        normed_two,
        grad_pre,
        grad_proj,
        cut,
        mixed,
    )
    mixed = lax.psum_scatter(mixed, "seq", scatter_dimension=0, tiled=True).astype(wider)
    grad_attended = grad_attended.reshape(n * block, wide)
    grad_projected, column_sums, (fc_part, proj_second) = attend_back(
        table,
        pairs,
        projected,
        keys_turned,
        grad_attended,
        attended,
        totals,
        block,
        trunk,
        nf,
        ((grad_fc.reshape(nf, rows, ff), 0, nf), (grad_proj, cut, n)),
        9,
    )
    output = (after(middle, grad_projected) + mixed + bias_proj).astype(low)[None]
    ready = output[0, :8, :128].astype(wider)
    grad_qkv = contract(normed_one, grad_projected, ready, block)
    input_grad, grad_gain_one, grad_shift_one, qkv_parts = seq_scatter(
        n,
        width,
        6,
        "scatter_one",
        lambda g, w: (nt(g, w[...]),),
        (grad_projected,),
        (qkv_mine,),
        rider=(grad_qkv.reshape(nf, rows, 3 * wide), False, nf),
        norm=(tokens[0], gain_one.reshape(1, -1), grad_middle, low),
    )
    input_grad = input_grad[None]

    out_part = lax.psum_scatter(grad_out, "seq", scatter_dimension=0, tiled=True).T
    out_part = after(out_part, qkv_parts).reshape(nf, rows, width // n)
    qkv_part = jnp.sum(qkv_parts.astype(wider), 0).astype(low).T

    column_sums = column_sums.reshape(3, wide)
    placed = lax.dynamic_update_slice_in_dim(
        jnp.zeros((3, n * wide), wider), column_sums, s * wide, 1
    )[:, :width]
    grad_qv = jnp.concatenate([placed[0], placed[2]])
    hidden_sums = hidden_sums.reshape(nf, 1, piece)
    grad_fc_bias = lax.dynamic_update_slice_in_dim(
        jnp.zeros((nf, n, piece), wider), hidden_sums, s, 1
    )
    parts = [
        grad_gain_one,
        grad_shift_one,
        grad_qv,
        jnp.sum(grad_branch.astype(wider), 0),
        grad_gain_two,
        grad_shift_two,
        grad_fc_bias,
        jnp.sum(upstream, 0),
    ]
    summed, qkv_out, proj_first, proj_second, fc_out, out_out = give_back(
        jnp.concatenate([p.reshape(nf, -1) for p in parts], 1),
        qkv_part,
        qkv_cols,
        proj_first,
        proj_second,
        fc_part,
        out_part,
        n,
        nf,
        back,
        7,
    )
    if not even:
        qkv_part = qkv_part.reshape(3, wide, rows)
        qkv_out = lax.all_gather(qkv_part, "seq", axis=1, tiled=True)[:, :width]
        qkv_out = qkv_out.reshape(3 * width, rows)
        qkv_out = lax.dynamic_slice_in_dim(qkv_out, s * qkv_cols, qkv_cols, 0)
    out_out = jnp.sum(out_out.astype(wider), 0)
    qkv_out = qkv_out.T.astype(wider)
    proj_out = jnp.concatenate([proj_first, proj_second], 1)
    proj_out = proj_out.reshape(n * piece, width // n).astype(wider)
    fc_out = fc_out.transpose(1, 0, 2).reshape(rows, nf * piece).astype(wider)
    vector_out = []
    at = 0
    for size in sizes:
        vector_out.append(summed[at : at + size])
        at += size
    return (
        output,
        input_grad,
        vector_out[0],
        vector_out[1],
        qkv_out,
        vector_out[2],
        out_out,
        vector_out[3],
        vector_out[4],
        vector_out[5],
        fc_out,
        vector_out[6],
        proj_out,
        vector_out[7],
    )


def solution(mesh):
    in_specs = (
        P("fsdp", "seq", None),
        P("fsdp"),
        P("fsdp"),
        P("fsdp", "seq"),
        P("fsdp"),
        P("fsdp", "seq"),
        P("fsdp"),
        P("fsdp"),
        P("fsdp"),
        P("fsdp", "seq"),
        P("fsdp"),
        P("fsdp", "seq"),
        P("fsdp"),
        P("fsdp", None),
        P("fsdp", None),
        P("fsdp", "seq", None),
    )
    out_specs = (
        P("fsdp", "seq", None),
        P("fsdp", "seq", None),
        P("fsdp"),
        P("fsdp"),
        P("fsdp", "seq"),
        P("fsdp"),
        P("fsdp", "seq"),
        P("fsdp"),
        P("fsdp"),
        P("fsdp"),
        P("fsdp", "seq"),
        P("fsdp"),
        P("fsdp", "seq"),
        P("fsdp"),
    )
    return jax.shard_map(local, mesh=mesh, in_specs=in_specs, out_specs=out_specs, check_vma=False)
```

```python
import functools
import math

import jax
import jax.numpy as jnp
import numpy as np
from jax import lax
from jax.experimental import pallas as pl
from jax.experimental.layout import Layout, with_layout_constraint
from jax.experimental.pallas import tpu as pltpu
from jax.sharding import PartitionSpec as P

MESH = pl.DeviceIdType.MESH
HEADS = 25
SMALL = pl.CostEstimate(flops=0, bytes_accessed=1 << 20, transcendentals=0)


def route_bits(n):
    bits = []
    b = 2
    while b < n:
        bits.append(b)
        b *= 2
    return bits


def flip(a, b):
    return jnp.where(lax.rem(lax.div(a, b), 2) == 0, a + b, a - b)


def place(me, r, n):
    if isinstance(r, int):
        for b in [1] + route_bits(n):
            if r & b:
                me = flip(me, b)
        return me
    for b in [1] + route_bits(n):
        me = jnp.where(lax.rem(lax.div(r, b), 2) == 0, me, flip(me, b))
    return me


def pick(table, q):
    value = jnp.int32(table[0])
    for i, entry in enumerate(table[1:]):
        value = jnp.where(q == i + 1, jnp.int32(entry), value)
    return value


def greet(ids):
    barrier = pltpu.get_barrier_semaphore()
    for i in ids:
        pl.semaphore_signal(barrier, inc=1, device_id=i, device_id_type=MESH)
    pl.semaphore_wait(barrier, len(ids))


def remote(src, dst, send, recv, device):
    return pltpu.make_async_remote_copy(
        src_ref=src, dst_ref=dst, send_sem=send, recv_sem=recv, device_id=device, device_id_type=MESH
    )


class Blocks:
    def __init__(self, axis, size, same, source, target, send, recv, local):
        self.axis, self.size, self.same = axis, size, same
        self.source, self.target = source, target
        self.send, self.recv, self.local = send, recv, local
        self.me = lax.axis_index(axis)

    @staticmethod
    def scratch(size):
        dma = pltpu.SemaphoreType.DMA
        return [dma((size - 1,)), dma((size - 1,)), dma]

    def peers(self):
        return [{self.axis: lax.rem(self.me + d, self.size)} for d in range(1, self.size)]

    def copy(self, d):
        to = lax.rem(self.me + d, self.size)
        src = self.source if self.same else self.source.at[to]
        return remote(src, self.target.at[self.me], self.send.at[d - 1], self.recv.at[d - 1], {self.axis: to})

    def own(self):
        src = self.source if self.same else self.source.at[self.me]
        return pltpu.make_async_copy(src, self.target.at[self.me], self.local)

    def start(self):
        for d in range(1, self.size):
            self.copy(d).start()
        self.own().start()

    def finish(self):
        for d in range(1, self.size):
            dst = self.target.at[lax.rem(self.me + self.size - d, self.size)]
            remote(dst, dst, self.send.at[d - 1], self.recv.at[d - 1], {self.axis: self.me}).wait_recv()
        self.own().wait()
        for d in range(1, self.size):
            self.copy(d).wait_send()


class Spread:
    def __init__(self, n, source, target, send, recv, local):
        self.n, self.source, self.target = n, source, target
        self.send, self.recv, self.local = send, recv, local
        self.me = lax.axis_index("seq")
        self.bits = route_bits(n)
        self.orders = [self.bits, self.bits[::-1]]
        self.h = source.shape[0] // 2

    @staticmethod
    def scratch(n):
        dma = pltpu.SemaphoreType.DMA
        return [dma((2, len(route_bits(n)) + 1, n)), dma((2, n)), dma]

    def device(self, b):
        return {"seq": flip(self.me, b)}

    def peers(self):
        return [self.device(b) for b in [1] + self.bits]

    def rows(self, half):
        return pl.ds(half * self.h, self.h)

    def ship(self, half, k, b):
        owner = place(self.me, k, self.n)
        src = self.source if k == 0 else self.target.at[owner]
        lane = 0 if b == 1 else 1 + self.bits.index(b)
        return remote(
            src.at[self.rows(half)],
            self.target.at[owner].at[self.rows(half)],
            self.send.at[half, lane, k],
            self.recv.at[half, k ^ b],
            self.device(b),
        )

    def arrive(self, half, k):
        dst = self.target.at[place(self.me, k, self.n)].at[self.rows(half)]
        remote(dst, dst, self.send.at[half, 0, 0], self.recv.at[half, k], self.device(1)).wait_recv()

    def own(self):
        return pltpu.make_async_copy(self.source, self.target.at[self.me], self.local)

    def fresh(self, half, i):
        had = [0]
        for b in self.orders[half][:i]:
            had = had + [k ^ b for k in had]
        return [k ^ self.orders[half][i] for k in had]

    def start(self):
        for i in range(len(self.bits)):
            for half in (0, 1):
                self.ship(half, 0, self.orders[half][i]).start()
        for half in (0, 1):
            self.ship(half, 0, 1).start()
        self.own().start()

    def phase(self, i):
        for half in (0, 1):
            for k in self.fresh(half, i):
                self.arrive(half, k)
                for b in self.orders[half][i + 1 :] + [1]:
                    self.ship(half, k, b).start()

    def finish(self):
        for half in (0, 1):
            for k in range(1, self.n, 2):
                self.arrive(half, k)
        self.own().wait()
        for half in (0, 1):
            for b in self.orders[half] + [1]:
                self.ship(half, 0, b).wait_send()
            for i in range(len(self.bits)):
                for k in self.fresh(half, i):
                    for b in self.orders[half][i + 1 :] + [1]:
                        self.ship(half, k, b).wait_send()


class PlaneSum(Blocks):
    def __init__(self, size, source, low, target, send, recv, local):
        super().__init__("fsdp", size, False, source, target, send, recv, local)
        self.window = pl.ds(low, target.shape[1])

    @staticmethod
    def scratch(size, rows, cols):
        return [pltpu.VMEM((size, rows, cols), jnp.bfloat16)] + Blocks.scratch(size)

    def copy(self, d):
        to = lax.rem(self.me + d, self.size)
        src = self.source.at[to].at[self.window]
        return remote(src, self.target.at[self.me], self.send.at[d - 1], self.recv.at[d - 1], {self.axis: to})

    def own(self):
        src = self.source.at[self.me].at[self.window]
        return pltpu.make_async_copy(src, self.target.at[self.me], self.local)

    def store(self, out):
        total = self.target[0].astype(jnp.float32)
        for i in range(1, self.size):
            total = total + self.target[i].astype(jnp.float32)
        cols = out.shape[2]
        for i in range(out.shape[0]):
            out[i] = total[:, i * cols : (i + 1) * cols].astype(out.dtype)


def blocks_shape(x, size, same):
    return jax.ShapeDtypeStruct(((size,) + x.shape) if same else x.shape, x.dtype)


def arrival_order(n):
    bits = route_bits(n)
    orders = [bits, bits[::-1]]
    lists = []
    for order in orders:
        held, phases = [0], [-1]
        for i, b in enumerate(order):
            fresh = [h ^ b for h in held]
            held, phases = held + fresh, phases + [i] * len(fresh)
        lists.append(list(zip(held, phases)))
    entries = []
    for i in range(n // 2):
        for odd in (0, 1):
            for half in (0, 1):
                k, phase = lists[half][i]
                entries.append((half, k ^ odd, phase, odd))
    return orders, entries


def gather_kernel(n, h, body, n_const, n_out, relative, modes, nf, same, second, *refs):
    if second:
        at = 1 + n_const
        out = at + 1 + min(nf, 1) + 1 + n_out
        w_ref, w_all = refs[at], refs[out]
        w_send, w_recv, w_keep = refs[-3:]
        refs = refs[:at] + refs[at + 1 : out] + refs[out + 1 : -3]
        w_half = w_ref.shape[1] // 256 * 128
        w_lanes = [pl.ds(0, w_half), pl.ds(w_half, w_ref.shape[1] - w_half)]
    refs, rider = split_rider(refs, nf, same, 1 + n_const, 1 + n_out)
    x_ref = refs[0]
    consts = refs[1 : 1 + n_const]
    all_ref = refs[1 + n_const]
    outs = refs[2 + n_const : 2 + n_const + n_out]
    held = refs[2 + n_const + n_out]
    stages = refs[3 + n_const + n_out : 3 + n_const + 2 * n_out]
    send, recv, keep, store = refs[3 + n_const + 2 * n_out :]
    me = lax.axis_index("seq")
    orders, entries = arrival_order(n)
    bits = orders[0]
    nb = len(bits)

    def device(b):
        return {"seq": flip(me, b)}

    def spot(half, k):
        return 2 * (k if relative else place(me, k, n)) + half

    def ship(half, k, b):
        at = spot(half, k)
        src = x_ref.at[pl.ds(half * h, h)] if isinstance(k, int) and k == 0 else held.at[at]
        lane = 0 if b == 1 else 1 + bits.index(b)
        to = k ^ b if isinstance(k, int) else place(k, b, n)
        dst = 2 * to + half if relative else at
        first = remote(src, held.at[dst], send.at[half, lane, k], recv.at[half, to], device(b))
        if not second:
            return [first]
        owner = place(me, k, n)
        lanes = w_lanes[half]
        src = w_ref if isinstance(k, int) and k == 0 else w_all.at[owner]
        other = remote(
            src.at[:, lanes], w_all.at[owner].at[:, lanes], w_send.at[half, lane, k], w_recv.at[half, to], device(b)
        )
        return [first, other]

    def each(copies, act):
        for c in copies:
            act(c)

    def w_arrive(half, k):
        dst = w_all.at[place(me, k, n)].at[:, w_lanes[half]]
        remote(dst, dst, w_send.at[0, 0, 0], w_recv.at[half, k], device(1)).wait_recv()

    greet([device(b) for b in [1] + bits] + (rider.peers() if nf else []))
    for i in range(nb):
        for half in (0, 1):
            each(ship(half, 0, orders[half][i]), lambda c: c.start())
    for half in (0, 1):
        each(ship(half, 0, 1), lambda c: c.start())
    if second:
        pltpu.make_async_copy(w_ref, w_all.at[me], w_keep).start()
    if nf:
        rider.start()

    def output(o, q, at):
        slot = lax.rem(q, 2)
        return pltpu.make_async_copy(stages[o].at[slot], outs[o].at[at], store.at[o, slot])

    def entry(q, at, value):
        results = body(value, *consts)
        for o in range(n_out):

            @pl.when(q >= 2)
            def _(o=o):
                output(o, q, at[modes[o]]).wait()

            stages[o][lax.rem(q, 2)] = results[o]
            output(o, q, at[modes[o]]).start()

    def step(q, carry):
        half = pick([e[0] for e in entries], q)
        k = pick([e[1] for e in entries], q)
        phase = pick([e[2] for e in entries], q)
        odd = pick([e[3] for e in entries], q)
        at = spot(half, k)

        @pl.when(k == 0)
        def _():
            held[at] = x_ref[pl.ds(pl.multiple_of(half * h, h), h)]

        @pl.when(k != 0)
        def _():
            remote(held.at[at], held.at[at], send.at[0, 0, 0], recv.at[half, k], device(1)).wait_recv()

        for side in (0, 1) if second else ():

            @pl.when((k != 0) & (half == side))
            def _(side=side):
                w_arrive(side, k)

        for side in (0, 1):
            for i in range(nb):

                @pl.when((half == side) & (odd == 0) & (k != 0) & (phase < i))
                def _(side=side, i=i):
                    each(ship(side, k, orders[side][i]), lambda c: c.start())

            @pl.when((half == side) & (odd == 0) & (k != 0))
            def _(side=side):
                each(ship(side, k, 1), lambda c: c.start())

        pltpu.make_async_copy(held.at[at], all_ref.at[at], keep.at[q]).start()
        if n_out:
            entry(q, (2 * place(me, k, n) + half, 2 * k + half), held[at])
        return carry

    lax.fori_loop(0, 2 * n, step, 0)
    for q, (half, k, phase, odd) in enumerate(entries):
        at = spot(half, k)
        pltpu.make_async_copy(held.at[at], all_ref.at[at], keep.at[q]).wait()
        if q >= 2 * n - 2:
            for o in range(n_out):
                output(o, jnp.int32(q), at).wait()
        if not odd:
            for i in range(nb):
                if phase < i:
                    each(ship(half, k, orders[half][i]), lambda c: c.wait_send())
            each(ship(half, k, 1), lambda c: c.wait_send())
    if second:
        pltpu.make_async_copy(w_ref, w_all.at[me], w_keep).wait()
    if nf:
        rider.finish()


def split_rider(refs, nf, same, n_in, n_out):
    if not nf:
        return refs, None
    source = refs[n_in]
    target = refs[n_in + 1 + n_out]
    rider = Blocks("fsdp", nf, same, source, target, *refs[-3:])
    return refs[:n_in] + refs[n_in + 1 : n_in + 1 + n_out] + refs[n_in + 2 + n_out : -3], rider


def rider_parts(rider):
    if rider is None:
        return [], [], [], [], 0, False
    x, same, nf = rider
    hbm = [pl.BlockSpec(memory_space=pl.ANY)]
    return [x], hbm, [blocks_shape(x, nf, same)], Blocks.scratch(nf), nf, same


def seq_gather(x, n, ident, name, body=None, consts=(), outs=(), relative=False, modes=None, rider=None, second=None):
    rows, cols = x.shape
    h = rows // 2
    nb = len(route_bits(n))
    shapes = [jax.ShapeDtypeStruct((2 * n, h, c), d) for c, d in outs]
    vmem = pl.BlockSpec(memory_space=pltpu.VMEM)
    hbm = pl.BlockSpec(memory_space=pl.ANY)
    more, spec, shape, scratch, nf, same = rider_parts(rider)
    also = [] if second is None else [second]
    out = pl.pallas_call(
        functools.partial(
            gather_kernel, n, h, body, len(consts), len(outs), relative, modes, nf, same, second is not None
        ),
        out_shape=[jax.ShapeDtypeStruct((2 * n, h, cols), x.dtype)]
        + shapes
        + [jax.ShapeDtypeStruct((n,) + w.shape, w.dtype) for w in also]
        + shape,
        in_specs=[vmem] * (1 + len(consts)) + [hbm] * len(also) + spec,
        out_specs=[hbm] * (1 + len(outs)) + [hbm] * len(also) + spec,
        scratch_shapes=[pltpu.VMEM((2 * n, h, cols), x.dtype)]
        + [pltpu.VMEM((2, h, c), d) for c, d in outs]
        + [
            pltpu.SemaphoreType.DMA((2, nb + 1, n)),
            pltpu.SemaphoreType.DMA((2, n)),
            pltpu.SemaphoreType.DMA((2 * n,)),
            pltpu.SemaphoreType.DMA((max(len(outs), 1), 2)),
        ]
        + scratch
        + [
            pltpu.SemaphoreType.DMA((2, nb + 1, n)),
            pltpu.SemaphoreType.DMA((2, n)),
            pltpu.SemaphoreType.DMA,
        ]
        * len(also),
        compiler_params=pltpu.CompilerParams(
            collective_id=ident, has_side_effects=True, vmem_limit_bytes=60 << 20
        ),
        cost_estimate=SMALL,
        name=name,
    )(x, *consts, *also, *more)
    return [o.reshape(2 * n * h, o.shape[2]) for o in out[: 1 + len(outs)]] + list(out[1 + len(outs) :])


class Side:
    def __init__(self, count, refs):
        self.count = count
        self.a, self.b, self.grad, self.sums, self.acc, self.abuf, self.bbuf, self.load = refs

    def fetch(self, i):
        slot = lax.rem(i, 2)
        return [
            pltpu.make_async_copy(self.a.at[i], self.abuf.at[slot], self.load.at[0, slot]),
            pltpu.make_async_copy(self.b.at[i], self.bbuf.at[slot], self.load.at[1, slot]),
        ]

    def begin(self):
        self.acc[...] = jnp.zeros_like(self.acc)
        self.sums[...] = jnp.zeros_like(self.sums)
        for c in self.fetch(jnp.int32(0)):
            c.start()

    def run(self, first, last):
        def step(i, carry):
            @pl.when(i + 1 < self.count)
            def _():
                for c in self.fetch(i + 1):
                    c.start()

            for c in self.fetch(i):
                c.wait()
            slot = lax.rem(i, 2)
            a, b = self.abuf[slot], self.bbuf[slot]
            self.acc[...] += lax.dot_general(
                a, b, (((0,), (0,)), ((), ())), preferred_element_type=jnp.float32
            )
            self.sums[...] += jnp.sum(b.astype(jnp.float32), 0, keepdims=True)
            return carry

        lax.fori_loop(first, last, step, 0)

    def end(self):
        self.grad[...] = self.acc[...].astype(self.grad.dtype)


def side_parts(side, count):
    if side is None:
        return [], [], [], [], []
    a, b = side
    h = a.shape[0] // count
    low = jnp.bfloat16
    hbm = pl.BlockSpec(memory_space=pl.ANY)
    vmem = pl.BlockSpec(memory_space=pltpu.VMEM)
    return (
        [x.reshape(count, h, x.shape[1]) for x in (a, b)],
        [
            jax.ShapeDtypeStruct((a.shape[1], b.shape[1]), low),
            jax.ShapeDtypeStruct((1, b.shape[1]), jnp.float32),
        ],
        [hbm, hbm],
        [vmem, vmem],
        [
            pltpu.VMEM((a.shape[1], b.shape[1]), jnp.float32),
            pltpu.VMEM((2, h, a.shape[1]), low),
            pltpu.VMEM((2, h, b.shape[1]), low),
            pltpu.SemaphoreType.DMA((2, 2)),
        ],
    )


def scatter_order(n):
    bits = route_bits(n)
    orders = [bits, bits[::-1]]
    lists = [
        sorted(range(0, n, 2), key=lambda k: [-int(bool(k & b)) for b in order]) for order in orders
    ]
    return orders, [(half, lists[half][i]) for i in range(n // 2) for half in (0, 1)]


def scatter_kernel(n, h, body, n_in, n_const, n_out, modes, nf, same, has_side, has_norm, carried, *refs):
    if carried:
        out = 1 + n_in + n_const + 2 * has_side + min(nf, 1) + 1 + n_out + 2 * has_side + min(nf, 1)
        refs = refs[1:out] + refs[out + 1 :]
    if has_norm:
        out = n_in + 3 + n_const + 2 * has_side + min(nf, 1)
        values, gain, joins = refs[:3]
        x_grad, g_grad, b_grad = refs[out], refs[out + 1], refs[out + 2]
        refs = refs[3:out] + (None,) + refs[out + 3 :]
    side = None
    if has_side:
        at = n_in + n_const
        out = at + 2 + min(nf, 1) + 1 + n_out
        extra = refs[at : at + 2] + refs[out : out + 2] + refs[-4:]
        refs = refs[:at] + refs[at + 2 : out] + refs[out + 2 : -4]
        side = Side(2 * n, extra)
    refs, rider = split_rider(refs, nf, same, n_in + n_const, 1 + n_out)
    ins = refs[:n_in]
    consts = refs[n_in : n_in + n_const]
    at = n_in + n_const
    sum_ref = refs[at]
    outs = refs[at + 1 : at + 1 + n_out]
    at += 1 + n_out
    give, pair, own, far, total = refs[at : at + 5]
    at += 5
    loads = refs[at : at + n_in]
    stages = refs[at + n_in : at + n_in + n_out]
    pair_send, pair_recv, far_send, far_recv, load, store, done = refs[at + n_in + n_out :]
    me = lax.axis_index("seq")
    orders, entries = scatter_order(n)
    bits = orders[0]
    slots = give.shape[0]
    index = {e: j for j, e in enumerate(entries)}

    def device(b):
        return {"seq": flip(me, b)}

    def phase_of(half, k):
        for i, b in enumerate(orders[half]):
            if k & b:
                return i
        return len(bits)

    landing = {}
    for half in (0, 1):
        for i, b in enumerate(orders[half]):
            for k in range(0, n, 2):
                if phase_of(half, k) == i:
                    landing[half, i, k ^ b] = len(landing)

    halves = [e[0] for e in entries]
    ks = [e[1] for e in entries]

    def spot(q, relative):
        j = lax.div(q, 2)
        k = pick(ks, j)
        k = jnp.where(lax.rem(q, 2) == 0, flip(k, 1), k)
        return 2 * (k if relative else place(me, k, n)) + pick(halves, j)

    def fetch(q):
        slot = lax.rem(q, 2)
        return [
            pltpu.make_async_copy(ins[i].at[spot(q, modes[0][i])], loads[i].at[slot], load.at[i, slot])
            for i in range(n_in)
        ]

    def output(o, q):
        slot = lax.rem(q, 2)
        return pltpu.make_async_copy(stages[o].at[slot], outs[o].at[spot(q, modes[1][o])], store.at[o, slot])

    def hand(j):
        slot = lax.rem(j, slots)
        return remote(give.at[slot], pair.at[j], pair_send.at[j], pair_recv.at[j], device(1))

    def launch(half, k):
        i = phase_of(half, k)
        b = orders[half][i]
        to = landing[half, i, k ^ b]
        return remote(own.at[index[half, k]], far.at[to], far_send.at[to], far_recv.at[to], device(b))

    def join(j):
        hand(j).wait_recv()
        own[j] = (own[j].astype(jnp.float32) + pair[j].astype(jnp.float32)).astype(own.dtype)
        for e, (half, k) in enumerate(entries):
            if phase_of(half, k) == 0:

                @pl.when(j == e)
                def _(half=half, k=k):
                    launch(half, k).start()

    for c in fetch(jnp.int32(0)):
        c.start()
    greet([device(b) for b in [1] + bits] + (rider.peers() if nf else []))
    if nf:
        rider.start()

    def step(q, carry):
        j = lax.div(q, 2)
        slot = lax.rem(q, 2)

        @pl.when(q + 1 < 2 * n)
        def _():
            for c in fetch(q + 1):
                c.start()

        for c in fetch(q):
            c.wait()
        part, *results = body(*[r[slot] for r in loads], *consts)
        for o in range(n_out):

            @pl.when(q >= 2)
            def _(o=o):
                output(o, q).wait()

            stages[o][slot] = results[o]
            output(o, q).start()

        @pl.when(slot == 0)
        def _():
            @pl.when(j >= slots)
            def _():
                hand(j - slots).wait_send()

            give[lax.rem(j, slots)] = part.astype(give.dtype)
            hand(j).start()

        @pl.when(slot == 1)
        def _():
            own[j] = part.astype(own.dtype)

            @pl.when(j >= 1)
            def _():
                join(j - 1)

        return carry

    lax.fori_loop(0, 2 * n, step, 0)
    if side:
        side.begin()
    join(jnp.int32(n - 1))
    first = n // 2
    cuts = [0, first] + [first + (2 * n - first) * i // (len(bits) - 1) for i in range(1, len(bits))]
    for i in range(len(bits)):
        if side:
            side.run(cuts[i], cuts[i + 1])
        for half in (0, 1):
            order = orders[half]
            for k in [k for hh, k in entries if hh == half and phase_of(half, k) > i]:
                to = landing[half, i, k]
                remote(far.at[to], far.at[to], far_send.at[to], far_recv.at[to], device(1)).wait_recv()
                j = index[half, k]
                rows = pl.ds(half * h, h)
                if i == len(bits) - 1:
                    total[rows] = own[j].astype(jnp.float32) + far[to].astype(jnp.float32)
                    if not has_norm:
                        pltpu.make_async_copy(total.at[rows], sum_ref.at[rows], done.at[half]).start()
                else:
                    own[j] = (own[j].astype(jnp.float32) + far[to].astype(jnp.float32)).astype(own.dtype)
                    if phase_of(half, k) == i + 1:
                        launch(half, k).start()
    if has_norm:
        g_grad[...] = jnp.zeros_like(g_grad)
        b_grad[...] = jnp.zeros_like(b_grad)

        def tile(i, carry):
            rows = pl.ds(pl.multiple_of(i * 64, 64), 64)
            x = values[rows].astype(jnp.float32)
            centred = x - jnp.mean(x, -1, keepdims=True)
            scale = lax.rsqrt(jnp.mean(centred * centred, -1, keepdims=True) + 1e-05)
            xhat = centred * scale
            grad = total[rows]
            g_grad[...] += jnp.sum(grad * xhat, 0, keepdims=True)
            b_grad[...] += jnp.sum(grad, 0, keepdims=True)
            e = gain[...] * grad
            inner = e - jnp.mean(e, -1, keepdims=True) - xhat * jnp.mean(e * xhat, -1, keepdims=True)
            x_grad[rows] = (joins[rows].astype(jnp.float32) + scale * inner).astype(x_grad.dtype)
            return carry

        lax.fori_loop(0, 2 * h // 64, tile, 0)
    for half in (0, 1) if not has_norm else ():
        rows = pl.ds(half * h, h)
        pltpu.make_async_copy(total.at[rows], sum_ref.at[rows], done.at[half]).wait()
    for q in (2 * n - 2, 2 * n - 1):
        for o in range(n_out):
            output(o, jnp.int32(q)).wait()
    for j in range(max(n - slots, 0), n):
        hand(jnp.int32(j)).wait_send()
    for half, k in entries:
        if phase_of(half, k) < len(bits):
            launch(half, k).wait_send()
    if nf:
        rider.finish()
    if side:
        side.end()


def seq_scatter(n, cols, ident, name, body, ins, consts, outs=(), modes=None, rider=None, side=None, norm=None, carry=None):
    h = ins[0].shape[0] // (2 * n)
    low = jnp.bfloat16
    slots = min(4, n)
    split = [a.reshape(2 * n, h, a.shape[1]) for a in ins]
    vmem = pl.BlockSpec(memory_space=pltpu.VMEM)
    hbm = pl.BlockSpec(memory_space=pl.ANY)
    reach = n - 2
    modes = modes or ([0] * len(ins), [0] * len(outs))
    more, spec, shape, scratch, nf, same = rider_parts(rider)
    s_ins, s_shapes, s_in_specs, s_out_specs, s_scratch = side_parts(side, 2 * n)
    sums = [jax.ShapeDtypeStruct((2 * h, cols), jnp.float32)]
    norms = []
    carries = [] if carry is None else [carry]
    if norm is not None:
        norms = list(norm[:3])
        line = jax.ShapeDtypeStruct((1, cols), jnp.float32)
        sums = [jax.ShapeDtypeStruct((2 * h, cols), norm[3]), line, line]
    out = pl.pallas_call(
        functools.partial(
            scatter_kernel, n, h, body, len(ins), len(consts), len(outs), modes, nf, same, int(side is not None), norm is not None, carry is not None
        ),
        out_shape=sums
        + [jax.ShapeDtypeStruct((2 * n, h, c), d) for c, d in outs]
        + s_shapes
        + shape
        + [jax.ShapeDtypeStruct(x.shape, x.dtype) for x in carries],
        in_specs=[hbm] * len(carries)
        + [vmem] * len(norms)
        + [hbm] * len(ins)
        + [vmem] * len(consts)
        + s_in_specs
        + spec,
        out_specs=([vmem] * 3 if norms else [hbm])
        + [hbm] * len(outs)
        + s_out_specs
        + spec
        + [hbm] * len(carries),
        input_output_aliases={0: len(sums + list(outs) + s_shapes + shape)} if carries else {},
        scratch_shapes=[
            pltpu.VMEM((slots, h, cols), low),
            pltpu.VMEM((n, h, cols), low),
            pltpu.VMEM((n, h, cols), low),
            pltpu.VMEM((reach, h, cols), low),
            pltpu.VMEM((2 * h, cols), jnp.float32),
        ]
        + [pltpu.VMEM((2, h, a.shape[2]), a.dtype) for a in split]
        + [pltpu.VMEM((2, h, c), d) for c, d in outs]
        + [
            pltpu.SemaphoreType.DMA((n,)),
            pltpu.SemaphoreType.DMA((n,)),
            pltpu.SemaphoreType.DMA((reach,)),
            pltpu.SemaphoreType.DMA((reach,)),
            pltpu.SemaphoreType.DMA((len(ins), 2)),
            pltpu.SemaphoreType.DMA((max(len(outs), 1), 2)),
            pltpu.SemaphoreType.DMA((2,)),
        ]
        + scratch
        + s_scratch,
        compiler_params=pltpu.CompilerParams(
            collective_id=ident, has_side_effects=True, vmem_limit_bytes=60 << 20
        ),
        cost_estimate=SMALL,
        name=name,
    )(*carries, *norms, *split, *consts, *s_ins, *more)
    lines = list(out[1:3]) if norms else []
    out = [out[0]] + list(out[1 + len(lines) :])
    many = 1 + len(outs)
    sides = [] if side is None else list(out[many : many + 2])
    more = list(out[many + len(sides) :])
    return [out[0]] + lines + [o.reshape(2 * n * h, o.shape[2]) for o in out[1:many]] + sides + more


class Rows:
    def __init__(self, n, held, width, wide, back):
        moves = []
        for to in range(n):
            for third in range(3):
                at, end = third * width + to * wide, third * width + min((to + 1) * wide, width)
                row = third * wide
                while at < end:
                    source = at // held
                    count = min(end, (source + 1) * held) - at
                    moves.append((source, at - source * held, to, row, count))
                    at, row = at + count, row + count
        self.n = n
        self.moves = [(c, d, a, b, e) if back else (a, b, c, d, e) for a, b, c, d, e in moves]
        self.out = [[m for m in self.moves if m[0] == i] for i in range(n)]
        self.into = [[m for m in self.moves if m[2] == i] for i in range(n)]
        self.most = max(len(v) for v in self.out + self.into)

    def scratch(self):
        dma = pltpu.SemaphoreType.DMA
        return [dma((self.most,)), dma((self.most,)), dma((self.most,))]

    def bind(self, source, target, send, recv, local):
        self.source, self.target, self.send, self.recv, self.local = source, target, send, recv, local
        return self

    def copy(self, i, m):
        src = self.source.at[pl.ds(m[1], m[4])]
        dst = self.target.at[pl.ds(m[3], m[4])]
        if m[0] == m[2]:
            return pltpu.make_async_copy(src, dst, self.local.at[i])
        return remote(src, dst, self.send.at[i], self.recv.at[self.into[m[2]].index(m)], {"seq": m[2]})

    def start(self):
        me = lax.axis_index("seq")
        for s in range(self.n):

            @pl.when(me == s)
            def _(s=s):
                for i, m in enumerate(self.out[s]):
                    self.copy(i, m).start()

    def finish(self):
        me = lax.axis_index("seq")
        for s in range(self.n):

            @pl.when(me == s)
            def _(s=s):
                for i, m in enumerate(self.into[s]):
                    if m[0] != s:
                        dst = self.target.at[pl.ds(m[3], m[4])]
                        remote(dst, dst, self.send.at[0], self.recv.at[i], {"seq": s}).wait_recv()
                for i, m in enumerate(self.out[s]):
                    if m[0] == m[2]:
                        self.copy(i, m).wait()
                    else:
                        self.copy(i, m).wait_send()


class Units:
    def __init__(self, n, nf, back, source, target, send, recv, local):
        self.n, self.nf, self.back = n, nf, back
        self.source, self.target, self.send, self.recv, self.local = source, target, send, recv, local
        self.me = lax.axis_index("seq")

    @staticmethod
    def scratch(nf):
        dma = pltpu.SemaphoreType.DMA
        return [dma((nf,)), dma((nf,)), dma]

    def ends(self, i):
        group = self.n // self.nf
        if self.back:
            return i * group + lax.div(self.me, self.nf), lax.rem(self.me, self.nf)
        return lax.rem(self.me, group) * self.nf + i, lax.div(self.me, group)

    def comes(self, i):
        group = self.n // self.nf
        if self.back:
            return lax.rem(self.me, group) * self.nf + i
        return i * group + lax.div(self.me, self.nf)

    def each(self, i, there, here):
        to, slot = self.ends(i)

        @pl.when(to != self.me)
        def _():
            there(remote(self.source.at[i], self.target.at[slot], self.send.at[i], self.recv.at[slot], {"seq": to}))

        @pl.when(to == self.me)
        def _():
            here(pltpu.make_async_copy(self.source.at[i], self.target.at[slot], self.local))

    def start(self):
        for i in range(self.nf):
            self.each(i, lambda c: c.start(), lambda c: c.start())

    def finish(self):
        for i in range(self.nf):
            source = self.comes(i)

            @pl.when(source != self.me)
            def _(i=i):
                dst = self.target.at[i]
                remote(dst, dst, self.send.at[0], self.recv.at[i], {"seq": self.me}).wait_recv()

        for i in range(self.nf):
            self.each(i, lambda c: c.wait_send(), lambda c: c.wait())


def all_peers(n, nf):
    me, f = lax.axis_index("seq"), lax.axis_index("fsdp")
    return [{"seq": place(me, r, n)} for r in range(1, n)] + [
        {"fsdp": lax.rem(f + d, nf)} for d in range(1, nf)
    ]


def exchange_kernel(n, nf, rows, count, *refs):
    ins, outs, sems = refs[: 4 + count], refs[4 + count : 8 + 2 * count], list(refs[8 + 2 * count :])
    take = lambda k: [sems.pop(0) for _ in range(k)]
    parts = []
    if rows is not None:
        parts.append(rows.bind(ins[0], outs[0], *take(3)))
    vectors = [Blocks("fsdp", nf, True, ins[4 + i], outs[4 + i], *take(3)) for i in range(count)]
    later = [
        Blocks("fsdp", nf, True, ins[3], outs[3], *take(3)),
        Units(n, nf, False, ins[2], outs[2], *take(3)),
        Blocks("seq", n, False, ins[1], outs[1], *take(3)),
    ]
    parts = vectors + parts + later
    greet(all_peers(n, nf))
    for p in parts:
        p.start()
    for p in parts:
        p.finish()


def exchange(w, p, c, o, vectors, n, nf, rows, wide, ident):
    hbm = pl.BlockSpec(memory_space=pl.ANY)
    count = len(vectors)
    out = pl.pallas_call(
        functools.partial(exchange_kernel, n, nf, rows, count),
        out_shape=[
            jax.ShapeDtypeStruct((3 * wide, w.shape[1]) if rows is not None else w.shape, w.dtype),
            blocks_shape(p, n, False),
            blocks_shape(c, nf, False),
            blocks_shape(o, nf, True),
        ]
        + [blocks_shape(v, nf, True) for v in vectors],
        in_specs=[hbm] * (4 + count),
        out_specs=[hbm] * (4 + count),
        scratch_shapes=(rows.scratch() if rows is not None else [])
        + sum([Blocks.scratch(nf) for _ in vectors], [])
        + Blocks.scratch(nf)
        + Units.scratch(nf)
        + Blocks.scratch(n),
        compiler_params=pltpu.CompilerParams(collective_id=ident, has_side_effects=True),
        cost_estimate=SMALL,
        name="exchange",
    )(w, p, c, o, *vectors)
    return out[0], out[1], out[2], out[3], out[4:]


def to_tokens_kernel(n, wide, x_ref, o_ref, send, recv, local):
    me = lax.axis_index("seq")

    def target(i):
        return o_ref.at[:, pl.ds(pl.multiple_of(i * wide, 128), wide)]

    greet([{"seq": place(me, r, n)} for r in range(1, n)])
    copies = []
    for r in range(n - 1, 0, -1):
        to = place(me, r, n)
        c = remote(x_ref.at[to], target(me), send.at[r - 1], recv.at[r - 1], {"seq": to})
        c.start()
        copies.append(c)
    mine = pltpu.make_async_copy(x_ref.at[me], target(me), local)
    mine.start()
    for r in range(1, n):
        dst = target(place(me, r, n))
        remote(dst, dst, send.at[0], recv.at[r - 1], {"seq": place(me, r, n)}).wait_recv()
    mine.wait()
    for c in copies:
        c.wait_send()


def to_tokens(x, n, wide, ident):
    rows = x.shape[1]
    hbm = pl.BlockSpec(memory_space=pl.ANY)
    return pl.pallas_call(
        functools.partial(to_tokens_kernel, n, wide),
        out_shape=jax.ShapeDtypeStruct((rows, n * wide), x.dtype),
        in_specs=[hbm],
        out_specs=hbm,
        scratch_shapes=Blocks.scratch(n),
        compiler_params=pltpu.CompilerParams(collective_id=ident, has_side_effects=True),
        cost_estimate=SMALL,
        name="to_tokens",
    )(x)


def to_heads_kernel(
    n, nf, wide, x_ref, w_ref, t_ref, a_ref, b_ref, z_ref, o_ref, g_ref, m_ref, z_out, t_out, made, *extra
):
    me = lax.axis_index("seq")
    send, recv, local = extra[:3]
    side = Side(2 * n, (a_ref, b_ref, g_ref, m_ref) + extra[3:7])
    planes = PlaneSum(nf, z_ref, 0, *extra[7:])
    side.begin()
    greet([{"seq": place(me, r, n)} for r in range(1, n)] + planes.peers())
    planes.start()

    def copy(r):
        to = place(me, r, n)
        return remote(made.at[r], o_ref.at[me], send.at[r - 1], recv.at[r - 1], {"seq": to})

    def mine():
        return pltpu.make_async_copy(made.at[0], o_ref.at[me], local)

    def step(i, carry):
        r = n - 1 - i
        at = place(me, r, n)
        whole, rest = w_ref.shape[1] // wide, w_ref.shape[1] % wide

        @pl.when(at < whole)
        def _():
            lanes = pl.ds(pl.multiple_of(at * wide, 128), wide)
            made[r] = mm(x_ref[...], w_ref[:, lanes]).astype(made.dtype)

        @pl.when(at >= whole)
        def _():
            made[r] = jnp.zeros(made.shape[1:], made.dtype)

        if rest:

            @pl.when(at == whole)
            def _():
                made[r, :, :rest] = mm(x_ref[...], w_ref[:, whole * wide :]).astype(made.dtype)

        @pl.when(r > 0)
        def _():
            copy(r).start()

        return carry

    lax.fori_loop(0, n, step, 0)
    mine().start()
    side.run(0, 2 * n)
    cols = t_out.shape[0]
    for at in range(0, cols, 512):
        end = min(at + 512, cols)
        t_out[at:end] = lax.dot_general(
            x_ref[:, at:end], t_ref[...], (((0,), (0,)), ((), ())), preferred_element_type=jnp.float32
        ).astype(t_out.dtype)
    side.end()
    planes.finish()
    planes.store(z_out)
    for r in range(1, n):
        dst = o_ref.at[place(me, r, n)]
        remote(dst, dst, send.at[0], recv.at[r - 1], {"seq": me}).wait_recv()
    mine().wait()
    for r in range(1, n):
        copy(r).wait_send()


def to_heads(x, w, t, n, nf, wide, ident, a, b, z, count):
    rows, cols = x.shape
    vmem = pl.BlockSpec(memory_space=pltpu.VMEM)
    hbm = pl.BlockSpec(memory_space=pl.ANY)
    s_ins, s_shapes, s_in_specs, s_out_specs, s_scratch = side_parts((a, b), 2 * n)
    return pl.pallas_call(
        functools.partial(to_heads_kernel, n, nf, wide),
        out_shape=[jax.ShapeDtypeStruct((n, rows, wide), x.dtype)]
        + s_shapes
        + [
            jax.ShapeDtypeStruct((n, count, z.shape[2] // n), z.dtype),
            jax.ShapeDtypeStruct((cols, t.shape[1]), x.dtype),
        ],
        in_specs=[vmem, vmem, vmem] + s_in_specs + [hbm],
        out_specs=[hbm] + s_out_specs + [vmem, vmem],
        scratch_shapes=[pltpu.VMEM((n, rows, wide), x.dtype)]
        + Blocks.scratch(n)
        + s_scratch
        + PlaneSum.scratch(nf, count, z.shape[2]),
        compiler_params=pltpu.CompilerParams(
            collective_id=ident, has_side_effects=True, vmem_limit_bytes=60 << 20
        ),
        cost_estimate=SMALL,
        name="to_heads",
    )(x, w, t, *s_ins, z)


def contract_kernel(a_ref, b_ref, x_ref, y_ref, s_ref, o_ref, sum_ref, acc):
    i = pl.program_id(0)
    sum_ref[...] = (x_ref[...] + y_ref[...].astype(jnp.float32) + s_ref[...]).astype(sum_ref.dtype)
    part = lax.dot_general(
        a_ref[...], b_ref[...], (((0,), (0,)), ((), ())), preferred_element_type=jnp.float32
    )

    @pl.when(i == 0)
    def _():
        acc[...] = part

    @pl.when(i > 0)
    def _():
        acc[...] += part

    @pl.when(i == pl.num_programs(0) - 1)
    def _():
        o_ref[...] = acc[...].astype(o_ref.dtype)


def contract(a, b, x, y, s, tile):
    steps = a.shape[0] // tile
    shape = (a.shape[1], b.shape[1])
    still = lambda s: pl.BlockSpec(s, lambda i: (0,) * len(s), pipeline_mode=pl.Buffered(1))
    part = lambda v: pl.BlockSpec((v.shape[0] // steps, v.shape[1]), lambda i: (i, 0))
    return pl.pallas_call(
        contract_kernel,
        out_shape=[jax.ShapeDtypeStruct(shape, a.dtype), jax.ShapeDtypeStruct(x.shape, a.dtype)],
        grid=(steps,),
        in_specs=[part(a), part(b), part(x), part(y), still(s.shape)],
        out_specs=[still(shape), part(x)],
        scratch_shapes=[pltpu.VMEM(shape, jnp.float32)],
        compiler_params=pltpu.CompilerParams(
            dimension_semantics=("arbitrary",), vmem_limit_bytes=40 << 20
        ),
        cost_estimate=SMALL,
        name="contract",
    )(a, b, x, y, s)


def give_back_kernel(
    n, nf, rows, v_ref, w_ref, p_ref, q_ref, c_ref, o_ref, v_out, w_out, p_out, q_out, c_out, o_out, planes, sums, *sems
):
    s = lax.axis_index("seq")
    f = lax.axis_index("fsdp")
    sems = list(sems)
    take = lambda k: [sems.pop(0) for _ in range(k)]
    send_z, recv_z, send_s, recv_s = take(4)
    parts = []
    if rows is not None:
        parts.append(rows.bind(w_ref, w_out, *take(3)))
    parts.append(Units(n, nf, True, c_ref, c_out, *take(3)))
    parts.append(Blocks("seq", n, False, p_ref, p_out, *take(3)))
    parts.append(Blocks("seq", n, False, q_ref, q_out, *take(3)))
    parts.append(Blocks("fsdp", nf, False, o_ref, o_out, *take(3)))
    others = [{"fsdp": lax.rem(f + d, nf)} for d in range(1, nf)]
    peers = [{"seq": place(s, r, n)} for r in range(1, n)]
    greet(peers + others)
    copies = []
    for d in range(1, nf):
        c = remote(v_ref.at[lax.rem(f + d, nf)], planes.at[d - 1], send_z.at[d - 1], recv_z.at[d - 1], others[d - 1])
        c.start()
        copies.append(c)
    for p in parts[:1]:
        p.start()
    total = v_ref[f]
    for d, c in enumerate(copies):
        c.wait_recv()
        total = total + planes[d]
    sums[0] = total
    spread = []
    for r in range(1, n):
        c = remote(sums.at[0], sums.at[r], send_s.at[r - 1], recv_s.at[r - 1], peers[r - 1])
        c.start()
        spread.append(c)
    for p in parts[1:]:
        p.start()
    for r, c in enumerate(spread):
        c.wait_recv()
        total = total + sums[r + 1]
    v_out[...] = total
    for p in parts:
        p.finish()
    for c in copies + spread:
        c.wait_send()


def give_back(vectors, w, held, p, q, c, o, n, nf, rows, ident):
    k = vectors.shape[1]
    tiles = -(-k // 1024) * 8
    padded = jnp.pad(vectors, ((0, 0), (0, tiles * 128 - k))).reshape(nf, tiles, 128)
    vmem = pl.BlockSpec(memory_space=pltpu.VMEM)
    hbm = pl.BlockSpec(memory_space=pl.ANY)
    dma = pltpu.SemaphoreType.DMA
    out = pl.pallas_call(
        functools.partial(give_back_kernel, n, nf, rows),
        out_shape=[
            jax.ShapeDtypeStruct((tiles, 128), jnp.float32),
            jax.ShapeDtypeStruct((held, w.shape[1]), w.dtype),
            blocks_shape(p, n, False),
            blocks_shape(q, n, False),
            blocks_shape(c, nf, False),
            blocks_shape(o, nf, False),
        ],
        in_specs=[vmem, hbm, hbm, hbm, hbm, hbm],
        out_specs=[vmem, hbm, hbm, hbm, hbm, hbm],
        scratch_shapes=[
            pltpu.VMEM((nf - 1, tiles, 128), jnp.float32),
            pltpu.VMEM((n, tiles, 128), jnp.float32),
            dma((nf - 1,)),
            dma((nf - 1,)),
            dma((n - 1,)),
            dma((n - 1,)),
        ]
        + (rows.scratch() if rows is not None else [])
        + Units.scratch(nf)
        + Blocks.scratch(n)
        + Blocks.scratch(n)
        + Blocks.scratch(nf),
        compiler_params=pltpu.CompilerParams(collective_id=ident, has_side_effects=True),
        cost_estimate=SMALL,
        name="give_back",
    )(padded, w, p, q, c, o)
    return (out[0].reshape(-1)[:k],) + tuple(out[1:])


HEAD=64
SCALE=0.125*math.log2(math.e)


def block_pairs(slots, trunk):
    branches = (slots - trunk) // 3
    pairs = []
    for t in range(slots):
        m = t - trunk
        if t < trunk:
            keys = [(c, int(c == t), -1, -1) for c in range(t + 1)]
        else:
            keys = [(c, 0, -1, -1) for c in range(trunk)]
            if m >= branches:
                keys.append((trunk, 0, -1, m))
            keys.append((t, 1, m, -1))
        for i, (c, causal, own, leaf) in enumerate(keys):
            pairs.append((t, c, causal, own, leaf, int(i == 0), int(i == len(keys) - 1)))
    return pairs


def block_fields(p, slots, trunk):
    branches = (slots - trunk) // 3
    counts = [t + 1 for t in range(trunk)] + [trunk + 1] * branches
    counts += [trunk + 2] * (slots - trunk - branches)
    starts = [sum(counts[:t]) for t in range(slots)]
    t, begin, end = jnp.int32(0), jnp.int32(0), jnp.int32(counts[0])
    for i in range(1, slots):
        here = p >= starts[i]
        t = jnp.where(here, i, t)
        begin = jnp.where(here, starts[i], begin)
        end = jnp.where(here, starts[i] + counts[i], end)
    i = p - begin
    last = p == end - 1
    leaf = (t >= trunk + branches) & (i == trunk)
    key = jnp.where((t >= trunk) & last, t, i)
    return t, key, last, leaf, i == 0, last


def block_values(lengths, parents, pairs, block):
    count = lengths.shape[0]
    segments = np.arange(count)
    own = np.array([p[3] for p in pairs])[None, :] == segments[:, None]
    leaf = np.array([p[4] for p in pairs])[None, :] == segments[:, None]
    above = jnp.sum(jnp.where(leaf, parents[:, None], 0), 0)
    source = own | (segments[:, None] + 1 == above[None, :])
    closed = np.array([p[3] < 0 and p[4] < 0 for p in pairs])
    reach = jnp.where(closed, block, jnp.sum(jnp.where(source, lengths[:, None], 0), 0))
    return jnp.stack([jnp.maximum(above - 1, 0), reach]).astype(jnp.int32)


def lane_half(shape):
    return lax.broadcasted_iota(jnp.int32, shape, len(shape) - 1) < HEAD


def nt(a, b):
    return lax.dot_general(a, b, (((1,), (1,)), ((), ())), preferred_element_type=jnp.float32)


def mm(a, b):
    return jnp.dot(a, b, preferred_element_type=jnp.float32)


def attend_kernel(width, block, trunk, n, values, x_ref, w_ref, b_ref, c_ref, qkv, low, att, tot, kt, c_all, acc, xbuf, xsem, *sems):
    p = pl.program_id(0)
    slot, key, causal, leaf, first, last = block_fields(p, n, trunk)
    rows = lambda slot: pl.ds(pl.multiple_of(slot * block, block), block)
    qrow = rows(slot)
    above = values[0, p]
    reach = values[1, p]
    branches = (n - trunk) // 3
    left = lane_half((block, 2 * HEAD))
    spread = Spread(n, c_ref, c_all, *sems)

    def fetch(i):
        slot = lax.rem(i, 2)
        return pltpu.make_async_copy(x_ref.at[i], xbuf.at[slot], xsem.at[slot])

    @pl.when(p == 0)
    def _():
        fetch(jnp.int32(0)).start()
        greet(spread.peers())
        spread.start()

        def step(i, carry):
            @pl.when(i + 1 < n)
            def _():
                fetch(i + 1).start()

            fetch(i).wait()
            made = (mm(xbuf[lax.rem(i, 2)], w_ref[...]) + b_ref[...]).astype(qkv.dtype)
            qkv[rows(i)] = made
            kt[:, rows(i)] = made[:, width : 2 * width].T
            return carry

        lax.fori_loop(0, n, step, 0)
        for i in range(len(spread.bits) - 1):
            spread.phase(i)

    @pl.when(first)
    def _():
        acc[...] = jnp.zeros_like(acc)

    def keyed(mask, read):
        got = read(rows(key))
        if mask is not None:
            for b in range(1, branches):
                got = jnp.where(leaf & (above == b), read(pl.ds((trunk + b) * block, block)), got)
        return got

    def step(mask):
        for j in range(width // (2 * HEAD)):
            lanes = slice(j * 2 * HEAD, (j + 1) * 2 * HEAD)
            q = qkv[qrow, lanes]
            k = keyed(mask, lambda at: qkv[at, width + j * 2 * HEAD : width + (j + 1) * 2 * HEAD])
            v = keyed(mask, lambda at: qkv[at, 2 * width + j * 2 * HEAD : 2 * width + (j + 1) * 2 * HEAD])
            for h in range(2):
                here = left if h == 0 else jnp.logical_not(left)
                s = nt(jnp.where(here, q, 0), k)
                e = jnp.exp2(s * SCALE)
                if mask is not None:
                    e = jnp.where(mask, e, 0.0)
                acc[2 * j + h] += mm(e.astype(jnp.bfloat16), jnp.where(here, v, 1))

    closes = causal | leaf
    shift = jnp.where(causal, 0, block)

    @pl.when(jnp.logical_not(closes))
    def _():
        step(None)

    @pl.when(closes)
    def _():
        row = lax.broadcasted_iota(jnp.int32, (block, block), 0)
        col = lax.broadcasted_iota(jnp.int32, (block, block), 1)
        step((col <= row + shift) & (col < reach))

    @pl.when(last)
    def _():
        for j in range(width // (2 * HEAD)):
            a, b = acc[2 * j], acc[2 * j + 1]
            total = jnp.where(left, pltpu.roll(a, HEAD, 1), pltpu.roll(b, HEAD, 1))
            value = jnp.where(left, a, b) / total
            lanes = slice(j * 2 * HEAD, (j + 1) * 2 * HEAD)
            low[:, lanes] = value.astype(jnp.bfloat16)
            att[:, lanes] = value
            tot[:, lanes] = total

    @pl.when(p == pl.num_programs(0) - 4)
    def _():
        spread.phase(len(spread.bits) - 1)

    @pl.when(p == pl.num_programs(0) - 1)
    def _():
        spread.finish()


def attend(values, pairs, x, w, bias, block, trunk, sent, n, ident):
    rows, width = x.shape[0], w.shape[1] // 3
    by_q = lambda p: (block_fields(p, n, trunk)[0], 0)
    heads = width // HEAD
    once = lambda s: pl.BlockSpec(s, lambda p: (0,) * len(s), pipeline_mode=pl.Buffered(1))
    hbm = pl.BlockSpec(memory_space=pl.ANY)
    out = pl.pallas_call(
        functools.partial(attend_kernel, width, block, trunk, n),
        grid=(len(pairs),),
        out_shape=(
            jax.ShapeDtypeStruct((rows, 3 * width), x.dtype),
            jax.ShapeDtypeStruct((rows, width), x.dtype),
            jax.ShapeDtypeStruct((rows, width), jnp.float32),
            jax.ShapeDtypeStruct((rows, width), jnp.float32),
            jax.ShapeDtypeStruct((width, rows), x.dtype),
            jax.ShapeDtypeStruct((n,) + sent.shape, sent.dtype),
        ),
        in_specs=[pl.BlockSpec(memory_space=pltpu.SMEM), hbm, once(w.shape), once(bias.shape), hbm],
        out_specs=[once((rows, 3 * width))]
        + [pl.BlockSpec((block, width), by_q)] * 3
        + [once((width, rows)), hbm],
        scratch_shapes=[
            pltpu.VMEM((heads, block, 2 * HEAD), jnp.float32),
            pltpu.VMEM((2, block, x.shape[1]), x.dtype),
            pltpu.SemaphoreType.DMA((2,)),
        ]
        + Spread.scratch(n),
        compiler_params=pltpu.CompilerParams(
            dimension_semantics=("arbitrary",),
            vmem_limit_bytes=60 << 20,
            collective_id=ident,
            has_side_effects=True,
        ),
        cost_estimate=SMALL,
        name="attend",
    )(values, x.reshape(n, block, x.shape[1]), w, bias, sent)
    return out[:5] + (out[5].reshape(n * sent.shape[0], sent.shape[1]),)


def attend_back_kernel(width, block, slots, trunk, branches, nf, lows, *refs):
    count = len(lows)
    values, qkv, kt, datt, att, tot = refs[:6]
    sources = refs[6 : 6 + count]
    out, sums = refs[6 + count : 8 + count]
    parts = refs[8 + count : 8 + 2 * count]
    dk, dv, dqt, aug = refs[8 + 2 * count : 12 + 2 * count]
    rest = refs[12 + 2 * count :]
    riders = [PlaneSum(nf, sources[i], lows[i], *rest[4 * i : 4 * i + 4]) for i in range(count)]
    p = pl.program_id(0)
    slot, key, causal, leaf, first, last = block_fields(p, slots, trunk)
    rows = lambda slot: pl.ds(pl.multiple_of(slot * block, block), block)
    above = values[0, p]
    reach = values[1, p]
    qrow = rows(slot)
    left = lane_half((block, 2 * HEAD))
    lane = lax.broadcasted_iota(jnp.int32, (block, 2 * HEAD), 1)
    columns = width // (2 * HEAD)

    @pl.when(p == 0)
    def _():
        greet(riders[0].peers())
        for r in riders:
            r.start()
        dk[...] = jnp.zeros_like(dk)
        dv[...] = jnp.zeros_like(dv)

    @pl.when(first)
    def _():
        dqt[...] = jnp.zeros_like(dqt)
        for j in range(columns):
            lanes = slice(j * 2 * HEAD, (j + 1) * 2 * HEAD)
            d = datt[:, lanes].astype(jnp.float32)
            total = tot[:, lanes]
            low = (d / total).astype(jnp.bfloat16)
            prod = d * att[:, lanes] / total
            for h in range(2):
                here = left if h == 0 else jnp.logical_not(left)
                delta = -jnp.sum(jnp.where(here, prod, 0.0), 1, keepdims=True)
                hi = delta.astype(jnp.bfloat16).astype(jnp.float32)
                mid = (delta - hi).astype(jnp.bfloat16).astype(jnp.float32)
                rest = delta - hi - mid
                at = HEAD * (1 - h)
                extra = jnp.where(
                    lane == at, hi, jnp.where(lane == at + 1, mid, jnp.where(lane == at + 2, rest, 0.0))
                )
                aug[2 * j + h] = jnp.where(here, low.astype(jnp.float32), extra).astype(jnp.bfloat16)

    def add(lanes, dks, dvs):
        @pl.when(jnp.logical_not(leaf))
        def _():
            at = rows(key)
            dk[at, lanes] += dks
            dv[at, lanes] += dvs

        @pl.when(leaf)
        def _():
            for b in range(branches):
                at = pl.ds((trunk + b) * block, block)
                dk[at, lanes] += jnp.where(above == b, dks, 0.0)
                dv[at, lanes] += jnp.where(above == b, dvs, 0.0)

    def keyed(mask, read):
        got = read(rows(key))
        if mask is not None:
            for b in range(1, branches):
                got = jnp.where(leaf & (above == b), read(pl.ds((trunk + b) * block, block)), got)
        return got

    def step(mask):
        for j in range(columns):
            lanes = slice(j * 2 * HEAD, (j + 1) * 2 * HEAD)
            q = qkv[qrow, lanes]
            k = keyed(mask, lambda at: qkv[at, width + j * 2 * HEAD : width + (j + 1) * 2 * HEAD])
            v = keyed(mask, lambda at: qkv[at, 2 * width + j * 2 * HEAD : 2 * width + (j + 1) * 2 * HEAD])
            dvs, dks = [], []
            for h in range(2):
                here = left if h == 0 else jnp.logical_not(left)
                qh = jnp.where(here, q, 0)
                e = jnp.exp2(nt(k, qh) * SCALE)
                if mask is not None:
                    e = jnp.where(mask, e, 0.0)
                dod = aug[2 * j + h]
                ds = (e * nt(jnp.where(here, v * 0.125, 0.125).astype(jnp.bfloat16), dod)).astype(
                    jnp.bfloat16
                )
                dvs.append(mm(e.astype(jnp.bfloat16), dod))
                dks.append(mm(ds, qh))
                at = j * 2 * HEAD + h * HEAD
                dqt[at : at + HEAD] += mm(keyed(mask, lambda i: kt[at : at + HEAD, i]), ds)
            add(lanes, dks[0] + dks[1], jnp.where(left, dvs[0], dvs[1]))

    closes = causal | leaf
    shift = jnp.where(causal, 0, block)

    @pl.when(jnp.logical_not(closes))
    def _():
        step(None)

    @pl.when(closes)
    def _():
        col = lax.broadcasted_iota(jnp.int32, (block, block), 0)
        row = lax.broadcasted_iota(jnp.int32, (block, block), 1)
        step((col <= row + shift) & (col < reach))

    @pl.when(last)
    def _():
        out[qrow, 0:width] = dqt[...].T.astype(jnp.bfloat16)

    @pl.when(p == pl.num_programs(0) - 1)
    def _():
        out[:, width : 2 * width] = dk[...].astype(jnp.bfloat16)
        out[:, 2 * width :] = dv[...].astype(jnp.bfloat16)
        for t in range(3):
            lanes = slice(t * width, (t + 1) * width)
            sums[:, lanes] = jnp.sum(out[:, lanes].astype(jnp.float32), 0, keepdims=True)
        for r, made in zip(riders, parts):
            r.finish()
            r.store(made)


def attend_back(values, pairs, qkv, kt, datt, att, tot, block, trunk, nf, riders, ident):
    rows, width = qkv.shape[0], qkv.shape[1] // 3
    by_q = lambda p: (block_fields(p, rows // block, trunk)[0], 0)
    heads = width // HEAD
    branches = (rows // block - trunk) // 3
    made = [(k, z.shape[1] - at, z.shape[2] // k) for z, at, k in riders]
    once = lambda s: pl.BlockSpec(s, lambda p: (0,) * len(s), pipeline_mode=pl.Buffered(1))
    hbm = pl.BlockSpec(memory_space=pl.ANY)
    out = pl.pallas_call(
        functools.partial(
            attend_back_kernel, width, block, rows // block, trunk, branches, nf, [r[1] for r in riders]
        ),
        grid=(len(pairs),),
        out_shape=[
            jax.ShapeDtypeStruct((rows, 3 * width), jnp.bfloat16),
            jax.ShapeDtypeStruct((1, 3 * width), jnp.float32),
        ]
        + [jax.ShapeDtypeStruct(s, jnp.bfloat16) for s in made],
        in_specs=[pl.BlockSpec(memory_space=pltpu.SMEM), once((rows, 3 * width)), once((width, rows))]
        + [pl.BlockSpec((block, width), by_q)] * 3
        + [hbm] * len(riders),
        out_specs=[once((rows, 3 * width)), once((1, 3 * width))] + [once(s) for s in made],
        scratch_shapes=[
            pltpu.VMEM((rows, width), jnp.float32),
            pltpu.VMEM((rows, width), jnp.float32),
            pltpu.VMEM((width, block), jnp.float32),
            pltpu.VMEM((heads, block, 2 * HEAD), jnp.bfloat16),
        ]
        + sum([PlaneSum.scratch(nf, z.shape[1] - at, z.shape[2]) for z, at, k in riders], []),
        compiler_params=pltpu.CompilerParams(
            dimension_semantics=("arbitrary",),
            vmem_limit_bytes=60 << 20,
            collective_id=ident,
            has_side_effects=True,
        ),
        cost_estimate=SMALL,
        name="attend_back",
    )(values, qkv, kt, datt, att, tot, *[r[0] for r in riders])
    return out[0], out[1], out[2:]


def layer_norm(values, gain, shift):
    centred = values - jnp.mean(values, -1, keepdims=True)
    spread = jnp.mean(centred * centred, -1, keepdims=True)
    return centred * lax.rsqrt(spread + 1e-05) * gain + shift


def contract_rows(left, right):
    return lax.dot_general(
        left, right, (((0,), (0,)), ((), ())), preferred_element_type=jnp.float32
    )


def contract_cols(left, right):
    return lax.dot_general(
        left, right, (((1,), (1,)), ((), ())), preferred_element_type=jnp.float32
    )


def after(value, other):
    return value + (other[(0,) * other.ndim] * 0).astype(value.dtype)


def row_major(x):
    return with_layout_constraint(x, Layout(major_to_minor=tuple(range(x.ndim))))


def local(
    tokens,
    ln1_gain,
    ln1_bias,
    qkv_weight,
    qv_bias,
    out_weight,
    out_bias,
    ln2_gain,
    ln2_bias,
    fc_weight,
    fc_bias,
    proj_weight,
    proj_bias,
    seg_lengths,
    parents,
    cotangent,
):
    n = lax.axis_size("seq")
    nf = lax.axis_size("fsdp")
    s = lax.axis_index("seq")
    f = lax.axis_index("fsdp")
    trunk = n // 4
    block, width = tokens.shape[1], tokens.shape[2]
    rows = width // nf
    hidden = fc_weight.shape[1] * n
    piece = hidden // (n * nf)
    group = n // nf
    wide = 2 * HEAD * (-(-HEADS // (2 * n)))
    low = jnp.bfloat16
    wider = jnp.float32

    vectors = [ln1_gain, ln1_bias, qv_bias, out_bias, ln2_gain, ln2_bias, fc_bias, proj_bias]
    sizes = [v.shape[0] for v in vectors]
    qkv_cols = qkv_weight.shape[1]
    even = qkv_cols % 8 == 0
    forth = Rows(n, qkv_cols, width, wide, False) if even else None
    back = Rows(n, qkv_cols, width, wide, True) if even else None
    turned, proj_blocks, fc_blocks, out_blocks, gathered = exchange(
        qkv_weight.T,
        proj_weight.reshape(n, piece, width // n),
        fc_weight.reshape(rows, nf, piece).transpose(1, 0, 2),
        out_weight,
        [jnp.stack([v for v in vectors if v.shape == ln1_gain.shape])]
        + [v.reshape(1, -1) for v in vectors if v.shape != ln1_gain.shape],
        n,
        nf,
        forth,
        wide,
        0,
    )
    short = iter(jnp.unstack(gathered[0], axis=1))
    long = iter(gathered[1:])
    whole = [next(short) if v.shape == ln1_gain.shape else next(long) for v in vectors]
    whole = [v.reshape(-1).astype(wider) for v in whole]
    gain_one, shift_one, bias_qv, bias_out, gain_two, shift_two, bias_fc, bias_proj = whole
    bias_three = jnp.stack([bias_qv[:width], jnp.zeros((width,), wider), bias_qv[width:]])
    bias_three = jnp.pad(bias_three, ((0, 0), (0, n * wide - width)))
    bias_mine = lax.dynamic_slice_in_dim(bias_three, s * wide, wide, 1).reshape(1, -1)
    bias_hidden = lax.dynamic_index_in_dim(bias_fc.reshape(nf, n, piece), s, 1, False)
    bias_hidden = bias_hidden.reshape(1, -1)

    if even:
        turned = turned.reshape(3, wide, rows)
        kept = lax.broadcasted_iota(jnp.int32, turned.shape, 1) + s * wide < width
        turned = jnp.where(kept, turned, 0).reshape(3 * wide, rows)
    else:
        turned = lax.all_gather(qkv_weight.T, "seq", axis=0, tiled=True).reshape(3, width, rows)
        turned = jnp.pad(turned, ((0, 0), (0, n * wide - width), (0, 0)))
        turned = lax.dynamic_slice_in_dim(turned, s * wide, wide, 1).reshape(3 * wide, rows)
    pairs = block_pairs(n, trunk)
    table = block_values(seg_lengths[0], parents[0], pairs, block)

    resid = tokens[0].astype(wider)
    out_turned = out_blocks.reshape(width, width // n).T
    normed_one, out_turned, qkv_mine = seq_gather(
        layer_norm(resid, gain_one, shift_one).astype(low),
        n,
        1,
        "gather_one",
        rider=(turned.T, True, nf),
        second=out_turned,
    )
    out_turned = out_turned.reshape(width, width)
    qkv_mine = qkv_mine.reshape(width, 3 * wide)
    fc_rows = fc_blocks.transpose(1, 0, 2).reshape(rows, nf * piece)
    fc_mine = lax.all_gather(fc_rows, "fsdp", axis=0, tiled=True)

    upstream = cotangent[0].astype(wider)
    proj_rows = proj_blocks.transpose(1, 0, 2).reshape(piece, width)
    proj_mine = lax.all_gather(after(proj_rows, normed_one), "fsdp", axis=0, tiled=True)
    projected, attended_low, attended, totals, keys_turned, upstream_all = attend(
        table, pairs, normed_one, qkv_mine, bias_mine, block, trunk, cotangent[0], n, 8
    )
    attended_mine = to_tokens(attended_low.reshape(n, block, wide), n, wide, 2)[:, :width]
    middle = resid + contract_cols(attended_mine, out_turned) + bias_out
    normed_two = layer_norm(middle, gain_two, shift_two).astype(low)
    ff = nf * piece

    def expand(value, fc, bias, proj):
        pre = mm(value, fc[...]) + bias[...]
        bend = math.sqrt(2 / math.pi)
        square = pre * pre
        inner = jnp.tanh(pre * (bend + bend * 0.044715 * square))
        half = 0.5 + 0.5 * inner
        act = (pre * half).astype(low)
        slope = half + 0.5 * pre * (1 - inner * inner) * (bend + 3 * bend * 0.044715 * square)
        return act, slope.astype(low), mm(act, proj[...]).astype(low)

    normed_two, hidden_act, hidden_slope, mixed = seq_gather(
        normed_two,
        n,
        3,
        "gather_two",
        expand,
        (fc_mine, bias_hidden, proj_mine),
        ((ff, low), (ff, low), (width, low)),
        modes=(0, 0, 0),
    )

    def shrink(up, slope, proj, fc):
        grad = (nt(up, proj[...]) * slope.astype(wider)).astype(low)
        return nt(grad, fc[...]), grad

    grad_normed_two, grad_pre, grad_proj, unused_sums, mixed = seq_scatter(
        n,
        width,
        4,
        "scatter_two",
        shrink,
        (upstream_all, hidden_slope),
        (proj_mine, fc_mine),
        ((ff, low),),
        side=(hidden_act, upstream_all),
        carry=mixed,
    )
    mixed = lax.psum_scatter(mixed, "seq", scatter_dimension=0, tiled=True)
    grad_proj = grad_proj.reshape(nf, piece, width)
    cut = piece // 16 * 8
    unused_two, norm_two_back = jax.vjp(layer_norm, middle, gain_two, shift_two)
    grad_middle_norm, grad_gain_two, grad_shift_two = norm_two_back(grad_normed_two)
    grad_middle = upstream + grad_middle_norm
    grad_branch = grad_middle.astype(low)
    grad_attended, grad_fc, hidden_sums, proj_first, grad_out = to_heads(
        grad_branch,
        out_turned,
        attended_mine,
        n,
        nf,
        wide,
        5,
        normed_two,
        grad_pre,
        grad_proj,
        cut,
    )
    grad_attended = grad_attended.reshape(n * block, wide)
    grad_projected, column_sums, (fc_part, proj_second) = attend_back(
        table,
        pairs,
        projected,
        keys_turned,
        grad_attended,
        attended,
        totals,
        block,
        trunk,
        nf,
        ((grad_fc.reshape(nf, rows, ff), 0, nf), (grad_proj, cut, n)),
        9,
    )
    grad_qkv, output = contract(
        normed_one, grad_projected, middle, mixed, bias_proj.reshape(1, -1), block
    )
    output = output[None]
    input_grad, grad_gain_one, grad_shift_one, qkv_parts = seq_scatter(
        n,
        width,
        6,
        "scatter_one",
        lambda g, w: (nt(g, w[...]),),
        (grad_projected,),
        (qkv_mine,),
        rider=(grad_qkv.reshape(nf, rows, 3 * wide), False, nf),
        norm=(tokens[0], gain_one.reshape(1, -1), grad_middle, low),
    )
    input_grad = input_grad[None]

    out_part = lax.psum_scatter(grad_out, "seq", scatter_dimension=0, tiled=True).T
    out_part = after(out_part, qkv_parts).reshape(nf, rows, width // n)
    qkv_part = jnp.sum(qkv_parts.astype(wider), 0).astype(low).T

    column_sums = column_sums.reshape(3, wide)
    placed = lax.dynamic_update_slice_in_dim(
        jnp.zeros((3, n * wide), wider), column_sums, s * wide, 1
    )[:, :width]
    grad_qv = jnp.concatenate([placed[0], placed[2]])
    hidden_sums = hidden_sums.reshape(nf, 1, piece)
    grad_fc_bias = lax.dynamic_update_slice_in_dim(
        jnp.zeros((nf, n, piece), wider), hidden_sums, s, 1
    )
    parts = [
        grad_gain_one,
        grad_shift_one,
        grad_qv,
        jnp.sum(grad_branch.astype(wider), 0),
        grad_gain_two,
        grad_shift_two,
        grad_fc_bias,
        jnp.sum(upstream, 0),
    ]
    summed, qkv_out, proj_first, proj_second, fc_out, out_out = give_back(
        jnp.concatenate([p.reshape(nf, -1) for p in parts], 1),
        qkv_part,
        qkv_cols,
        proj_first,
        proj_second,
        fc_part,
        out_part,
        n,
        nf,
        back,
        7,
    )
    if not even:
        qkv_part = qkv_part.reshape(3, wide, rows)
        qkv_out = lax.all_gather(qkv_part, "seq", axis=1, tiled=True)[:, :width]
        qkv_out = qkv_out.reshape(3 * width, rows)
        qkv_out = lax.dynamic_slice_in_dim(qkv_out, s * qkv_cols, qkv_cols, 0)
    out_out = jnp.sum(out_out.astype(wider), 0)
    qkv_out = qkv_out.T.astype(wider)
    proj_out = jnp.concatenate([proj_first, proj_second], 1)
    proj_out = proj_out.reshape(n * piece, width // n).astype(wider)
    fc_out = fc_out.transpose(1, 0, 2).reshape(rows, nf * piece).astype(wider)
    vector_out = []
    at = 0
    for size in sizes:
        vector_out.append(summed[at : at + size])
        at += size
    return (
        output,
        input_grad,
        vector_out[0],
        vector_out[1],
        qkv_out,
        vector_out[2],
        out_out,
        vector_out[3],
        vector_out[4],
        vector_out[5],
        fc_out,
        vector_out[6],
        proj_out,
        vector_out[7],
    )


def solution(mesh):
    in_specs = (
        P("fsdp", "seq", None),
        P("fsdp"),
        P("fsdp"),
        P("fsdp", "seq"),
        P("fsdp"),
        P("fsdp", "seq"),
        P("fsdp"),
        P("fsdp"),
        P("fsdp"),
        P("fsdp", "seq"),
        P("fsdp"),
        P("fsdp", "seq"),
        P("fsdp"),
        P("fsdp", None),
        P("fsdp", None),
        P("fsdp", "seq", None),
    )
    out_specs = (
        P("fsdp", "seq", None),
        P("fsdp", "seq", None),
        P("fsdp"),
        P("fsdp"),
        P("fsdp", "seq"),
        P("fsdp"),
        P("fsdp", "seq"),
        P("fsdp"),
        P("fsdp"),
        P("fsdp"),
        P("fsdp", "seq"),
        P("fsdp"),
        P("fsdp", "seq"),
        P("fsdp"),
    )
    return jax.shard_map(local, mesh=mesh, in_specs=in_specs, out_specs=out_specs, check_vma=False)
```

```python
import functools
import math

import jax
import jax.numpy as jnp
import numpy as np
from jax import lax
from jax.experimental import pallas as pl
from jax.experimental.layout import Layout, with_layout_constraint
from jax.experimental.pallas import tpu as pltpu
from jax.sharding import PartitionSpec as P

MESH = pl.DeviceIdType.MESH
HEADS = 25
SMALL = pl.CostEstimate(flops=0, bytes_accessed=1 << 20, transcendentals=0)


def route_bits(n):
    bits = []
    b = 2
    while b < n:
        bits.append(b)
        b *= 2
    return bits


def flip(a, b):
    return jnp.where(lax.rem(lax.div(a, b), 2) == 0, a + b, a - b)


def place(me, r, n):
    if isinstance(r, int):
        for b in [1] + route_bits(n):
            if r & b:
                me = flip(me, b)
        return me
    for b in [1] + route_bits(n):
        me = jnp.where(lax.rem(lax.div(r, b), 2) == 0, me, flip(me, b))
    return me


def pick(table, q):
    value = jnp.int32(table[0])
    for i, entry in enumerate(table[1:]):
        value = jnp.where(q == i + 1, jnp.int32(entry), value)
    return value


def greet(ids):
    barrier = pltpu.get_barrier_semaphore()
    for i in ids:
        pl.semaphore_signal(barrier, inc=1, device_id=i, device_id_type=MESH)
    pl.semaphore_wait(barrier, len(ids))


def remote(src, dst, send, recv, device):
    return pltpu.make_async_remote_copy(
        src_ref=src, dst_ref=dst, send_sem=send, recv_sem=recv, device_id=device, device_id_type=MESH
    )


class Blocks:
    def __init__(self, axis, size, same, source, target, send, recv, local):
        self.axis, self.size, self.same = axis, size, same
        self.source, self.target = source, target
        self.send, self.recv, self.local = send, recv, local
        self.me = lax.axis_index(axis)

    @staticmethod
    def scratch(size):
        dma = pltpu.SemaphoreType.DMA
        return [dma((size - 1,)), dma((size - 1,)), dma]

    def peers(self):
        return [{self.axis: lax.rem(self.me + d, self.size)} for d in range(1, self.size)]

    def copy(self, d):
        to = lax.rem(self.me + d, self.size)
        src = self.source if self.same else self.source.at[to]
        return remote(src, self.target.at[self.me], self.send.at[d - 1], self.recv.at[d - 1], {self.axis: to})

    def own(self):
        src = self.source if self.same else self.source.at[self.me]
        return pltpu.make_async_copy(src, self.target.at[self.me], self.local)

    def start(self):
        for d in range(1, self.size):
            self.copy(d).start()
        self.own().start()

    def finish(self):
        for d in range(1, self.size):
            dst = self.target.at[lax.rem(self.me + self.size - d, self.size)]
            remote(dst, dst, self.send.at[d - 1], self.recv.at[d - 1], {self.axis: self.me}).wait_recv()
        self.own().wait()
        for d in range(1, self.size):
            self.copy(d).wait_send()


class Spread:
    def __init__(self, n, source, target, send, recv, local):
        self.n, self.source, self.target = n, source, target
        self.send, self.recv, self.local = send, recv, local
        self.me = lax.axis_index("seq")
        self.bits = route_bits(n)
        self.orders = [self.bits, self.bits[::-1]]
        self.h = source.shape[0] // 2

    @staticmethod
    def scratch(n):
        dma = pltpu.SemaphoreType.DMA
        return [dma((2, len(route_bits(n)) + 1, n)), dma((2, n)), dma]

    def device(self, b):
        return {"seq": flip(self.me, b)}

    def peers(self):
        return [self.device(b) for b in [1] + self.bits]

    def rows(self, half):
        return pl.ds(half * self.h, self.h)

    def ship(self, half, k, b):
        owner = place(self.me, k, self.n)
        src = self.source if k == 0 else self.target.at[owner]
        lane = 0 if b == 1 else 1 + self.bits.index(b)
        return remote(
            src.at[self.rows(half)],
            self.target.at[owner].at[self.rows(half)],
            self.send.at[half, lane, k],
            self.recv.at[half, k ^ b],
            self.device(b),
        )

    def arrive(self, half, k):
        dst = self.target.at[place(self.me, k, self.n)].at[self.rows(half)]
        remote(dst, dst, self.send.at[half, 0, 0], self.recv.at[half, k], self.device(1)).wait_recv()

    def own(self):
        return pltpu.make_async_copy(self.source, self.target.at[self.me], self.local)

    def fresh(self, half, i):
        had = [0]
        for b in self.orders[half][:i]:
            had = had + [k ^ b for k in had]
        return [k ^ self.orders[half][i] for k in had]

    def start(self):
        for i in range(len(self.bits)):
            for half in (0, 1):
                self.ship(half, 0, self.orders[half][i]).start()
        for half in (0, 1):
            self.ship(half, 0, 1).start()
        self.own().start()

    def phase(self, i):
        for half in (0, 1):
            for k in self.fresh(half, i):
                self.arrive(half, k)
                for b in self.orders[half][i + 1 :] + [1]:
                    self.ship(half, k, b).start()

    def finish(self):
        for half in (0, 1):
            for k in range(1, self.n, 2):
                self.arrive(half, k)
        self.own().wait()
        for half in (0, 1):
            for b in self.orders[half] + [1]:
                self.ship(half, 0, b).wait_send()
            for i in range(len(self.bits)):
                for k in self.fresh(half, i):
                    for b in self.orders[half][i + 1 :] + [1]:
                        self.ship(half, k, b).wait_send()


class PlaneSum(Blocks):
    def __init__(self, size, source, low, target, send, recv, local):
        super().__init__("fsdp", size, False, source, target, send, recv, local)
        self.window = pl.ds(low, target.shape[1])

    @staticmethod
    def scratch(size, rows, cols):
        return [pltpu.VMEM((size, rows, cols), jnp.bfloat16)] + Blocks.scratch(size)

    def copy(self, d):
        to = lax.rem(self.me + d, self.size)
        src = self.source.at[to].at[self.window]
        return remote(src, self.target.at[self.me], self.send.at[d - 1], self.recv.at[d - 1], {self.axis: to})

    def own(self):
        src = self.source.at[self.me].at[self.window]
        return pltpu.make_async_copy(src, self.target.at[self.me], self.local)

    def store(self, out):
        total = self.target[0].astype(jnp.float32)
        for i in range(1, self.size):
            total = total + self.target[i].astype(jnp.float32)
        cols = out.shape[2]
        for i in range(out.shape[0]):
            out[i] = total[:, i * cols : (i + 1) * cols].astype(out.dtype)


def blocks_shape(x, size, same):
    return jax.ShapeDtypeStruct(((size,) + x.shape) if same else x.shape, x.dtype)


def arrival_order(n):
    bits = route_bits(n)
    orders = [bits, bits[::-1]]
    lists = []
    for order in orders:
        held, phases = [0], [-1]
        for i, b in enumerate(order):
            fresh = [h ^ b for h in held]
            held, phases = held + fresh, phases + [i] * len(fresh)
        lists.append(list(zip(held, phases)))
    entries = []
    for i in range(n // 2):
        for odd in (0, 1):
            for half in (0, 1):
                k, phase = lists[half][i]
                entries.append((half, k ^ odd, phase, odd))
    return orders, entries


def gather_kernel(n, h, body, n_const, n_out, relative, modes, nf, same, second, *refs):
    if second:
        at = 1 + n_const
        out = at + 1 + min(nf, 1) + 1 + n_out
        w_ref, w_all = refs[at], refs[out]
        w_send, w_recv, w_keep = refs[-3:]
        refs = refs[:at] + refs[at + 1 : out] + refs[out + 1 : -3]
        w_half = w_ref.shape[1] // 256 * 128
        w_lanes = [pl.ds(0, w_half), pl.ds(w_half, w_ref.shape[1] - w_half)]
    refs, rider = split_rider(refs, nf, same, 1 + n_const, 1 + n_out)
    x_ref = refs[0]
    consts = refs[1 : 1 + n_const]
    all_ref = refs[1 + n_const]
    outs = refs[2 + n_const : 2 + n_const + n_out]
    held = refs[2 + n_const + n_out]
    stages = refs[3 + n_const + n_out : 3 + n_const + 2 * n_out]
    send, recv, keep, store = refs[3 + n_const + 2 * n_out :]
    me = lax.axis_index("seq")
    orders, entries = arrival_order(n)
    bits = orders[0]
    nb = len(bits)

    def device(b):
        return {"seq": flip(me, b)}

    def spot(half, k):
        return 2 * (k if relative else place(me, k, n)) + half

    def ship(half, k, b):
        at = spot(half, k)
        src = x_ref.at[pl.ds(half * h, h)] if isinstance(k, int) and k == 0 else held.at[at]
        lane = 0 if b == 1 else 1 + bits.index(b)
        to = k ^ b if isinstance(k, int) else place(k, b, n)
        dst = 2 * to + half if relative else at
        first = remote(src, held.at[dst], send.at[half, lane, k], recv.at[half, to], device(b))
        if not second:
            return [first]
        owner = place(me, k, n)
        lanes = w_lanes[half]
        src = w_ref if isinstance(k, int) and k == 0 else w_all.at[owner]
        other = remote(
            src.at[:, lanes], w_all.at[owner].at[:, lanes], w_send.at[half, lane, k], w_recv.at[half, to], device(b)
        )
        return [first, other]

    def each(copies, act):
        for c in copies:
            act(c)

    def w_arrive(half, k):
        dst = w_all.at[place(me, k, n)].at[:, w_lanes[half]]
        remote(dst, dst, w_send.at[0, 0, 0], w_recv.at[half, k], device(1)).wait_recv()

    greet([device(b) for b in [1] + bits] + (rider.peers() if nf else []))
    for i in range(nb):
        for half in (0, 1):
            each(ship(half, 0, orders[half][i]), lambda c: c.start())
    for half in (0, 1):
        each(ship(half, 0, 1), lambda c: c.start())
    if second:
        pltpu.make_async_copy(w_ref, w_all.at[me], w_keep).start()
    if nf:
        rider.start()

    def output(o, q, at):
        slot = lax.rem(q, 2)
        return pltpu.make_async_copy(stages[o].at[slot], outs[o].at[at], store.at[o, slot])

    def entry(q, at, value):
        results = body(value, *consts)
        for o in range(n_out):

            @pl.when(q >= 2)
            def _(o=o):
                output(o, q, at[modes[o]]).wait()

            stages[o][lax.rem(q, 2)] = results[o]
            output(o, q, at[modes[o]]).start()

    def step(q, carry):
        half = pick([e[0] for e in entries], q)
        k = pick([e[1] for e in entries], q)
        phase = pick([e[2] for e in entries], q)
        odd = pick([e[3] for e in entries], q)
        at = spot(half, k)

        @pl.when(k == 0)
        def _():
            held[at] = x_ref[pl.ds(pl.multiple_of(half * h, h), h)]

        @pl.when(k != 0)
        def _():
            remote(held.at[at], held.at[at], send.at[0, 0, 0], recv.at[half, k], device(1)).wait_recv()

        for side in (0, 1) if second else ():

            @pl.when((k != 0) & (half == side))
            def _(side=side):
                w_arrive(side, k)

        for side in (0, 1):
            for i in range(nb):

                @pl.when((half == side) & (odd == 0) & (k != 0) & (phase < i))
                def _(side=side, i=i):
                    each(ship(side, k, orders[side][i]), lambda c: c.start())

            @pl.when((half == side) & (odd == 0) & (k != 0))
            def _(side=side):
                each(ship(side, k, 1), lambda c: c.start())

        pltpu.make_async_copy(held.at[at], all_ref.at[at], keep.at[q]).start()
        if n_out:
            entry(q, (2 * place(me, k, n) + half, 2 * k + half), held[at])
        return carry

    lax.fori_loop(0, 2 * n, step, 0)
    for q, (half, k, phase, odd) in enumerate(entries):
        at = spot(half, k)
        pltpu.make_async_copy(held.at[at], all_ref.at[at], keep.at[q]).wait()
        if q >= 2 * n - 2:
            for o in range(n_out):
                output(o, jnp.int32(q), at).wait()
        if not odd:
            for i in range(nb):
                if phase < i:
                    each(ship(half, k, orders[half][i]), lambda c: c.wait_send())
            each(ship(half, k, 1), lambda c: c.wait_send())
    if second:
        pltpu.make_async_copy(w_ref, w_all.at[me], w_keep).wait()
    if nf:
        rider.finish()


def split_rider(refs, nf, same, n_in, n_out):
    if not nf:
        return refs, None
    source = refs[n_in]
    target = refs[n_in + 1 + n_out]
    rider = Blocks("fsdp", nf, same, source, target, *refs[-3:])
    return refs[:n_in] + refs[n_in + 1 : n_in + 1 + n_out] + refs[n_in + 2 + n_out : -3], rider


def rider_parts(rider):
    if rider is None:
        return [], [], [], [], 0, False
    x, same, nf = rider
    hbm = [pl.BlockSpec(memory_space=pl.ANY)]
    return [x], hbm, [blocks_shape(x, nf, same)], Blocks.scratch(nf), nf, same


def seq_gather(x, n, ident, name, body=None, consts=(), outs=(), relative=False, modes=None, rider=None, second=None):
    rows, cols = x.shape
    h = rows // 2
    nb = len(route_bits(n))
    shapes = [jax.ShapeDtypeStruct((2 * n, h, c), d) for c, d in outs]
    vmem = pl.BlockSpec(memory_space=pltpu.VMEM)
    hbm = pl.BlockSpec(memory_space=pl.ANY)
    more, spec, shape, scratch, nf, same = rider_parts(rider)
    also = [] if second is None else [second]
    out = pl.pallas_call(
        functools.partial(
            gather_kernel, n, h, body, len(consts), len(outs), relative, modes, nf, same, second is not None
        ),
        out_shape=[jax.ShapeDtypeStruct((2 * n, h, cols), x.dtype)]
        + shapes
        + [jax.ShapeDtypeStruct((n,) + w.shape, w.dtype) for w in also]
        + shape,
        in_specs=[vmem] * (1 + len(consts)) + [hbm] * len(also) + spec,
        out_specs=[hbm] * (1 + len(outs)) + [hbm] * len(also) + spec,
        scratch_shapes=[pltpu.VMEM((2 * n, h, cols), x.dtype)]
        + [pltpu.VMEM((2, h, c), d) for c, d in outs]
        + [
            pltpu.SemaphoreType.DMA((2, nb + 1, n)),
            pltpu.SemaphoreType.DMA((2, n)),
            pltpu.SemaphoreType.DMA((2 * n,)),
            pltpu.SemaphoreType.DMA((max(len(outs), 1), 2)),
        ]
        + scratch
        + [
            pltpu.SemaphoreType.DMA((2, nb + 1, n)),
            pltpu.SemaphoreType.DMA((2, n)),
            pltpu.SemaphoreType.DMA,
        ]
        * len(also),
        compiler_params=pltpu.CompilerParams(
            collective_id=ident, has_side_effects=True, vmem_limit_bytes=60 << 20
        ),
        cost_estimate=SMALL,
        name=name,
    )(x, *consts, *also, *more)
    return [o.reshape(2 * n * h, o.shape[2]) for o in out[: 1 + len(outs)]] + list(out[1 + len(outs) :])


class Side:
    def __init__(self, count, refs):
        self.count = count
        self.a, self.b, self.grad, self.sums, self.acc, self.abuf, self.bbuf, self.load = refs

    def fetch(self, i):
        slot = lax.rem(i, 2)
        return [
            pltpu.make_async_copy(self.a.at[i], self.abuf.at[slot], self.load.at[0, slot]),
            pltpu.make_async_copy(self.b.at[i], self.bbuf.at[slot], self.load.at[1, slot]),
        ]

    def begin(self):
        self.acc[...] = jnp.zeros_like(self.acc)
        self.sums[...] = jnp.zeros_like(self.sums)
        for c in self.fetch(jnp.int32(0)):
            c.start()

    def run(self, first, last):
        def step(i, carry):
            @pl.when(i + 1 < self.count)
            def _():
                for c in self.fetch(i + 1):
                    c.start()

            for c in self.fetch(i):
                c.wait()
            slot = lax.rem(i, 2)
            a, b = self.abuf[slot], self.bbuf[slot]
            self.acc[...] += lax.dot_general(
                a, b, (((0,), (0,)), ((), ())), preferred_element_type=jnp.float32
            )
            self.sums[...] += jnp.sum(b.astype(jnp.float32), 0, keepdims=True)
            return carry

        lax.fori_loop(first, last, step, 0)

    def end(self):
        self.grad[...] = self.acc[...].astype(self.grad.dtype)


def side_parts(side, count):
    if side is None:
        return [], [], [], [], []
    a, b = side
    h = a.shape[0] // count
    low = jnp.bfloat16
    hbm = pl.BlockSpec(memory_space=pl.ANY)
    vmem = pl.BlockSpec(memory_space=pltpu.VMEM)
    return (
        [x.reshape(count, h, x.shape[1]) for x in (a, b)],
        [
            jax.ShapeDtypeStruct((a.shape[1], b.shape[1]), low),
            jax.ShapeDtypeStruct((1, b.shape[1]), jnp.float32),
        ],
        [hbm, hbm],
        [vmem, vmem],
        [
            pltpu.VMEM((a.shape[1], b.shape[1]), jnp.float32),
            pltpu.VMEM((2, h, a.shape[1]), low),
            pltpu.VMEM((2, h, b.shape[1]), low),
            pltpu.SemaphoreType.DMA((2, 2)),
        ],
    )


def scatter_order(n):
    bits = route_bits(n)
    orders = [bits, bits[::-1]]
    lists = [
        sorted(range(0, n, 2), key=lambda k: [-int(bool(k & b)) for b in order]) for order in orders
    ]
    return orders, [(half, lists[half][i]) for i in range(n // 2) for half in (0, 1)]


def scatter_kernel(n, h, body, n_in, n_const, n_out, modes, nf, same, has_side, has_norm, carried, *refs):
    if carried:
        out = 1 + n_in + n_const + 2 * has_side + min(nf, 1) + 1 + n_out + 2 * has_side + min(nf, 1)
        refs = refs[1:out] + refs[out + 1 :]
    if has_norm:
        out = n_in + 3 + n_const + 2 * has_side + min(nf, 1)
        values, gain, joins = refs[:3]
        x_grad, g_grad, b_grad = refs[out], refs[out + 1], refs[out + 2]
        refs = refs[3:out] + (None,) + refs[out + 3 :]
    side = None
    if has_side:
        at = n_in + n_const
        out = at + 2 + min(nf, 1) + 1 + n_out
        extra = refs[at : at + 2] + refs[out : out + 2] + refs[-4:]
        refs = refs[:at] + refs[at + 2 : out] + refs[out + 2 : -4]
        side = Side(2 * n, extra)
    refs, rider = split_rider(refs, nf, same, n_in + n_const, 1 + n_out)
    ins = refs[:n_in]
    consts = refs[n_in : n_in + n_const]
    at = n_in + n_const
    sum_ref = refs[at]
    outs = refs[at + 1 : at + 1 + n_out]
    at += 1 + n_out
    give, pair, own, far, total = refs[at : at + 5]
    at += 5
    loads = refs[at : at + n_in]
    stages = refs[at + n_in : at + n_in + n_out]
    pair_send, pair_recv, far_send, far_recv, load, store, done = refs[at + n_in + n_out :]
    me = lax.axis_index("seq")
    orders, entries = scatter_order(n)
    bits = orders[0]
    slots = give.shape[0]
    index = {e: j for j, e in enumerate(entries)}

    def device(b):
        return {"seq": flip(me, b)}

    def phase_of(half, k):
        for i, b in enumerate(orders[half]):
            if k & b:
                return i
        return len(bits)

    landing = {}
    for half in (0, 1):
        for i, b in enumerate(orders[half]):
            for k in range(0, n, 2):
                if phase_of(half, k) == i:
                    landing[half, i, k ^ b] = len(landing)

    halves = [e[0] for e in entries]
    ks = [e[1] for e in entries]

    def spot(q, relative):
        j = lax.div(q, 2)
        k = pick(ks, j)
        k = jnp.where(lax.rem(q, 2) == 0, flip(k, 1), k)
        return 2 * (k if relative else place(me, k, n)) + pick(halves, j)

    def fetch(q):
        slot = lax.rem(q, 2)
        return [
            pltpu.make_async_copy(ins[i].at[spot(q, modes[0][i])], loads[i].at[slot], load.at[i, slot])
            for i in range(n_in)
        ]

    def output(o, q):
        slot = lax.rem(q, 2)
        return pltpu.make_async_copy(stages[o].at[slot], outs[o].at[spot(q, modes[1][o])], store.at[o, slot])

    def hand(j):
        slot = lax.rem(j, slots)
        return remote(give.at[slot], pair.at[j], pair_send.at[j], pair_recv.at[j], device(1))

    def launch(half, k):
        i = phase_of(half, k)
        b = orders[half][i]
        to = landing[half, i, k ^ b]
        return remote(own.at[index[half, k]], far.at[to], far_send.at[to], far_recv.at[to], device(b))

    def join(j):
        hand(j).wait_recv()
        own[j] = (own[j].astype(jnp.float32) + pair[j].astype(jnp.float32)).astype(own.dtype)
        for e, (half, k) in enumerate(entries):
            if phase_of(half, k) == 0:

                @pl.when(j == e)
                def _(half=half, k=k):
                    launch(half, k).start()

    for c in fetch(jnp.int32(0)):
        c.start()
    greet([device(b) for b in [1] + bits] + (rider.peers() if nf else []))
    if nf:
        rider.start()

    def step(q, carry):
        j = lax.div(q, 2)
        slot = lax.rem(q, 2)

        @pl.when(q + 1 < 2 * n)
        def _():
            for c in fetch(q + 1):
                c.start()

        for c in fetch(q):
            c.wait()
        part, *results = body(*[r[slot] for r in loads], *consts)
        for o in range(n_out):

            @pl.when(q >= 2)
            def _(o=o):
                output(o, q).wait()

            stages[o][slot] = results[o]
            output(o, q).start()

        @pl.when(slot == 0)
        def _():
            @pl.when(j >= slots)
            def _():
                hand(j - slots).wait_send()

            give[lax.rem(j, slots)] = part.astype(give.dtype)
            hand(j).start()

        @pl.when(slot == 1)
        def _():
            own[j] = part.astype(own.dtype)

            @pl.when(j >= 1)
            def _():
                join(j - 1)

        return carry

    lax.fori_loop(0, 2 * n, step, 0)
    if side:
        side.begin()
    join(jnp.int32(n - 1))
    first = n // 2
    cuts = [0, first] + [first + (2 * n - first) * i // (len(bits) - 1) for i in range(1, len(bits))]
    for i in range(len(bits)):
        if side:
            side.run(cuts[i], cuts[i + 1])
        for half in (0, 1):
            order = orders[half]
            for k in [k for hh, k in entries if hh == half and phase_of(half, k) > i]:
                to = landing[half, i, k]
                remote(far.at[to], far.at[to], far_send.at[to], far_recv.at[to], device(1)).wait_recv()
                j = index[half, k]
                rows = pl.ds(half * h, h)
                if i == len(bits) - 1:
                    total[rows] = own[j].astype(jnp.float32) + far[to].astype(jnp.float32)
                    if not has_norm:
                        pltpu.make_async_copy(total.at[rows], sum_ref.at[rows], done.at[half]).start()
                else:
                    own[j] = (own[j].astype(jnp.float32) + far[to].astype(jnp.float32)).astype(own.dtype)
                    if phase_of(half, k) == i + 1:
                        launch(half, k).start()
    if has_norm:
        g_grad[...] = jnp.zeros_like(g_grad)
        b_grad[...] = jnp.zeros_like(b_grad)

        def tile(i, carry):
            rows = pl.ds(pl.multiple_of(i * 64, 64), 64)
            x = values[rows].astype(jnp.float32)
            centred = x - jnp.mean(x, -1, keepdims=True)
            scale = lax.rsqrt(jnp.mean(centred * centred, -1, keepdims=True) + 1e-05)
            xhat = centred * scale
            grad = total[rows]
            g_grad[...] += jnp.sum(grad * xhat, 0, keepdims=True)
            b_grad[...] += jnp.sum(grad, 0, keepdims=True)
            e = gain[...] * grad
            inner = e - jnp.mean(e, -1, keepdims=True) - xhat * jnp.mean(e * xhat, -1, keepdims=True)
            x_grad[rows] = (joins[rows].astype(jnp.float32) + scale * inner).astype(x_grad.dtype)
            return carry

        lax.fori_loop(0, 2 * h // 64, tile, 0)
    for half in (0, 1) if not has_norm else ():
        rows = pl.ds(half * h, h)
        pltpu.make_async_copy(total.at[rows], sum_ref.at[rows], done.at[half]).wait()
    for q in (2 * n - 2, 2 * n - 1):
        for o in range(n_out):
            output(o, jnp.int32(q)).wait()
    for j in range(max(n - slots, 0), n):
        hand(jnp.int32(j)).wait_send()
    for half, k in entries:
        if phase_of(half, k) < len(bits):
            launch(half, k).wait_send()
    if nf:
        rider.finish()
    if side:
        side.end()


def seq_scatter(n, cols, ident, name, body, ins, consts, outs=(), modes=None, rider=None, side=None, norm=None, carry=None):
    h = ins[0].shape[0] // (2 * n)
    low = jnp.bfloat16
    slots = min(4, n)
    split = [a.reshape(2 * n, h, a.shape[1]) for a in ins]
    vmem = pl.BlockSpec(memory_space=pltpu.VMEM)
    hbm = pl.BlockSpec(memory_space=pl.ANY)
    reach = n - 2
    modes = modes or ([0] * len(ins), [0] * len(outs))
    more, spec, shape, scratch, nf, same = rider_parts(rider)
    s_ins, s_shapes, s_in_specs, s_out_specs, s_scratch = side_parts(side, 2 * n)
    sums = [jax.ShapeDtypeStruct((2 * h, cols), jnp.float32)]
    norms = []
    carries = [] if carry is None else [carry]
    if norm is not None:
        norms = list(norm[:3])
        line = jax.ShapeDtypeStruct((1, cols), jnp.float32)
        sums = [jax.ShapeDtypeStruct((2 * h, cols), norm[3]), line, line]
    out = pl.pallas_call(
        functools.partial(
            scatter_kernel, n, h, body, len(ins), len(consts), len(outs), modes, nf, same, int(side is not None), norm is not None, carry is not None
        ),
        out_shape=sums
        + [jax.ShapeDtypeStruct((2 * n, h, c), d) for c, d in outs]
        + s_shapes
        + shape
        + [jax.ShapeDtypeStruct(x.shape, x.dtype) for x in carries],
        in_specs=[hbm] * len(carries)
        + [vmem] * len(norms)
        + [hbm] * len(ins)
        + [vmem] * len(consts)
        + s_in_specs
        + spec,
        out_specs=([vmem] * 3 if norms else [hbm])
        + [hbm] * len(outs)
        + s_out_specs
        + spec
        + [hbm] * len(carries),
        input_output_aliases={0: len(sums + list(outs) + s_shapes + shape)} if carries else {},
        scratch_shapes=[
            pltpu.VMEM((slots, h, cols), low),
            pltpu.VMEM((n, h, cols), low),
            pltpu.VMEM((n, h, cols), low),
            pltpu.VMEM((reach, h, cols), low),
            pltpu.VMEM((2 * h, cols), jnp.float32),
        ]
        + [pltpu.VMEM((2, h, a.shape[2]), a.dtype) for a in split]
        + [pltpu.VMEM((2, h, c), d) for c, d in outs]
        + [
            pltpu.SemaphoreType.DMA((n,)),
            pltpu.SemaphoreType.DMA((n,)),
            pltpu.SemaphoreType.DMA((reach,)),
            pltpu.SemaphoreType.DMA((reach,)),
            pltpu.SemaphoreType.DMA((len(ins), 2)),
            pltpu.SemaphoreType.DMA((max(len(outs), 1), 2)),
            pltpu.SemaphoreType.DMA((2,)),
        ]
        + scratch
        + s_scratch,
        compiler_params=pltpu.CompilerParams(
            collective_id=ident, has_side_effects=True, vmem_limit_bytes=60 << 20
        ),
        cost_estimate=SMALL,
        name=name,
    )(*carries, *norms, *split, *consts, *s_ins, *more)
    lines = list(out[1:3]) if norms else []
    out = [out[0]] + list(out[1 + len(lines) :])
    many = 1 + len(outs)
    sides = [] if side is None else list(out[many : many + 2])
    more = list(out[many + len(sides) :])
    return [out[0]] + lines + [o.reshape(2 * n * h, o.shape[2]) for o in out[1:many]] + sides + more


class Rows:
    def __init__(self, n, held, width, wide, back):
        moves = []
        for to in range(n):
            for third in range(3):
                at, end = third * width + to * wide, third * width + min((to + 1) * wide, width)
                row = third * wide
                while at < end:
                    source = at // held
                    count = min(end, (source + 1) * held) - at
                    moves.append((source, at - source * held, to, row, count))
                    at, row = at + count, row + count
        self.n = n
        self.moves = [(c, d, a, b, e) if back else (a, b, c, d, e) for a, b, c, d, e in moves]
        self.out = [[m for m in self.moves if m[0] == i] for i in range(n)]
        self.into = [[m for m in self.moves if m[2] == i] for i in range(n)]
        self.most = max(len(v) for v in self.out + self.into)

    def scratch(self):
        dma = pltpu.SemaphoreType.DMA
        return [dma((self.most,)), dma((self.most,)), dma((self.most,))]

    def bind(self, source, target, send, recv, local):
        self.source, self.target, self.send, self.recv, self.local = source, target, send, recv, local
        return self

    def copy(self, i, m):
        src = self.source.at[pl.ds(m[1], m[4])]
        dst = self.target.at[pl.ds(m[3], m[4])]
        if m[0] == m[2]:
            return pltpu.make_async_copy(src, dst, self.local.at[i])
        return remote(src, dst, self.send.at[i], self.recv.at[self.into[m[2]].index(m)], {"seq": m[2]})

    def start(self):
        me = lax.axis_index("seq")
        for s in range(self.n):

            @pl.when(me == s)
            def _(s=s):
                for i, m in enumerate(self.out[s]):
                    self.copy(i, m).start()

    def finish(self):
        me = lax.axis_index("seq")
        for s in range(self.n):

            @pl.when(me == s)
            def _(s=s):
                for i, m in enumerate(self.into[s]):
                    if m[0] != s:
                        dst = self.target.at[pl.ds(m[3], m[4])]
                        remote(dst, dst, self.send.at[0], self.recv.at[i], {"seq": s}).wait_recv()
                for i, m in enumerate(self.out[s]):
                    if m[0] == m[2]:
                        self.copy(i, m).wait()
                    else:
                        self.copy(i, m).wait_send()


class Units:
    def __init__(self, n, nf, back, source, target, send, recv, local):
        self.n, self.nf, self.back = n, nf, back
        self.source, self.target, self.send, self.recv, self.local = source, target, send, recv, local
        self.me = lax.axis_index("seq")

    @staticmethod
    def scratch(nf):
        dma = pltpu.SemaphoreType.DMA
        return [dma((nf,)), dma((nf,)), dma]

    def ends(self, i):
        group = self.n // self.nf
        if self.back:
            return i * group + lax.div(self.me, self.nf), lax.rem(self.me, self.nf)
        return lax.rem(self.me, group) * self.nf + i, lax.div(self.me, group)

    def comes(self, i):
        group = self.n // self.nf
        if self.back:
            return lax.rem(self.me, group) * self.nf + i
        return i * group + lax.div(self.me, self.nf)

    def each(self, i, there, here):
        to, slot = self.ends(i)

        @pl.when(to != self.me)
        def _():
            there(remote(self.source.at[i], self.target.at[slot], self.send.at[i], self.recv.at[slot], {"seq": to}))

        @pl.when(to == self.me)
        def _():
            here(pltpu.make_async_copy(self.source.at[i], self.target.at[slot], self.local))

    def start(self):
        for i in range(self.nf):
            self.each(i, lambda c: c.start(), lambda c: c.start())

    def finish(self):
        for i in range(self.nf):
            source = self.comes(i)

            @pl.when(source != self.me)
            def _(i=i):
                dst = self.target.at[i]
                remote(dst, dst, self.send.at[0], self.recv.at[i], {"seq": self.me}).wait_recv()

        for i in range(self.nf):
            self.each(i, lambda c: c.wait_send(), lambda c: c.wait())


def all_peers(n, nf):
    me, f = lax.axis_index("seq"), lax.axis_index("fsdp")
    return [{"seq": place(me, r, n)} for r in range(1, n)] + [
        {"fsdp": lax.rem(f + d, nf)} for d in range(1, nf)
    ]


def exchange_kernel(n, nf, rows, count, *refs):
    ins, outs, sems = refs[: 4 + count], refs[4 + count : 8 + 2 * count], list(refs[8 + 2 * count :])
    take = lambda k: [sems.pop(0) for _ in range(k)]
    parts = []
    if rows is not None:
        parts.append(rows.bind(ins[0], outs[0], *take(3)))
    vectors = [Blocks("fsdp", nf, True, ins[4 + i], outs[4 + i], *take(3)) for i in range(count)]
    later = [
        Blocks("fsdp", nf, True, ins[3], outs[3], *take(3)),
        Units(n, nf, False, ins[2], outs[2], *take(3)),
        Blocks("seq", n, False, ins[1], outs[1], *take(3)),
    ]
    parts = vectors + parts + later
    greet(all_peers(n, nf))
    for p in parts:
        p.start()
    for p in parts:
        p.finish()


def exchange(w, p, c, o, vectors, n, nf, rows, wide, ident):
    hbm = pl.BlockSpec(memory_space=pl.ANY)
    count = len(vectors)
    out = pl.pallas_call(
        functools.partial(exchange_kernel, n, nf, rows, count),
        out_shape=[
            jax.ShapeDtypeStruct((3 * wide, w.shape[1]) if rows is not None else w.shape, w.dtype),
            blocks_shape(p, n, False),
            blocks_shape(c, nf, False),
            blocks_shape(o, nf, True),
        ]
        + [blocks_shape(v, nf, True) for v in vectors],
        in_specs=[hbm] * (4 + count),
        out_specs=[hbm] * (4 + count),
        scratch_shapes=(rows.scratch() if rows is not None else [])
        + sum([Blocks.scratch(nf) for _ in vectors], [])
        + Blocks.scratch(nf)
        + Units.scratch(nf)
        + Blocks.scratch(n),
        compiler_params=pltpu.CompilerParams(collective_id=ident, has_side_effects=True),
        cost_estimate=SMALL,
        name="exchange",
    )(w, p, c, o, *vectors)
    return out[0], out[1], out[2], out[3], out[4:]


def to_tokens_kernel(n, wide, x_ref, o_ref, send, recv, local):
    me = lax.axis_index("seq")

    def target(i):
        return o_ref.at[:, pl.ds(pl.multiple_of(i * wide, 128), wide)]

    greet([{"seq": place(me, r, n)} for r in range(1, n)])
    copies = []
    for r in range(n - 1, 0, -1):
        to = place(me, r, n)
        c = remote(x_ref.at[to], target(me), send.at[r - 1], recv.at[r - 1], {"seq": to})
        c.start()
        copies.append(c)
    mine = pltpu.make_async_copy(x_ref.at[me], target(me), local)
    mine.start()
    for r in range(1, n):
        dst = target(place(me, r, n))
        remote(dst, dst, send.at[0], recv.at[r - 1], {"seq": place(me, r, n)}).wait_recv()
    mine.wait()
    for c in copies:
        c.wait_send()


def to_tokens(x, n, wide, ident):
    rows = x.shape[1]
    hbm = pl.BlockSpec(memory_space=pl.ANY)
    return pl.pallas_call(
        functools.partial(to_tokens_kernel, n, wide),
        out_shape=jax.ShapeDtypeStruct((rows, n * wide), x.dtype),
        in_specs=[hbm],
        out_specs=hbm,
        scratch_shapes=Blocks.scratch(n),
        compiler_params=pltpu.CompilerParams(collective_id=ident, has_side_effects=True),
        cost_estimate=SMALL,
        name="to_tokens",
    )(x)


def to_heads_kernel(
    n, nf, wide, carried, x_ref, w_ref, t_ref, a_ref, b_ref, z_ref, o_ref, g_ref, m_ref, z_out, t_out, handed, made, *extra
):
    me = lax.axis_index("seq")
    send, recv, local = extra[:3]
    side = Side(2 * n, (a_ref, b_ref, g_ref, m_ref) + extra[3:7])
    planes = PlaneSum(nf, z_ref, 0, *extra[7:])
    side.begin()
    greet([{"seq": place(me, r, n)} for r in range(1, n)] + planes.peers())
    planes.start()

    def copy(r):
        to = place(me, r, n)
        return remote(made.at[r], o_ref.at[me], send.at[r - 1], recv.at[r - 1], {"seq": to})

    def mine():
        return pltpu.make_async_copy(made.at[0], o_ref.at[me], local)

    def step(i, carry):
        r = n - 1 - i
        at = place(me, r, n)
        whole, rest = w_ref.shape[1] // wide, w_ref.shape[1] % wide

        @pl.when(at < whole)
        def _():
            lanes = pl.ds(pl.multiple_of(at * wide, 128), wide)
            made[r] = mm(x_ref[...], w_ref[:, lanes]).astype(made.dtype)

        @pl.when(at >= whole)
        def _():
            made[r] = jnp.zeros(made.shape[1:], made.dtype)

        if rest:

            @pl.when(at == whole)
            def _():
                made[r, :, :rest] = mm(x_ref[...], w_ref[:, whole * wide :]).astype(made.dtype)

        @pl.when(r > 0)
        def _():
            copy(r).start()

        return carry

    lax.fori_loop(0, n, step, 0)
    mine().start()
    side.run(0, 2 * n)
    cols = t_out.shape[0]
    for at in range(0, cols, 512):
        end = min(at + 512, cols)
        t_out[at:end] = lax.dot_general(
            x_ref[:, at:end], t_ref[...], (((0,), (0,)), ((), ())), preferred_element_type=jnp.float32
        ).astype(t_out.dtype)
    side.end()
    planes.finish()
    planes.store(z_out)
    for r in range(1, n):
        dst = o_ref.at[place(me, r, n)]
        remote(dst, dst, send.at[0], recv.at[r - 1], {"seq": me}).wait_recv()
    mine().wait()
    for r in range(1, n):
        copy(r).wait_send()


def to_heads(x, w, t, n, nf, wide, ident, a, b, z, count, carry):
    rows, cols = x.shape
    vmem = pl.BlockSpec(memory_space=pltpu.VMEM)
    hbm = pl.BlockSpec(memory_space=pl.ANY)
    s_ins, s_shapes, s_in_specs, s_out_specs, s_scratch = side_parts((a, b), 2 * n)
    return pl.pallas_call(
        functools.partial(to_heads_kernel, n, nf, wide),
        out_shape=[jax.ShapeDtypeStruct((n, rows, wide), x.dtype)]
        + s_shapes
        + [
            jax.ShapeDtypeStruct((n, count, z.shape[2] // n), z.dtype),
            jax.ShapeDtypeStruct((cols, t.shape[1]), x.dtype),
            jax.ShapeDtypeStruct(carry.shape, carry.dtype),
        ],
        in_specs=[hbm, vmem, vmem, vmem] + s_in_specs + [hbm],
        out_specs=[hbm] + s_out_specs + [vmem, vmem, hbm],
        input_output_aliases={0: 5},
        scratch_shapes=[pltpu.VMEM((n, rows, wide), x.dtype)]
        + Blocks.scratch(n)
        + s_scratch
        + PlaneSum.scratch(nf, count, z.shape[2]),
        compiler_params=pltpu.CompilerParams(
            collective_id=ident, has_side_effects=True, vmem_limit_bytes=60 << 20
        ),
        cost_estimate=SMALL,
        name="to_heads",
    )(carry, x, w, t, *s_ins, z)


def contract_kernel(
    n, nf, a_ref, b_ref, x_ref, y_ref, s_ref, p_ref, q_ref, c_ref, o_ref, sum_ref, p_out, q_out, c_out, acc, *sems
):
    i = pl.program_id(0)
    parts = [
        Blocks("seq", n, False, p_ref, p_out, *sems[:3]),
        Blocks("seq", n, False, q_ref, q_out, *sems[3:6]),
        Units(n, nf, True, c_ref, c_out, *sems[6:]),
    ]

    @pl.when(i == 0)
    def _():
        me = lax.axis_index("seq")
        greet([{"seq": place(me, r, n)} for r in range(1, n)])
        for part in parts:
            part.start()

    sum_ref[...] = (x_ref[...] + y_ref[...].astype(jnp.float32) + s_ref[...]).astype(sum_ref.dtype)
    part = lax.dot_general(
        a_ref[...], b_ref[...], (((0,), (0,)), ((), ())), preferred_element_type=jnp.float32
    )

    @pl.when(i == 0)
    def _():
        acc[...] = part

    @pl.when(i > 0)
    def _():
        acc[...] += part

    @pl.when(i == pl.num_programs(0) - 1)
    def _():
        o_ref[...] = acc[...].astype(o_ref.dtype)
        for part in parts:
            part.finish()


def contract(a, b, x, y, s, p, q, c, n, nf, tile, ident):
    steps = a.shape[0] // tile
    shape = (a.shape[1], b.shape[1])
    still = lambda s: pl.BlockSpec(s, lambda i: (0,) * len(s), pipeline_mode=pl.Buffered(1))
    part = lambda v: pl.BlockSpec((v.shape[0] // steps, v.shape[1]), lambda i: (i, 0))
    hbm = pl.BlockSpec(memory_space=pl.ANY)
    return pl.pallas_call(
        functools.partial(contract_kernel, n, nf),
        out_shape=[
            jax.ShapeDtypeStruct(shape, a.dtype),
            jax.ShapeDtypeStruct(x.shape, a.dtype),
            blocks_shape(p, n, False),
            blocks_shape(q, n, False),
            blocks_shape(c, nf, False),
        ],
        grid=(steps,),
        in_specs=[part(a), part(b), part(x), part(y), still(s.shape), hbm, hbm, hbm],
        out_specs=[still(shape), part(x), hbm, hbm, hbm],
        scratch_shapes=[pltpu.VMEM(shape, jnp.float32)]
        + Blocks.scratch(n)
        + Blocks.scratch(n)
        + Units.scratch(nf),
        compiler_params=pltpu.CompilerParams(
            dimension_semantics=("arbitrary",),
            vmem_limit_bytes=40 << 20,
            collective_id=ident,
            has_side_effects=True,
        ),
        cost_estimate=SMALL,
        name="contract",
    )(a, b, x, y, s, p, q, c)


def give_back_kernel(
    n, nf, rows, v_ref, w_ref, o_ref, v_out, w_out, o_out, planes, sums, *sems
):
    s = lax.axis_index("seq")
    f = lax.axis_index("fsdp")
    sems = list(sems)
    take = lambda k: [sems.pop(0) for _ in range(k)]
    send_z, recv_z, send_s, recv_s = take(4)
    parts = []
    if rows is not None:
        parts.append(rows.bind(w_ref, w_out, *take(3)))
    parts.append(Blocks("fsdp", nf, False, o_ref, o_out, *take(3)))
    others = [{"fsdp": lax.rem(f + d, nf)} for d in range(1, nf)]
    peers = [{"seq": place(s, r, n)} for r in range(1, n)]
    greet(peers + others)
    copies = []
    for d in range(1, nf):
        c = remote(v_ref.at[lax.rem(f + d, nf)], planes.at[d - 1], send_z.at[d - 1], recv_z.at[d - 1], others[d - 1])
        c.start()
        copies.append(c)
    for p in parts:
        p.start()
    total = v_ref[f]
    for d, c in enumerate(copies):
        c.wait_recv()
        total = total + planes[d]
    sums[0] = total
    spread = []
    for r in range(1, n):
        c = remote(sums.at[0], sums.at[r], send_s.at[r - 1], recv_s.at[r - 1], peers[r - 1])
        c.start()
        spread.append(c)
    for r, c in enumerate(spread):
        c.wait_recv()
        total = total + sums[r + 1]
    v_out[...] = total
    for p in parts:
        p.finish()
    for c in copies + spread:
        c.wait_send()


def give_back(vectors, w, held, o, n, nf, rows, ident):
    k = vectors.shape[1]
    tiles = -(-k // 1024) * 8
    padded = jnp.pad(vectors, ((0, 0), (0, tiles * 128 - k))).reshape(nf, tiles, 128)
    vmem = pl.BlockSpec(memory_space=pltpu.VMEM)
    hbm = pl.BlockSpec(memory_space=pl.ANY)
    dma = pltpu.SemaphoreType.DMA
    out = pl.pallas_call(
        functools.partial(give_back_kernel, n, nf, rows),
        out_shape=[
            jax.ShapeDtypeStruct((tiles, 128), jnp.float32),
            jax.ShapeDtypeStruct((held, w.shape[1]), w.dtype),
            blocks_shape(o, nf, False),
        ],
        in_specs=[vmem, hbm, hbm],
        out_specs=[vmem, hbm, hbm],
        scratch_shapes=[
            pltpu.VMEM((nf - 1, tiles, 128), jnp.float32),
            pltpu.VMEM((n, tiles, 128), jnp.float32),
            dma((nf - 1,)),
            dma((nf - 1,)),
            dma((n - 1,)),
            dma((n - 1,)),
        ]
        + (rows.scratch() if rows is not None else [])
        + Blocks.scratch(nf),
        compiler_params=pltpu.CompilerParams(collective_id=ident, has_side_effects=True),
        cost_estimate=SMALL,
        name="give_back",
    )(padded, w, o)
    return (out[0].reshape(-1)[:k],) + tuple(out[1:])


HEAD=64
SCALE=0.125*math.log2(math.e)


def block_pairs(slots, trunk):
    branches = (slots - trunk) // 3
    pairs = []
    for t in range(slots):
        m = t - trunk
        if t < trunk:
            keys = [(c, int(c == t), -1, -1) for c in range(t + 1)]
        else:
            keys = [(c, 0, -1, -1) for c in range(trunk)]
            if m >= branches:
                keys.append((trunk, 0, -1, m))
            keys.append((t, 1, m, -1))
        for i, (c, causal, own, leaf) in enumerate(keys):
            pairs.append((t, c, causal, own, leaf, int(i == 0), int(i == len(keys) - 1)))
    return pairs


def block_fields(p, slots, trunk):
    branches = (slots - trunk) // 3
    counts = [t + 1 for t in range(trunk)] + [trunk + 1] * branches
    counts += [trunk + 2] * (slots - trunk - branches)
    starts = [sum(counts[:t]) for t in range(slots)]
    t, begin, end = jnp.int32(0), jnp.int32(0), jnp.int32(counts[0])
    for i in range(1, slots):
        here = p >= starts[i]
        t = jnp.where(here, i, t)
        begin = jnp.where(here, starts[i], begin)
        end = jnp.where(here, starts[i] + counts[i], end)
    i = p - begin
    last = p == end - 1
    leaf = (t >= trunk + branches) & (i == trunk)
    key = jnp.where((t >= trunk) & last, t, i)
    return t, key, last, leaf, i == 0, last


def block_values(lengths, parents, pairs, block):
    count = lengths.shape[0]
    segments = np.arange(count)
    own = np.array([p[3] for p in pairs])[None, :] == segments[:, None]
    leaf = np.array([p[4] for p in pairs])[None, :] == segments[:, None]
    above = jnp.sum(jnp.where(leaf, parents[:, None], 0), 0)
    source = own | (segments[:, None] + 1 == above[None, :])
    closed = np.array([p[3] < 0 and p[4] < 0 for p in pairs])
    reach = jnp.where(closed, block, jnp.sum(jnp.where(source, lengths[:, None], 0), 0))
    return jnp.stack([jnp.maximum(above - 1, 0), reach]).astype(jnp.int32)


def lane_half(shape):
    return lax.broadcasted_iota(jnp.int32, shape, len(shape) - 1) < HEAD


def nt(a, b):
    return lax.dot_general(a, b, (((1,), (1,)), ((), ())), preferred_element_type=jnp.float32)


def mm(a, b):
    return jnp.dot(a, b, preferred_element_type=jnp.float32)


def attend_kernel(width, block, trunk, n, values, x_ref, w_ref, b_ref, c_ref, qkv, low, att, tot, kt, c_all, acc, xbuf, xsem, *sems):
    p = pl.program_id(0)
    slot, key, causal, leaf, first, last = block_fields(p, n, trunk)
    rows = lambda slot: pl.ds(pl.multiple_of(slot * block, block), block)
    qrow = rows(slot)
    above = values[0, p]
    reach = values[1, p]
    branches = (n - trunk) // 3
    left = lane_half((block, 2 * HEAD))
    spread = Spread(n, c_ref, c_all, *sems)

    def fetch(i):
        slot = lax.rem(i, 2)
        return pltpu.make_async_copy(x_ref.at[i], xbuf.at[slot], xsem.at[slot])

    @pl.when(p == 0)
    def _():
        fetch(jnp.int32(0)).start()
        greet(spread.peers())
        spread.start()

        def step(i, carry):
            @pl.when(i + 1 < n)
            def _():
                fetch(i + 1).start()

            fetch(i).wait()
            made = (mm(xbuf[lax.rem(i, 2)], w_ref[...]) + b_ref[...]).astype(qkv.dtype)
            qkv[rows(i)] = made
            kt[:, rows(i)] = made[:, width : 2 * width].T
            return carry

        lax.fori_loop(0, n, step, 0)
        for i in range(len(spread.bits) - 1):
            spread.phase(i)

    @pl.when(first)
    def _():
        acc[...] = jnp.zeros_like(acc)

    def keyed(mask, read):
        got = read(rows(key))
        if mask is not None:
            for b in range(1, branches):
                got = jnp.where(leaf & (above == b), read(pl.ds((trunk + b) * block, block)), got)
        return got

    def step(mask):
        for j in range(width // (2 * HEAD)):
            lanes = slice(j * 2 * HEAD, (j + 1) * 2 * HEAD)
            q = qkv[qrow, lanes]
            k = keyed(mask, lambda at: qkv[at, width + j * 2 * HEAD : width + (j + 1) * 2 * HEAD])
            v = keyed(mask, lambda at: qkv[at, 2 * width + j * 2 * HEAD : 2 * width + (j + 1) * 2 * HEAD])
            for h in range(2):
                here = left if h == 0 else jnp.logical_not(left)
                s = nt(jnp.where(here, q, 0), k)
                e = jnp.exp2(s * SCALE)
                if mask is not None:
                    e = jnp.where(mask, e, 0.0)
                acc[2 * j + h] += mm(e.astype(jnp.bfloat16), jnp.where(here, v, 1))

    closes = causal | leaf
    shift = jnp.where(causal, 0, block)

    @pl.when(jnp.logical_not(closes))
    def _():
        step(None)

    @pl.when(closes)
    def _():
        row = lax.broadcasted_iota(jnp.int32, (block, block), 0)
        col = lax.broadcasted_iota(jnp.int32, (block, block), 1)
        step((col <= row + shift) & (col < reach))

    @pl.when(last)
    def _():
        for j in range(width // (2 * HEAD)):
            a, b = acc[2 * j], acc[2 * j + 1]
            total = jnp.where(left, pltpu.roll(a, HEAD, 1), pltpu.roll(b, HEAD, 1))
            value = jnp.where(left, a, b) / total
            lanes = slice(j * 2 * HEAD, (j + 1) * 2 * HEAD)
            low[:, lanes] = value.astype(jnp.bfloat16)
            att[:, lanes] = value
            tot[:, lanes] = total

    @pl.when(p == pl.num_programs(0) - 4)
    def _():
        spread.phase(len(spread.bits) - 1)

    @pl.when(p == pl.num_programs(0) - 1)
    def _():
        spread.finish()


def attend(values, pairs, x, w, bias, block, trunk, sent, n, ident):
    rows, width = x.shape[0], w.shape[1] // 3
    by_q = lambda p: (block_fields(p, n, trunk)[0], 0)
    heads = width // HEAD
    once = lambda s: pl.BlockSpec(s, lambda p: (0,) * len(s), pipeline_mode=pl.Buffered(1))
    hbm = pl.BlockSpec(memory_space=pl.ANY)
    out = pl.pallas_call(
        functools.partial(attend_kernel, width, block, trunk, n),
        grid=(len(pairs),),
        out_shape=(
            jax.ShapeDtypeStruct((rows, 3 * width), x.dtype),
            jax.ShapeDtypeStruct((rows, width), x.dtype),
            jax.ShapeDtypeStruct((rows, width), jnp.float32),
            jax.ShapeDtypeStruct((rows, width), jnp.float32),
            jax.ShapeDtypeStruct((width, rows), x.dtype),
            jax.ShapeDtypeStruct((n,) + sent.shape, sent.dtype),
        ),
        in_specs=[pl.BlockSpec(memory_space=pltpu.SMEM), hbm, once(w.shape), once(bias.shape), hbm],
        out_specs=[once((rows, 3 * width))]
        + [pl.BlockSpec((block, width), by_q)] * 3
        + [once((width, rows)), hbm],
        scratch_shapes=[
            pltpu.VMEM((heads, block, 2 * HEAD), jnp.float32),
            pltpu.VMEM((2, block, x.shape[1]), x.dtype),
            pltpu.SemaphoreType.DMA((2,)),
        ]
        + Spread.scratch(n),
        compiler_params=pltpu.CompilerParams(
            dimension_semantics=("arbitrary",),
            vmem_limit_bytes=60 << 20,
            collective_id=ident,
            has_side_effects=True,
        ),
        cost_estimate=SMALL,
        name="attend",
    )(values, x.reshape(n, block, x.shape[1]), w, bias, sent)
    return out[:5] + (out[5].reshape(n * sent.shape[0], sent.shape[1]),)


def attend_back_kernel(width, block, slots, trunk, branches, nf, lows, *refs):
    count = len(lows)
    values, qkv, kt, datt, att, tot = refs[:6]
    sources = refs[6 : 6 + count]
    out, sums = refs[6 + count : 8 + count]
    parts = refs[8 + count : 8 + 2 * count]
    dk, dv, dqt, aug = refs[8 + 2 * count : 12 + 2 * count]
    rest = refs[12 + 2 * count :]
    riders = [PlaneSum(nf, sources[i], lows[i], *rest[4 * i : 4 * i + 4]) for i in range(count)]
    p = pl.program_id(0)
    slot, key, causal, leaf, first, last = block_fields(p, slots, trunk)
    rows = lambda slot: pl.ds(pl.multiple_of(slot * block, block), block)
    above = values[0, p]
    reach = values[1, p]
    qrow = rows(slot)
    left = lane_half((block, 2 * HEAD))
    lane = lax.broadcasted_iota(jnp.int32, (block, 2 * HEAD), 1)
    columns = width // (2 * HEAD)

    @pl.when(p == 0)
    def _():
        greet(riders[0].peers())
        for r in riders:
            r.start()
        dk[...] = jnp.zeros_like(dk)
        dv[...] = jnp.zeros_like(dv)

    @pl.when(first)
    def _():
        dqt[...] = jnp.zeros_like(dqt)
        for j in range(columns):
            lanes = slice(j * 2 * HEAD, (j + 1) * 2 * HEAD)
            d = datt[:, lanes].astype(jnp.float32)
            total = tot[:, lanes]
            low = (d / total).astype(jnp.bfloat16)
            prod = d * att[:, lanes] / total
            for h in range(2):
                here = left if h == 0 else jnp.logical_not(left)
                delta = -jnp.sum(jnp.where(here, prod, 0.0), 1, keepdims=True)
                hi = delta.astype(jnp.bfloat16).astype(jnp.float32)
                mid = (delta - hi).astype(jnp.bfloat16).astype(jnp.float32)
                rest = delta - hi - mid
                at = HEAD * (1 - h)
                extra = jnp.where(
                    lane == at, hi, jnp.where(lane == at + 1, mid, jnp.where(lane == at + 2, rest, 0.0))
                )
                aug[2 * j + h] = jnp.where(here, low.astype(jnp.float32), extra).astype(jnp.bfloat16)

    def add(mask, lanes, dks, dvs):
        at = rows(key)
        if mask is None:
            dk[at, lanes] += dks
            dv[at, lanes] += dvs
            return
        for b in range(branches):
            chosen = causal | (above == b) if b == 0 else leaf & (above == b)
            if b > 0:
                at = pl.ds((trunk + b) * block, block)
            dk[at, lanes] += jnp.where(chosen, dks, 0.0)
            dv[at, lanes] += jnp.where(chosen, dvs, 0.0)

    def keyed(mask, read):
        got = read(rows(key))
        if mask is not None:
            for b in range(1, branches):
                got = jnp.where(leaf & (above == b), read(pl.ds((trunk + b) * block, block)), got)
        return got

    def step(mask):
        for j in range(columns):
            lanes = slice(j * 2 * HEAD, (j + 1) * 2 * HEAD)
            q = qkv[qrow, lanes]
            k = keyed(mask, lambda at: qkv[at, width + j * 2 * HEAD : width + (j + 1) * 2 * HEAD])
            v = keyed(mask, lambda at: qkv[at, 2 * width + j * 2 * HEAD : 2 * width + (j + 1) * 2 * HEAD])
            dvs, dks = [], []
            for h in range(2):
                here = left if h == 0 else jnp.logical_not(left)
                qh = jnp.where(here, q, 0)
                e = jnp.exp2(nt(k, qh) * SCALE)
                if mask is not None:
                    e = jnp.where(mask, e, 0.0)
                dod = aug[2 * j + h]
                ds = (e * nt(jnp.where(here, v * 0.125, 0.125).astype(jnp.bfloat16), dod)).astype(
                    jnp.bfloat16
                )
                dvs.append(mm(e.astype(jnp.bfloat16), dod))
                dks.append(mm(ds, qh))
                at = j * 2 * HEAD + h * HEAD
                dqt[at : at + HEAD] += mm(keyed(mask, lambda i: kt[at : at + HEAD, i]), ds)
            add(mask, lanes, dks[0] + dks[1], jnp.where(left, dvs[0], dvs[1]))

    closes = causal | leaf
    shift = jnp.where(causal, 0, block)

    @pl.when(jnp.logical_not(closes))
    def _():
        step(None)

    @pl.when(closes)
    def _():
        col = lax.broadcasted_iota(jnp.int32, (block, block), 0)
        row = lax.broadcasted_iota(jnp.int32, (block, block), 1)
        step((col <= row + shift) & (col < reach))

    @pl.when(last)
    def _():
        out[qrow, 0:width] = dqt[...].T.astype(jnp.bfloat16)

    @pl.when(p == pl.num_programs(0) - 1)
    def _():
        out[:, width : 2 * width] = dk[...].astype(jnp.bfloat16)
        out[:, 2 * width :] = dv[...].astype(jnp.bfloat16)
        for t in range(3):
            lanes = slice(t * width, (t + 1) * width)
            sums[:, lanes] = jnp.sum(out[:, lanes].astype(jnp.float32), 0, keepdims=True)
        for r, made in zip(riders, parts):
            r.finish()
            r.store(made)


def attend_back(values, pairs, qkv, kt, datt, att, tot, block, trunk, nf, riders, ident):
    rows, width = qkv.shape[0], qkv.shape[1] // 3
    by_q = lambda p: (block_fields(p, rows // block, trunk)[0], 0)
    heads = width // HEAD
    branches = (rows // block - trunk) // 3
    made = [(k, z.shape[1] - at, z.shape[2] // k) for z, at, k in riders]
    once = lambda s: pl.BlockSpec(s, lambda p: (0,) * len(s), pipeline_mode=pl.Buffered(1))
    hbm = pl.BlockSpec(memory_space=pl.ANY)
    out = pl.pallas_call(
        functools.partial(
            attend_back_kernel, width, block, rows // block, trunk, branches, nf, [r[1] for r in riders]
        ),
        grid=(len(pairs),),
        out_shape=[
            jax.ShapeDtypeStruct((rows, 3 * width), jnp.bfloat16),
            jax.ShapeDtypeStruct((1, 3 * width), jnp.float32),
        ]
        + [jax.ShapeDtypeStruct(s, jnp.bfloat16) for s in made],
        in_specs=[pl.BlockSpec(memory_space=pltpu.SMEM), once((rows, 3 * width)), once((width, rows))]
        + [pl.BlockSpec((block, width), by_q)] * 3
        + [hbm] * len(riders),
        out_specs=[once((rows, 3 * width)), once((1, 3 * width))] + [once(s) for s in made],
        scratch_shapes=[
            pltpu.VMEM((rows, width), jnp.float32),
            pltpu.VMEM((rows, width), jnp.float32),
            pltpu.VMEM((width, block), jnp.float32),
            pltpu.VMEM((heads, block, 2 * HEAD), jnp.bfloat16),
        ]
        + sum([PlaneSum.scratch(nf, z.shape[1] - at, z.shape[2]) for z, at, k in riders], []),
        compiler_params=pltpu.CompilerParams(
            dimension_semantics=("arbitrary",),
            vmem_limit_bytes=60 << 20,
            collective_id=ident,
            has_side_effects=True,
        ),
        cost_estimate=SMALL,
        name="attend_back",
    )(values, qkv, kt, datt, att, tot, *[r[0] for r in riders])
    return out[0], out[1], out[2:]


def layer_norm(values, gain, shift):
    centred = values - jnp.mean(values, -1, keepdims=True)
    spread = jnp.mean(centred * centred, -1, keepdims=True)
    return centred * lax.rsqrt(spread + 1e-05) * gain + shift


def contract_rows(left, right):
    return lax.dot_general(
        left, right, (((0,), (0,)), ((), ())), preferred_element_type=jnp.float32
    )


def contract_cols(left, right):
    return lax.dot_general(
        left, right, (((1,), (1,)), ((), ())), preferred_element_type=jnp.float32
    )


def after(value, other):
    return value + (other[(0,) * other.ndim] * 0).astype(value.dtype)


def row_major(x):
    return with_layout_constraint(x, Layout(major_to_minor=tuple(range(x.ndim))))


def local(
    tokens,
    ln1_gain,
    ln1_bias,
    qkv_weight,
    qv_bias,
    out_weight,
    out_bias,
    ln2_gain,
    ln2_bias,
    fc_weight,
    fc_bias,
    proj_weight,
    proj_bias,
    seg_lengths,
    parents,
    cotangent,
):
    n = lax.axis_size("seq")
    nf = lax.axis_size("fsdp")
    s = lax.axis_index("seq")
    f = lax.axis_index("fsdp")
    trunk = n // 4
    block, width = tokens.shape[1], tokens.shape[2]
    rows = width // nf
    hidden = fc_weight.shape[1] * n
    piece = hidden // (n * nf)
    group = n // nf
    wide = 2 * HEAD * (-(-HEADS // (2 * n)))
    low = jnp.bfloat16
    wider = jnp.float32

    vectors = [ln1_gain, ln1_bias, qv_bias, out_bias, ln2_gain, ln2_bias, fc_bias, proj_bias]
    sizes = [v.shape[0] for v in vectors]
    qkv_cols = qkv_weight.shape[1]
    even = qkv_cols % 8 == 0
    forth = Rows(n, qkv_cols, width, wide, False) if even else None
    back = Rows(n, qkv_cols, width, wide, True) if even else None
    turned, proj_blocks, fc_blocks, out_blocks, gathered = exchange(
        qkv_weight.T,
        proj_weight.reshape(n, piece, width // n),
        fc_weight.reshape(rows, nf, piece).transpose(1, 0, 2),
        out_weight,
        [jnp.stack([v for v in vectors if v.shape == ln1_gain.shape])]
        + [v.reshape(1, -1) for v in vectors if v.shape != ln1_gain.shape],
        n,
        nf,
        forth,
        wide,
        0,
    )
    short = iter(jnp.unstack(gathered[0], axis=1))
    long = iter(gathered[1:])
    whole = [next(short) if v.shape == ln1_gain.shape else next(long) for v in vectors]
    whole = [v.reshape(-1).astype(wider) for v in whole]
    gain_one, shift_one, bias_qv, bias_out, gain_two, shift_two, bias_fc, bias_proj = whole
    bias_three = jnp.stack([bias_qv[:width], jnp.zeros((width,), wider), bias_qv[width:]])
    bias_three = jnp.pad(bias_three, ((0, 0), (0, n * wide - width)))
    bias_mine = lax.dynamic_slice_in_dim(bias_three, s * wide, wide, 1).reshape(1, -1)
    bias_hidden = lax.dynamic_index_in_dim(bias_fc.reshape(nf, n, piece), s, 1, False)
    bias_hidden = bias_hidden.reshape(1, -1)

    if even:
        turned = turned.reshape(3, wide, rows)
        kept = lax.broadcasted_iota(jnp.int32, turned.shape, 1) + s * wide < width
        turned = jnp.where(kept, turned, 0).reshape(3 * wide, rows)
    else:
        turned = lax.all_gather(qkv_weight.T, "seq", axis=0, tiled=True).reshape(3, width, rows)
        turned = jnp.pad(turned, ((0, 0), (0, n * wide - width), (0, 0)))
        turned = lax.dynamic_slice_in_dim(turned, s * wide, wide, 1).reshape(3 * wide, rows)
    pairs = block_pairs(n, trunk)
    table = block_values(seg_lengths[0], parents[0], pairs, block)

    resid = tokens[0].astype(wider)
    out_turned = out_blocks.reshape(width, width // n).T
    normed_one, out_turned, qkv_mine = seq_gather(
        layer_norm(resid, gain_one, shift_one).astype(low),
        n,
        1,
        "gather_one",
        rider=(turned.T, True, nf),
        second=out_turned,
    )
    out_turned = out_turned.reshape(width, width)
    qkv_mine = qkv_mine.reshape(width, 3 * wide)
    fc_rows = fc_blocks.transpose(1, 0, 2).reshape(rows, nf * piece)
    fc_mine = lax.all_gather(fc_rows, "fsdp", axis=0, tiled=True)

    upstream = cotangent[0].astype(wider)
    proj_rows = proj_blocks.transpose(1, 0, 2).reshape(piece, width)
    proj_mine = lax.all_gather(after(proj_rows, normed_one), "fsdp", axis=0, tiled=True)
    projected, attended_low, attended, totals, keys_turned, upstream_all = attend(
        table, pairs, normed_one, qkv_mine, bias_mine, block, trunk, cotangent[0], n, 8
    )
    attended_mine = to_tokens(attended_low.reshape(n, block, wide), n, wide, 2)[:, :width]
    middle = resid + contract_cols(attended_mine, out_turned) + bias_out
    normed_two = layer_norm(middle, gain_two, shift_two).astype(low)
    ff = nf * piece

    def expand(value, fc, bias, proj):
        pre = mm(value, fc[...]) + bias[...]
        bend = math.sqrt(2 / math.pi)
        square = pre * pre
        inner = jnp.tanh(pre * (bend + bend * 0.044715 * square))
        half = 0.5 + 0.5 * inner
        act = (pre * half).astype(low)
        slope = half + 0.5 * pre * (1 - inner * inner) * (bend + 3 * bend * 0.044715 * square)
        return act, slope.astype(low), mm(act, proj[...]).astype(low)

    normed_two, hidden_act, hidden_slope, mixed = seq_gather(
        normed_two,
        n,
        3,
        "gather_two",
        expand,
        (fc_mine, bias_hidden, proj_mine),
        ((ff, low), (ff, low), (width, low)),
        modes=(0, 0, 0),
    )

    def shrink(up, slope, proj, fc):
        grad = (nt(up, proj[...]) * slope.astype(wider)).astype(low)
        return nt(grad, fc[...]), grad

    grad_normed_two, grad_pre, grad_proj, unused_sums = seq_scatter(
        n,
        width,
        4,
        "scatter_two",
        shrink,
        (upstream_all, hidden_slope),
        (proj_mine, fc_mine),
        ((ff, low),),
        side=(hidden_act, upstream_all),
    )
    grad_proj = grad_proj.reshape(nf, piece, width)
    cut = piece // 16 * 8
    unused_two, norm_two_back = jax.vjp(layer_norm, middle, gain_two, shift_two)
    grad_middle_norm, grad_gain_two, grad_shift_two = norm_two_back(grad_normed_two)
    grad_middle = upstream + grad_middle_norm
    grad_branch = grad_middle.astype(low)
    grad_attended, grad_fc, hidden_sums, proj_first, grad_out, mixed = to_heads(
        grad_branch,
        out_turned,
        attended_mine,
        n,
        nf,
        wide,
        5,
        normed_two,
        grad_pre,
        grad_proj,
        cut,
        mixed,
    )
    mixed = lax.psum_scatter(mixed, "seq", scatter_dimension=0, tiled=True)
    grad_attended = grad_attended.reshape(n * block, wide)
    grad_projected, column_sums, (fc_part, proj_second) = attend_back(
        table,
        pairs,
        projected,
        keys_turned,
        grad_attended,
        attended,
        totals,
        block,
        trunk,
        nf,
        ((grad_fc.reshape(nf, rows, ff), 0, nf), (grad_proj, cut, n)),
        9,
    )
    grad_qkv, output, proj_first, proj_second, fc_out = contract(
        normed_one,
        grad_projected,
        middle,
        mixed,
        bias_proj.reshape(1, -1),
        proj_first,
        proj_second,
        fc_part,
        n,
        nf,
        block,
        10,
    )
    output = output[None]
    input_grad, grad_gain_one, grad_shift_one, qkv_parts = seq_scatter(
        n,
        width,
        6,
        "scatter_one",
        lambda g, w: (nt(g, w[...]),),
        (grad_projected,),
        (qkv_mine,),
        rider=(grad_qkv.reshape(nf, rows, 3 * wide), False, nf),
        norm=(tokens[0], gain_one.reshape(1, -1), grad_middle, low),
    )
    input_grad = input_grad[None]

    out_part = lax.psum_scatter(grad_out, "seq", scatter_dimension=0, tiled=True).T
    out_part = after(out_part, qkv_parts).reshape(nf, rows, width // n)
    qkv_part = jnp.sum(qkv_parts.astype(wider), 0).astype(low).T

    column_sums = column_sums.reshape(3, wide)
    placed = lax.dynamic_update_slice_in_dim(
        jnp.zeros((3, n * wide), wider), column_sums, s * wide, 1
    )[:, :width]
    grad_qv = jnp.concatenate([placed[0], placed[2]])
    hidden_sums = hidden_sums.reshape(nf, 1, piece)
    grad_fc_bias = lax.dynamic_update_slice_in_dim(
        jnp.zeros((nf, n, piece), wider), hidden_sums, s, 1
    )
    parts = [
        grad_gain_one,
        grad_shift_one,
        grad_qv,
        jnp.sum(grad_branch.astype(wider), 0),
        grad_gain_two,
        grad_shift_two,
        grad_fc_bias,
        jnp.sum(upstream, 0),
    ]
    summed, qkv_out, out_out = give_back(
        jnp.concatenate([p.reshape(nf, -1) for p in parts], 1),
        qkv_part,
        qkv_cols,
        out_part,
        n,
        nf,
        back,
        7,
    )
    if not even:
        qkv_part = qkv_part.reshape(3, wide, rows)
        qkv_out = lax.all_gather(qkv_part, "seq", axis=1, tiled=True)[:, :width]
        qkv_out = qkv_out.reshape(3 * width, rows)
        qkv_out = lax.dynamic_slice_in_dim(qkv_out, s * qkv_cols, qkv_cols, 0)
    out_out = jnp.sum(out_out.astype(wider), 0)
    qkv_out = qkv_out.T.astype(wider)
    proj_out = jnp.concatenate([proj_first, proj_second], 1)
    proj_out = proj_out.reshape(n * piece, width // n).astype(wider)
    fc_out = fc_out.transpose(1, 0, 2).reshape(rows, nf * piece).astype(wider)
    vector_out = []
    at = 0
    for size in sizes:
        vector_out.append(summed[at : at + size])
        at += size
    return (
        output,
        input_grad,
        vector_out[0],
        vector_out[1],
        qkv_out,
        vector_out[2],
        out_out,
        vector_out[3],
        vector_out[4],
        vector_out[5],
        fc_out,
        vector_out[6],
        proj_out,
        vector_out[7],
    )


def solution(mesh):
    in_specs = (
        P("fsdp", "seq", None),
        P("fsdp"),
        P("fsdp"),
        P("fsdp", "seq"),
        P("fsdp"),
        P("fsdp", "seq"),
        P("fsdp"),
        P("fsdp"),
        P("fsdp"),
        P("fsdp", "seq"),
        P("fsdp"),
        P("fsdp", "seq"),
        P("fsdp"),
        P("fsdp", None),
        P("fsdp", None),
        P("fsdp", "seq", None),
    )
    out_specs = (
        P("fsdp", "seq", None),
        P("fsdp", "seq", None),
        P("fsdp"),
        P("fsdp"),
        P("fsdp", "seq"),
        P("fsdp"),
        P("fsdp", "seq"),
        P("fsdp"),
        P("fsdp"),
        P("fsdp"),
        P("fsdp", "seq"),
        P("fsdp"),
        P("fsdp", "seq"),
        P("fsdp"),
    )
    return jax.shard_map(local, mesh=mesh, in_specs=in_specs, out_specs=out_specs, check_vma=False)
```

```python
import functools
import math

import jax
import jax.numpy as jnp
import numpy as np
from jax import lax
from jax.experimental import pallas as pl
from jax.experimental.layout import Layout, with_layout_constraint
from jax.experimental.pallas import tpu as pltpu
from jax.sharding import PartitionSpec as P

MESH = pl.DeviceIdType.MESH
HEADS = 25
SMALL = pl.CostEstimate(flops=0, bytes_accessed=1 << 20, transcendentals=0)


def route_bits(n):
    bits = []
    b = 2
    while b < n:
        bits.append(b)
        b *= 2
    return bits


def flip(a, b):
    return jnp.where(lax.rem(lax.div(a, b), 2) == 0, a + b, a - b)


def place(me, r, n):
    if isinstance(r, int):
        for b in [1] + route_bits(n):
            if r & b:
                me = flip(me, b)
        return me
    for b in [1] + route_bits(n):
        me = jnp.where(lax.rem(lax.div(r, b), 2) == 0, me, flip(me, b))
    return me


def pick(table, q):
    value = jnp.int32(table[0])
    for i, entry in enumerate(table[1:]):
        value = jnp.where(q == i + 1, jnp.int32(entry), value)
    return value


def greet(ids):
    barrier = pltpu.get_barrier_semaphore()
    for i in ids:
        pl.semaphore_signal(barrier, inc=1, device_id=i, device_id_type=MESH)
    pl.semaphore_wait(barrier, len(ids))


def remote(src, dst, send, recv, device):
    return pltpu.make_async_remote_copy(
        src_ref=src, dst_ref=dst, send_sem=send, recv_sem=recv, device_id=device, device_id_type=MESH
    )


class Blocks:
    def __init__(self, axis, size, same, source, target, send, recv, local):
        self.axis, self.size, self.same = axis, size, same
        self.source, self.target = source, target
        self.send, self.recv, self.local = send, recv, local
        self.me = lax.axis_index(axis)

    @staticmethod
    def scratch(size):
        dma = pltpu.SemaphoreType.DMA
        return [dma((size - 1,)), dma((size - 1,)), dma]

    def peers(self):
        return [{self.axis: lax.rem(self.me + d, self.size)} for d in range(1, self.size)]

    def copy(self, d):
        to = lax.rem(self.me + d, self.size)
        src = self.source if self.same else self.source.at[to]
        return remote(src, self.target.at[self.me], self.send.at[d - 1], self.recv.at[d - 1], {self.axis: to})

    def own(self):
        src = self.source if self.same else self.source.at[self.me]
        return pltpu.make_async_copy(src, self.target.at[self.me], self.local)

    def start(self):
        for d in range(1, self.size):
            self.copy(d).start()
        self.own().start()

    def finish(self):
        for d in range(1, self.size):
            dst = self.target.at[lax.rem(self.me + self.size - d, self.size)]
            remote(dst, dst, self.send.at[d - 1], self.recv.at[d - 1], {self.axis: self.me}).wait_recv()
        self.own().wait()
        for d in range(1, self.size):
            self.copy(d).wait_send()


class Spread:
    def __init__(self, n, source, target, send, recv, local):
        self.n, self.source, self.target = n, source, target
        self.send, self.recv, self.local = send, recv, local
        self.me = lax.axis_index("seq")
        self.bits = route_bits(n)
        self.orders = [self.bits, self.bits[::-1]]
        self.h = source.shape[0] // 2

    @staticmethod
    def scratch(n):
        dma = pltpu.SemaphoreType.DMA
        return [dma((2, len(route_bits(n)) + 1, n)), dma((2, n)), dma]

    def device(self, b):
        return {"seq": flip(self.me, b)}

    def peers(self):
        return [self.device(b) for b in [1] + self.bits]

    def rows(self, half):
        return pl.ds(half * self.h, self.h)

    def ship(self, half, k, b):
        owner = place(self.me, k, self.n)
        src = self.source if k == 0 else self.target.at[owner]
        lane = 0 if b == 1 else 1 + self.bits.index(b)
        return remote(
            src.at[self.rows(half)],
            self.target.at[owner].at[self.rows(half)],
            self.send.at[half, lane, k],
            self.recv.at[half, k ^ b],
            self.device(b),
        )

    def arrive(self, half, k):
        dst = self.target.at[place(self.me, k, self.n)].at[self.rows(half)]
        remote(dst, dst, self.send.at[half, 0, 0], self.recv.at[half, k], self.device(1)).wait_recv()

    def own(self):
        return pltpu.make_async_copy(self.source, self.target.at[self.me], self.local)

    def fresh(self, half, i):
        had = [0]
        for b in self.orders[half][:i]:
            had = had + [k ^ b for k in had]
        return [k ^ self.orders[half][i] for k in had]

    def start(self):
        for i in range(len(self.bits)):
            for half in (0, 1):
                self.ship(half, 0, self.orders[half][i]).start()
        for half in (0, 1):
            self.ship(half, 0, 1).start()
        self.own().start()

    def phase(self, i):
        for half in (0, 1):
            for k in self.fresh(half, i):
                self.arrive(half, k)
                for b in self.orders[half][i + 1 :] + [1]:
                    self.ship(half, k, b).start()

    def finish(self):
        for half in (0, 1):
            for k in range(1, self.n, 2):
                self.arrive(half, k)
        self.own().wait()
        for half in (0, 1):
            for b in self.orders[half] + [1]:
                self.ship(half, 0, b).wait_send()
            for i in range(len(self.bits)):
                for k in self.fresh(half, i):
                    for b in self.orders[half][i + 1 :] + [1]:
                        self.ship(half, k, b).wait_send()


class PlaneSum(Blocks):
    def __init__(self, size, source, low, target, send, recv, local):
        super().__init__("fsdp", size, False, source, target, send, recv, local)
        self.window = pl.ds(low, target.shape[1])

    @staticmethod
    def scratch(size, rows, cols):
        return [pltpu.VMEM((size, rows, cols), jnp.bfloat16)] + Blocks.scratch(size)

    def copy(self, d):
        to = lax.rem(self.me + d, self.size)
        src = self.source.at[to].at[self.window]
        return remote(src, self.target.at[self.me], self.send.at[d - 1], self.recv.at[d - 1], {self.axis: to})

    def own(self):
        src = self.source.at[self.me].at[self.window]
        return pltpu.make_async_copy(src, self.target.at[self.me], self.local)

    def store(self, out):
        total = self.target[0].astype(jnp.float32)
        for i in range(1, self.size):
            total = total + self.target[i].astype(jnp.float32)
        cols = out.shape[2]
        for i in range(out.shape[0]):
            out[i] = total[:, i * cols : (i + 1) * cols].astype(out.dtype)


def blocks_shape(x, size, same):
    return jax.ShapeDtypeStruct(((size,) + x.shape) if same else x.shape, x.dtype)


def arrival_order(n):
    bits = route_bits(n)
    orders = [bits, bits[::-1]]
    lists = []
    for order in orders:
        held, phases = [0], [-1]
        for i, b in enumerate(order):
            fresh = [h ^ b for h in held]
            held, phases = held + fresh, phases + [i] * len(fresh)
        lists.append(list(zip(held, phases)))
    entries = []
    for i in range(n // 2):
        for odd in (0, 1):
            for half in (0, 1):
                k, phase = lists[half][i]
                entries.append((half, k ^ odd, phase, odd))
    return orders, entries


def gather_kernel(n, h, body, n_const, n_out, relative, modes, nf, same, second, *refs):
    if second:
        at = 1 + n_const
        out = at + 1 + min(nf, 1) + 1 + n_out
        w_ref, w_all = refs[at], refs[out]
        w_send, w_recv, w_keep = refs[-3:]
        refs = refs[:at] + refs[at + 1 : out] + refs[out + 1 : -3]
        w_half = w_ref.shape[1] // 256 * 128
        w_lanes = [pl.ds(0, w_half), pl.ds(w_half, w_ref.shape[1] - w_half)]
    refs, rider = split_rider(refs, nf, same, 1 + n_const, 1 + n_out)
    x_ref = refs[0]
    consts = refs[1 : 1 + n_const]
    all_ref = refs[1 + n_const]
    outs = refs[2 + n_const : 2 + n_const + n_out]
    held = refs[2 + n_const + n_out]
    stages = refs[3 + n_const + n_out : 3 + n_const + 2 * n_out]
    send, recv, keep, store = refs[3 + n_const + 2 * n_out :]
    me = lax.axis_index("seq")
    orders, entries = arrival_order(n)
    bits = orders[0]
    nb = len(bits)

    def device(b):
        return {"seq": flip(me, b)}

    def spot(half, k):
        return 2 * (k if relative else place(me, k, n)) + half

    def ship(half, k, b):
        at = spot(half, k)
        src = x_ref.at[pl.ds(half * h, h)] if isinstance(k, int) and k == 0 else held.at[at]
        lane = 0 if b == 1 else 1 + bits.index(b)
        to = k ^ b if isinstance(k, int) else place(k, b, n)
        dst = 2 * to + half if relative else at
        first = remote(src, held.at[dst], send.at[half, lane, k], recv.at[half, to], device(b))
        if not second:
            return [first]
        owner = place(me, k, n)
        lanes = w_lanes[half]
        src = w_ref if isinstance(k, int) and k == 0 else w_all.at[owner]
        other = remote(
            src.at[:, lanes], w_all.at[owner].at[:, lanes], w_send.at[half, lane, k], w_recv.at[half, to], device(b)
        )
        return [first, other]

    def each(copies, act):
        for c in copies:
            act(c)

    def w_arrive(half, k):
        dst = w_all.at[place(me, k, n)].at[:, w_lanes[half]]
        remote(dst, dst, w_send.at[0, 0, 0], w_recv.at[half, k], device(1)).wait_recv()

    greet([device(b) for b in [1] + bits] + (rider.peers() if nf else []))
    for i in range(nb):
        for half in (0, 1):
            each(ship(half, 0, orders[half][i]), lambda c: c.start())
    for half in (0, 1):
        each(ship(half, 0, 1), lambda c: c.start())
    if second:
        pltpu.make_async_copy(w_ref, w_all.at[me], w_keep).start()
    if nf:
        rider.start()

    def output(o, q, at):
        slot = lax.rem(q, 2)
        return pltpu.make_async_copy(stages[o].at[slot], outs[o].at[at], store.at[o, slot])

    def entry(q, at, value):
        results = body(value, *consts)
        for o in range(n_out):

            @pl.when(q >= 2)
            def _(o=o):
                output(o, q, at[modes[o]]).wait()

            stages[o][lax.rem(q, 2)] = results[o]
            output(o, q, at[modes[o]]).start()

    def step(q, carry):
        half = pick([e[0] for e in entries], q)
        k = pick([e[1] for e in entries], q)
        phase = pick([e[2] for e in entries], q)
        odd = pick([e[3] for e in entries], q)
        at = spot(half, k)

        @pl.when(k == 0)
        def _():
            held[at] = x_ref[pl.ds(pl.multiple_of(half * h, h), h)]

        @pl.when(k != 0)
        def _():
            remote(held.at[at], held.at[at], send.at[0, 0, 0], recv.at[half, k], device(1)).wait_recv()

        for side in (0, 1) if second else ():

            @pl.when((k != 0) & (half == side))
            def _(side=side):
                w_arrive(side, k)

        for side in (0, 1):
            for i in range(nb):

                @pl.when((half == side) & (odd == 0) & (k != 0) & (phase < i))
                def _(side=side, i=i):
                    each(ship(side, k, orders[side][i]), lambda c: c.start())

            @pl.when((half == side) & (odd == 0) & (k != 0))
            def _(side=side):
                each(ship(side, k, 1), lambda c: c.start())

        pltpu.make_async_copy(held.at[at], all_ref.at[at], keep.at[q]).start()
        if n_out:
            entry(q, (2 * place(me, k, n) + half, 2 * k + half), held[at])
        return carry

    lax.fori_loop(0, 2 * n, step, 0)
    for q, (half, k, phase, odd) in enumerate(entries):
        at = spot(half, k)
        pltpu.make_async_copy(held.at[at], all_ref.at[at], keep.at[q]).wait()
        if q >= 2 * n - 2:
            for o in range(n_out):
                output(o, jnp.int32(q), at).wait()
        if not odd:
            for i in range(nb):
                if phase < i:
                    each(ship(half, k, orders[half][i]), lambda c: c.wait_send())
            each(ship(half, k, 1), lambda c: c.wait_send())
    if second:
        pltpu.make_async_copy(w_ref, w_all.at[me], w_keep).wait()
    if nf:
        rider.finish()


def split_rider(refs, nf, same, n_in, n_out):
    if not nf:
        return refs, None
    source = refs[n_in]
    target = refs[n_in + 1 + n_out]
    rider = Blocks("fsdp", nf, same, source, target, *refs[-3:])
    return refs[:n_in] + refs[n_in + 1 : n_in + 1 + n_out] + refs[n_in + 2 + n_out : -3], rider


def rider_parts(rider):
    if rider is None:
        return [], [], [], [], 0, False
    x, same, nf = rider
    hbm = [pl.BlockSpec(memory_space=pl.ANY)]
    return [x], hbm, [blocks_shape(x, nf, same)], Blocks.scratch(nf), nf, same


def seq_gather(x, n, ident, name, body=None, consts=(), outs=(), relative=False, modes=None, rider=None, second=None):
    rows, cols = x.shape
    h = rows // 2
    nb = len(route_bits(n))
    shapes = [jax.ShapeDtypeStruct((2 * n, h, c), d) for c, d in outs]
    vmem = pl.BlockSpec(memory_space=pltpu.VMEM)
    hbm = pl.BlockSpec(memory_space=pl.ANY)
    more, spec, shape, scratch, nf, same = rider_parts(rider)
    also = [] if second is None else [second]
    out = pl.pallas_call(
        functools.partial(
            gather_kernel, n, h, body, len(consts), len(outs), relative, modes, nf, same, second is not None
        ),
        out_shape=[jax.ShapeDtypeStruct((2 * n, h, cols), x.dtype)]
        + shapes
        + [jax.ShapeDtypeStruct((n,) + w.shape, w.dtype) for w in also]
        + shape,
        in_specs=[vmem] * (1 + len(consts)) + [hbm] * len(also) + spec,
        out_specs=[hbm] * (1 + len(outs)) + [hbm] * len(also) + spec,
        scratch_shapes=[pltpu.VMEM((2 * n, h, cols), x.dtype)]
        + [pltpu.VMEM((2, h, c), d) for c, d in outs]
        + [
            pltpu.SemaphoreType.DMA((2, nb + 1, n)),
            pltpu.SemaphoreType.DMA((2, n)),
            pltpu.SemaphoreType.DMA((2 * n,)),
            pltpu.SemaphoreType.DMA((max(len(outs), 1), 2)),
        ]
        + scratch
        + [
            pltpu.SemaphoreType.DMA((2, nb + 1, n)),
            pltpu.SemaphoreType.DMA((2, n)),
            pltpu.SemaphoreType.DMA,
        ]
        * len(also),
        compiler_params=pltpu.CompilerParams(
            collective_id=ident, has_side_effects=True, vmem_limit_bytes=60 << 20
        ),
        cost_estimate=SMALL,
        name=name,
    )(x, *consts, *also, *more)
    return [o.reshape(2 * n * h, o.shape[2]) for o in out[: 1 + len(outs)]] + list(out[1 + len(outs) :])


class Side:
    def __init__(self, count, refs):
        self.count = count
        self.a, self.b, self.grad, self.sums, self.acc, self.abuf, self.bbuf, self.load = refs

    def fetch(self, i):
        slot = lax.rem(i, 2)
        return [
            pltpu.make_async_copy(self.a.at[i], self.abuf.at[slot], self.load.at[0, slot]),
            pltpu.make_async_copy(self.b.at[i], self.bbuf.at[slot], self.load.at[1, slot]),
        ]

    def begin(self):
        self.acc[...] = jnp.zeros_like(self.acc)
        self.sums[...] = jnp.zeros_like(self.sums)
        for c in self.fetch(jnp.int32(0)):
            c.start()

    def run(self, first, last):
        def step(i, carry):
            @pl.when(i + 1 < self.count)
            def _():
                for c in self.fetch(i + 1):
                    c.start()

            for c in self.fetch(i):
                c.wait()
            slot = lax.rem(i, 2)
            a, b = self.abuf[slot], self.bbuf[slot]
            self.acc[...] += lax.dot_general(
                a, b, (((0,), (0,)), ((), ())), preferred_element_type=jnp.float32
            )
            self.sums[...] += jnp.sum(b.astype(jnp.float32), 0, keepdims=True)
            return carry

        lax.fori_loop(first, last, step, 0)

    def end(self):
        self.grad[...] = self.acc[...].astype(self.grad.dtype)


def side_parts(side, count):
    if side is None:
        return [], [], [], [], []
    a, b = side
    h = a.shape[0] // count
    low = jnp.bfloat16
    hbm = pl.BlockSpec(memory_space=pl.ANY)
    vmem = pl.BlockSpec(memory_space=pltpu.VMEM)
    return (
        [x.reshape(count, h, x.shape[1]) for x in (a, b)],
        [
            jax.ShapeDtypeStruct((a.shape[1], b.shape[1]), low),
            jax.ShapeDtypeStruct((1, b.shape[1]), jnp.float32),
        ],
        [hbm, hbm],
        [vmem, vmem],
        [
            pltpu.VMEM((a.shape[1], b.shape[1]), jnp.float32),
            pltpu.VMEM((2, h, a.shape[1]), low),
            pltpu.VMEM((2, h, b.shape[1]), low),
            pltpu.SemaphoreType.DMA((2, 2)),
        ],
    )


def scatter_order(n):
    bits = route_bits(n)
    orders = [bits, bits[::-1]]
    lists = [
        sorted(range(0, n, 2), key=lambda k: [-int(bool(k & b)) for b in order]) for order in orders
    ]
    return orders, [(half, lists[half][i]) for i in range(n // 2) for half in (0, 1)]


def scatter_kernel(n, h, body, n_in, n_const, n_out, modes, nf, same, has_side, has_norm, carried, *refs):
    if carried:
        out = 1 + n_in + n_const + 2 * has_side + min(nf, 1) + 1 + n_out + 2 * has_side + min(nf, 1)
        refs = refs[1:out] + refs[out + 1 :]
    if has_norm:
        out = n_in + 3 + n_const + 2 * has_side + min(nf, 1)
        values, gain, joins = refs[:3]
        x_grad, g_grad, b_grad = refs[out], refs[out + 1], refs[out + 2]
        refs = refs[3:out] + (None,) + refs[out + 3 :]
    side = None
    if has_side:
        at = n_in + n_const
        out = at + 2 + min(nf, 1) + 1 + n_out
        extra = refs[at : at + 2] + refs[out : out + 2] + refs[-4:]
        refs = refs[:at] + refs[at + 2 : out] + refs[out + 2 : -4]
        side = Side(2 * n, extra)
    refs, rider = split_rider(refs, nf, same, n_in + n_const, 1 + n_out)
    ins = refs[:n_in]
    consts = refs[n_in : n_in + n_const]
    at = n_in + n_const
    sum_ref = refs[at]
    outs = refs[at + 1 : at + 1 + n_out]
    at += 1 + n_out
    give, pair, own, far, total = refs[at : at + 5]
    at += 5
    loads = refs[at : at + n_in]
    stages = refs[at + n_in : at + n_in + n_out]
    pair_send, pair_recv, far_send, far_recv, load, store, done = refs[at + n_in + n_out :]
    me = lax.axis_index("seq")
    orders, entries = scatter_order(n)
    bits = orders[0]
    slots = give.shape[0]
    index = {e: j for j, e in enumerate(entries)}

    def device(b):
        return {"seq": flip(me, b)}

    def phase_of(half, k):
        for i, b in enumerate(orders[half]):
            if k & b:
                return i
        return len(bits)

    landing = {}
    for half in (0, 1):
        for i, b in enumerate(orders[half]):
            for k in range(0, n, 2):
                if phase_of(half, k) == i:
                    landing[half, i, k ^ b] = len(landing)

    halves = [e[0] for e in entries]
    ks = [e[1] for e in entries]

    def spot(q, relative):
        j = lax.div(q, 2)
        k = pick(ks, j)
        k = jnp.where(lax.rem(q, 2) == 0, flip(k, 1), k)
        return 2 * (k if relative else place(me, k, n)) + pick(halves, j)

    def fetch(q):
        slot = lax.rem(q, 2)
        return [
            pltpu.make_async_copy(ins[i].at[spot(q, modes[0][i])], loads[i].at[slot], load.at[i, slot])
            for i in range(n_in)
        ]

    def output(o, q):
        slot = lax.rem(q, 2)
        return pltpu.make_async_copy(stages[o].at[slot], outs[o].at[spot(q, modes[1][o])], store.at[o, slot])

    def hand(j):
        slot = lax.rem(j, slots)
        return remote(give.at[slot], pair.at[j], pair_send.at[j], pair_recv.at[j], device(1))

    def launch(half, k):
        i = phase_of(half, k)
        b = orders[half][i]
        to = landing[half, i, k ^ b]
        return remote(own.at[index[half, k]], far.at[to], far_send.at[to], far_recv.at[to], device(b))

    def join(j):
        hand(j).wait_recv()
        own[j] = (own[j].astype(jnp.float32) + pair[j].astype(jnp.float32)).astype(own.dtype)
        for e, (half, k) in enumerate(entries):
            if phase_of(half, k) == 0:

                @pl.when(j == e)
                def _(half=half, k=k):
                    launch(half, k).start()

    for c in fetch(jnp.int32(0)):
        c.start()
    greet([device(b) for b in [1] + bits] + (rider.peers() if nf else []))
    if nf:
        rider.start()

    def step(q, carry):
        j = lax.div(q, 2)
        slot = lax.rem(q, 2)

        @pl.when(q + 1 < 2 * n)
        def _():
            for c in fetch(q + 1):
                c.start()

        for c in fetch(q):
            c.wait()
        part, *results = body(*[r[slot] for r in loads], *consts)
        for o in range(n_out):

            @pl.when(q >= 2)
            def _(o=o):
                output(o, q).wait()

            stages[o][slot] = results[o]
            output(o, q).start()

        @pl.when(slot == 0)
        def _():
            @pl.when(j >= slots)
            def _():
                hand(j - slots).wait_send()

            give[lax.rem(j, slots)] = part.astype(give.dtype)
            hand(j).start()

        @pl.when(slot == 1)
        def _():
            own[j] = part.astype(own.dtype)

            @pl.when(j >= 1)
            def _():
                join(j - 1)

        return carry

    lax.fori_loop(0, 2 * n, step, 0)
    if side:
        side.begin()
    join(jnp.int32(n - 1))
    first = n // 2
    cuts = [0, first] + [first + (2 * n - first) * i // (len(bits) - 1) for i in range(1, len(bits))]
    for i in range(len(bits)):
        if side:
            side.run(cuts[i], cuts[i + 1])
        for half in (0, 1):
            order = orders[half]
            for k in [k for hh, k in entries if hh == half and phase_of(half, k) > i]:
                to = landing[half, i, k]
                remote(far.at[to], far.at[to], far_send.at[to], far_recv.at[to], device(1)).wait_recv()
                j = index[half, k]
                rows = pl.ds(half * h, h)
                if i == len(bits) - 1:
                    total[rows] = own[j].astype(jnp.float32) + far[to].astype(jnp.float32)
                    if not has_norm:
                        pltpu.make_async_copy(total.at[rows], sum_ref.at[rows], done.at[half]).start()
                else:
                    own[j] = (own[j].astype(jnp.float32) + far[to].astype(jnp.float32)).astype(own.dtype)
                    if phase_of(half, k) == i + 1:
                        launch(half, k).start()
    if has_norm:
        g_grad[...] = jnp.zeros_like(g_grad)
        b_grad[...] = jnp.zeros_like(b_grad)

        def tile(i, carry):
            rows = pl.ds(pl.multiple_of(i * 64, 64), 64)
            x = values[rows].astype(jnp.float32)
            centred = x - jnp.mean(x, -1, keepdims=True)
            scale = lax.rsqrt(jnp.mean(centred * centred, -1, keepdims=True) + 1e-05)
            xhat = centred * scale
            grad = total[rows]
            g_grad[...] += jnp.sum(grad * xhat, 0, keepdims=True)
            b_grad[...] += jnp.sum(grad, 0, keepdims=True)
            e = gain[...] * grad
            inner = e - jnp.mean(e, -1, keepdims=True) - xhat * jnp.mean(e * xhat, -1, keepdims=True)
            x_grad[rows] = (joins[rows].astype(jnp.float32) + scale * inner).astype(x_grad.dtype)
            return carry

        lax.fori_loop(0, 2 * h // 64, tile, 0)
    for half in (0, 1) if not has_norm else ():
        rows = pl.ds(half * h, h)
        pltpu.make_async_copy(total.at[rows], sum_ref.at[rows], done.at[half]).wait()
    for q in (2 * n - 2, 2 * n - 1):
        for o in range(n_out):
            output(o, jnp.int32(q)).wait()
    for j in range(max(n - slots, 0), n):
        hand(jnp.int32(j)).wait_send()
    for half, k in entries:
        if phase_of(half, k) < len(bits):
            launch(half, k).wait_send()
    if nf:
        rider.finish()
    if side:
        side.end()


def seq_scatter(n, cols, ident, name, body, ins, consts, outs=(), modes=None, rider=None, side=None, norm=None, carry=None):
    h = ins[0].shape[0] // (2 * n)
    low = jnp.bfloat16
    slots = min(4, n)
    split = [a.reshape(2 * n, h, a.shape[1]) for a in ins]
    vmem = pl.BlockSpec(memory_space=pltpu.VMEM)
    hbm = pl.BlockSpec(memory_space=pl.ANY)
    reach = n - 2
    modes = modes or ([0] * len(ins), [0] * len(outs))
    more, spec, shape, scratch, nf, same = rider_parts(rider)
    s_ins, s_shapes, s_in_specs, s_out_specs, s_scratch = side_parts(side, 2 * n)
    sums = [jax.ShapeDtypeStruct((2 * h, cols), jnp.float32)]
    norms = []
    carries = [] if carry is None else [carry]
    if norm is not None:
        norms = list(norm[:3])
        line = jax.ShapeDtypeStruct((1, cols), jnp.float32)
        sums = [jax.ShapeDtypeStruct((2 * h, cols), norm[3]), line, line]
    out = pl.pallas_call(
        functools.partial(
            scatter_kernel, n, h, body, len(ins), len(consts), len(outs), modes, nf, same, int(side is not None), norm is not None, carry is not None
        ),
        out_shape=sums
        + [jax.ShapeDtypeStruct((2 * n, h, c), d) for c, d in outs]
        + s_shapes
        + shape
        + [jax.ShapeDtypeStruct(x.shape, x.dtype) for x in carries],
        in_specs=[hbm] * len(carries)
        + [vmem] * len(norms)
        + [hbm] * len(ins)
        + [vmem] * len(consts)
        + s_in_specs
        + spec,
        out_specs=([vmem] * 3 if norms else [hbm])
        + [hbm] * len(outs)
        + s_out_specs
        + spec
        + [hbm] * len(carries),
        input_output_aliases={0: len(sums + list(outs) + s_shapes + shape)} if carries else {},
        scratch_shapes=[
            pltpu.VMEM((slots, h, cols), low),
            pltpu.VMEM((n, h, cols), low),
            pltpu.VMEM((n, h, cols), low),
            pltpu.VMEM((reach, h, cols), low),
            pltpu.VMEM((2 * h, cols), jnp.float32),
        ]
        + [pltpu.VMEM((2, h, a.shape[2]), a.dtype) for a in split]
        + [pltpu.VMEM((2, h, c), d) for c, d in outs]
        + [
            pltpu.SemaphoreType.DMA((n,)),
            pltpu.SemaphoreType.DMA((n,)),
            pltpu.SemaphoreType.DMA((reach,)),
            pltpu.SemaphoreType.DMA((reach,)),
            pltpu.SemaphoreType.DMA((len(ins), 2)),
            pltpu.SemaphoreType.DMA((max(len(outs), 1), 2)),
            pltpu.SemaphoreType.DMA((2,)),
        ]
        + scratch
        + s_scratch,
        compiler_params=pltpu.CompilerParams(
            collective_id=ident, has_side_effects=True, vmem_limit_bytes=60 << 20
        ),
        cost_estimate=SMALL,
        name=name,
    )(*carries, *norms, *split, *consts, *s_ins, *more)
    lines = list(out[1:3]) if norms else []
    out = [out[0]] + list(out[1 + len(lines) :])
    many = 1 + len(outs)
    sides = [] if side is None else list(out[many : many + 2])
    more = list(out[many + len(sides) :])
    return [out[0]] + lines + [o.reshape(2 * n * h, o.shape[2]) for o in out[1:many]] + sides + more


class Rows:
    def __init__(self, n, held, width, wide, back):
        moves = []
        for to in range(n):
            for third in range(3):
                at, end = third * width + to * wide, third * width + min((to + 1) * wide, width)
                row = third * wide
                while at < end:
                    source = at // held
                    count = min(end, (source + 1) * held) - at
                    moves.append((source, at - source * held, to, row, count))
                    at, row = at + count, row + count
        self.n = n
        self.moves = [(c, d, a, b, e) if back else (a, b, c, d, e) for a, b, c, d, e in moves]
        self.out = [[m for m in self.moves if m[0] == i] for i in range(n)]
        self.into = [[m for m in self.moves if m[2] == i] for i in range(n)]
        self.most = max(len(v) for v in self.out + self.into)

    def scratch(self):
        dma = pltpu.SemaphoreType.DMA
        return [dma((self.most,)), dma((self.most,)), dma((self.most,))]

    def bind(self, source, target, send, recv, local):
        self.source, self.target, self.send, self.recv, self.local = source, target, send, recv, local
        return self

    def copy(self, i, m):
        src = self.source.at[pl.ds(m[1], m[4])]
        dst = self.target.at[pl.ds(m[3], m[4])]
        if m[0] == m[2]:
            return pltpu.make_async_copy(src, dst, self.local.at[i])
        return remote(src, dst, self.send.at[i], self.recv.at[self.into[m[2]].index(m)], {"seq": m[2]})

    def start(self):
        me = lax.axis_index("seq")
        for s in range(self.n):

            @pl.when(me == s)
            def _(s=s):
                for i, m in enumerate(self.out[s]):
                    self.copy(i, m).start()

    def finish(self):
        me = lax.axis_index("seq")
        for s in range(self.n):

            @pl.when(me == s)
            def _(s=s):
                for i, m in enumerate(self.into[s]):
                    if m[0] != s:
                        dst = self.target.at[pl.ds(m[3], m[4])]
                        remote(dst, dst, self.send.at[0], self.recv.at[i], {"seq": s}).wait_recv()
                for i, m in enumerate(self.out[s]):
                    if m[0] == m[2]:
                        self.copy(i, m).wait()
                    else:
                        self.copy(i, m).wait_send()


class Units:
    def __init__(self, n, nf, back, source, target, send, recv, local):
        self.n, self.nf, self.back = n, nf, back
        self.source, self.target, self.send, self.recv, self.local = source, target, send, recv, local
        self.me = lax.axis_index("seq")

    @staticmethod
    def scratch(nf):
        dma = pltpu.SemaphoreType.DMA
        return [dma((nf,)), dma((nf,)), dma]

    def ends(self, i):
        group = self.n // self.nf
        if self.back:
            return i * group + lax.div(self.me, self.nf), lax.rem(self.me, self.nf)
        return lax.rem(self.me, group) * self.nf + i, lax.div(self.me, group)

    def comes(self, i):
        group = self.n // self.nf
        if self.back:
            return lax.rem(self.me, group) * self.nf + i
        return i * group + lax.div(self.me, self.nf)

    def each(self, i, there, here):
        to, slot = self.ends(i)

        @pl.when(to != self.me)
        def _():
            there(remote(self.source.at[i], self.target.at[slot], self.send.at[i], self.recv.at[slot], {"seq": to}))

        @pl.when(to == self.me)
        def _():
            here(pltpu.make_async_copy(self.source.at[i], self.target.at[slot], self.local))

    def start(self):
        for i in range(self.nf):
            self.each(i, lambda c: c.start(), lambda c: c.start())

    def finish(self):
        for i in range(self.nf):
            source = self.comes(i)

            @pl.when(source != self.me)
            def _(i=i):
                dst = self.target.at[i]
                remote(dst, dst, self.send.at[0], self.recv.at[i], {"seq": self.me}).wait_recv()

        for i in range(self.nf):
            self.each(i, lambda c: c.wait_send(), lambda c: c.wait())


def all_peers(n, nf):
    me, f = lax.axis_index("seq"), lax.axis_index("fsdp")
    return [{"seq": place(me, r, n)} for r in range(1, n)] + [
        {"fsdp": lax.rem(f + d, nf)} for d in range(1, nf)
    ]


def exchange_kernel(n, nf, rows, count, *refs):
    ins, outs, sems = refs[: 4 + count], refs[4 + count : 8 + 2 * count], list(refs[8 + 2 * count :])
    take = lambda k: [sems.pop(0) for _ in range(k)]
    parts = []
    if rows is not None:
        parts.append(rows.bind(ins[0], outs[0], *take(3)))
    vectors = [Blocks("fsdp", nf, True, ins[4 + i], outs[4 + i], *take(3)) for i in range(count)]
    later = [
        Blocks("fsdp", nf, True, ins[3], outs[3], *take(3)),
        Units(n, nf, False, ins[2], outs[2], *take(3)),
        Blocks("seq", n, False, ins[1], outs[1], *take(3)),
    ]
    parts = vectors + parts + later
    greet(all_peers(n, nf))
    for p in parts:
        p.start()
    for p in parts:
        p.finish()


def exchange(w, p, c, o, vectors, n, nf, rows, wide, ident):
    hbm = pl.BlockSpec(memory_space=pl.ANY)
    count = len(vectors)
    out = pl.pallas_call(
        functools.partial(exchange_kernel, n, nf, rows, count),
        out_shape=[
            jax.ShapeDtypeStruct((3 * wide, w.shape[1]) if rows is not None else w.shape, w.dtype),
            blocks_shape(p, n, False),
            blocks_shape(c, nf, False),
            blocks_shape(o, nf, True),
        ]
        + [blocks_shape(v, nf, True) for v in vectors],
        in_specs=[hbm] * (4 + count),
        out_specs=[hbm] * (4 + count),
        scratch_shapes=(rows.scratch() if rows is not None else [])
        + sum([Blocks.scratch(nf) for _ in vectors], [])
        + Blocks.scratch(nf)
        + Units.scratch(nf)
        + Blocks.scratch(n),
        compiler_params=pltpu.CompilerParams(collective_id=ident, has_side_effects=True),
        cost_estimate=SMALL,
        name="exchange",
    )(w, p, c, o, *vectors)
    return out[0], out[1], out[2], out[3], out[4:]


def to_tokens_kernel(n, wide, x_ref, o_ref, send, recv, local):
    me = lax.axis_index("seq")

    def target(i):
        return o_ref.at[:, pl.ds(pl.multiple_of(i * wide, 128), wide)]

    greet([{"seq": place(me, r, n)} for r in range(1, n)])
    copies = []
    for r in range(n - 1, 0, -1):
        to = place(me, r, n)
        c = remote(x_ref.at[to], target(me), send.at[r - 1], recv.at[r - 1], {"seq": to})
        c.start()
        copies.append(c)
    mine = pltpu.make_async_copy(x_ref.at[me], target(me), local)
    mine.start()
    for r in range(1, n):
        dst = target(place(me, r, n))
        remote(dst, dst, send.at[0], recv.at[r - 1], {"seq": place(me, r, n)}).wait_recv()
    mine.wait()
    for c in copies:
        c.wait_send()


def to_tokens(x, n, wide, ident):
    rows = x.shape[1]
    hbm = pl.BlockSpec(memory_space=pl.ANY)
    return pl.pallas_call(
        functools.partial(to_tokens_kernel, n, wide),
        out_shape=jax.ShapeDtypeStruct((rows, n * wide), x.dtype),
        in_specs=[hbm],
        out_specs=hbm,
        scratch_shapes=Blocks.scratch(n),
        compiler_params=pltpu.CompilerParams(collective_id=ident, has_side_effects=True),
        cost_estimate=SMALL,
        name="to_tokens",
    )(x)


def to_heads_kernel(
    n, nf, wide, x_ref, w_ref, t_ref, a_ref, b_ref, z_ref, o_ref, g_ref, m_ref, z_out, t_out, made, *extra
):
    me = lax.axis_index("seq")
    send, recv, local = extra[:3]
    side = Side(2 * n, (a_ref, b_ref, g_ref, m_ref) + extra[3:7])
    planes = PlaneSum(nf, z_ref, 0, *extra[7:])
    side.begin()
    greet([{"seq": place(me, r, n)} for r in range(1, n)] + planes.peers())
    planes.start()

    def copy(r):
        to = place(me, r, n)
        return remote(made.at[r], o_ref.at[me], send.at[r - 1], recv.at[r - 1], {"seq": to})

    def mine():
        return pltpu.make_async_copy(made.at[0], o_ref.at[me], local)

    def step(i, carry):
        r = n - 1 - i
        at = place(me, r, n)
        whole, rest = w_ref.shape[1] // wide, w_ref.shape[1] % wide

        @pl.when(at < whole)
        def _():
            lanes = pl.ds(pl.multiple_of(at * wide, 128), wide)
            made[r] = mm(x_ref[...], w_ref[:, lanes]).astype(made.dtype)

        @pl.when(at >= whole)
        def _():
            made[r] = jnp.zeros(made.shape[1:], made.dtype)

        if rest:

            @pl.when(at == whole)
            def _():
                made[r, :, :rest] = mm(x_ref[...], w_ref[:, whole * wide :]).astype(made.dtype)

        @pl.when(r > 0)
        def _():
            copy(r).start()

        return carry

    lax.fori_loop(0, n, step, 0)
    mine().start()
    side.run(0, 2 * n)
    cols = t_out.shape[0]
    for at in range(0, cols, 512):
        end = min(at + 512, cols)
        t_out[at:end] = lax.dot_general(
            x_ref[:, at:end], t_ref[...], (((0,), (0,)), ((), ())), preferred_element_type=jnp.float32
        ).astype(t_out.dtype)
    side.end()
    planes.finish()
    planes.store(z_out)
    for r in range(1, n):
        dst = o_ref.at[place(me, r, n)]
        remote(dst, dst, send.at[0], recv.at[r - 1], {"seq": me}).wait_recv()
    mine().wait()
    for r in range(1, n):
        copy(r).wait_send()


def to_heads(x, w, t, n, nf, wide, ident, a, b, z, count):
    rows, cols = x.shape
    vmem = pl.BlockSpec(memory_space=pltpu.VMEM)
    hbm = pl.BlockSpec(memory_space=pl.ANY)
    s_ins, s_shapes, s_in_specs, s_out_specs, s_scratch = side_parts((a, b), 2 * n)
    return pl.pallas_call(
        functools.partial(to_heads_kernel, n, nf, wide),
        out_shape=[jax.ShapeDtypeStruct((n, rows, wide), x.dtype)]
        + s_shapes
        + [
            jax.ShapeDtypeStruct((n, count, z.shape[2] // n), z.dtype),
            jax.ShapeDtypeStruct((cols, t.shape[1]), x.dtype),
        ],
        in_specs=[vmem, vmem, vmem] + s_in_specs + [hbm],
        out_specs=[hbm] + s_out_specs + [vmem, vmem],
        scratch_shapes=[pltpu.VMEM((n, rows, wide), x.dtype)]
        + Blocks.scratch(n)
        + s_scratch
        + PlaneSum.scratch(nf, count, z.shape[2]),
        compiler_params=pltpu.CompilerParams(
            collective_id=ident, has_side_effects=True, vmem_limit_bytes=60 << 20
        ),
        cost_estimate=SMALL,
        name="to_heads",
    )(x, w, t, *s_ins, z)


def contract_kernel(
    n, nf, a_ref, b_ref, x_ref, y_ref, s_ref, p_ref, q_ref, c_ref, o_ref, sum_ref, p_out, q_out, c_out, acc, *sems
):
    i = pl.program_id(0)
    parts = [
        Blocks("seq", n, False, p_ref, p_out, *sems[:3]),
        Blocks("seq", n, False, q_ref, q_out, *sems[3:6]),
        Units(n, nf, True, c_ref, c_out, *sems[6:]),
    ]

    @pl.when(i == 0)
    def _():
        me = lax.axis_index("seq")
        greet([{"seq": place(me, r, n)} for r in range(1, n)])
        for part in parts:
            part.start()

    sum_ref[...] = (x_ref[...] + y_ref[...].astype(jnp.float32) + s_ref[...]).astype(sum_ref.dtype)
    part = lax.dot_general(
        a_ref[...], b_ref[...], (((0,), (0,)), ((), ())), preferred_element_type=jnp.float32
    )

    @pl.when(i == 0)
    def _():
        acc[...] = part

    @pl.when(i > 0)
    def _():
        acc[...] += part

    @pl.when(i == pl.num_programs(0) - 1)
    def _():
        o_ref[...] = acc[...].astype(o_ref.dtype)
        for part in parts:
            part.finish()


def contract(a, b, x, y, s, p, q, c, n, nf, tile, ident):
    steps = a.shape[0] // tile
    shape = (a.shape[1], b.shape[1])
    still = lambda s: pl.BlockSpec(s, lambda i: (0,) * len(s), pipeline_mode=pl.Buffered(1))
    part = lambda v: pl.BlockSpec((v.shape[0] // steps, v.shape[1]), lambda i: (i, 0))
    hbm = pl.BlockSpec(memory_space=pl.ANY)
    return pl.pallas_call(
        functools.partial(contract_kernel, n, nf),
        out_shape=[
            jax.ShapeDtypeStruct(shape, a.dtype),
            jax.ShapeDtypeStruct(x.shape, a.dtype),
            blocks_shape(p, n, False),
            blocks_shape(q, n, False),
            blocks_shape(c, nf, False),
        ],
        grid=(steps,),
        in_specs=[part(a), part(b), part(x), part(y), still(s.shape), hbm, hbm, hbm],
        out_specs=[still(shape), part(x), hbm, hbm, hbm],
        scratch_shapes=[pltpu.VMEM(shape, jnp.float32)]
        + Blocks.scratch(n)
        + Blocks.scratch(n)
        + Units.scratch(nf),
        compiler_params=pltpu.CompilerParams(
            dimension_semantics=("arbitrary",),
            vmem_limit_bytes=40 << 20,
            collective_id=ident,
            has_side_effects=True,
        ),
        cost_estimate=SMALL,
        name="contract",
    )(a, b, x, y, s, p, q, c)


def give_back_kernel(
    n, nf, rows, v_ref, w_ref, o_ref, v_out, w_out, o_out, planes, sums, *sems
):
    s = lax.axis_index("seq")
    f = lax.axis_index("fsdp")
    sems = list(sems)
    take = lambda k: [sems.pop(0) for _ in range(k)]
    send_z, recv_z, send_s, recv_s = take(4)
    parts = []
    if rows is not None:
        parts.append(rows.bind(w_ref, w_out, *take(3)))
    parts.append(Blocks("fsdp", nf, False, o_ref, o_out, *take(3)))
    others = [{"fsdp": lax.rem(f + d, nf)} for d in range(1, nf)]
    peers = [{"seq": place(s, r, n)} for r in range(1, n)]
    greet(peers + others)
    copies = []
    for d in range(1, nf):
        c = remote(v_ref.at[lax.rem(f + d, nf)], planes.at[d - 1], send_z.at[d - 1], recv_z.at[d - 1], others[d - 1])
        c.start()
        copies.append(c)
    for p in parts:
        p.start()
    total = v_ref[f]
    for d, c in enumerate(copies):
        c.wait_recv()
        total = total + planes[d]
    sums[0] = total
    spread = []
    for r in range(1, n):
        c = remote(sums.at[0], sums.at[r], send_s.at[r - 1], recv_s.at[r - 1], peers[r - 1])
        c.start()
        spread.append(c)
    for r, c in enumerate(spread):
        c.wait_recv()
        total = total + sums[r + 1]
    v_out[...] = total
    for p in parts:
        p.finish()
    for c in copies + spread:
        c.wait_send()


def give_back(vectors, w, held, o, n, nf, rows, ident):
    k = vectors.shape[1]
    tiles = -(-k // 1024) * 8
    padded = jnp.pad(vectors, ((0, 0), (0, tiles * 128 - k))).reshape(nf, tiles, 128)
    vmem = pl.BlockSpec(memory_space=pltpu.VMEM)
    hbm = pl.BlockSpec(memory_space=pl.ANY)
    dma = pltpu.SemaphoreType.DMA
    out = pl.pallas_call(
        functools.partial(give_back_kernel, n, nf, rows),
        out_shape=[
            jax.ShapeDtypeStruct((tiles, 128), jnp.float32),
            jax.ShapeDtypeStruct((held, w.shape[1]), w.dtype),
            blocks_shape(o, nf, False),
        ],
        in_specs=[vmem, hbm, hbm],
        out_specs=[vmem, hbm, hbm],
        scratch_shapes=[
            pltpu.VMEM((nf - 1, tiles, 128), jnp.float32),
            pltpu.VMEM((n, tiles, 128), jnp.float32),
            dma((nf - 1,)),
            dma((nf - 1,)),
            dma((n - 1,)),
            dma((n - 1,)),
        ]
        + (rows.scratch() if rows is not None else [])
        + Blocks.scratch(nf),
        compiler_params=pltpu.CompilerParams(collective_id=ident, has_side_effects=True),
        cost_estimate=SMALL,
        name="give_back",
    )(padded, w, o)
    return (out[0].reshape(-1)[:k],) + tuple(out[1:])


HEAD=64
SCALE=0.125*math.log2(math.e)


def block_pairs(slots, trunk):
    branches = (slots - trunk) // 3
    pairs = []
    for t in range(slots):
        m = t - trunk
        if t < trunk:
            keys = [(c, int(c == t), -1, -1) for c in range(t + 1)]
        else:
            keys = [(c, 0, -1, -1) for c in range(trunk)]
            if m >= branches:
                keys.append((trunk, 0, -1, m))
            keys.append((t, 1, m, -1))
        for i, (c, causal, own, leaf) in enumerate(keys):
            pairs.append((t, c, causal, own, leaf, int(i == 0), int(i == len(keys) - 1)))
    return pairs


def block_fields(p, slots, trunk):
    branches = (slots - trunk) // 3
    counts = [t + 1 for t in range(trunk)] + [trunk + 1] * branches
    counts += [trunk + 2] * (slots - trunk - branches)
    starts = [sum(counts[:t]) for t in range(slots)]
    t, begin, end = jnp.int32(0), jnp.int32(0), jnp.int32(counts[0])
    for i in range(1, slots):
        here = p >= starts[i]
        t = jnp.where(here, i, t)
        begin = jnp.where(here, starts[i], begin)
        end = jnp.where(here, starts[i] + counts[i], end)
    i = p - begin
    last = p == end - 1
    leaf = (t >= trunk + branches) & (i == trunk)
    key = jnp.where((t >= trunk) & last, t, i)
    return t, key, last, leaf, i == 0, last


def block_values(lengths, parents, pairs, block):
    count = lengths.shape[0]
    segments = np.arange(count)
    own = np.array([p[3] for p in pairs])[None, :] == segments[:, None]
    leaf = np.array([p[4] for p in pairs])[None, :] == segments[:, None]
    above = jnp.sum(jnp.where(leaf, parents[:, None], 0), 0)
    source = own | (segments[:, None] + 1 == above[None, :])
    closed = np.array([p[3] < 0 and p[4] < 0 for p in pairs])
    reach = jnp.where(closed, block, jnp.sum(jnp.where(source, lengths[:, None], 0), 0))
    return jnp.stack([jnp.maximum(above - 1, 0), reach]).astype(jnp.int32)


def lane_half(shape):
    return lax.broadcasted_iota(jnp.int32, shape, len(shape) - 1) < HEAD


def nt(a, b):
    return lax.dot_general(a, b, (((1,), (1,)), ((), ())), preferred_element_type=jnp.float32)


def mm(a, b):
    return jnp.dot(a, b, preferred_element_type=jnp.float32)


def attend_kernel(width, block, trunk, n, values, x_ref, w_ref, b_ref, c_ref, qkv, low, att, tot, kt, c_all, acc, xbuf, xsem, *sems):
    p = pl.program_id(0)
    slot, key, causal, leaf, first, last = block_fields(p, n, trunk)
    rows = lambda slot: pl.ds(pl.multiple_of(slot * block, block), block)
    qrow = rows(slot)
    above = values[0, p]
    reach = values[1, p]
    branches = (n - trunk) // 3
    left = lane_half((block, 2 * HEAD))
    spread = Spread(n, c_ref, c_all, *sems)

    def fetch(i):
        slot = lax.rem(i, 2)
        return pltpu.make_async_copy(x_ref.at[i], xbuf.at[slot], xsem.at[slot])

    @pl.when(p == 0)
    def _():
        fetch(jnp.int32(0)).start()
        greet(spread.peers())
        spread.start()

        def step(i, carry):
            @pl.when(i + 1 < n)
            def _():
                fetch(i + 1).start()

            fetch(i).wait()
            made = (mm(xbuf[lax.rem(i, 2)], w_ref[...]) + b_ref[...]).astype(qkv.dtype)
            qkv[rows(i)] = made
            kt[:, rows(i)] = made[:, width : 2 * width].T
            return carry

        lax.fori_loop(0, n, step, 0)
        for i in range(len(spread.bits) - 1):
            spread.phase(i)

    @pl.when(first)
    def _():
        acc[...] = jnp.zeros_like(acc)

    def keyed(mask, read):
        got = read(rows(key))
        if mask is not None:
            for b in range(1, branches):
                got = jnp.where(leaf & (above == b), read(pl.ds((trunk + b) * block, block)), got)
        return got

    def step(mask):
        for j in range(width // (2 * HEAD)):
            lanes = slice(j * 2 * HEAD, (j + 1) * 2 * HEAD)
            q = qkv[qrow, lanes]
            k = keyed(mask, lambda at: qkv[at, width + j * 2 * HEAD : width + (j + 1) * 2 * HEAD])
            v = keyed(mask, lambda at: qkv[at, 2 * width + j * 2 * HEAD : 2 * width + (j + 1) * 2 * HEAD])
            for h in range(2):
                here = left if h == 0 else jnp.logical_not(left)
                s = nt(jnp.where(here, q, 0), k)
                e = jnp.exp2(s * SCALE)
                if mask is not None:
                    e = jnp.where(mask, e, 0.0)
                acc[2 * j + h] += mm(e.astype(jnp.bfloat16), jnp.where(here, v, 1))

    closes = causal | leaf
    shift = jnp.where(causal, 0, block)

    @pl.when(jnp.logical_not(closes))
    def _():
        step(None)

    @pl.when(closes)
    def _():
        row = lax.broadcasted_iota(jnp.int32, (block, block), 0)
        col = lax.broadcasted_iota(jnp.int32, (block, block), 1)
        step((col <= row + shift) & (col < reach))

    @pl.when(last)
    def _():
        for j in range(width // (2 * HEAD)):
            a, b = acc[2 * j], acc[2 * j + 1]
            total = jnp.where(left, pltpu.roll(a, HEAD, 1), pltpu.roll(b, HEAD, 1))
            value = jnp.where(left, a, b) / total
            lanes = slice(j * 2 * HEAD, (j + 1) * 2 * HEAD)
            low[:, lanes] = value.astype(jnp.bfloat16)
            att[:, lanes] = value
            tot[:, lanes] = total

    @pl.when(p == pl.num_programs(0) - 4)
    def _():
        spread.phase(len(spread.bits) - 1)

    @pl.when(p == pl.num_programs(0) - 1)
    def _():
        spread.finish()


def attend(values, pairs, x, w, bias, block, trunk, sent, n, ident):
    rows, width = x.shape[0], w.shape[1] // 3
    by_q = lambda p: (block_fields(p, n, trunk)[0], 0)
    heads = width // HEAD
    once = lambda s: pl.BlockSpec(s, lambda p: (0,) * len(s), pipeline_mode=pl.Buffered(1))
    hbm = pl.BlockSpec(memory_space=pl.ANY)
    out = pl.pallas_call(
        functools.partial(attend_kernel, width, block, trunk, n),
        grid=(len(pairs),),
        out_shape=(
            jax.ShapeDtypeStruct((rows, 3 * width), x.dtype),
            jax.ShapeDtypeStruct((rows, width), x.dtype),
            jax.ShapeDtypeStruct((rows, width), jnp.float32),
            jax.ShapeDtypeStruct((rows, width), jnp.float32),
            jax.ShapeDtypeStruct((width, rows), x.dtype),
            jax.ShapeDtypeStruct((n,) + sent.shape, sent.dtype),
        ),
        in_specs=[pl.BlockSpec(memory_space=pltpu.SMEM), hbm, once(w.shape), once(bias.shape), hbm],
        out_specs=[once((rows, 3 * width))]
        + [pl.BlockSpec((block, width), by_q)] * 3
        + [once((width, rows)), hbm],
        scratch_shapes=[
            pltpu.VMEM((heads, block, 2 * HEAD), jnp.float32),
            pltpu.VMEM((2, block, x.shape[1]), x.dtype),
            pltpu.SemaphoreType.DMA((2,)),
        ]
        + Spread.scratch(n),
        compiler_params=pltpu.CompilerParams(
            dimension_semantics=("arbitrary",),
            vmem_limit_bytes=60 << 20,
            collective_id=ident,
            has_side_effects=True,
        ),
        cost_estimate=SMALL,
        name="attend",
    )(values, x.reshape(n, block, x.shape[1]), w, bias, sent)
    return out[:5] + (out[5].reshape(n * sent.shape[0], sent.shape[1]),)


def attend_back_kernel(width, block, slots, trunk, branches, nf, lows, *refs):
    count = len(lows)
    values, qkv, kt, datt, att, tot = refs[:6]
    sources = refs[6 : 6 + count]
    out, sums = refs[6 + count : 8 + count]
    parts = refs[8 + count : 8 + 2 * count]
    dk, dv, dqt, aug = refs[8 + 2 * count : 12 + 2 * count]
    rest = refs[12 + 2 * count :]
    riders = [PlaneSum(nf, sources[i], lows[i], *rest[4 * i : 4 * i + 4]) for i in range(count)]
    p = pl.program_id(0)
    slot, key, causal, leaf, first, last = block_fields(p, slots, trunk)
    rows = lambda slot: pl.ds(pl.multiple_of(slot * block, block), block)
    above = values[0, p]
    reach = values[1, p]
    qrow = rows(slot)
    left = lane_half((block, 2 * HEAD))
    lane = lax.broadcasted_iota(jnp.int32, (block, 2 * HEAD), 1)
    columns = width // (2 * HEAD)

    @pl.when(p == 0)
    def _():
        greet(riders[0].peers())
        for r in riders:
            r.start()
        dk[...] = jnp.zeros_like(dk)
        dv[...] = jnp.zeros_like(dv)

    @pl.when(first)
    def _():
        dqt[...] = jnp.zeros_like(dqt)
        for j in range(columns):
            lanes = slice(j * 2 * HEAD, (j + 1) * 2 * HEAD)
            d = datt[:, lanes].astype(jnp.float32)
            total = tot[:, lanes]
            low = (d / total).astype(jnp.bfloat16)
            prod = d * att[:, lanes] / total
            for h in range(2):
                here = left if h == 0 else jnp.logical_not(left)
                delta = -jnp.sum(jnp.where(here, prod, 0.0), 1, keepdims=True)
                hi = delta.astype(jnp.bfloat16).astype(jnp.float32)
                mid = (delta - hi).astype(jnp.bfloat16).astype(jnp.float32)
                rest = delta - hi - mid
                at = HEAD * (1 - h)
                extra = jnp.where(
                    lane == at, hi, jnp.where(lane == at + 1, mid, jnp.where(lane == at + 2, rest, 0.0))
                )
                aug[2 * j + h] = jnp.where(here, low.astype(jnp.float32), extra).astype(jnp.bfloat16)

    def add(mask, lanes, dks, dvs):
        at = rows(key)
        if mask is None:
            dk[at, lanes] += dks
            dv[at, lanes] += dvs
            return
        for b in range(branches):
            chosen = causal | (above == b) if b == 0 else leaf & (above == b)
            if b > 0:
                at = pl.ds((trunk + b) * block, block)
            dk[at, lanes] += jnp.where(chosen, dks, 0.0)
            dv[at, lanes] += jnp.where(chosen, dvs, 0.0)

    def keyed(mask, read):
        got = read(rows(key))
        if mask is not None:
            for b in range(1, branches):
                got = jnp.where(leaf & (above == b), read(pl.ds((trunk + b) * block, block)), got)
        return got

    def step(mask):
        for j in range(columns):
            lanes = slice(j * 2 * HEAD, (j + 1) * 2 * HEAD)
            q = qkv[qrow, lanes]
            k = keyed(mask, lambda at: qkv[at, width + j * 2 * HEAD : width + (j + 1) * 2 * HEAD])
            v = keyed(mask, lambda at: qkv[at, 2 * width + j * 2 * HEAD : 2 * width + (j + 1) * 2 * HEAD])
            dvs, dks = [], []
            for h in range(2):
                here = left if h == 0 else jnp.logical_not(left)
                qh = jnp.where(here, q, 0)
                e = jnp.exp2(nt(k, qh) * SCALE)
                if mask is not None:
                    e = jnp.where(mask, e, 0.0)
                dod = aug[2 * j + h]
                ds = (e * nt(jnp.where(here, v * 0.125, 0.125).astype(jnp.bfloat16), dod)).astype(
                    jnp.bfloat16
                )
                dvs.append(mm(e.astype(jnp.bfloat16), dod))
                dks.append(mm(ds, qh))
                at = j * 2 * HEAD + h * HEAD
                dqt[at : at + HEAD] += mm(keyed(mask, lambda i: kt[at : at + HEAD, i]), ds)
            add(mask, lanes, dks[0] + dks[1], jnp.where(left, dvs[0], dvs[1]))

    closes = causal | leaf
    shift = jnp.where(causal, 0, block)

    @pl.when(jnp.logical_not(closes))
    def _():
        step(None)

    @pl.when(closes)
    def _():
        col = lax.broadcasted_iota(jnp.int32, (block, block), 0)
        row = lax.broadcasted_iota(jnp.int32, (block, block), 1)
        step((col <= row + shift) & (col < reach))

    @pl.when(last)
    def _():
        out[qrow, 0:width] = dqt[...].T.astype(jnp.bfloat16)

    @pl.when(p == pl.num_programs(0) - 1)
    def _():
        out[:, width : 2 * width] = dk[...].astype(jnp.bfloat16)
        out[:, 2 * width :] = dv[...].astype(jnp.bfloat16)
        for t in range(3):
            lanes = slice(t * width, (t + 1) * width)
            sums[:, lanes] = jnp.sum(out[:, lanes].astype(jnp.float32), 0, keepdims=True)
        for r, made in zip(riders, parts):
            r.finish()
            r.store(made)


def attend_back(values, pairs, qkv, kt, datt, att, tot, block, trunk, nf, riders, ident):
    rows, width = qkv.shape[0], qkv.shape[1] // 3
    by_q = lambda p: (block_fields(p, rows // block, trunk)[0], 0)
    heads = width // HEAD
    branches = (rows // block - trunk) // 3
    made = [(k, z.shape[1] - at, z.shape[2] // k) for z, at, k in riders]
    once = lambda s: pl.BlockSpec(s, lambda p: (0,) * len(s), pipeline_mode=pl.Buffered(1))
    hbm = pl.BlockSpec(memory_space=pl.ANY)
    out = pl.pallas_call(
        functools.partial(
            attend_back_kernel, width, block, rows // block, trunk, branches, nf, [r[1] for r in riders]
        ),
        grid=(len(pairs),),
        out_shape=[
            jax.ShapeDtypeStruct((rows, 3 * width), jnp.bfloat16),
            jax.ShapeDtypeStruct((1, 3 * width), jnp.float32),
        ]
        + [jax.ShapeDtypeStruct(s, jnp.bfloat16) for s in made],
        in_specs=[pl.BlockSpec(memory_space=pltpu.SMEM), once((rows, 3 * width)), once((width, rows))]
        + [pl.BlockSpec((block, width), by_q)] * 3
        + [hbm] * len(riders),
        out_specs=[once((rows, 3 * width)), once((1, 3 * width))] + [once(s) for s in made],
        scratch_shapes=[
            pltpu.VMEM((rows, width), jnp.float32),
            pltpu.VMEM((rows, width), jnp.float32),
            pltpu.VMEM((width, block), jnp.float32),
            pltpu.VMEM((heads, block, 2 * HEAD), jnp.bfloat16),
        ]
        + sum([PlaneSum.scratch(nf, z.shape[1] - at, z.shape[2]) for z, at, k in riders], []),
        compiler_params=pltpu.CompilerParams(
            dimension_semantics=("arbitrary",),
            vmem_limit_bytes=60 << 20,
            collective_id=ident,
            has_side_effects=True,
        ),
        cost_estimate=SMALL,
        name="attend_back",
    )(values, qkv, kt, datt, att, tot, *[r[0] for r in riders])
    return out[0], out[1], out[2:]


def layer_norm(values, gain, shift):
    centred = values - jnp.mean(values, -1, keepdims=True)
    spread = jnp.mean(centred * centred, -1, keepdims=True)
    return centred * lax.rsqrt(spread + 1e-05) * gain + shift


def contract_rows(left, right):
    return lax.dot_general(
        left, right, (((0,), (0,)), ((), ())), preferred_element_type=jnp.float32
    )


def contract_cols(left, right):
    return lax.dot_general(
        left, right, (((1,), (1,)), ((), ())), preferred_element_type=jnp.float32
    )


def after(value, other):
    return value + (other[(0,) * other.ndim] * 0).astype(value.dtype)


def row_major(x):
    return with_layout_constraint(x, Layout(major_to_minor=tuple(range(x.ndim))))


def local(
    tokens,
    ln1_gain,
    ln1_bias,
    qkv_weight,
    qv_bias,
    out_weight,
    out_bias,
    ln2_gain,
    ln2_bias,
    fc_weight,
    fc_bias,
    proj_weight,
    proj_bias,
    seg_lengths,
    parents,
    cotangent,
):
    n = lax.axis_size("seq")
    nf = lax.axis_size("fsdp")
    s = lax.axis_index("seq")
    f = lax.axis_index("fsdp")
    trunk = n // 4
    block, width = tokens.shape[1], tokens.shape[2]
    rows = width // nf
    hidden = fc_weight.shape[1] * n
    piece = hidden // (n * nf)
    group = n // nf
    wide = 2 * HEAD * (-(-HEADS // (2 * n)))
    low = jnp.bfloat16
    wider = jnp.float32

    vectors = [ln1_gain, ln1_bias, qv_bias, out_bias, ln2_gain, ln2_bias, fc_bias, proj_bias]
    sizes = [v.shape[0] for v in vectors]
    qkv_cols = qkv_weight.shape[1]
    even = qkv_cols % 8 == 0
    forth = Rows(n, qkv_cols, width, wide, False) if even else None
    back = Rows(n, qkv_cols, width, wide, True) if even else None
    turned, proj_blocks, fc_blocks, out_blocks, gathered = exchange(
        qkv_weight.T,
        proj_weight.reshape(n, piece, width // n),
        fc_weight.reshape(rows, nf, piece).transpose(1, 0, 2),
        out_weight,
        [jnp.stack([v for v in vectors if v.shape == ln1_gain.shape])]
        + [v.reshape(1, -1) for v in vectors if v.shape != ln1_gain.shape],
        n,
        nf,
        forth,
        wide,
        0,
    )
    short = iter(jnp.unstack(gathered[0], axis=1))
    long = iter(gathered[1:])
    whole = [next(short) if v.shape == ln1_gain.shape else next(long) for v in vectors]
    whole = [v.reshape(-1).astype(wider) for v in whole]
    gain_one, shift_one, bias_qv, bias_out, gain_two, shift_two, bias_fc, bias_proj = whole
    bias_three = jnp.stack([bias_qv[:width], jnp.zeros((width,), wider), bias_qv[width:]])
    bias_three = jnp.pad(bias_three, ((0, 0), (0, n * wide - width)))
    bias_mine = lax.dynamic_slice_in_dim(bias_three, s * wide, wide, 1).reshape(1, -1)
    bias_hidden = lax.dynamic_index_in_dim(bias_fc.reshape(nf, n, piece), s, 1, False)
    bias_hidden = bias_hidden.reshape(1, -1)

    if even:
        turned = turned.reshape(3, wide, rows)
        kept = lax.broadcasted_iota(jnp.int32, turned.shape, 1) + s * wide < width
        turned = jnp.where(kept, turned, 0).reshape(3 * wide, rows)
    else:
        turned = lax.all_gather(qkv_weight.T, "seq", axis=0, tiled=True).reshape(3, width, rows)
        turned = jnp.pad(turned, ((0, 0), (0, n * wide - width), (0, 0)))
        turned = lax.dynamic_slice_in_dim(turned, s * wide, wide, 1).reshape(3 * wide, rows)
    pairs = block_pairs(n, trunk)
    table = block_values(seg_lengths[0], parents[0], pairs, block)

    resid = tokens[0].astype(wider)
    out_turned = out_blocks.reshape(width, width // n).T
    normed_one, out_turned, qkv_mine = seq_gather(
        layer_norm(resid, gain_one, shift_one).astype(low),
        n,
        1,
        "gather_one",
        rider=(turned.T, True, nf),
        second=out_turned,
    )
    out_turned = out_turned.reshape(width, width)
    qkv_mine = qkv_mine.reshape(width, 3 * wide)
    fc_rows = fc_blocks.transpose(1, 0, 2).reshape(rows, nf * piece)
    fc_mine = lax.all_gather(fc_rows, "fsdp", axis=0, tiled=True)

    upstream = cotangent[0].astype(wider)
    proj_rows = proj_blocks.transpose(1, 0, 2).reshape(piece, width)
    proj_mine = lax.all_gather(after(proj_rows, normed_one), "fsdp", axis=0, tiled=True)
    projected, attended_low, attended, totals, keys_turned, upstream_all = attend(
        table, pairs, normed_one, qkv_mine, bias_mine, block, trunk, cotangent[0], n, 8
    )
    attended_mine = to_tokens(attended_low.reshape(n, block, wide), n, wide, 2)[:, :width]
    middle = resid + contract_cols(attended_mine, out_turned) + bias_out
    normed_two = layer_norm(middle, gain_two, shift_two).astype(low)
    ff = nf * piece

    def expand(value, fc, bias, proj):
        pre = mm(value, fc[...]) + bias[...]
        bend = math.sqrt(2 / math.pi)
        square = pre * pre
        inner = jnp.tanh(pre * (bend + bend * 0.044715 * square))
        half = 0.5 + 0.5 * inner
        act = (pre * half).astype(low)
        slope = half + 0.5 * pre * (1 - inner * inner) * (bend + 3 * bend * 0.044715 * square)
        return act, slope.astype(low), mm(act, proj[...]).astype(low)

    normed_two, hidden_act, hidden_slope, mixed = seq_gather(
        normed_two,
        n,
        3,
        "gather_two",
        expand,
        (fc_mine, bias_hidden, proj_mine),
        ((ff, low), (ff, low), (width, low)),
        modes=(0, 0, 0),
    )

    def shrink(up, slope, proj, fc):
        grad = (nt(up, proj[...]) * slope.astype(wider)).astype(low)
        return nt(grad, fc[...]), grad

    grad_normed_two, grad_pre, grad_proj, unused_sums, mixed = seq_scatter(
        n,
        width,
        4,
        "scatter_two",
        shrink,
        (upstream_all, hidden_slope),
        (proj_mine, fc_mine),
        ((ff, low),),
        side=(hidden_act, upstream_all),
        carry=mixed,
    )
    mixed = lax.psum_scatter(mixed, "seq", scatter_dimension=0, tiled=True)
    grad_proj = grad_proj.reshape(nf, piece, width)
    cut = piece // 16 * 8
    unused_two, norm_two_back = jax.vjp(layer_norm, middle, gain_two, shift_two)
    grad_middle_norm, grad_gain_two, grad_shift_two = norm_two_back(grad_normed_two)
    grad_middle = upstream + grad_middle_norm
    grad_branch = grad_middle.astype(low)
    grad_attended, grad_fc, hidden_sums, proj_first, grad_out = to_heads(
        grad_branch,
        out_turned,
        attended_mine,
        n,
        nf,
        wide,
        5,
        normed_two,
        grad_pre,
        grad_proj,
        cut,
    )
    grad_attended = grad_attended.reshape(n * block, wide)
    grad_projected, column_sums, (fc_part, proj_second) = attend_back(
        table,
        pairs,
        projected,
        keys_turned,
        grad_attended,
        attended,
        totals,
        block,
        trunk,
        nf,
        ((grad_fc.reshape(nf, rows, ff), 0, nf), (grad_proj, cut, n)),
        9,
    )
    grad_qkv, output, proj_first, proj_second, fc_out = contract(
        normed_one,
        grad_projected,
        middle,
        mixed,
        bias_proj.reshape(1, -1),
        proj_first,
        proj_second,
        fc_part,
        n,
        nf,
        block,
        10,
    )
    output = output[None]
    input_grad, grad_gain_one, grad_shift_one, qkv_parts = seq_scatter(
        n,
        width,
        6,
        "scatter_one",
        lambda g, w: (nt(g, w[...]),),
        (grad_projected,),
        (qkv_mine,),
        rider=(grad_qkv.reshape(nf, rows, 3 * wide), False, nf),
        norm=(tokens[0], gain_one.reshape(1, -1), grad_middle, low),
    )
    input_grad = input_grad[None]

    out_part = lax.psum_scatter(grad_out, "seq", scatter_dimension=0, tiled=True).T
    out_part = after(out_part, qkv_parts).reshape(nf, rows, width // n)
    qkv_part = jnp.sum(qkv_parts.astype(wider), 0).astype(low).T

    column_sums = column_sums.reshape(3, wide)
    placed = lax.dynamic_update_slice_in_dim(
        jnp.zeros((3, n * wide), wider), column_sums, s * wide, 1
    )[:, :width]
    grad_qv = jnp.concatenate([placed[0], placed[2]])
    hidden_sums = hidden_sums.reshape(nf, 1, piece)
    grad_fc_bias = lax.dynamic_update_slice_in_dim(
        jnp.zeros((nf, n, piece), wider), hidden_sums, s, 1
    )
    parts = [
        grad_gain_one,
        grad_shift_one,
        grad_qv,
        jnp.sum(grad_branch.astype(wider), 0),
        grad_gain_two,
        grad_shift_two,
        grad_fc_bias,
        jnp.sum(upstream, 0),
    ]
    summed, qkv_out, out_out = give_back(
        jnp.concatenate([p.reshape(nf, -1) for p in parts], 1),
        qkv_part,
        qkv_cols,
        out_part,
        n,
        nf,
        back,
        7,
    )
    if not even:
        qkv_part = qkv_part.reshape(3, wide, rows)
        qkv_out = lax.all_gather(qkv_part, "seq", axis=1, tiled=True)[:, :width]
        qkv_out = qkv_out.reshape(3 * width, rows)
        qkv_out = lax.dynamic_slice_in_dim(qkv_out, s * qkv_cols, qkv_cols, 0)
    out_out = jnp.sum(out_out.astype(wider), 0)
    qkv_out = qkv_out.T.astype(wider)
    proj_out = jnp.concatenate([proj_first, proj_second], 1)
    proj_out = proj_out.reshape(n * piece, width // n).astype(wider)
    fc_out = fc_out.transpose(1, 0, 2).reshape(rows, nf * piece).astype(wider)
    vector_out = []
    at = 0
    for size in sizes:
        vector_out.append(summed[at : at + size])
        at += size
    return (
        output,
        input_grad,
        vector_out[0],
        vector_out[1],
        qkv_out,
        vector_out[2],
        out_out,
        vector_out[3],
        vector_out[4],
        vector_out[5],
        fc_out,
        vector_out[6],
        proj_out,
        vector_out[7],
    )


def solution(mesh):
    in_specs = (
        P("fsdp", "seq", None),
        P("fsdp"),
        P("fsdp"),
        P("fsdp", "seq"),
        P("fsdp"),
        P("fsdp", "seq"),
        P("fsdp"),
        P("fsdp"),
        P("fsdp"),
        P("fsdp", "seq"),
        P("fsdp"),
        P("fsdp", "seq"),
        P("fsdp"),
        P("fsdp", None),
        P("fsdp", None),
        P("fsdp", "seq", None),
    )
    out_specs = (
        P("fsdp", "seq", None),
        P("fsdp", "seq", None),
        P("fsdp"),
        P("fsdp"),
        P("fsdp", "seq"),
        P("fsdp"),
        P("fsdp", "seq"),
        P("fsdp"),
        P("fsdp"),
        P("fsdp"),
        P("fsdp", "seq"),
        P("fsdp"),
        P("fsdp", "seq"),
        P("fsdp"),
    )
    return jax.shard_map(local, mesh=mesh, in_specs=in_specs, out_specs=out_specs, check_vma=False)
```

```python
import functools
import math

import jax
import jax.numpy as jnp
import numpy as np
from jax import lax
from jax.experimental import pallas as pl
from jax.experimental.layout import Layout, with_layout_constraint
from jax.experimental.pallas import tpu as pltpu
from jax.sharding import PartitionSpec as P

MESH = pl.DeviceIdType.MESH
HEADS = 25
SMALL = pl.CostEstimate(flops=0, bytes_accessed=1 << 20, transcendentals=0)


def route_bits(n):
    bits = []
    b = 2
    while b < n:
        bits.append(b)
        b *= 2
    return bits


def flip(a, b):
    return jnp.where(lax.rem(lax.div(a, b), 2) == 0, a + b, a - b)


def place(me, r, n):
    if isinstance(r, int):
        for b in [1] + route_bits(n):
            if r & b:
                me = flip(me, b)
        return me
    for b in [1] + route_bits(n):
        me = jnp.where(lax.rem(lax.div(r, b), 2) == 0, me, flip(me, b))
    return me


def pick(table, q):
    value = jnp.int32(table[0])
    for i, entry in enumerate(table[1:]):
        value = jnp.where(q == i + 1, jnp.int32(entry), value)
    return value


def greet(ids):
    barrier = pltpu.get_barrier_semaphore()
    for i in ids:
        pl.semaphore_signal(barrier, inc=1, device_id=i, device_id_type=MESH)
    pl.semaphore_wait(barrier, len(ids))


def remote(src, dst, send, recv, device):
    return pltpu.make_async_remote_copy(
        src_ref=src, dst_ref=dst, send_sem=send, recv_sem=recv, device_id=device, device_id_type=MESH
    )


class Blocks:
    def __init__(self, axis, size, same, source, target, send, recv, local):
        self.axis, self.size, self.same = axis, size, same
        self.source, self.target = source, target
        self.send, self.recv, self.local = send, recv, local
        self.me = lax.axis_index(axis)

    @staticmethod
    def scratch(size):
        dma = pltpu.SemaphoreType.DMA
        return [dma((size - 1,)), dma((size - 1,)), dma]

    def peers(self):
        return [{self.axis: lax.rem(self.me + d, self.size)} for d in range(1, self.size)]

    def copy(self, d):
        to = lax.rem(self.me + d, self.size)
        src = self.source if self.same else self.source.at[to]
        return remote(src, self.target.at[self.me], self.send.at[d - 1], self.recv.at[d - 1], {self.axis: to})

    def own(self):
        src = self.source if self.same else self.source.at[self.me]
        return pltpu.make_async_copy(src, self.target.at[self.me], self.local)

    def start(self):
        for d in range(1, self.size):
            self.copy(d).start()
        self.own().start()

    def finish(self):
        for d in range(1, self.size):
            dst = self.target.at[lax.rem(self.me + self.size - d, self.size)]
            remote(dst, dst, self.send.at[d - 1], self.recv.at[d - 1], {self.axis: self.me}).wait_recv()
        self.own().wait()
        for d in range(1, self.size):
            self.copy(d).wait_send()


class Spread:
    def __init__(self, n, source, target, send, recv, local):
        self.n, self.source, self.target = n, source, target
        self.send, self.recv, self.local = send, recv, local
        self.me = lax.axis_index("seq")
        self.bits = route_bits(n)
        self.orders = [self.bits, self.bits[::-1]]
        self.h = source.shape[0] // 2

    @staticmethod
    def scratch(n):
        dma = pltpu.SemaphoreType.DMA
        return [dma((2, len(route_bits(n)) + 1, n)), dma((2, n)), dma]

    def device(self, b):
        return {"seq": flip(self.me, b)}

    def peers(self):
        return [self.device(b) for b in [1] + self.bits]

    def rows(self, half):
        return pl.ds(half * self.h, self.h)

    def ship(self, half, k, b):
        owner = place(self.me, k, self.n)
        src = self.source if k == 0 else self.target.at[owner]
        lane = 0 if b == 1 else 1 + self.bits.index(b)
        return remote(
            src.at[self.rows(half)],
            self.target.at[owner].at[self.rows(half)],
            self.send.at[half, lane, k],
            self.recv.at[half, k ^ b],
            self.device(b),
        )

    def arrive(self, half, k):
        dst = self.target.at[place(self.me, k, self.n)].at[self.rows(half)]
        remote(dst, dst, self.send.at[half, 0, 0], self.recv.at[half, k], self.device(1)).wait_recv()

    def own(self):
        return pltpu.make_async_copy(self.source, self.target.at[self.me], self.local)

    def fresh(self, half, i):
        had = [0]
        for b in self.orders[half][:i]:
            had = had + [k ^ b for k in had]
        return [k ^ self.orders[half][i] for k in had]

    def start(self):
        for i in range(len(self.bits)):
            for half in (0, 1):
                self.ship(half, 0, self.orders[half][i]).start()
        for half in (0, 1):
            self.ship(half, 0, 1).start()
        self.own().start()

    def phase(self, i):
        for half in (0, 1):
            for k in self.fresh(half, i):
                self.arrive(half, k)
                for b in self.orders[half][i + 1 :] + [1]:
                    self.ship(half, k, b).start()

    def finish(self):
        for half in (0, 1):
            for k in range(1, self.n, 2):
                self.arrive(half, k)
        self.own().wait()
        for half in (0, 1):
            for b in self.orders[half] + [1]:
                self.ship(half, 0, b).wait_send()
            for i in range(len(self.bits)):
                for k in self.fresh(half, i):
                    for b in self.orders[half][i + 1 :] + [1]:
                        self.ship(half, k, b).wait_send()


class PlaneSum(Blocks):
    def __init__(self, size, source, low, target, send, recv, local):
        super().__init__("fsdp", size, False, source, target, send, recv, local)
        self.window = pl.ds(low, target.shape[1])

    @staticmethod
    def scratch(size, rows, cols):
        return [pltpu.VMEM((size, rows, cols), jnp.bfloat16)] + Blocks.scratch(size)

    def copy(self, d):
        to = lax.rem(self.me + d, self.size)
        src = self.source.at[to].at[self.window]
        return remote(src, self.target.at[self.me], self.send.at[d - 1], self.recv.at[d - 1], {self.axis: to})

    def own(self):
        src = self.source.at[self.me].at[self.window]
        return pltpu.make_async_copy(src, self.target.at[self.me], self.local)

    def store(self, out):
        total = self.target[0].astype(jnp.float32)
        for i in range(1, self.size):
            total = total + self.target[i].astype(jnp.float32)
        cols = out.shape[2]
        for i in range(out.shape[0]):
            out[i] = total[:, i * cols : (i + 1) * cols].astype(out.dtype)


def blocks_shape(x, size, same):
    return jax.ShapeDtypeStruct(((size,) + x.shape) if same else x.shape, x.dtype)


def arrival_order(n):
    bits = route_bits(n)
    orders = [bits, bits[::-1]]
    lists = []
    for order in orders:
        held, phases = [0], [-1]
        for i, b in enumerate(order):
            fresh = [h ^ b for h in held]
            held, phases = held + fresh, phases + [i] * len(fresh)
        lists.append(list(zip(held, phases)))
    entries = []
    for i in range(n // 2):
        for odd in (0, 1):
            for half in (0, 1):
                k, phase = lists[half][i]
                entries.append((half, k ^ odd, phase, odd))
    return orders, entries


def gather_kernel(n, h, body, n_const, n_out, relative, modes, nf, same, second, *refs):
    if second:
        at = 1 + n_const
        out = at + 1 + min(nf, 1) + 1 + n_out
        w_ref, w_all = refs[at], refs[out]
        w_send, w_recv, w_keep = refs[-3:]
        refs = refs[:at] + refs[at + 1 : out] + refs[out + 1 : -3]
        w_half = w_ref.shape[1] // 256 * 128
        w_lanes = [pl.ds(0, w_half), pl.ds(w_half, w_ref.shape[1] - w_half)]
    refs, rider = split_rider(refs, nf, same, 1 + n_const, 1 + n_out)
    x_ref = refs[0]
    consts = refs[1 : 1 + n_const]
    all_ref = refs[1 + n_const]
    outs = refs[2 + n_const : 2 + n_const + n_out]
    held = refs[2 + n_const + n_out]
    stages = refs[3 + n_const + n_out : 3 + n_const + 2 * n_out]
    send, recv, keep, store = refs[3 + n_const + 2 * n_out :]
    me = lax.axis_index("seq")
    orders, entries = arrival_order(n)
    bits = orders[0]
    nb = len(bits)

    def device(b):
        return {"seq": flip(me, b)}

    def spot(half, k):
        return 2 * (k if relative else place(me, k, n)) + half

    def ship(half, k, b):
        at = spot(half, k)
        src = x_ref.at[pl.ds(half * h, h)] if isinstance(k, int) and k == 0 else held.at[at]
        lane = 0 if b == 1 else 1 + bits.index(b)
        to = k ^ b if isinstance(k, int) else place(k, b, n)
        dst = 2 * to + half if relative else at
        first = remote(src, held.at[dst], send.at[half, lane, k], recv.at[half, to], device(b))
        if not second:
            return [first]
        owner = place(me, k, n)
        lanes = w_lanes[half]
        src = w_ref if isinstance(k, int) and k == 0 else w_all.at[owner]
        other = remote(
            src.at[:, lanes], w_all.at[owner].at[:, lanes], w_send.at[half, lane, k], w_recv.at[half, to], device(b)
        )
        return [first, other]

    def each(copies, act):
        for c in copies:
            act(c)

    def w_arrive(half, k):
        dst = w_all.at[place(me, k, n)].at[:, w_lanes[half]]
        remote(dst, dst, w_send.at[0, 0, 0], w_recv.at[half, k], device(1)).wait_recv()

    greet([device(b) for b in [1] + bits] + (rider.peers() if nf else []))
    for i in range(nb):
        for half in (0, 1):
            each(ship(half, 0, orders[half][i]), lambda c: c.start())
    for half in (0, 1):
        each(ship(half, 0, 1), lambda c: c.start())
    if second:
        pltpu.make_async_copy(w_ref, w_all.at[me], w_keep).start()
    if nf:
        rider.start()

    def output(o, q, at):
        slot = lax.rem(q, 2)
        return pltpu.make_async_copy(stages[o].at[slot], outs[o].at[at], store.at[o, slot])

    def entry(q, at, value):
        results = body(value, *consts)
        for o in range(n_out):

            @pl.when(q >= 2)
            def _(o=o):
                output(o, q, at[modes[o]]).wait()

            stages[o][lax.rem(q, 2)] = results[o]
            output(o, q, at[modes[o]]).start()

    def step(q, carry):
        half = pick([e[0] for e in entries], q)
        k = pick([e[1] for e in entries], q)
        phase = pick([e[2] for e in entries], q)
        odd = pick([e[3] for e in entries], q)
        at = spot(half, k)

        @pl.when(k == 0)
        def _():
            held[at] = x_ref[pl.ds(pl.multiple_of(half * h, h), h)]

        @pl.when(k != 0)
        def _():
            remote(held.at[at], held.at[at], send.at[0, 0, 0], recv.at[half, k], device(1)).wait_recv()

        for side in (0, 1) if second else ():

            @pl.when((k != 0) & (half == side))
            def _(side=side):
                w_arrive(side, k)

        for side in (0, 1):
            for i in range(nb):

                @pl.when((half == side) & (odd == 0) & (k != 0) & (phase < i))
                def _(side=side, i=i):
                    each(ship(side, k, orders[side][i]), lambda c: c.start())

            @pl.when((half == side) & (odd == 0) & (k != 0))
            def _(side=side):
                each(ship(side, k, 1), lambda c: c.start())

        pltpu.make_async_copy(held.at[at], all_ref.at[at], keep.at[q]).start()
        if n_out:
            entry(q, (2 * place(me, k, n) + half, 2 * k + half), held[at])
        return carry

    lax.fori_loop(0, 2 * n, step, 0)
    for q, (half, k, phase, odd) in enumerate(entries):
        at = spot(half, k)
        pltpu.make_async_copy(held.at[at], all_ref.at[at], keep.at[q]).wait()
        if q >= 2 * n - 2:
            for o in range(n_out):
                output(o, jnp.int32(q), at).wait()
        if not odd:
            for i in range(nb):
                if phase < i:
                    each(ship(half, k, orders[half][i]), lambda c: c.wait_send())
            each(ship(half, k, 1), lambda c: c.wait_send())
    if second:
        pltpu.make_async_copy(w_ref, w_all.at[me], w_keep).wait()
    if nf:
        rider.finish()


def split_rider(refs, nf, same, n_in, n_out):
    if not nf:
        return refs, None
    source = refs[n_in]
    target = refs[n_in + 1 + n_out]
    rider = Blocks("fsdp", nf, same, source, target, *refs[-3:])
    return refs[:n_in] + refs[n_in + 1 : n_in + 1 + n_out] + refs[n_in + 2 + n_out : -3], rider


def rider_parts(rider):
    if rider is None:
        return [], [], [], [], 0, False
    x, same, nf = rider
    hbm = [pl.BlockSpec(memory_space=pl.ANY)]
    return [x], hbm, [blocks_shape(x, nf, same)], Blocks.scratch(nf), nf, same


def seq_gather(x, n, ident, name, body=None, consts=(), outs=(), relative=False, modes=None, rider=None, second=None):
    rows, cols = x.shape
    h = rows // 2
    nb = len(route_bits(n))
    shapes = [jax.ShapeDtypeStruct((2 * n, h, c), d) for c, d in outs]
    vmem = pl.BlockSpec(memory_space=pltpu.VMEM)
    hbm = pl.BlockSpec(memory_space=pl.ANY)
    more, spec, shape, scratch, nf, same = rider_parts(rider)
    also = [] if second is None else [second]
    out = pl.pallas_call(
        functools.partial(
            gather_kernel, n, h, body, len(consts), len(outs), relative, modes, nf, same, second is not None
        ),
        out_shape=[jax.ShapeDtypeStruct((2 * n, h, cols), x.dtype)]
        + shapes
        + [jax.ShapeDtypeStruct((n,) + w.shape, w.dtype) for w in also]
        + shape,
        in_specs=[vmem] * (1 + len(consts)) + [hbm] * len(also) + spec,
        out_specs=[hbm] * (1 + len(outs)) + [hbm] * len(also) + spec,
        scratch_shapes=[pltpu.VMEM((2 * n, h, cols), x.dtype)]
        + [pltpu.VMEM((2, h, c), d) for c, d in outs]
        + [
            pltpu.SemaphoreType.DMA((2, nb + 1, n)),
            pltpu.SemaphoreType.DMA((2, n)),
            pltpu.SemaphoreType.DMA((2 * n,)),
            pltpu.SemaphoreType.DMA((max(len(outs), 1), 2)),
        ]
        + scratch
        + [
            pltpu.SemaphoreType.DMA((2, nb + 1, n)),
            pltpu.SemaphoreType.DMA((2, n)),
            pltpu.SemaphoreType.DMA,
        ]
        * len(also),
        compiler_params=pltpu.CompilerParams(
            collective_id=ident, has_side_effects=True, vmem_limit_bytes=60 << 20
        ),
        cost_estimate=SMALL,
        name=name,
    )(x, *consts, *also, *more)
    return [o.reshape(2 * n * h, o.shape[2]) for o in out[: 1 + len(outs)]] + list(out[1 + len(outs) :])


class Side:
    def __init__(self, count, refs):
        self.count = count
        self.a, self.b, self.grad, self.sums, self.acc, self.abuf, self.bbuf, self.load = refs

    def fetch(self, i):
        slot = lax.rem(i, 2)
        return [
            pltpu.make_async_copy(self.a.at[i], self.abuf.at[slot], self.load.at[0, slot]),
            pltpu.make_async_copy(self.b.at[i], self.bbuf.at[slot], self.load.at[1, slot]),
        ]

    def begin(self):
        self.acc[...] = jnp.zeros_like(self.acc)
        self.sums[...] = jnp.zeros_like(self.sums)
        for c in self.fetch(jnp.int32(0)):
            c.start()

    def run(self, first, last):
        def step(i, carry):
            @pl.when(i + 1 < self.count)
            def _():
                for c in self.fetch(i + 1):
                    c.start()

            for c in self.fetch(i):
                c.wait()
            slot = lax.rem(i, 2)
            a, b = self.abuf[slot], self.bbuf[slot]
            self.acc[...] += lax.dot_general(
                a, b, (((0,), (0,)), ((), ())), preferred_element_type=jnp.float32
            )
            self.sums[...] += jnp.sum(b.astype(jnp.float32), 0, keepdims=True)
            return carry

        lax.fori_loop(first, last, step, 0)

    def end(self):
        self.grad[...] = self.acc[...].astype(self.grad.dtype)


def side_parts(side, count):
    if side is None:
        return [], [], [], [], []
    a, b = side
    h = a.shape[0] // count
    low = jnp.bfloat16
    hbm = pl.BlockSpec(memory_space=pl.ANY)
    vmem = pl.BlockSpec(memory_space=pltpu.VMEM)
    return (
        [x.reshape(count, h, x.shape[1]) for x in (a, b)],
        [
            jax.ShapeDtypeStruct((a.shape[1], b.shape[1]), low),
            jax.ShapeDtypeStruct((1, b.shape[1]), jnp.float32),
        ],
        [hbm, hbm],
        [vmem, vmem],
        [
            pltpu.VMEM((a.shape[1], b.shape[1]), jnp.float32),
            pltpu.VMEM((2, h, a.shape[1]), low),
            pltpu.VMEM((2, h, b.shape[1]), low),
            pltpu.SemaphoreType.DMA((2, 2)),
        ],
    )


def scatter_order(n):
    bits = route_bits(n)
    orders = [bits, bits[::-1]]
    lists = [
        sorted(range(0, n, 2), key=lambda k: [-int(bool(k & b)) for b in order]) for order in orders
    ]
    return orders, [(half, lists[half][i]) for i in range(n // 2) for half in (0, 1)]


def scatter_kernel(n, h, body, n_in, n_const, n_out, modes, nf, same, has_side, has_norm, carried, *refs):
    if carried:
        out = 1 + n_in + n_const + 2 * has_side + min(nf, 1) + 1 + n_out + 2 * has_side + min(nf, 1)
        refs = refs[1:out] + refs[out + 1 :]
    if has_norm:
        out = n_in + 3 + n_const + 2 * has_side + min(nf, 1)
        values, gain, joins = refs[:3]
        x_grad, g_grad, b_grad = refs[out], refs[out + 1], refs[out + 2]
        refs = refs[3:out] + (None,) + refs[out + 3 :]
    side = None
    if has_side:
        at = n_in + n_const
        out = at + 2 + min(nf, 1) + 1 + n_out
        extra = refs[at : at + 2] + refs[out : out + 2] + refs[-4:]
        refs = refs[:at] + refs[at + 2 : out] + refs[out + 2 : -4]
        side = Side(2 * n, extra)
    refs, rider = split_rider(refs, nf, same, n_in + n_const, 1 + n_out)
    ins = refs[:n_in]
    consts = refs[n_in : n_in + n_const]
    at = n_in + n_const
    sum_ref = refs[at]
    outs = refs[at + 1 : at + 1 + n_out]
    at += 1 + n_out
    give, pair, own, far, total = refs[at : at + 5]
    at += 5
    loads = refs[at : at + n_in]
    stages = refs[at + n_in : at + n_in + n_out]
    pair_send, pair_recv, far_send, far_recv, load, store, done = refs[at + n_in + n_out :]
    me = lax.axis_index("seq")
    orders, entries = scatter_order(n)
    bits = orders[0]
    slots = give.shape[0]
    index = {e: j for j, e in enumerate(entries)}

    def device(b):
        return {"seq": flip(me, b)}

    def phase_of(half, k):
        for i, b in enumerate(orders[half]):
            if k & b:
                return i
        return len(bits)

    landing = {}
    for half in (0, 1):
        for i, b in enumerate(orders[half]):
            for k in range(0, n, 2):
                if phase_of(half, k) == i:
                    landing[half, i, k ^ b] = len(landing)

    halves = [e[0] for e in entries]
    ks = [e[1] for e in entries]

    def spot(q, relative):
        j = lax.div(q, 2)
        k = pick(ks, j)
        k = jnp.where(lax.rem(q, 2) == 0, flip(k, 1), k)
        return 2 * (k if relative else place(me, k, n)) + pick(halves, j)

    def fetch(q):
        slot = lax.rem(q, 2)
        return [
            pltpu.make_async_copy(ins[i].at[spot(q, modes[0][i])], loads[i].at[slot], load.at[i, slot])
            for i in range(n_in)
        ]

    def output(o, q):
        slot = lax.rem(q, 2)
        return pltpu.make_async_copy(stages[o].at[slot], outs[o].at[spot(q, modes[1][o])], store.at[o, slot])

    def hand(j):
        slot = lax.rem(j, slots)
        return remote(give.at[slot], pair.at[j], pair_send.at[j], pair_recv.at[j], device(1))

    def launch(half, k):
        i = phase_of(half, k)
        b = orders[half][i]
        to = landing[half, i, k ^ b]
        return remote(own.at[index[half, k]], far.at[to], far_send.at[to], far_recv.at[to], device(b))

    def join(j):
        hand(j).wait_recv()
        own[j] = (own[j].astype(jnp.float32) + pair[j].astype(jnp.float32)).astype(own.dtype)
        for e, (half, k) in enumerate(entries):
            if phase_of(half, k) == 0:

                @pl.when(j == e)
                def _(half=half, k=k):
                    launch(half, k).start()

    for c in fetch(jnp.int32(0)):
        c.start()
    greet([device(b) for b in [1] + bits] + (rider.peers() if nf else []))
    if nf:
        rider.start()

    def step(q, carry):
        j = lax.div(q, 2)
        slot = lax.rem(q, 2)

        @pl.when(q + 1 < 2 * n)
        def _():
            for c in fetch(q + 1):
                c.start()

        for c in fetch(q):
            c.wait()
        part, *results = body(*[r[slot] for r in loads], *consts)
        for o in range(n_out):

            @pl.when(q >= 2)
            def _(o=o):
                output(o, q).wait()

            stages[o][slot] = results[o]
            output(o, q).start()

        @pl.when(slot == 0)
        def _():
            @pl.when(j >= slots)
            def _():
                hand(j - slots).wait_send()

            give[lax.rem(j, slots)] = part.astype(give.dtype)
            hand(j).start()

        @pl.when(slot == 1)
        def _():
            own[j] = part.astype(own.dtype)

            @pl.when(j >= 1)
            def _():
                join(j - 1)

        return carry

    lax.fori_loop(0, 2 * n, step, 0)
    if side:
        side.begin()
    join(jnp.int32(n - 1))
    first = n // 2
    cuts = [0, first] + [first + (2 * n - first) * i // (len(bits) - 1) for i in range(1, len(bits))]
    for i in range(len(bits)):
        if side:
            side.run(cuts[i], cuts[i + 1])
        for half in (0, 1):
            order = orders[half]
            for k in [k for hh, k in entries if hh == half and phase_of(half, k) > i]:
                to = landing[half, i, k]
                remote(far.at[to], far.at[to], far_send.at[to], far_recv.at[to], device(1)).wait_recv()
                j = index[half, k]
                rows = pl.ds(half * h, h)
                if i == len(bits) - 1:
                    total[rows] = own[j].astype(jnp.float32) + far[to].astype(jnp.float32)
                    if not has_norm:
                        pltpu.make_async_copy(total.at[rows], sum_ref.at[rows], done.at[half]).start()
                else:
                    own[j] = (own[j].astype(jnp.float32) + far[to].astype(jnp.float32)).astype(own.dtype)
                    if phase_of(half, k) == i + 1:
                        launch(half, k).start()
    if has_norm:
        g_grad[...] = jnp.zeros_like(g_grad)
        b_grad[...] = jnp.zeros_like(b_grad)

        def tile(i, carry):
            rows = pl.ds(pl.multiple_of(i * 64, 64), 64)
            x = values[rows].astype(jnp.float32)
            centred = x - jnp.mean(x, -1, keepdims=True)
            scale = lax.rsqrt(jnp.mean(centred * centred, -1, keepdims=True) + 1e-05)
            xhat = centred * scale
            grad = total[rows]
            g_grad[...] += jnp.sum(grad * xhat, 0, keepdims=True)
            b_grad[...] += jnp.sum(grad, 0, keepdims=True)
            e = gain[...] * grad
            inner = e - jnp.mean(e, -1, keepdims=True) - xhat * jnp.mean(e * xhat, -1, keepdims=True)
            x_grad[rows] = (joins[rows].astype(jnp.float32) + scale * inner).astype(x_grad.dtype)
            return carry

        lax.fori_loop(0, 2 * h // 64, tile, 0)
    for half in (0, 1) if not has_norm else ():
        rows = pl.ds(half * h, h)
        pltpu.make_async_copy(total.at[rows], sum_ref.at[rows], done.at[half]).wait()
    for q in (2 * n - 2, 2 * n - 1):
        for o in range(n_out):
            output(o, jnp.int32(q)).wait()
    for j in range(max(n - slots, 0), n):
        hand(jnp.int32(j)).wait_send()
    for half, k in entries:
        if phase_of(half, k) < len(bits):
            launch(half, k).wait_send()
    if nf:
        rider.finish()
    if side:
        side.end()


def seq_scatter(n, cols, ident, name, body, ins, consts, outs=(), modes=None, rider=None, side=None, norm=None, carry=None):
    h = ins[0].shape[0] // (2 * n)
    low = jnp.bfloat16
    slots = min(4, n)
    split = [a.reshape(2 * n, h, a.shape[1]) for a in ins]
    vmem = pl.BlockSpec(memory_space=pltpu.VMEM)
    hbm = pl.BlockSpec(memory_space=pl.ANY)
    reach = n - 2
    modes = modes or ([0] * len(ins), [0] * len(outs))
    more, spec, shape, scratch, nf, same = rider_parts(rider)
    s_ins, s_shapes, s_in_specs, s_out_specs, s_scratch = side_parts(side, 2 * n)
    sums = [jax.ShapeDtypeStruct((2 * h, cols), jnp.float32)]
    norms = []
    carries = [] if carry is None else [carry]
    if norm is not None:
        norms = list(norm[:3])
        line = jax.ShapeDtypeStruct((1, cols), jnp.float32)
        sums = [jax.ShapeDtypeStruct((2 * h, cols), norm[3]), line, line]
    out = pl.pallas_call(
        functools.partial(
            scatter_kernel, n, h, body, len(ins), len(consts), len(outs), modes, nf, same, int(side is not None), norm is not None, carry is not None
        ),
        out_shape=sums
        + [jax.ShapeDtypeStruct((2 * n, h, c), d) for c, d in outs]
        + s_shapes
        + shape
        + [jax.ShapeDtypeStruct(x.shape, x.dtype) for x in carries],
        in_specs=[hbm] * len(carries)
        + [vmem] * len(norms)
        + [hbm] * len(ins)
        + [vmem] * len(consts)
        + s_in_specs
        + spec,
        out_specs=([vmem] * 3 if norms else [hbm])
        + [hbm] * len(outs)
        + s_out_specs
        + spec
        + [hbm] * len(carries),
        input_output_aliases={0: len(sums + list(outs) + s_shapes + shape)} if carries else {},
        scratch_shapes=[
            pltpu.VMEM((slots, h, cols), low),
            pltpu.VMEM((n, h, cols), low),
            pltpu.VMEM((n, h, cols), low),
            pltpu.VMEM((reach, h, cols), low),
            pltpu.VMEM((2 * h, cols), jnp.float32),
        ]
        + [pltpu.VMEM((2, h, a.shape[2]), a.dtype) for a in split]
        + [pltpu.VMEM((2, h, c), d) for c, d in outs]
        + [
            pltpu.SemaphoreType.DMA((n,)),
            pltpu.SemaphoreType.DMA((n,)),
            pltpu.SemaphoreType.DMA((reach,)),
            pltpu.SemaphoreType.DMA((reach,)),
            pltpu.SemaphoreType.DMA((len(ins), 2)),
            pltpu.SemaphoreType.DMA((max(len(outs), 1), 2)),
            pltpu.SemaphoreType.DMA((2,)),
        ]
        + scratch
        + s_scratch,
        compiler_params=pltpu.CompilerParams(
            collective_id=ident, has_side_effects=True, vmem_limit_bytes=60 << 20
        ),
        cost_estimate=SMALL,
        name=name,
    )(*carries, *norms, *split, *consts, *s_ins, *more)
    lines = list(out[1:3]) if norms else []
    out = [out[0]] + list(out[1 + len(lines) :])
    many = 1 + len(outs)
    sides = [] if side is None else list(out[many : many + 2])
    more = list(out[many + len(sides) :])
    return [out[0]] + lines + [o.reshape(2 * n * h, o.shape[2]) for o in out[1:many]] + sides + more


class Rows:
    def __init__(self, n, held, width, wide, back):
        moves = []
        for to in range(n):
            for third in range(3):
                at, end = third * width + to * wide, third * width + min((to + 1) * wide, width)
                row = third * wide
                while at < end:
                    source = at // held
                    count = min(end, (source + 1) * held) - at
                    moves.append((source, at - source * held, to, row, count))
                    at, row = at + count, row + count
        self.n = n
        self.moves = [(c, d, a, b, e) if back else (a, b, c, d, e) for a, b, c, d, e in moves]
        self.out = [[m for m in self.moves if m[0] == i] for i in range(n)]
        self.into = [[m for m in self.moves if m[2] == i] for i in range(n)]
        self.most = max(len(v) for v in self.out + self.into)

    def scratch(self):
        dma = pltpu.SemaphoreType.DMA
        return [dma((self.most,)), dma((self.most,)), dma((self.most,))]

    def bind(self, source, target, send, recv, local):
        self.source, self.target, self.send, self.recv, self.local = source, target, send, recv, local
        return self

    def copy(self, i, m):
        src = self.source.at[pl.ds(m[1], m[4])]
        dst = self.target.at[pl.ds(m[3], m[4])]
        if m[0] == m[2]:
            return pltpu.make_async_copy(src, dst, self.local.at[i])
        return remote(src, dst, self.send.at[i], self.recv.at[self.into[m[2]].index(m)], {"seq": m[2]})

    def start(self):
        me = lax.axis_index("seq")
        for s in range(self.n):

            @pl.when(me == s)
            def _(s=s):
                for i, m in enumerate(self.out[s]):
                    self.copy(i, m).start()

    def finish(self):
        me = lax.axis_index("seq")
        for s in range(self.n):

            @pl.when(me == s)
            def _(s=s):
                for i, m in enumerate(self.into[s]):
                    if m[0] != s:
                        dst = self.target.at[pl.ds(m[3], m[4])]
                        remote(dst, dst, self.send.at[0], self.recv.at[i], {"seq": s}).wait_recv()
                for i, m in enumerate(self.out[s]):
                    if m[0] == m[2]:
                        self.copy(i, m).wait()
                    else:
                        self.copy(i, m).wait_send()


class Units:
    def __init__(self, n, nf, back, source, target, send, recv, local):
        self.n, self.nf, self.back = n, nf, back
        self.source, self.target, self.send, self.recv, self.local = source, target, send, recv, local
        self.me = lax.axis_index("seq")

    @staticmethod
    def scratch(nf):
        dma = pltpu.SemaphoreType.DMA
        return [dma((nf,)), dma((nf,)), dma]

    def ends(self, i):
        group = self.n // self.nf
        if self.back:
            return i * group + lax.div(self.me, self.nf), lax.rem(self.me, self.nf)
        return lax.rem(self.me, group) * self.nf + i, lax.div(self.me, group)

    def comes(self, i):
        group = self.n // self.nf
        if self.back:
            return lax.rem(self.me, group) * self.nf + i
        return i * group + lax.div(self.me, self.nf)

    def each(self, i, there, here):
        to, slot = self.ends(i)

        @pl.when(to != self.me)
        def _():
            there(remote(self.source.at[i], self.target.at[slot], self.send.at[i], self.recv.at[slot], {"seq": to}))

        @pl.when(to == self.me)
        def _():
            here(pltpu.make_async_copy(self.source.at[i], self.target.at[slot], self.local))

    def start(self):
        for i in range(self.nf):
            self.each(i, lambda c: c.start(), lambda c: c.start())

    def finish(self):
        for i in range(self.nf):
            source = self.comes(i)

            @pl.when(source != self.me)
            def _(i=i):
                dst = self.target.at[i]
                remote(dst, dst, self.send.at[0], self.recv.at[i], {"seq": self.me}).wait_recv()

        for i in range(self.nf):
            self.each(i, lambda c: c.wait_send(), lambda c: c.wait())


def all_peers(n, nf):
    me, f = lax.axis_index("seq"), lax.axis_index("fsdp")
    return [{"seq": place(me, r, n)} for r in range(1, n)] + [
        {"fsdp": lax.rem(f + d, nf)} for d in range(1, nf)
    ]


def exchange_kernel(n, nf, rows, count, *refs):
    ins, outs, sems = refs[: 4 + count], refs[4 + count : 8 + 2 * count], list(refs[8 + 2 * count :])
    take = lambda k: [sems.pop(0) for _ in range(k)]
    parts = []
    if rows is not None:
        parts.append(rows.bind(ins[0], outs[0], *take(3)))
    vectors = [Blocks("fsdp", nf, True, ins[4 + i], outs[4 + i], *take(3)) for i in range(count)]
    later = [
        Blocks("fsdp", nf, True, ins[3], outs[3], *take(3)),
        Units(n, nf, False, ins[2], outs[2], *take(3)),
        Blocks("seq", n, False, ins[1], outs[1], *take(3)),
    ]
    parts = vectors + parts + later
    greet(all_peers(n, nf))
    for p in parts:
        p.start()
    for p in parts:
        p.finish()


def exchange(w, p, c, o, vectors, n, nf, rows, wide, ident):
    hbm = pl.BlockSpec(memory_space=pl.ANY)
    count = len(vectors)
    out = pl.pallas_call(
        functools.partial(exchange_kernel, n, nf, rows, count),
        out_shape=[
            jax.ShapeDtypeStruct((3 * wide, w.shape[1]) if rows is not None else w.shape, w.dtype),
            blocks_shape(p, n, False),
            blocks_shape(c, nf, False),
            blocks_shape(o, nf, True),
        ]
        + [blocks_shape(v, nf, True) for v in vectors],
        in_specs=[hbm] * (4 + count),
        out_specs=[hbm] * (4 + count),
        scratch_shapes=(rows.scratch() if rows is not None else [])
        + sum([Blocks.scratch(nf) for _ in vectors], [])
        + Blocks.scratch(nf)
        + Units.scratch(nf)
        + Blocks.scratch(n),
        compiler_params=pltpu.CompilerParams(collective_id=ident, has_side_effects=True),
        cost_estimate=SMALL,
        name="exchange",
    )(w, p, c, o, *vectors)
    return out[0], out[1], out[2], out[3], out[4:]


def to_tokens_kernel(n, wide, x_ref, o_ref, send, recv, local):
    me = lax.axis_index("seq")

    def target(i):
        return o_ref.at[:, pl.ds(pl.multiple_of(i * wide, 128), wide)]

    greet([{"seq": place(me, r, n)} for r in range(1, n)])
    copies = []
    for r in range(n - 1, 0, -1):
        to = place(me, r, n)
        c = remote(x_ref.at[to], target(me), send.at[r - 1], recv.at[r - 1], {"seq": to})
        c.start()
        copies.append(c)
    mine = pltpu.make_async_copy(x_ref.at[me], target(me), local)
    mine.start()
    for r in range(1, n):
        dst = target(place(me, r, n))
        remote(dst, dst, send.at[0], recv.at[r - 1], {"seq": place(me, r, n)}).wait_recv()
    mine.wait()
    for c in copies:
        c.wait_send()


def to_tokens(x, n, wide, ident):
    rows = x.shape[1]
    hbm = pl.BlockSpec(memory_space=pl.ANY)
    return pl.pallas_call(
        functools.partial(to_tokens_kernel, n, wide),
        out_shape=jax.ShapeDtypeStruct((rows, n * wide), x.dtype),
        in_specs=[hbm],
        out_specs=hbm,
        scratch_shapes=Blocks.scratch(n),
        compiler_params=pltpu.CompilerParams(collective_id=ident, has_side_effects=True),
        cost_estimate=SMALL,
        name="to_tokens",
    )(x)


def to_heads_kernel(
    n, nf, wide, x_ref, w_ref, t_ref, a_ref, b_ref, z_ref, o_ref, g_ref, m_ref, z_out, t_out, made, *extra
):
    me = lax.axis_index("seq")
    send, recv, local = extra[:3]
    side = Side(2 * n, (a_ref, b_ref, g_ref, m_ref) + extra[3:7])
    planes = PlaneSum(nf, z_ref, 0, *extra[7:])
    side.begin()
    greet([{"seq": place(me, r, n)} for r in range(1, n)] + planes.peers())
    planes.start()

    def copy(r):
        to = place(me, r, n)
        return remote(made.at[r], o_ref.at[me], send.at[r - 1], recv.at[r - 1], {"seq": to})

    def mine():
        return pltpu.make_async_copy(made.at[0], o_ref.at[me], local)

    def step(i, carry):
        r = n - 1 - i
        at = place(me, r, n)
        whole, rest = w_ref.shape[1] // wide, w_ref.shape[1] % wide

        @pl.when(at < whole)
        def _():
            lanes = pl.ds(pl.multiple_of(at * wide, 128), wide)
            made[r] = mm(x_ref[...], w_ref[:, lanes]).astype(made.dtype)

        @pl.when(at >= whole)
        def _():
            made[r] = jnp.zeros(made.shape[1:], made.dtype)

        if rest:

            @pl.when(at == whole)
            def _():
                made[r, :, :rest] = mm(x_ref[...], w_ref[:, whole * wide :]).astype(made.dtype)

        @pl.when(r > 0)
        def _():
            copy(r).start()

        return carry

    lax.fori_loop(0, n, step, 0)
    mine().start()
    side.run(0, 2 * n)
    cols = t_out.shape[0]
    for at in range(0, cols, 512):
        end = min(at + 512, cols)
        t_out[at:end] = lax.dot_general(
            x_ref[:, at:end], t_ref[...], (((0,), (0,)), ((), ())), preferred_element_type=jnp.float32
        ).astype(t_out.dtype)
    side.end()
    planes.finish()
    planes.store(z_out)
    for r in range(1, n):
        dst = o_ref.at[place(me, r, n)]
        remote(dst, dst, send.at[0], recv.at[r - 1], {"seq": me}).wait_recv()
    mine().wait()
    for r in range(1, n):
        copy(r).wait_send()


def to_heads(x, w, t, n, nf, wide, ident, a, b, z, count):
    rows, cols = x.shape
    vmem = pl.BlockSpec(memory_space=pltpu.VMEM)
    hbm = pl.BlockSpec(memory_space=pl.ANY)
    s_ins, s_shapes, s_in_specs, s_out_specs, s_scratch = side_parts((a, b), 2 * n)
    return pl.pallas_call(
        functools.partial(to_heads_kernel, n, nf, wide),
        out_shape=[jax.ShapeDtypeStruct((n, rows, wide), x.dtype)]
        + s_shapes
        + [
            jax.ShapeDtypeStruct((n, count, z.shape[2] // n), z.dtype),
            jax.ShapeDtypeStruct((cols, t.shape[1]), x.dtype),
        ],
        in_specs=[vmem, vmem, vmem] + s_in_specs + [hbm],
        out_specs=[hbm] + s_out_specs + [vmem, vmem],
        scratch_shapes=[pltpu.VMEM((n, rows, wide), x.dtype)]
        + Blocks.scratch(n)
        + s_scratch
        + PlaneSum.scratch(nf, count, z.shape[2]),
        compiler_params=pltpu.CompilerParams(
            collective_id=ident, has_side_effects=True, vmem_limit_bytes=60 << 20
        ),
        cost_estimate=SMALL,
        name="to_heads",
    )(x, w, t, *s_ins, z)


def contract_kernel(
    n, nf, a_ref, b_ref, x_ref, y_ref, s_ref, p_ref, q_ref, c_ref, o_ref, sum_ref, p_out, q_out, c_out, acc, *sems
):
    i = pl.program_id(0)
    parts = [
        Blocks("seq", n, False, p_ref, p_out, *sems[:3]),
        Blocks("seq", n, False, q_ref, q_out, *sems[3:6]),
        Units(n, nf, True, c_ref, c_out, *sems[6:]),
    ]

    @pl.when(i == 0)
    def _():
        me = lax.axis_index("seq")
        greet([{"seq": place(me, r, n)} for r in range(1, n)])
        for part in parts:
            part.start()

    sum_ref[...] = (x_ref[...] + y_ref[...].astype(jnp.float32) + s_ref[...]).astype(sum_ref.dtype)
    part = lax.dot_general(
        a_ref[...], b_ref[...], (((0,), (0,)), ((), ())), preferred_element_type=jnp.float32
    )

    @pl.when(i == 0)
    def _():
        acc[...] = part

    @pl.when(i > 0)
    def _():
        acc[...] += part

    @pl.when(i == pl.num_programs(0) - 1)
    def _():
        o_ref[...] = acc[...].astype(o_ref.dtype)
        for part in parts:
            part.finish()


def contract(a, b, x, y, s, p, q, c, n, nf, tile, ident):
    steps = a.shape[0] // tile
    shape = (a.shape[1], b.shape[1])
    still = lambda s: pl.BlockSpec(s, lambda i: (0,) * len(s), pipeline_mode=pl.Buffered(1))
    part = lambda v: pl.BlockSpec((v.shape[0] // steps, v.shape[1]), lambda i: (i, 0))
    hbm = pl.BlockSpec(memory_space=pl.ANY)
    return pl.pallas_call(
        functools.partial(contract_kernel, n, nf),
        out_shape=[
            jax.ShapeDtypeStruct(shape, a.dtype),
            jax.ShapeDtypeStruct(x.shape, a.dtype),
            blocks_shape(p, n, False),
            blocks_shape(q, n, False),
            blocks_shape(c, nf, False),
        ],
        grid=(steps,),
        in_specs=[part(a), part(b), part(x), part(y), still(s.shape), hbm, hbm, hbm],
        out_specs=[still(shape), part(x), hbm, hbm, hbm],
        scratch_shapes=[pltpu.VMEM(shape, jnp.float32)]
        + Blocks.scratch(n)
        + Blocks.scratch(n)
        + Units.scratch(nf),
        compiler_params=pltpu.CompilerParams(
            dimension_semantics=("arbitrary",),
            vmem_limit_bytes=40 << 20,
            collective_id=ident,
            has_side_effects=True,
        ),
        cost_estimate=SMALL,
        name="contract",
    )(a, b, x, y, s, p, q, c)


def give_back_kernel(
    n, nf, rows, v_ref, w_ref, o_ref, v_out, w_out, o_out, planes, sums, *sems
):
    s = lax.axis_index("seq")
    f = lax.axis_index("fsdp")
    sems = list(sems)
    take = lambda k: [sems.pop(0) for _ in range(k)]
    send_z, recv_z, send_s, recv_s = take(4)
    parts = []
    if rows is not None:
        parts.append(rows.bind(w_ref, w_out, *take(3)))
    parts.append(Blocks("fsdp", nf, False, o_ref, o_out, *take(3)))
    others = [{"fsdp": lax.rem(f + d, nf)} for d in range(1, nf)]
    peers = [{"seq": place(s, r, n)} for r in range(1, n)]
    greet(peers + others)
    copies = []
    for d in range(1, nf):
        c = remote(v_ref.at[lax.rem(f + d, nf)], planes.at[d - 1], send_z.at[d - 1], recv_z.at[d - 1], others[d - 1])
        c.start()
        copies.append(c)
    for p in parts:
        p.start()
    total = v_ref[f]
    for d, c in enumerate(copies):
        c.wait_recv()
        total = total + planes[d]
    sums[0] = total
    spread = []
    for r in range(1, n):
        c = remote(sums.at[0], sums.at[r], send_s.at[r - 1], recv_s.at[r - 1], peers[r - 1])
        c.start()
        spread.append(c)
    for r, c in enumerate(spread):
        c.wait_recv()
        total = total + sums[r + 1]
    v_out[...] = total
    for p in parts:
        p.finish()
    for c in copies + spread:
        c.wait_send()


def give_back(vectors, w, held, o, n, nf, rows, ident):
    k = vectors.shape[1]
    tiles = -(-k // 1024) * 8
    padded = jnp.pad(vectors, ((0, 0), (0, tiles * 128 - k))).reshape(nf, tiles, 128)
    vmem = pl.BlockSpec(memory_space=pltpu.VMEM)
    hbm = pl.BlockSpec(memory_space=pl.ANY)
    dma = pltpu.SemaphoreType.DMA
    out = pl.pallas_call(
        functools.partial(give_back_kernel, n, nf, rows),
        out_shape=[
            jax.ShapeDtypeStruct((tiles, 128), jnp.float32),
            jax.ShapeDtypeStruct((held, w.shape[1]), w.dtype),
            blocks_shape(o, nf, False),
        ],
        in_specs=[vmem, hbm, hbm],
        out_specs=[vmem, hbm, hbm],
        scratch_shapes=[
            pltpu.VMEM((nf - 1, tiles, 128), jnp.float32),
            pltpu.VMEM((n, tiles, 128), jnp.float32),
            dma((nf - 1,)),
            dma((nf - 1,)),
            dma((n - 1,)),
            dma((n - 1,)),
        ]
        + (rows.scratch() if rows is not None else [])
        + Blocks.scratch(nf),
        compiler_params=pltpu.CompilerParams(collective_id=ident, has_side_effects=True),
        cost_estimate=SMALL,
        name="give_back",
    )(padded, w, o)
    return (out[0].reshape(-1)[:k],) + tuple(out[1:])


HEAD=64
SCALE=0.125*math.log2(math.e)


def block_pairs(slots, trunk):
    branches = (slots - trunk) // 3
    pairs = []
    for t in range(slots):
        m = t - trunk
        if t < trunk:
            keys = [(c, int(c == t), -1, -1) for c in range(t + 1)]
        else:
            keys = [(c, 0, -1, -1) for c in range(trunk)]
            if m >= branches:
                keys.append((trunk, 0, -1, m))
            keys.append((t, 1, m, -1))
        for i, (c, causal, own, leaf) in enumerate(keys):
            pairs.append((t, c, causal, own, leaf, int(i == 0), int(i == len(keys) - 1)))
    return pairs


def block_fields(p, slots, trunk):
    branches = (slots - trunk) // 3
    counts = [t + 1 for t in range(trunk)] + [trunk + 1] * branches
    counts += [trunk + 2] * (slots - trunk - branches)
    starts = [sum(counts[:t]) for t in range(slots)]
    t, begin, end = jnp.int32(0), jnp.int32(0), jnp.int32(counts[0])
    for i in range(1, slots):
        here = p >= starts[i]
        t = jnp.where(here, i, t)
        begin = jnp.where(here, starts[i], begin)
        end = jnp.where(here, starts[i] + counts[i], end)
    i = p - begin
    last = p == end - 1
    leaf = (t >= trunk + branches) & (i == trunk)
    key = jnp.where((t >= trunk) & last, t, i)
    return t, key, last, leaf, i == 0, last


def block_values(lengths, parents, pairs, block):
    count = lengths.shape[0]
    segments = np.arange(count)
    own = np.array([p[3] for p in pairs])[None, :] == segments[:, None]
    leaf = np.array([p[4] for p in pairs])[None, :] == segments[:, None]
    above = jnp.sum(jnp.where(leaf, parents[:, None], 0), 0)
    source = own | (segments[:, None] + 1 == above[None, :])
    closed = np.array([p[3] < 0 and p[4] < 0 for p in pairs])
    reach = jnp.where(closed, block, jnp.sum(jnp.where(source, lengths[:, None], 0), 0))
    return jnp.stack([jnp.maximum(above - 1, 0), reach]).astype(jnp.int32)


def lane_half(shape):
    return lax.broadcasted_iota(jnp.int32, shape, len(shape) - 1) < HEAD


def nt(a, b):
    return lax.dot_general(a, b, (((1,), (1,)), ((), ())), preferred_element_type=jnp.float32)


def mm(a, b):
    return jnp.dot(a, b, preferred_element_type=jnp.float32)


def attend_kernel(width, block, trunk, n, values, x_ref, w_ref, b_ref, c_ref, qkv, low, att, tot, kt, c_all, acc, xbuf, xsem, *sems):
    p = pl.program_id(0)
    slot, key, causal, leaf, first, last = block_fields(p, n, trunk)
    rows = lambda slot: pl.ds(pl.multiple_of(slot * block, block), block)
    qrow = rows(slot)
    above = values[0, p]
    reach = values[1, p]
    branches = (n - trunk) // 3
    left = lane_half((block, 2 * HEAD))
    spread = Spread(n, c_ref, c_all, *sems)

    def fetch(i):
        slot = lax.rem(i, 2)
        return pltpu.make_async_copy(x_ref.at[i], xbuf.at[slot], xsem.at[slot])

    @pl.when(p == 0)
    def _():
        fetch(jnp.int32(0)).start()
        greet(spread.peers())
        spread.start()

        def step(i, carry):
            @pl.when(i + 1 < n)
            def _():
                fetch(i + 1).start()

            fetch(i).wait()
            made = (mm(xbuf[lax.rem(i, 2)], w_ref[...]) + b_ref[...]).astype(qkv.dtype)
            qkv[rows(i)] = made
            kt[:, rows(i)] = made[:, width : 2 * width].T
            return carry

        lax.fori_loop(0, n, step, 0)
        for i in range(len(spread.bits) - 1):
            spread.phase(i)

    @pl.when(first)
    def _():
        acc[...] = jnp.zeros_like(acc)

    def keyed(mask, read):
        got = read(rows(key))
        if mask is not None:
            for b in range(1, branches):
                got = jnp.where(leaf & (above == b), read(pl.ds((trunk + b) * block, block)), got)
        return got

    def step(mask):
        for j in range(width // (2 * HEAD)):
            lanes = slice(j * 2 * HEAD, (j + 1) * 2 * HEAD)
            q = qkv[qrow, lanes]
            k = keyed(mask, lambda at: qkv[at, width + j * 2 * HEAD : width + (j + 1) * 2 * HEAD])
            v = keyed(mask, lambda at: qkv[at, 2 * width + j * 2 * HEAD : 2 * width + (j + 1) * 2 * HEAD])
            for h in range(2):
                here = left if h == 0 else jnp.logical_not(left)
                s = nt(jnp.where(here, q, 0), k)
                e = jnp.exp2(s * SCALE)
                if mask is not None:
                    e = jnp.where(mask, e, 0.0)
                acc[2 * j + h] += mm(e.astype(jnp.bfloat16), jnp.where(here, v, 1))

    closes = causal | leaf
    shift = jnp.where(causal, 0, block)

    @pl.when(jnp.logical_not(closes))
    def _():
        step(None)

    @pl.when(closes)
    def _():
        row = lax.broadcasted_iota(jnp.int32, (block, block), 0)
        col = lax.broadcasted_iota(jnp.int32, (block, block), 1)
        step((col <= row + shift) & (col < reach))

    @pl.when(last)
    def _():
        for j in range(width // (2 * HEAD)):
            a, b = acc[2 * j], acc[2 * j + 1]
            total = jnp.where(left, pltpu.roll(a, HEAD, 1), pltpu.roll(b, HEAD, 1))
            value = jnp.where(left, a, b) / total
            lanes = slice(j * 2 * HEAD, (j + 1) * 2 * HEAD)
            low[:, lanes] = value.astype(jnp.bfloat16)
            att[:, lanes] = value
            tot[:, lanes] = total

    @pl.when(p == pl.num_programs(0) - 4)
    def _():
        spread.phase(len(spread.bits) - 1)

    @pl.when(p == pl.num_programs(0) - 1)
    def _():
        spread.finish()


def attend(values, pairs, x, w, bias, block, trunk, sent, n, ident):
    rows, width = x.shape[0], w.shape[1] // 3
    by_q = lambda p: (block_fields(p, n, trunk)[0], 0)
    heads = width // HEAD
    once = lambda s: pl.BlockSpec(s, lambda p: (0,) * len(s), pipeline_mode=pl.Buffered(1))
    hbm = pl.BlockSpec(memory_space=pl.ANY)
    out = pl.pallas_call(
        functools.partial(attend_kernel, width, block, trunk, n),
        grid=(len(pairs),),
        out_shape=(
            jax.ShapeDtypeStruct((rows, 3 * width), x.dtype),
            jax.ShapeDtypeStruct((rows, width), x.dtype),
            jax.ShapeDtypeStruct((rows, width), jnp.float32),
            jax.ShapeDtypeStruct((rows, width), jnp.float32),
            jax.ShapeDtypeStruct((width, rows), x.dtype),
            jax.ShapeDtypeStruct((n,) + sent.shape, sent.dtype),
        ),
        in_specs=[pl.BlockSpec(memory_space=pltpu.SMEM), hbm, once(w.shape), once(bias.shape), hbm],
        out_specs=[once((rows, 3 * width))]
        + [pl.BlockSpec((block, width), by_q)] * 3
        + [once((width, rows)), hbm],
        scratch_shapes=[
            pltpu.VMEM((heads, block, 2 * HEAD), jnp.float32),
            pltpu.VMEM((2, block, x.shape[1]), x.dtype),
            pltpu.SemaphoreType.DMA((2,)),
        ]
        + Spread.scratch(n),
        compiler_params=pltpu.CompilerParams(
            dimension_semantics=("arbitrary",),
            vmem_limit_bytes=60 << 20,
            collective_id=ident,
            has_side_effects=True,
        ),
        cost_estimate=SMALL,
        name="attend",
    )(values, x.reshape(n, block, x.shape[1]), w, bias, sent)
    return out[:5] + (out[5].reshape(n * sent.shape[0], sent.shape[1]),)


def attend_back_kernel(width, block, slots, trunk, branches, nf, lows, *refs):
    count = len(lows)
    values, qkv, kt, datt, att, tot = refs[:6]
    sources = refs[6 : 6 + count]
    out, sums = refs[6 + count : 8 + count]
    parts = refs[8 + count : 8 + 2 * count]
    dk, dv, dqt, aug = refs[8 + 2 * count : 12 + 2 * count]
    rest = refs[12 + 2 * count :]
    riders = [PlaneSum(nf, sources[i], lows[i], *rest[4 * i : 4 * i + 4]) for i in range(count)]
    p = pl.program_id(0)
    slot, key, causal, leaf, first, last = block_fields(p, slots, trunk)
    rows = lambda slot: pl.ds(pl.multiple_of(slot * block, block), block)
    above = values[0, p]
    reach = values[1, p]
    qrow = rows(slot)
    left = lane_half((block, 2 * HEAD))
    lane = lax.broadcasted_iota(jnp.int32, (block, 2 * HEAD), 1)
    columns = width // (2 * HEAD)

    @pl.when(p == 0)
    def _():
        greet(riders[0].peers())
        for r in riders:
            r.start()
        dk[...] = jnp.zeros_like(dk)
        dv[...] = jnp.zeros_like(dv)

    @pl.when(first)
    def _():
        dqt[...] = jnp.zeros_like(dqt)
        for j in range(columns):
            lanes = slice(j * 2 * HEAD, (j + 1) * 2 * HEAD)
            d = datt[:, lanes].astype(jnp.float32)
            total = tot[:, lanes]
            low = (d / total).astype(jnp.bfloat16)
            prod = d * att[:, lanes] / total
            for h in range(2):
                here = left if h == 0 else jnp.logical_not(left)
                delta = -jnp.sum(jnp.where(here, prod, 0.0), 1, keepdims=True)
                hi = delta.astype(jnp.bfloat16).astype(jnp.float32)
                mid = (delta - hi).astype(jnp.bfloat16).astype(jnp.float32)
                rest = delta - hi - mid
                at = HEAD * (1 - h)
                extra = jnp.where(
                    lane == at, hi, jnp.where(lane == at + 1, mid, jnp.where(lane == at + 2, rest, 0.0))
                )
                aug[2 * j + h] = jnp.where(here, low.astype(jnp.float32), extra).astype(jnp.bfloat16)

    def add(mask, lanes, dks, dvs):
        at = rows(key)
        if mask is None:
            dk[at, lanes] += dks
            dv[at, lanes] += dvs
            return
        for b in range(branches):
            chosen = causal | (above == b) if b == 0 else leaf & (above == b)
            if b > 0:
                at = pl.ds((trunk + b) * block, block)
            dk[at, lanes] += jnp.where(chosen, dks, 0.0)
            dv[at, lanes] += jnp.where(chosen, dvs, 0.0)

    def keyed(mask, read):
        got = read(rows(key))
        if mask is not None:
            for b in range(1, branches):
                got = jnp.where(leaf & (above == b), read(pl.ds((trunk + b) * block, block)), got)
        return got

    def step(mask):
        for j in range(columns):
            lanes = slice(j * 2 * HEAD, (j + 1) * 2 * HEAD)
            q = qkv[qrow, lanes]
            k = keyed(mask, lambda at: qkv[at, width + j * 2 * HEAD : width + (j + 1) * 2 * HEAD])
            v = keyed(mask, lambda at: qkv[at, 2 * width + j * 2 * HEAD : 2 * width + (j + 1) * 2 * HEAD])
            dvs, dks = [], []
            for h in range(2):
                here = left if h == 0 else jnp.logical_not(left)
                qh = jnp.where(here, q, 0)
                e = jnp.exp2(nt(k, qh) * SCALE)
                if mask is not None:
                    e = jnp.where(mask, e, 0.0)
                dod = aug[2 * j + h]
                ds = (e * nt(jnp.where(here, v * 0.125, 0.125).astype(jnp.bfloat16), dod)).astype(
                    jnp.bfloat16
                )
                dvs.append(mm(e.astype(jnp.bfloat16), dod))
                dks.append(mm(ds, qh))
                at = j * 2 * HEAD + h * HEAD
                dqt[at : at + HEAD] += mm(keyed(mask, lambda i: kt[at : at + HEAD, i]), ds)
            add(mask, lanes, dks[0] + dks[1], jnp.where(left, dvs[0], dvs[1]))

    closes = causal | leaf
    shift = jnp.where(causal, 0, block)

    @pl.when(jnp.logical_not(closes))
    def _():
        step(None)

    @pl.when(closes)
    def _():
        col = lax.broadcasted_iota(jnp.int32, (block, block), 0)
        row = lax.broadcasted_iota(jnp.int32, (block, block), 1)
        step((col <= row + shift) & (col < reach))

    @pl.when(last)
    def _():
        out[qrow, 0:width] = dqt[...].T.astype(jnp.bfloat16)

    @pl.when(p == pl.num_programs(0) - 1)
    def _():
        out[:, width : 2 * width] = dk[...].astype(jnp.bfloat16)
        out[:, 2 * width :] = dv[...].astype(jnp.bfloat16)
        for t in range(3):
            lanes = slice(t * width, (t + 1) * width)
            sums[:, lanes] = jnp.sum(out[:, lanes].astype(jnp.float32), 0, keepdims=True)
        for r, made in zip(riders, parts):
            r.finish()
            r.store(made)


def attend_back(values, pairs, qkv, kt, datt, att, tot, block, trunk, nf, riders, ident):
    rows, width = qkv.shape[0], qkv.shape[1] // 3
    by_q = lambda p: (block_fields(p, rows // block, trunk)[0], 0)
    heads = width // HEAD
    branches = (rows // block - trunk) // 3
    made = [(k, z.shape[1] - at, z.shape[2] // k) for z, at, k in riders]
    once = lambda s: pl.BlockSpec(s, lambda p: (0,) * len(s), pipeline_mode=pl.Buffered(1))
    hbm = pl.BlockSpec(memory_space=pl.ANY)
    out = pl.pallas_call(
        functools.partial(
            attend_back_kernel, width, block, rows // block, trunk, branches, nf, [r[1] for r in riders]
        ),
        grid=(len(pairs),),
        out_shape=[
            jax.ShapeDtypeStruct((rows, 3 * width), jnp.bfloat16),
            jax.ShapeDtypeStruct((1, 3 * width), jnp.float32),
        ]
        + [jax.ShapeDtypeStruct(s, jnp.bfloat16) for s in made],
        in_specs=[pl.BlockSpec(memory_space=pltpu.SMEM), once((rows, 3 * width)), once((width, rows))]
        + [pl.BlockSpec((block, width), by_q)] * 3
        + [hbm] * len(riders),
        out_specs=[once((rows, 3 * width)), once((1, 3 * width))] + [once(s) for s in made],
        scratch_shapes=[
            pltpu.VMEM((rows, width), jnp.float32),
            pltpu.VMEM((rows, width), jnp.float32),
            pltpu.VMEM((width, block), jnp.float32),
            pltpu.VMEM((heads, block, 2 * HEAD), jnp.bfloat16),
        ]
        + sum([PlaneSum.scratch(nf, z.shape[1] - at, z.shape[2]) for z, at, k in riders], []),
        compiler_params=pltpu.CompilerParams(
            dimension_semantics=("arbitrary",),
            vmem_limit_bytes=60 << 20,
            collective_id=ident,
            has_side_effects=True,
        ),
        cost_estimate=SMALL,
        name="attend_back",
    )(values, qkv, kt, datt, att, tot, *[r[0] for r in riders])
    return out[0], out[1], out[2:]


def layer_norm(values, gain, shift):
    centred = values - jnp.mean(values, -1, keepdims=True)
    spread = jnp.mean(centred * centred, -1, keepdims=True)
    return centred * lax.rsqrt(spread + 1e-05) * gain + shift


def contract_rows(left, right):
    return lax.dot_general(
        left, right, (((0,), (0,)), ((), ())), preferred_element_type=jnp.float32
    )


def contract_cols(left, right):
    return lax.dot_general(
        left, right, (((1,), (1,)), ((), ())), preferred_element_type=jnp.float32
    )


def after(value, other):
    return value + (other[(0,) * other.ndim] * 0).astype(value.dtype)


def row_major(x):
    return with_layout_constraint(x, Layout(major_to_minor=tuple(range(x.ndim))))


def local(
    tokens,
    ln1_gain,
    ln1_bias,
    qkv_weight,
    qv_bias,
    out_weight,
    out_bias,
    ln2_gain,
    ln2_bias,
    fc_weight,
    fc_bias,
    proj_weight,
    proj_bias,
    seg_lengths,
    parents,
    cotangent,
):
    n = lax.axis_size("seq")
    nf = lax.axis_size("fsdp")
    s = lax.axis_index("seq")
    f = lax.axis_index("fsdp")
    trunk = n // 4
    block, width = tokens.shape[1], tokens.shape[2]
    rows = width // nf
    hidden = fc_weight.shape[1] * n
    piece = hidden // (n * nf)
    group = n // nf
    wide = 2 * HEAD * (-(-HEADS // (2 * n)))
    low = jnp.bfloat16
    wider = jnp.float32

    vectors = [ln1_gain, ln1_bias, qv_bias, out_bias, ln2_gain, ln2_bias, fc_bias, proj_bias]
    sizes = [v.shape[0] for v in vectors]
    qkv_cols = qkv_weight.shape[1]
    even = qkv_cols % 8 == 0
    forth = Rows(n, qkv_cols, width, wide, False) if even else None
    back = Rows(n, qkv_cols, width, wide, True) if even else None
    turned, proj_blocks, fc_blocks, out_blocks, gathered = exchange(
        qkv_weight.T,
        proj_weight.reshape(n, piece, width // n),
        fc_weight.reshape(rows, nf, piece).transpose(1, 0, 2),
        out_weight,
        [jnp.stack([v for v in vectors if v.shape == ln1_gain.shape])]
        + [v.reshape(1, -1) for v in vectors if v.shape != ln1_gain.shape],
        n,
        nf,
        forth,
        wide,
        0,
    )
    short = iter(jnp.unstack(gathered[0], axis=1))
    long = iter(gathered[1:])
    whole = [next(short) if v.shape == ln1_gain.shape else next(long) for v in vectors]
    whole = [v.reshape(-1).astype(wider) for v in whole]
    gain_one, shift_one, bias_qv, bias_out, gain_two, shift_two, bias_fc, bias_proj = whole
    bias_three = jnp.stack([bias_qv[:width], jnp.zeros((width,), wider), bias_qv[width:]])
    bias_three = jnp.pad(bias_three, ((0, 0), (0, n * wide - width)))
    bias_mine = lax.dynamic_slice_in_dim(bias_three, s * wide, wide, 1).reshape(1, -1)
    bias_hidden = lax.dynamic_index_in_dim(bias_fc.reshape(nf, n, piece), s, 1, False)
    bias_hidden = bias_hidden.reshape(1, -1)

    if even:
        turned = turned.reshape(3, wide, rows)
        kept = lax.broadcasted_iota(jnp.int32, turned.shape, 1) + s * wide < width
        turned = jnp.where(kept, turned, 0).reshape(3 * wide, rows)
    else:
        turned = lax.all_gather(qkv_weight.T, "seq", axis=0, tiled=True).reshape(3, width, rows)
        turned = jnp.pad(turned, ((0, 0), (0, n * wide - width), (0, 0)))
        turned = lax.dynamic_slice_in_dim(turned, s * wide, wide, 1).reshape(3 * wide, rows)
    pairs = block_pairs(n, trunk)
    table = block_values(seg_lengths[0], parents[0], pairs, block)

    resid = tokens[0].astype(wider)
    out_turned = out_blocks.reshape(width, width // n).T
    normed_one, out_turned, qkv_mine = seq_gather(
        layer_norm(resid, gain_one, shift_one).astype(low),
        n,
        1,
        "gather_one",
        rider=(turned.T, True, nf),
        second=out_turned,
    )
    out_turned = out_turned.reshape(width, width)
    qkv_mine = qkv_mine.reshape(width, 3 * wide)
    fc_rows = fc_blocks.transpose(1, 0, 2).reshape(rows, nf * piece)
    fc_mine = lax.all_gather(after(fc_rows, normed_one), "fsdp", axis=0, tiled=True)

    upstream = cotangent[0].astype(wider)
    proj_rows = proj_blocks.transpose(1, 0, 2).reshape(piece, width)
    proj_mine = lax.all_gather(after(proj_rows, normed_one), "fsdp", axis=0, tiled=True)
    projected, attended_low, attended, totals, keys_turned, upstream_all = attend(
        table, pairs, normed_one, qkv_mine, bias_mine, block, trunk, cotangent[0], n, 8
    )
    attended_mine = to_tokens(attended_low.reshape(n, block, wide), n, wide, 2)[:, :width]
    middle = resid + contract_cols(attended_mine, out_turned) + bias_out
    normed_two = layer_norm(middle, gain_two, shift_two).astype(low)
    ff = nf * piece

    def expand(value, fc, bias, proj):
        pre = mm(value, fc[...]) + bias[...]
        bend = math.sqrt(2 / math.pi)
        square = pre * pre
        inner = jnp.tanh(pre * (bend + bend * 0.044715 * square))
        half = 0.5 + 0.5 * inner
        act = (pre * half).astype(low)
        slope = half + 0.5 * pre * (1 - inner * inner) * (bend + 3 * bend * 0.044715 * square)
        return act, slope.astype(low), mm(act, proj[...]).astype(low)

    normed_two, hidden_act, hidden_slope, mixed = seq_gather(
        normed_two,
        n,
        3,
        "gather_two",
        expand,
        (fc_mine, bias_hidden, proj_mine),
        ((ff, low), (ff, low), (width, low)),
        modes=(0, 0, 0),
    )

    def shrink(up, slope, proj, fc):
        grad = (nt(up, proj[...]) * slope.astype(wider)).astype(low)
        return nt(grad, fc[...]), grad

    grad_normed_two, grad_pre, grad_proj, unused_sums, mixed = seq_scatter(
        n,
        width,
        4,
        "scatter_two",
        shrink,
        (upstream_all, hidden_slope),
        (proj_mine, fc_mine),
        ((ff, low),),
        side=(hidden_act, upstream_all),
        carry=mixed,
    )
    mixed = lax.psum_scatter(mixed, "seq", scatter_dimension=0, tiled=True)
    grad_proj = grad_proj.reshape(nf, piece, width)
    cut = piece // 16 * 8
    unused_two, norm_two_back = jax.vjp(layer_norm, middle, gain_two, shift_two)
    grad_middle_norm, grad_gain_two, grad_shift_two = norm_two_back(grad_normed_two)
    grad_middle = upstream + grad_middle_norm
    grad_branch = grad_middle.astype(low)
    grad_attended, grad_fc, hidden_sums, proj_first, grad_out = to_heads(
        grad_branch,
        out_turned,
        attended_mine,
        n,
        nf,
        wide,
        5,
        normed_two,
        grad_pre,
        grad_proj,
        cut,
    )
    grad_attended = grad_attended.reshape(n * block, wide)
    grad_projected, column_sums, (fc_part, proj_second) = attend_back(
        table,
        pairs,
        projected,
        keys_turned,
        grad_attended,
        attended,
        totals,
        block,
        trunk,
        nf,
        ((grad_fc.reshape(nf, rows, ff), 0, nf), (grad_proj, cut, n)),
        9,
    )
    grad_qkv, output, proj_first, proj_second, fc_out = contract(
        normed_one,
        grad_projected,
        middle,
        mixed,
        bias_proj.reshape(1, -1),
        proj_first,
        proj_second,
        fc_part,
        n,
        nf,
        block,
        10,
    )
    output = output[None]
    input_grad, grad_gain_one, grad_shift_one, qkv_parts = seq_scatter(
        n,
        width,
        6,
        "scatter_one",
        lambda g, w: (nt(g, w[...]),),
        (grad_projected,),
        (qkv_mine,),
        rider=(grad_qkv.reshape(nf, rows, 3 * wide), False, nf),
        norm=(tokens[0], gain_one.reshape(1, -1), grad_middle, low),
    )
    input_grad = input_grad[None]

    out_part = lax.psum_scatter(grad_out, "seq", scatter_dimension=0, tiled=True).T
    out_part = after(out_part, qkv_parts).reshape(nf, rows, width // n)
    qkv_part = jnp.sum(qkv_parts.astype(wider), 0).astype(low).T

    column_sums = column_sums.reshape(3, wide)
    placed = lax.dynamic_update_slice_in_dim(
        jnp.zeros((3, n * wide), wider), column_sums, s * wide, 1
    )[:, :width]
    grad_qv = jnp.concatenate([placed[0], placed[2]])
    hidden_sums = hidden_sums.reshape(nf, 1, piece)
    grad_fc_bias = lax.dynamic_update_slice_in_dim(
        jnp.zeros((nf, n, piece), wider), hidden_sums, s, 1
    )
    parts = [
        grad_gain_one,
        grad_shift_one,
        grad_qv,
        jnp.sum(grad_branch.astype(wider), 0),
        grad_gain_two,
        grad_shift_two,
        grad_fc_bias,
        jnp.sum(upstream, 0),
    ]
    summed, qkv_out, out_out = give_back(
        jnp.concatenate([p.reshape(nf, -1) for p in parts], 1),
        qkv_part,
        qkv_cols,
        out_part,
        n,
        nf,
        back,
        7,
    )
    if not even:
        qkv_part = qkv_part.reshape(3, wide, rows)
        qkv_out = lax.all_gather(qkv_part, "seq", axis=1, tiled=True)[:, :width]
        qkv_out = qkv_out.reshape(3 * width, rows)
        qkv_out = lax.dynamic_slice_in_dim(qkv_out, s * qkv_cols, qkv_cols, 0)
    out_out = jnp.sum(out_out.astype(wider), 0)
    qkv_out = qkv_out.T.astype(wider)
    proj_out = jnp.concatenate([proj_first, proj_second], 1)
    proj_out = proj_out.reshape(n * piece, width // n).astype(wider)
    fc_out = fc_out.transpose(1, 0, 2).reshape(rows, nf * piece).astype(wider)
    vector_out = []
    at = 0
    for size in sizes:
        vector_out.append(summed[at : at + size])
        at += size
    return (
        output,
        input_grad,
        vector_out[0],
        vector_out[1],
        qkv_out,
        vector_out[2],
        out_out,
        vector_out[3],
        vector_out[4],
        vector_out[5],
        fc_out,
        vector_out[6],
        proj_out,
        vector_out[7],
    )


def solution(mesh):
    in_specs = (
        P("fsdp", "seq", None),
        P("fsdp"),
        P("fsdp"),
        P("fsdp", "seq"),
        P("fsdp"),
        P("fsdp", "seq"),
        P("fsdp"),
        P("fsdp"),
        P("fsdp"),
        P("fsdp", "seq"),
        P("fsdp"),
        P("fsdp", "seq"),
        P("fsdp"),
        P("fsdp", None),
        P("fsdp", None),
        P("fsdp", "seq", None),
    )
    out_specs = (
        P("fsdp", "seq", None),
        P("fsdp", "seq", None),
        P("fsdp"),
        P("fsdp"),
        P("fsdp", "seq"),
        P("fsdp"),
        P("fsdp", "seq"),
        P("fsdp"),
        P("fsdp"),
        P("fsdp"),
        P("fsdp", "seq"),
        P("fsdp"),
        P("fsdp", "seq"),
        P("fsdp"),
    )
    return jax.shard_map(local, mesh=mesh, in_specs=in_specs, out_specs=out_specs, check_vma=False)
```

```python
import functools
import math

import jax
import jax.numpy as jnp
import numpy as np
from jax import lax
from jax.experimental import pallas as pl
from jax.experimental.layout import Layout, with_layout_constraint
from jax.experimental.pallas import tpu as pltpu
from jax.sharding import PartitionSpec as P

MESH = pl.DeviceIdType.MESH
HEADS = 25
SMALL = pl.CostEstimate(flops=0, bytes_accessed=1 << 20, transcendentals=0)


def route_bits(n):
    bits = []
    b = 2
    while b < n:
        bits.append(b)
        b *= 2
    return bits


def flip(a, b):
    return jnp.where(lax.rem(lax.div(a, b), 2) == 0, a + b, a - b)


def place(me, r, n):
    if isinstance(r, int):
        for b in [1] + route_bits(n):
            if r & b:
                me = flip(me, b)
        return me
    for b in [1] + route_bits(n):
        me = jnp.where(lax.rem(lax.div(r, b), 2) == 0, me, flip(me, b))
    return me


def pick(table, q):
    value = jnp.int32(table[0])
    for i, entry in enumerate(table[1:]):
        value = jnp.where(q == i + 1, jnp.int32(entry), value)
    return value


def greet(ids):
    barrier = pltpu.get_barrier_semaphore()
    for i in ids:
        pl.semaphore_signal(barrier, inc=1, device_id=i, device_id_type=MESH)
    pl.semaphore_wait(barrier, len(ids))


def remote(src, dst, send, recv, device):
    return pltpu.make_async_remote_copy(
        src_ref=src, dst_ref=dst, send_sem=send, recv_sem=recv, device_id=device, device_id_type=MESH
    )


class Blocks:
    def __init__(self, axis, size, same, source, target, send, recv, local):
        self.axis, self.size, self.same = axis, size, same
        self.source, self.target = source, target
        self.send, self.recv, self.local = send, recv, local
        self.me = lax.axis_index(axis)

    @staticmethod
    def scratch(size):
        dma = pltpu.SemaphoreType.DMA
        return [dma((size - 1,)), dma((size - 1,)), dma]

    def peers(self):
        return [{self.axis: lax.rem(self.me + d, self.size)} for d in range(1, self.size)]

    def copy(self, d):
        to = lax.rem(self.me + d, self.size)
        src = self.source if self.same else self.source.at[to]
        return remote(src, self.target.at[self.me], self.send.at[d - 1], self.recv.at[d - 1], {self.axis: to})

    def own(self):
        src = self.source if self.same else self.source.at[self.me]
        return pltpu.make_async_copy(src, self.target.at[self.me], self.local)

    def start(self):
        for d in range(1, self.size):
            self.copy(d).start()
        self.own().start()

    def finish(self):
        for d in range(1, self.size):
            dst = self.target.at[lax.rem(self.me + self.size - d, self.size)]
            remote(dst, dst, self.send.at[d - 1], self.recv.at[d - 1], {self.axis: self.me}).wait_recv()
        self.own().wait()
        for d in range(1, self.size):
            self.copy(d).wait_send()


class Spread:
    def __init__(self, n, source, target, send, recv, local):
        self.n, self.source, self.target = n, source, target
        self.send, self.recv, self.local = send, recv, local
        self.me = lax.axis_index("seq")
        self.bits = route_bits(n)
        self.orders = [self.bits, self.bits[::-1]]
        self.h = source.shape[0] // 2

    @staticmethod
    def scratch(n):
        dma = pltpu.SemaphoreType.DMA
        return [dma((2, len(route_bits(n)) + 1, n)), dma((2, n)), dma]

    def device(self, b):
        return {"seq": flip(self.me, b)}

    def peers(self):
        return [self.device(b) for b in [1] + self.bits]

    def rows(self, half):
        return pl.ds(half * self.h, self.h)

    def ship(self, half, k, b):
        owner = place(self.me, k, self.n)
        src = self.source if k == 0 else self.target.at[owner]
        lane = 0 if b == 1 else 1 + self.bits.index(b)
        return remote(
            src.at[self.rows(half)],
            self.target.at[owner].at[self.rows(half)],
            self.send.at[half, lane, k],
            self.recv.at[half, k ^ b],
            self.device(b),
        )

    def arrive(self, half, k):
        dst = self.target.at[place(self.me, k, self.n)].at[self.rows(half)]
        remote(dst, dst, self.send.at[half, 0, 0], self.recv.at[half, k], self.device(1)).wait_recv()

    def own(self):
        return pltpu.make_async_copy(self.source, self.target.at[self.me], self.local)

    def fresh(self, half, i):
        had = [0]
        for b in self.orders[half][:i]:
            had = had + [k ^ b for k in had]
        return [k ^ self.orders[half][i] for k in had]

    def start(self):
        for i in range(len(self.bits)):
            for half in (0, 1):
                self.ship(half, 0, self.orders[half][i]).start()
        for half in (0, 1):
            self.ship(half, 0, 1).start()
        self.own().start()

    def phase(self, i):
        for half in (0, 1):
            for k in self.fresh(half, i):
                self.arrive(half, k)
                for b in self.orders[half][i + 1 :] + [1]:
                    self.ship(half, k, b).start()

    def finish(self):
        for half in (0, 1):
            for k in range(1, self.n, 2):
                self.arrive(half, k)
        self.own().wait()
        for half in (0, 1):
            for b in self.orders[half] + [1]:
                self.ship(half, 0, b).wait_send()
            for i in range(len(self.bits)):
                for k in self.fresh(half, i):
                    for b in self.orders[half][i + 1 :] + [1]:
                        self.ship(half, k, b).wait_send()


class PlaneSum(Blocks):
    def __init__(self, size, source, low, target, send, recv, local):
        super().__init__("fsdp", size, False, source, target, send, recv, local)
        self.window = pl.ds(low, target.shape[1])

    @staticmethod
    def scratch(size, rows, cols):
        return [pltpu.VMEM((size, rows, cols), jnp.bfloat16)] + Blocks.scratch(size)

    def copy(self, d):
        to = lax.rem(self.me + d, self.size)
        src = self.source.at[to].at[self.window]
        return remote(src, self.target.at[self.me], self.send.at[d - 1], self.recv.at[d - 1], {self.axis: to})

    def own(self):
        src = self.source.at[self.me].at[self.window]
        return pltpu.make_async_copy(src, self.target.at[self.me], self.local)

    def store(self, out):
        total = self.target[0].astype(jnp.float32)
        for i in range(1, self.size):
            total = total + self.target[i].astype(jnp.float32)
        cols = out.shape[2]
        for i in range(out.shape[0]):
            out[i] = total[:, i * cols : (i + 1) * cols].astype(out.dtype)


def blocks_shape(x, size, same):
    return jax.ShapeDtypeStruct(((size,) + x.shape) if same else x.shape, x.dtype)


def arrival_order(n):
    bits = route_bits(n)
    orders = [bits, bits[::-1]]
    lists = []
    for order in orders:
        held, phases = [0], [-1]
        for i, b in enumerate(order):
            fresh = [h ^ b for h in held]
            held, phases = held + fresh, phases + [i] * len(fresh)
        lists.append(list(zip(held, phases)))
    entries = []
    for i in range(n // 2):
        for odd in (0, 1):
            for half in (0, 1):
                k, phase = lists[half][i]
                entries.append((half, k ^ odd, phase, odd))
    return orders, entries


def gather_kernel(n, h, body, n_const, n_out, relative, modes, nf, same, second, *refs):
    if second:
        at = 1 + n_const
        out = at + 1 + min(nf, 1) + 1 + n_out
        w_ref, w_all = refs[at], refs[out]
        w_send, w_recv, w_keep = refs[-3:]
        refs = refs[:at] + refs[at + 1 : out] + refs[out + 1 : -3]
        w_half = w_ref.shape[1] // 256 * 128
        w_lanes = [pl.ds(0, w_half), pl.ds(w_half, w_ref.shape[1] - w_half)]
    refs, rider = split_rider(refs, nf, same, 1 + n_const, 1 + n_out)
    x_ref = refs[0]
    consts = refs[1 : 1 + n_const]
    all_ref = refs[1 + n_const]
    outs = refs[2 + n_const : 2 + n_const + n_out]
    held = refs[2 + n_const + n_out]
    stages = refs[3 + n_const + n_out : 3 + n_const + 2 * n_out]
    send, recv, keep, store = refs[3 + n_const + 2 * n_out :]
    me = lax.axis_index("seq")
    orders, entries = arrival_order(n)
    bits = orders[0]
    nb = len(bits)

    def device(b):
        return {"seq": flip(me, b)}

    def spot(half, k):
        return 2 * (k if relative else place(me, k, n)) + half

    def ship(half, k, b):
        at = spot(half, k)
        src = x_ref.at[pl.ds(half * h, h)] if isinstance(k, int) and k == 0 else held.at[at]
        lane = 0 if b == 1 else 1 + bits.index(b)
        to = k ^ b if isinstance(k, int) else place(k, b, n)
        dst = 2 * to + half if relative else at
        first = remote(src, held.at[dst], send.at[half, lane, k], recv.at[half, to], device(b))
        if not second:
            return [first]
        owner = place(me, k, n)
        lanes = w_lanes[half]
        src = w_ref if isinstance(k, int) and k == 0 else w_all.at[owner]
        other = remote(
            src.at[:, lanes], w_all.at[owner].at[:, lanes], w_send.at[half, lane, k], w_recv.at[half, to], device(b)
        )
        return [first, other]

    def each(copies, act):
        for c in copies:
            act(c)

    def w_arrive(half, k):
        dst = w_all.at[place(me, k, n)].at[:, w_lanes[half]]
        remote(dst, dst, w_send.at[0, 0, 0], w_recv.at[half, k], device(1)).wait_recv()

    greet([device(b) for b in [1] + bits] + (rider.peers() if nf else []))
    for i in range(nb):
        for half in (0, 1):
            each(ship(half, 0, orders[half][i]), lambda c: c.start())
    for half in (0, 1):
        each(ship(half, 0, 1), lambda c: c.start())
    if second:
        pltpu.make_async_copy(w_ref, w_all.at[me], w_keep).start()
    if nf:
        rider.start()

    def output(o, q, at):
        slot = lax.rem(q, 2)
        return pltpu.make_async_copy(stages[o].at[slot], outs[o].at[at], store.at[o, slot])

    def entry(q, at, value):
        results = body(value, *consts)
        for o in range(n_out):

            @pl.when(q >= 2)
            def _(o=o):
                output(o, q, at[modes[o]]).wait()

            stages[o][lax.rem(q, 2)] = results[o]
            output(o, q, at[modes[o]]).start()

    def step(q, carry):
        half = pick([e[0] for e in entries], q)
        k = pick([e[1] for e in entries], q)
        phase = pick([e[2] for e in entries], q)
        odd = pick([e[3] for e in entries], q)
        at = spot(half, k)

        @pl.when(k == 0)
        def _():
            held[at] = x_ref[pl.ds(pl.multiple_of(half * h, h), h)]

        @pl.when(k != 0)
        def _():
            remote(held.at[at], held.at[at], send.at[0, 0, 0], recv.at[half, k], device(1)).wait_recv()

        for side in (0, 1) if second else ():

            @pl.when((k != 0) & (half == side))
            def _(side=side):
                w_arrive(side, k)

        for side in (0, 1):
            for i in range(nb):

                @pl.when((half == side) & (odd == 0) & (k != 0) & (phase < i))
                def _(side=side, i=i):
                    each(ship(side, k, orders[side][i]), lambda c: c.start())

            @pl.when((half == side) & (odd == 0) & (k != 0))
            def _(side=side):
                each(ship(side, k, 1), lambda c: c.start())

        pltpu.make_async_copy(held.at[at], all_ref.at[at], keep.at[q]).start()
        if n_out:
            entry(q, (2 * place(me, k, n) + half, 2 * k + half), held[at])
        return carry

    lax.fori_loop(0, 2 * n, step, 0)
    for q, (half, k, phase, odd) in enumerate(entries):
        at = spot(half, k)
        pltpu.make_async_copy(held.at[at], all_ref.at[at], keep.at[q]).wait()
        if q >= 2 * n - 2:
            for o in range(n_out):
                output(o, jnp.int32(q), at).wait()
        if not odd:
            for i in range(nb):
                if phase < i:
                    each(ship(half, k, orders[half][i]), lambda c: c.wait_send())
            each(ship(half, k, 1), lambda c: c.wait_send())
    if second:
        pltpu.make_async_copy(w_ref, w_all.at[me], w_keep).wait()
    if nf:
        rider.finish()


def split_rider(refs, nf, same, n_in, n_out):
    if not nf:
        return refs, None
    source = refs[n_in]
    target = refs[n_in + 1 + n_out]
    rider = Blocks("fsdp", nf, same, source, target, *refs[-3:])
    return refs[:n_in] + refs[n_in + 1 : n_in + 1 + n_out] + refs[n_in + 2 + n_out : -3], rider


def rider_parts(rider):
    if rider is None:
        return [], [], [], [], 0, False
    x, same, nf = rider
    hbm = [pl.BlockSpec(memory_space=pl.ANY)]
    return [x], hbm, [blocks_shape(x, nf, same)], Blocks.scratch(nf), nf, same


def seq_gather(x, n, ident, name, body=None, consts=(), outs=(), relative=False, modes=None, rider=None, second=None):
    rows, cols = x.shape
    h = rows // 2
    nb = len(route_bits(n))
    shapes = [jax.ShapeDtypeStruct((2 * n, h, c), d) for c, d in outs]
    vmem = pl.BlockSpec(memory_space=pltpu.VMEM)
    hbm = pl.BlockSpec(memory_space=pl.ANY)
    more, spec, shape, scratch, nf, same = rider_parts(rider)
    also = [] if second is None else [second]
    out = pl.pallas_call(
        functools.partial(
            gather_kernel, n, h, body, len(consts), len(outs), relative, modes, nf, same, second is not None
        ),
        out_shape=[jax.ShapeDtypeStruct((2 * n, h, cols), x.dtype)]
        + shapes
        + [jax.ShapeDtypeStruct((n,) + w.shape, w.dtype) for w in also]
        + shape,
        in_specs=[vmem] * (1 + len(consts)) + [hbm] * len(also) + spec,
        out_specs=[hbm] * (1 + len(outs)) + [hbm] * len(also) + spec,
        scratch_shapes=[pltpu.VMEM((2 * n, h, cols), x.dtype)]
        + [pltpu.VMEM((2, h, c), d) for c, d in outs]
        + [
            pltpu.SemaphoreType.DMA((2, nb + 1, n)),
            pltpu.SemaphoreType.DMA((2, n)),
            pltpu.SemaphoreType.DMA((2 * n,)),
            pltpu.SemaphoreType.DMA((max(len(outs), 1), 2)),
        ]
        + scratch
        + [
            pltpu.SemaphoreType.DMA((2, nb + 1, n)),
            pltpu.SemaphoreType.DMA((2, n)),
            pltpu.SemaphoreType.DMA,
        ]
        * len(also),
        compiler_params=pltpu.CompilerParams(
            collective_id=ident, has_side_effects=True, vmem_limit_bytes=60 << 20
        ),
        cost_estimate=SMALL,
        name=name,
    )(x, *consts, *also, *more)
    return [o.reshape(2 * n * h, o.shape[2]) for o in out[: 1 + len(outs)]] + list(out[1 + len(outs) :])


class Side:
    def __init__(self, count, refs):
        self.count = count
        self.a, self.b, self.grad, self.sums, self.acc, self.abuf, self.bbuf, self.load = refs

    def fetch(self, i):
        slot = lax.rem(i, 2)
        return [
            pltpu.make_async_copy(self.a.at[i], self.abuf.at[slot], self.load.at[0, slot]),
            pltpu.make_async_copy(self.b.at[i], self.bbuf.at[slot], self.load.at[1, slot]),
        ]

    def begin(self):
        self.acc[...] = jnp.zeros_like(self.acc)
        self.sums[...] = jnp.zeros_like(self.sums)
        for c in self.fetch(jnp.int32(0)):
            c.start()

    def run(self, first, last):
        def step(i, carry):
            @pl.when(i + 1 < self.count)
            def _():
                for c in self.fetch(i + 1):
                    c.start()

            for c in self.fetch(i):
                c.wait()
            slot = lax.rem(i, 2)
            a, b = self.abuf[slot], self.bbuf[slot]
            self.acc[...] += lax.dot_general(
                a, b, (((0,), (0,)), ((), ())), preferred_element_type=jnp.float32
            )
            self.sums[...] += jnp.sum(b.astype(jnp.float32), 0, keepdims=True)
            return carry

        lax.fori_loop(first, last, step, 0)

    def end(self):
        self.grad[...] = self.acc[...].astype(self.grad.dtype)


def side_parts(side, count):
    if side is None:
        return [], [], [], [], []
    a, b = side
    h = a.shape[0] // count
    low = jnp.bfloat16
    hbm = pl.BlockSpec(memory_space=pl.ANY)
    vmem = pl.BlockSpec(memory_space=pltpu.VMEM)
    return (
        [x.reshape(count, h, x.shape[1]) for x in (a, b)],
        [
            jax.ShapeDtypeStruct((a.shape[1], b.shape[1]), low),
            jax.ShapeDtypeStruct((1, b.shape[1]), jnp.float32),
        ],
        [hbm, hbm],
        [vmem, vmem],
        [
            pltpu.VMEM((a.shape[1], b.shape[1]), jnp.float32),
            pltpu.VMEM((2, h, a.shape[1]), low),
            pltpu.VMEM((2, h, b.shape[1]), low),
            pltpu.SemaphoreType.DMA((2, 2)),
        ],
    )


def scatter_order(n):
    bits = route_bits(n)
    orders = [bits, bits[::-1]]
    lists = [
        sorted(range(0, n, 2), key=lambda k: [-int(bool(k & b)) for b in order]) for order in orders
    ]
    return orders, [(half, lists[half][i]) for i in range(n // 2) for half in (0, 1)]


def scatter_kernel(n, h, body, n_in, n_const, n_out, modes, nf, same, has_side, has_norm, carried, *refs):
    if carried:
        out = 1 + n_in + n_const + 2 * has_side + min(nf, 1) + 1 + n_out + 2 * has_side + min(nf, 1)
        refs = refs[1:out] + refs[out + 1 :]
    if has_norm:
        out = n_in + 3 + n_const + 2 * has_side + min(nf, 1)
        values, gain, joins = refs[:3]
        x_grad, g_grad, b_grad = refs[out], refs[out + 1], refs[out + 2]
        refs = refs[3:out] + (None,) + refs[out + 3 :]
    side = None
    if has_side:
        at = n_in + n_const
        out = at + 2 + min(nf, 1) + 1 + n_out
        extra = refs[at : at + 2] + refs[out : out + 2] + refs[-4:]
        refs = refs[:at] + refs[at + 2 : out] + refs[out + 2 : -4]
        side = Side(2 * n, extra)
    refs, rider = split_rider(refs, nf, same, n_in + n_const, 1 + n_out)
    ins = refs[:n_in]
    consts = refs[n_in : n_in + n_const]
    at = n_in + n_const
    sum_ref = refs[at]
    outs = refs[at + 1 : at + 1 + n_out]
    at += 1 + n_out
    give, pair, own, far, total = refs[at : at + 5]
    at += 5
    loads = refs[at : at + n_in]
    stages = refs[at + n_in : at + n_in + n_out]
    pair_send, pair_recv, far_send, far_recv, load, store, done = refs[at + n_in + n_out :]
    me = lax.axis_index("seq")
    orders, entries = scatter_order(n)
    bits = orders[0]
    slots = give.shape[0]
    index = {e: j for j, e in enumerate(entries)}

    def device(b):
        return {"seq": flip(me, b)}

    def phase_of(half, k):
        for i, b in enumerate(orders[half]):
            if k & b:
                return i
        return len(bits)

    landing = {}
    for half in (0, 1):
        for i, b in enumerate(orders[half]):
            for k in range(0, n, 2):
                if phase_of(half, k) == i:
                    landing[half, i, k ^ b] = len(landing)

    halves = [e[0] for e in entries]
    ks = [e[1] for e in entries]

    def spot(q, relative):
        j = lax.div(q, 2)
        k = pick(ks, j)
        k = jnp.where(lax.rem(q, 2) == 0, flip(k, 1), k)
        return 2 * (k if relative else place(me, k, n)) + pick(halves, j)

    def fetch(q):
        slot = lax.rem(q, 2)
        return [
            pltpu.make_async_copy(ins[i].at[spot(q, modes[0][i])], loads[i].at[slot], load.at[i, slot])
            for i in range(n_in)
        ]

    def output(o, q):
        slot = lax.rem(q, 2)
        return pltpu.make_async_copy(stages[o].at[slot], outs[o].at[spot(q, modes[1][o])], store.at[o, slot])

    def hand(j):
        slot = lax.rem(j, slots)
        return remote(give.at[slot], pair.at[j], pair_send.at[j], pair_recv.at[j], device(1))

    def launch(half, k):
        i = phase_of(half, k)
        b = orders[half][i]
        to = landing[half, i, k ^ b]
        return remote(own.at[index[half, k]], far.at[to], far_send.at[to], far_recv.at[to], device(b))

    def join(j):
        hand(j).wait_recv()
        own[j] = (own[j].astype(jnp.float32) + pair[j].astype(jnp.float32)).astype(own.dtype)
        for e, (half, k) in enumerate(entries):
            if phase_of(half, k) == 0:

                @pl.when(j == e)
                def _(half=half, k=k):
                    launch(half, k).start()

    for c in fetch(jnp.int32(0)):
        c.start()
    greet([device(b) for b in [1] + bits] + (rider.peers() if nf else []))
    if nf:
        rider.start()

    def step(q, carry):
        j = lax.div(q, 2)
        slot = lax.rem(q, 2)

        @pl.when(q + 1 < 2 * n)
        def _():
            for c in fetch(q + 1):
                c.start()

        for c in fetch(q):
            c.wait()
        part, *results = body(*[r[slot] for r in loads], *consts)
        for o in range(n_out):

            @pl.when(q >= 2)
            def _(o=o):
                output(o, q).wait()

            stages[o][slot] = results[o]
            output(o, q).start()

        @pl.when(slot == 0)
        def _():
            @pl.when(j >= slots)
            def _():
                hand(j - slots).wait_send()

            give[lax.rem(j, slots)] = part.astype(give.dtype)
            hand(j).start()

        @pl.when(slot == 1)
        def _():
            own[j] = part.astype(own.dtype)

            @pl.when(j >= 1)
            def _():
                join(j - 1)

        return carry

    lax.fori_loop(0, 2 * n, step, 0)
    if side:
        side.begin()
    join(jnp.int32(n - 1))
    first = n // 2
    cuts = [0, first] + [first + (2 * n - first) * i // (len(bits) - 1) for i in range(1, len(bits))]
    for i in range(len(bits)):
        if side:
            side.run(cuts[i], cuts[i + 1])
        for half in (0, 1):
            order = orders[half]
            for k in [k for hh, k in entries if hh == half and phase_of(half, k) > i]:
                to = landing[half, i, k]
                remote(far.at[to], far.at[to], far_send.at[to], far_recv.at[to], device(1)).wait_recv()
                j = index[half, k]
                rows = pl.ds(half * h, h)
                if i == len(bits) - 1:
                    total[rows] = own[j].astype(jnp.float32) + far[to].astype(jnp.float32)
                    if not has_norm:
                        pltpu.make_async_copy(total.at[rows], sum_ref.at[rows], done.at[half]).start()
                else:
                    own[j] = (own[j].astype(jnp.float32) + far[to].astype(jnp.float32)).astype(own.dtype)
                    if phase_of(half, k) == i + 1:
                        launch(half, k).start()
    if has_norm:
        g_grad[...] = jnp.zeros_like(g_grad)
        b_grad[...] = jnp.zeros_like(b_grad)

        def tile(i, carry):
            rows = pl.ds(pl.multiple_of(i * 64, 64), 64)
            x = values[rows].astype(jnp.float32)
            centred = x - jnp.mean(x, -1, keepdims=True)
            scale = lax.rsqrt(jnp.mean(centred * centred, -1, keepdims=True) + 1e-05)
            xhat = centred * scale
            grad = total[rows]
            g_grad[...] += jnp.sum(grad * xhat, 0, keepdims=True)
            b_grad[...] += jnp.sum(grad, 0, keepdims=True)
            e = gain[...] * grad
            inner = e - jnp.mean(e, -1, keepdims=True) - xhat * jnp.mean(e * xhat, -1, keepdims=True)
            x_grad[rows] = (joins[rows].astype(jnp.float32) + scale * inner).astype(x_grad.dtype)
            return carry

        lax.fori_loop(0, 2 * h // 64, tile, 0)
    for half in (0, 1) if not has_norm else ():
        rows = pl.ds(half * h, h)
        pltpu.make_async_copy(total.at[rows], sum_ref.at[rows], done.at[half]).wait()
    for q in (2 * n - 2, 2 * n - 1):
        for o in range(n_out):
            output(o, jnp.int32(q)).wait()
    for j in range(max(n - slots, 0), n):
        hand(jnp.int32(j)).wait_send()
    for half, k in entries:
        if phase_of(half, k) < len(bits):
            launch(half, k).wait_send()
    if nf:
        rider.finish()
    if side:
        side.end()


def seq_scatter(n, cols, ident, name, body, ins, consts, outs=(), modes=None, rider=None, side=None, norm=None, carry=None):
    h = ins[0].shape[0] // (2 * n)
    low = jnp.bfloat16
    slots = min(4, n)
    split = [a.reshape(2 * n, h, a.shape[1]) for a in ins]
    vmem = pl.BlockSpec(memory_space=pltpu.VMEM)
    hbm = pl.BlockSpec(memory_space=pl.ANY)
    reach = n - 2
    modes = modes or ([0] * len(ins), [0] * len(outs))
    more, spec, shape, scratch, nf, same = rider_parts(rider)
    s_ins, s_shapes, s_in_specs, s_out_specs, s_scratch = side_parts(side, 2 * n)
    sums = [jax.ShapeDtypeStruct((2 * h, cols), jnp.float32)]
    norms = []
    carries = [] if carry is None else [carry]
    if norm is not None:
        norms = list(norm[:3])
        line = jax.ShapeDtypeStruct((1, cols), jnp.float32)
        sums = [jax.ShapeDtypeStruct((2 * h, cols), norm[3]), line, line]
    out = pl.pallas_call(
        functools.partial(
            scatter_kernel, n, h, body, len(ins), len(consts), len(outs), modes, nf, same, int(side is not None), norm is not None, carry is not None
        ),
        out_shape=sums
        + [jax.ShapeDtypeStruct((2 * n, h, c), d) for c, d in outs]
        + s_shapes
        + shape
        + [jax.ShapeDtypeStruct(x.shape, x.dtype) for x in carries],
        in_specs=[hbm] * len(carries)
        + [vmem] * len(norms)
        + [hbm] * len(ins)
        + [vmem] * len(consts)
        + s_in_specs
        + spec,
        out_specs=([vmem] * 3 if norms else [hbm])
        + [hbm] * len(outs)
        + s_out_specs
        + spec
        + [hbm] * len(carries),
        input_output_aliases={0: len(sums + list(outs) + s_shapes + shape)} if carries else {},
        scratch_shapes=[
            pltpu.VMEM((slots, h, cols), low),
            pltpu.VMEM((n, h, cols), low),
            pltpu.VMEM((n, h, cols), low),
            pltpu.VMEM((reach, h, cols), low),
            pltpu.VMEM((2 * h, cols), jnp.float32),
        ]
        + [pltpu.VMEM((2, h, a.shape[2]), a.dtype) for a in split]
        + [pltpu.VMEM((2, h, c), d) for c, d in outs]
        + [
            pltpu.SemaphoreType.DMA((n,)),
            pltpu.SemaphoreType.DMA((n,)),
            pltpu.SemaphoreType.DMA((reach,)),
            pltpu.SemaphoreType.DMA((reach,)),
            pltpu.SemaphoreType.DMA((len(ins), 2)),
            pltpu.SemaphoreType.DMA((max(len(outs), 1), 2)),
            pltpu.SemaphoreType.DMA((2,)),
        ]
        + scratch
        + s_scratch,
        compiler_params=pltpu.CompilerParams(
            collective_id=ident, has_side_effects=True, vmem_limit_bytes=60 << 20
        ),
        cost_estimate=SMALL,
        name=name,
    )(*carries, *norms, *split, *consts, *s_ins, *more)
    lines = list(out[1:3]) if norms else []
    out = [out[0]] + list(out[1 + len(lines) :])
    many = 1 + len(outs)
    sides = [] if side is None else list(out[many : many + 2])
    more = list(out[many + len(sides) :])
    return [out[0]] + lines + [o.reshape(2 * n * h, o.shape[2]) for o in out[1:many]] + sides + more


class Rows:
    def __init__(self, n, held, width, wide, back):
        moves = []
        for to in range(n):
            for third in range(3):
                at, end = third * width + to * wide, third * width + min((to + 1) * wide, width)
                row = third * wide
                while at < end:
                    source = at // held
                    count = min(end, (source + 1) * held) - at
                    moves.append((source, at - source * held, to, row, count))
                    at, row = at + count, row + count
        self.n = n
        self.moves = [(c, d, a, b, e) if back else (a, b, c, d, e) for a, b, c, d, e in moves]
        self.out = [[m for m in self.moves if m[0] == i] for i in range(n)]
        self.into = [[m for m in self.moves if m[2] == i] for i in range(n)]
        self.most = max(len(v) for v in self.out + self.into)

    def scratch(self):
        dma = pltpu.SemaphoreType.DMA
        return [dma((self.most,)), dma((self.most,)), dma((self.most,))]

    def bind(self, source, target, send, recv, local):
        self.source, self.target, self.send, self.recv, self.local = source, target, send, recv, local
        return self

    def copy(self, i, m):
        src = self.source.at[pl.ds(m[1], m[4])]
        dst = self.target.at[pl.ds(m[3], m[4])]
        if m[0] == m[2]:
            return pltpu.make_async_copy(src, dst, self.local.at[i])
        return remote(src, dst, self.send.at[i], self.recv.at[self.into[m[2]].index(m)], {"seq": m[2]})

    def start(self):
        me = lax.axis_index("seq")
        for s in range(self.n):

            @pl.when(me == s)
            def _(s=s):
                for i, m in enumerate(self.out[s]):
                    self.copy(i, m).start()

    def finish(self):
        me = lax.axis_index("seq")
        for s in range(self.n):

            @pl.when(me == s)
            def _(s=s):
                for i, m in enumerate(self.into[s]):
                    if m[0] != s:
                        dst = self.target.at[pl.ds(m[3], m[4])]
                        remote(dst, dst, self.send.at[0], self.recv.at[i], {"seq": s}).wait_recv()
                for i, m in enumerate(self.out[s]):
                    if m[0] == m[2]:
                        self.copy(i, m).wait()
                    else:
                        self.copy(i, m).wait_send()


class Units:
    def __init__(self, n, nf, back, source, target, send, recv, local):
        self.n, self.nf, self.back = n, nf, back
        self.source, self.target, self.send, self.recv, self.local = source, target, send, recv, local
        self.me = lax.axis_index("seq")

    @staticmethod
    def scratch(nf):
        dma = pltpu.SemaphoreType.DMA
        return [dma((nf,)), dma((nf,)), dma]

    def ends(self, i):
        group = self.n // self.nf
        if self.back:
            return i * group + lax.div(self.me, self.nf), lax.rem(self.me, self.nf)
        return lax.rem(self.me, group) * self.nf + i, lax.div(self.me, group)

    def comes(self, i):
        group = self.n // self.nf
        if self.back:
            return lax.rem(self.me, group) * self.nf + i
        return i * group + lax.div(self.me, self.nf)

    def each(self, i, there, here):
        to, slot = self.ends(i)

        @pl.when(to != self.me)
        def _():
            there(remote(self.source.at[i], self.target.at[slot], self.send.at[i], self.recv.at[slot], {"seq": to}))

        @pl.when(to == self.me)
        def _():
            here(pltpu.make_async_copy(self.source.at[i], self.target.at[slot], self.local))

    def start(self):
        for i in range(self.nf):
            self.each(i, lambda c: c.start(), lambda c: c.start())

    def finish(self):
        for i in range(self.nf):
            source = self.comes(i)

            @pl.when(source != self.me)
            def _(i=i):
                dst = self.target.at[i]
                remote(dst, dst, self.send.at[0], self.recv.at[i], {"seq": self.me}).wait_recv()

        for i in range(self.nf):
            self.each(i, lambda c: c.wait_send(), lambda c: c.wait())


def all_peers(n, nf):
    me, f = lax.axis_index("seq"), lax.axis_index("fsdp")
    return [{"seq": place(me, r, n)} for r in range(1, n)] + [
        {"fsdp": lax.rem(f + d, nf)} for d in range(1, nf)
    ]


def exchange_kernel(n, nf, rows, count, *refs):
    ins, outs, sems = refs[: 4 + count], refs[4 + count : 8 + 2 * count], list(refs[8 + 2 * count :])
    take = lambda k: [sems.pop(0) for _ in range(k)]
    parts = []
    if rows is not None:
        parts.append(rows.bind(ins[0], outs[0], *take(3)))
    vectors = [Blocks("fsdp", nf, True, ins[4 + i], outs[4 + i], *take(3)) for i in range(count)]
    later = [
        Blocks("fsdp", nf, True, ins[3], outs[3], *take(3)),
        Units(n, nf, False, ins[2], outs[2], *take(3)),
        Blocks("seq", n, False, ins[1], outs[1], *take(3)),
    ]
    parts = vectors + parts + later
    greet(all_peers(n, nf))
    for p in parts:
        p.start()
    for p in parts:
        p.finish()


def exchange(w, p, c, o, vectors, n, nf, rows, wide, ident):
    hbm = pl.BlockSpec(memory_space=pl.ANY)
    count = len(vectors)
    out = pl.pallas_call(
        functools.partial(exchange_kernel, n, nf, rows, count),
        out_shape=[
            jax.ShapeDtypeStruct((3 * wide, w.shape[1]) if rows is not None else w.shape, w.dtype),
            blocks_shape(p, n, False),
            blocks_shape(c, nf, False),
            blocks_shape(o, nf, True),
        ]
        + [blocks_shape(v, nf, True) for v in vectors],
        in_specs=[hbm] * (4 + count),
        out_specs=[hbm] * (4 + count),
        scratch_shapes=(rows.scratch() if rows is not None else [])
        + sum([Blocks.scratch(nf) for _ in vectors], [])
        + Blocks.scratch(nf)
        + Units.scratch(nf)
        + Blocks.scratch(n),
        compiler_params=pltpu.CompilerParams(collective_id=ident, has_side_effects=True),
        cost_estimate=SMALL,
        name="exchange",
    )(w, p, c, o, *vectors)
    return out[0], out[1], out[2], out[3], out[4:]


def to_tokens_kernel(n, wide, x_ref, o_ref, send, recv, local):
    me = lax.axis_index("seq")

    def target(i):
        return o_ref.at[:, pl.ds(pl.multiple_of(i * wide, 128), wide)]

    greet([{"seq": place(me, r, n)} for r in range(1, n)])
    copies = []
    for r in range(n - 1, 0, -1):
        to = place(me, r, n)
        c = remote(x_ref.at[to], target(me), send.at[r - 1], recv.at[r - 1], {"seq": to})
        c.start()
        copies.append(c)
    mine = pltpu.make_async_copy(x_ref.at[me], target(me), local)
    mine.start()
    for r in range(1, n):
        dst = target(place(me, r, n))
        remote(dst, dst, send.at[0], recv.at[r - 1], {"seq": place(me, r, n)}).wait_recv()
    mine.wait()
    for c in copies:
        c.wait_send()


def to_tokens(x, n, wide, ident):
    rows = x.shape[1]
    hbm = pl.BlockSpec(memory_space=pl.ANY)
    return pl.pallas_call(
        functools.partial(to_tokens_kernel, n, wide),
        out_shape=jax.ShapeDtypeStruct((rows, n * wide), x.dtype),
        in_specs=[hbm],
        out_specs=hbm,
        scratch_shapes=Blocks.scratch(n),
        compiler_params=pltpu.CompilerParams(collective_id=ident, has_side_effects=True),
        cost_estimate=SMALL,
        name="to_tokens",
    )(x)


def to_heads_kernel(
    n, nf, wide, x_ref, w_ref, t_ref, a_ref, b_ref, z_ref, o_ref, g_ref, m_ref, z_out, t_out, made, *extra
):
    me = lax.axis_index("seq")
    send, recv, local = extra[:3]
    side = Side(2 * n, (a_ref, b_ref, g_ref, m_ref) + extra[3:7])
    planes = PlaneSum(nf, z_ref, 0, *extra[7:])
    side.begin()
    greet([{"seq": place(me, r, n)} for r in range(1, n)] + planes.peers())
    planes.start()

    def copy(r):
        to = place(me, r, n)
        return remote(made.at[r], o_ref.at[me], send.at[r - 1], recv.at[r - 1], {"seq": to})

    def mine():
        return pltpu.make_async_copy(made.at[0], o_ref.at[me], local)

    def step(i, carry):
        r = n - 1 - i
        at = place(me, r, n)
        whole, rest = w_ref.shape[1] // wide, w_ref.shape[1] % wide

        @pl.when(at < whole)
        def _():
            lanes = pl.ds(pl.multiple_of(at * wide, 128), wide)
            made[r] = mm(x_ref[...], w_ref[:, lanes]).astype(made.dtype)

        @pl.when(at >= whole)
        def _():
            made[r] = jnp.zeros(made.shape[1:], made.dtype)

        if rest:

            @pl.when(at == whole)
            def _():
                made[r, :, :rest] = mm(x_ref[...], w_ref[:, whole * wide :]).astype(made.dtype)

        @pl.when(r > 0)
        def _():
            copy(r).start()

        return carry

    lax.fori_loop(0, n, step, 0)
    mine().start()
    side.run(0, 2 * n)
    cols = t_out.shape[0]
    for at in range(0, cols, 512):
        end = min(at + 512, cols)
        t_out[at:end] = lax.dot_general(
            x_ref[:, at:end], t_ref[...], (((0,), (0,)), ((), ())), preferred_element_type=jnp.float32
        ).astype(t_out.dtype)
    side.end()
    planes.finish()
    planes.store(z_out)
    for r in range(1, n):
        dst = o_ref.at[place(me, r, n)]
        remote(dst, dst, send.at[0], recv.at[r - 1], {"seq": me}).wait_recv()
    mine().wait()
    for r in range(1, n):
        copy(r).wait_send()


def to_heads(x, w, t, n, nf, wide, ident, a, b, z, count):
    rows, cols = x.shape
    vmem = pl.BlockSpec(memory_space=pltpu.VMEM)
    hbm = pl.BlockSpec(memory_space=pl.ANY)
    s_ins, s_shapes, s_in_specs, s_out_specs, s_scratch = side_parts((a, b), 2 * n)
    return pl.pallas_call(
        functools.partial(to_heads_kernel, n, nf, wide),
        out_shape=[jax.ShapeDtypeStruct((n, rows, wide), x.dtype)]
        + s_shapes
        + [
            jax.ShapeDtypeStruct((n, count, z.shape[2] // n), z.dtype),
            jax.ShapeDtypeStruct((cols, t.shape[1]), x.dtype),
        ],
        in_specs=[vmem, vmem, vmem] + s_in_specs + [hbm],
        out_specs=[hbm] + s_out_specs + [vmem, vmem],
        scratch_shapes=[pltpu.VMEM((n, rows, wide), x.dtype)]
        + Blocks.scratch(n)
        + s_scratch
        + PlaneSum.scratch(nf, count, z.shape[2]),
        compiler_params=pltpu.CompilerParams(
            collective_id=ident, has_side_effects=True, vmem_limit_bytes=60 << 20
        ),
        cost_estimate=SMALL,
        name="to_heads",
    )(x, w, t, *s_ins, z)


def contract_kernel(
    n, nf, a_ref, b_ref, x_ref, y_ref, s_ref, p_ref, q_ref, c_ref, o_ref, sum_ref, p_out, q_out, c_out, acc, *sems
):
    i = pl.program_id(0)
    parts = [
        Blocks("seq", n, False, p_ref, p_out, *sems[:3]),
        Blocks("seq", n, False, q_ref, q_out, *sems[3:6]),
        Units(n, nf, True, c_ref, c_out, *sems[6:]),
    ]

    @pl.when(i == 0)
    def _():
        me = lax.axis_index("seq")
        greet([{"seq": place(me, r, n)} for r in range(1, n)])
        for part in parts:
            part.start()

    sum_ref[...] = (x_ref[...] + y_ref[...].astype(jnp.float32) + s_ref[...]).astype(sum_ref.dtype)
    part = lax.dot_general(
        a_ref[...], b_ref[...], (((0,), (0,)), ((), ())), preferred_element_type=jnp.float32
    )

    @pl.when(i == 0)
    def _():
        acc[...] = part

    @pl.when(i > 0)
    def _():
        acc[...] += part

    @pl.when(i == pl.num_programs(0) - 1)
    def _():
        o_ref[...] = acc[...].astype(o_ref.dtype)
        for part in parts:
            part.finish()


def contract(a, b, x, y, s, p, q, c, n, nf, tile, ident):
    steps = a.shape[0] // tile
    shape = (a.shape[1], b.shape[1])
    still = lambda s: pl.BlockSpec(s, lambda i: (0,) * len(s), pipeline_mode=pl.Buffered(1))
    part = lambda v: pl.BlockSpec((v.shape[0] // steps, v.shape[1]), lambda i: (i, 0))
    hbm = pl.BlockSpec(memory_space=pl.ANY)
    return pl.pallas_call(
        functools.partial(contract_kernel, n, nf),
        out_shape=[
            jax.ShapeDtypeStruct(shape, a.dtype),
            jax.ShapeDtypeStruct(x.shape, a.dtype),
            blocks_shape(p, n, False),
            blocks_shape(q, n, False),
            blocks_shape(c, nf, False),
        ],
        grid=(steps,),
        in_specs=[part(a), part(b), part(x), part(y), still(s.shape), hbm, hbm, hbm],
        out_specs=[still(shape), part(x), hbm, hbm, hbm],
        scratch_shapes=[pltpu.VMEM(shape, jnp.float32)]
        + Blocks.scratch(n)
        + Blocks.scratch(n)
        + Units.scratch(nf),
        compiler_params=pltpu.CompilerParams(
            dimension_semantics=("arbitrary",),
            vmem_limit_bytes=40 << 20,
            collective_id=ident,
            has_side_effects=True,
        ),
        cost_estimate=SMALL,
        name="contract",
    )(a, b, x, y, s, p, q, c)


def give_back_kernel(
    n, nf, rows, v_ref, w_ref, o_ref, v_out, w_out, o_out, planes, sums, *sems
):
    s = lax.axis_index("seq")
    f = lax.axis_index("fsdp")
    sems = list(sems)
    take = lambda k: [sems.pop(0) for _ in range(k)]
    send_z, recv_z, send_s, recv_s = take(4)
    parts = []
    if rows is not None:
        parts.append(rows.bind(w_ref, w_out, *take(3)))
    parts.append(Blocks("fsdp", nf, False, o_ref, o_out, *take(3)))
    others = [{"fsdp": lax.rem(f + d, nf)} for d in range(1, nf)]
    peers = [{"seq": place(s, r, n)} for r in range(1, n)]
    greet(peers + others)
    copies = []
    for d in range(1, nf):
        c = remote(v_ref.at[lax.rem(f + d, nf)], planes.at[d - 1], send_z.at[d - 1], recv_z.at[d - 1], others[d - 1])
        c.start()
        copies.append(c)
    for p in parts:
        p.start()
    total = v_ref[f]
    for d, c in enumerate(copies):
        c.wait_recv()
        total = total + planes[d]
    sums[0] = total
    spread = []
    for r in range(1, n):
        c = remote(sums.at[0], sums.at[r], send_s.at[r - 1], recv_s.at[r - 1], peers[r - 1])
        c.start()
        spread.append(c)
    for r, c in enumerate(spread):
        c.wait_recv()
        total = total + sums[r + 1]
    v_out[...] = total
    for p in parts:
        p.finish()
    for c in copies + spread:
        c.wait_send()


def give_back(vectors, w, held, o, n, nf, rows, ident):
    k = vectors.shape[1]
    tiles = -(-k // 1024) * 8
    padded = jnp.pad(vectors, ((0, 0), (0, tiles * 128 - k))).reshape(nf, tiles, 128)
    vmem = pl.BlockSpec(memory_space=pltpu.VMEM)
    hbm = pl.BlockSpec(memory_space=pl.ANY)
    dma = pltpu.SemaphoreType.DMA
    out = pl.pallas_call(
        functools.partial(give_back_kernel, n, nf, rows),
        out_shape=[
            jax.ShapeDtypeStruct((tiles, 128), jnp.float32),
            jax.ShapeDtypeStruct((held, w.shape[1]), w.dtype),
            blocks_shape(o, nf, False),
        ],
        in_specs=[vmem, hbm, hbm],
        out_specs=[vmem, hbm, hbm],
        scratch_shapes=[
            pltpu.VMEM((nf - 1, tiles, 128), jnp.float32),
            pltpu.VMEM((n, tiles, 128), jnp.float32),
            dma((nf - 1,)),
            dma((nf - 1,)),
            dma((n - 1,)),
            dma((n - 1,)),
        ]
        + (rows.scratch() if rows is not None else [])
        + Blocks.scratch(nf),
        compiler_params=pltpu.CompilerParams(collective_id=ident, has_side_effects=True),
        cost_estimate=SMALL,
        name="give_back",
    )(padded, w, o)
    return (out[0].reshape(-1)[:k],) + tuple(out[1:])


HEAD=64
SCALE=0.125*math.log2(math.e)


def block_pairs(slots, trunk):
    branches = (slots - trunk) // 3
    pairs = []
    for t in range(slots):
        m = t - trunk
        if t < trunk:
            keys = [(c, int(c == t), -1, -1) for c in range(t + 1)]
        else:
            keys = [(c, 0, -1, -1) for c in range(trunk)]
            if m >= branches:
                keys.append((trunk, 0, -1, m))
            keys.append((t, 1, m, -1))
        for i, (c, causal, own, leaf) in enumerate(keys):
            pairs.append((t, c, causal, own, leaf, int(i == 0), int(i == len(keys) - 1)))
    return pairs


def block_fields(p, slots, trunk):
    branches = (slots - trunk) // 3
    counts = [t + 1 for t in range(trunk)] + [trunk + 1] * branches
    counts += [trunk + 2] * (slots - trunk - branches)
    starts = [sum(counts[:t]) for t in range(slots)]
    t, begin, end = jnp.int32(0), jnp.int32(0), jnp.int32(counts[0])
    for i in range(1, slots):
        here = p >= starts[i]
        t = jnp.where(here, i, t)
        begin = jnp.where(here, starts[i], begin)
        end = jnp.where(here, starts[i] + counts[i], end)
    i = p - begin
    last = p == end - 1
    leaf = (t >= trunk + branches) & (i == trunk)
    key = jnp.where((t >= trunk) & last, t, i)
    return t, key, last, leaf, i == 0, last


def block_values(lengths, parents, pairs, block):
    count = lengths.shape[0]
    segments = np.arange(count)
    own = np.array([p[3] for p in pairs])[None, :] == segments[:, None]
    leaf = np.array([p[4] for p in pairs])[None, :] == segments[:, None]
    above = jnp.sum(jnp.where(leaf, parents[:, None], 0), 0)
    source = own | (segments[:, None] + 1 == above[None, :])
    closed = np.array([p[3] < 0 and p[4] < 0 for p in pairs])
    reach = jnp.where(closed, block, jnp.sum(jnp.where(source, lengths[:, None], 0), 0))
    return jnp.stack([jnp.maximum(above - 1, 0), reach]).astype(jnp.int32)


def lane_half(shape):
    return lax.broadcasted_iota(jnp.int32, shape, len(shape) - 1) < HEAD


def nt(a, b):
    return lax.dot_general(a, b, (((1,), (1,)), ((), ())), preferred_element_type=jnp.float32)


def mm(a, b):
    return jnp.dot(a, b, preferred_element_type=jnp.float32)


def attend_kernel(width, block, trunk, n, values, x_ref, w_ref, b_ref, c_ref, qkv, low, att, tot, kt, c_all, acc, xbuf, xsem, *sems):
    p = pl.program_id(0)
    slot, key, causal, leaf, first, last = block_fields(p, n, trunk)
    rows = lambda slot: pl.ds(pl.multiple_of(slot * block, block), block)
    qrow = rows(slot)
    above = values[0, p]
    reach = values[1, p]
    branches = (n - trunk) // 3
    left = lane_half((block, 2 * HEAD))
    spread = Spread(n, c_ref, c_all, *sems)

    def fetch(i):
        slot = lax.rem(i, 2)
        return pltpu.make_async_copy(x_ref.at[i], xbuf.at[slot], xsem.at[slot])

    @pl.when(p == 0)
    def _():
        fetch(jnp.int32(0)).start()
        greet(spread.peers())
        spread.start()

        def step(i, carry):
            @pl.when(i + 1 < n)
            def _():
                fetch(i + 1).start()

            fetch(i).wait()
            made = (mm(xbuf[lax.rem(i, 2)], w_ref[...]) + b_ref[...]).astype(qkv.dtype)
            qkv[rows(i)] = made
            kt[:, rows(i)] = made[:, width : 2 * width].T
            return carry

        lax.fori_loop(0, n, step, 0)
        for i in range(len(spread.bits) - 1):
            spread.phase(i)

    @pl.when(first)
    def _():
        acc[...] = jnp.zeros_like(acc)

    def keyed(mask, read):
        got = read(rows(key))
        if mask is not None:
            for b in range(1, branches):
                got = jnp.where(leaf & (above == b), read(pl.ds((trunk + b) * block, block)), got)
        return got

    def step(mask):
        for j in range(width // (2 * HEAD)):
            lanes = slice(j * 2 * HEAD, (j + 1) * 2 * HEAD)
            q = qkv[qrow, lanes]
            k = keyed(mask, lambda at: qkv[at, width + j * 2 * HEAD : width + (j + 1) * 2 * HEAD])
            v = keyed(mask, lambda at: qkv[at, 2 * width + j * 2 * HEAD : 2 * width + (j + 1) * 2 * HEAD])
            for h in range(2):
                here = left if h == 0 else jnp.logical_not(left)
                s = nt(jnp.where(here, q, 0), k)
                e = jnp.exp2(s * SCALE)
                if mask is not None:
                    e = jnp.where(mask, e, 0.0)
                acc[2 * j + h] += mm(e.astype(jnp.bfloat16), jnp.where(here, v, 1))

    closes = causal | leaf
    shift = jnp.where(causal, 0, block)

    @pl.when(jnp.logical_not(closes))
    def _():
        step(None)

    @pl.when(closes)
    def _():
        row = lax.broadcasted_iota(jnp.int32, (block, block), 0)
        col = lax.broadcasted_iota(jnp.int32, (block, block), 1)
        step((col <= row + shift) & (col < reach))

    @pl.when(last)
    def _():
        for j in range(width // (2 * HEAD)):
            a, b = acc[2 * j], acc[2 * j + 1]
            total = jnp.where(left, pltpu.roll(a, HEAD, 1), pltpu.roll(b, HEAD, 1))
            value = jnp.where(left, a, b) / total
            lanes = slice(j * 2 * HEAD, (j + 1) * 2 * HEAD)
            low[:, lanes] = value.astype(jnp.bfloat16)
            att[:, lanes] = value
            tot[:, lanes] = total

    @pl.when(p == pl.num_programs(0) - 4)
    def _():
        spread.phase(len(spread.bits) - 1)

    @pl.when(p == pl.num_programs(0) - 1)
    def _():
        spread.finish()


def attend(values, pairs, x, w, bias, block, trunk, sent, n, ident):
    rows, width = x.shape[0], w.shape[1] // 3
    by_q = lambda p: (block_fields(p, n, trunk)[0], 0)
    heads = width // HEAD
    once = lambda s: pl.BlockSpec(s, lambda p: (0,) * len(s), pipeline_mode=pl.Buffered(1))
    hbm = pl.BlockSpec(memory_space=pl.ANY)
    out = pl.pallas_call(
        functools.partial(attend_kernel, width, block, trunk, n),
        grid=(len(pairs),),
        out_shape=(
            jax.ShapeDtypeStruct((rows, 3 * width), x.dtype),
            jax.ShapeDtypeStruct((rows, width), x.dtype),
            jax.ShapeDtypeStruct((rows, width), jnp.float32),
            jax.ShapeDtypeStruct((rows, width), jnp.float32),
            jax.ShapeDtypeStruct((width, rows), x.dtype),
            jax.ShapeDtypeStruct((n,) + sent.shape, sent.dtype),
        ),
        in_specs=[pl.BlockSpec(memory_space=pltpu.SMEM), hbm, once(w.shape), once(bias.shape), hbm],
        out_specs=[once((rows, 3 * width))]
        + [pl.BlockSpec((block, width), by_q)] * 3
        + [once((width, rows)), hbm],
        scratch_shapes=[
            pltpu.VMEM((heads, block, 2 * HEAD), jnp.float32),
            pltpu.VMEM((2, block, x.shape[1]), x.dtype),
            pltpu.SemaphoreType.DMA((2,)),
        ]
        + Spread.scratch(n),
        compiler_params=pltpu.CompilerParams(
            dimension_semantics=("arbitrary",),
            vmem_limit_bytes=60 << 20,
            collective_id=ident,
            has_side_effects=True,
        ),
        cost_estimate=SMALL,
        name="attend",
    )(values, x.reshape(n, block, x.shape[1]), w, bias, sent)
    return out[:5] + (out[5].reshape(n * sent.shape[0], sent.shape[1]),)


def attend_back_kernel(width, block, slots, trunk, branches, nf, lows, *refs):
    count = len(lows)
    values, qkv, kt, datt, att, tot = refs[:6]
    sources = refs[6 : 6 + count]
    out, sums = refs[6 + count : 8 + count]
    parts = refs[8 + count : 8 + 2 * count]
    dk, dv, dqt, aug = refs[8 + 2 * count : 12 + 2 * count]
    rest = refs[12 + 2 * count :]
    riders = [PlaneSum(nf, sources[i], lows[i], *rest[4 * i : 4 * i + 4]) for i in range(count)]
    p = pl.program_id(0)
    slot, key, causal, leaf, first, last = block_fields(p, slots, trunk)
    rows = lambda slot: pl.ds(pl.multiple_of(slot * block, block), block)
    above = values[0, p]
    reach = values[1, p]
    qrow = rows(slot)
    left = lane_half((block, 2 * HEAD))
    lane = lax.broadcasted_iota(jnp.int32, (block, 2 * HEAD), 1)
    columns = width // (2 * HEAD)

    @pl.when(p == 0)
    def _():
        greet(riders[0].peers())
        for r in riders:
            r.start()
        dk[...] = jnp.zeros_like(dk)
        dv[...] = jnp.zeros_like(dv)

    @pl.when(first)
    def _():
        dqt[...] = jnp.zeros_like(dqt)
        for j in range(columns):
            lanes = slice(j * 2 * HEAD, (j + 1) * 2 * HEAD)
            d = datt[:, lanes].astype(jnp.float32)
            total = tot[:, lanes]
            low = (d / total).astype(jnp.bfloat16)
            prod = d * att[:, lanes] / total
            for h in range(2):
                here = left if h == 0 else jnp.logical_not(left)
                delta = -jnp.sum(jnp.where(here, prod, 0.0), 1, keepdims=True)
                hi = delta.astype(jnp.bfloat16).astype(jnp.float32)
                mid = (delta - hi).astype(jnp.bfloat16).astype(jnp.float32)
                rest = delta - hi - mid
                at = HEAD * (1 - h)
                extra = jnp.where(
                    lane == at, hi, jnp.where(lane == at + 1, mid, jnp.where(lane == at + 2, rest, 0.0))
                )
                aug[2 * j + h] = jnp.where(here, low.astype(jnp.float32), extra).astype(jnp.bfloat16)

    def add(mask, lanes, dks, dvs):
        at = rows(key)
        if mask is None:
            dk[at, lanes] += dks
            dv[at, lanes] += dvs
            return
        for b in range(branches):
            chosen = causal | (above == b) if b == 0 else leaf & (above == b)
            if b > 0:
                at = pl.ds((trunk + b) * block, block)
            dk[at, lanes] += jnp.where(chosen, dks, 0.0)
            dv[at, lanes] += jnp.where(chosen, dvs, 0.0)

    def keyed(mask, read):
        got = read(rows(key))
        if mask is not None:
            for b in range(1, branches):
                got = jnp.where(leaf & (above == b), read(pl.ds((trunk + b) * block, block)), got)
        return got

    def step(mask):
        for j in range(columns):
            lanes = slice(j * 2 * HEAD, (j + 1) * 2 * HEAD)
            q = qkv[qrow, lanes]
            k = keyed(mask, lambda at: qkv[at, width + j * 2 * HEAD : width + (j + 1) * 2 * HEAD])
            v = keyed(mask, lambda at: qkv[at, 2 * width + j * 2 * HEAD : 2 * width + (j + 1) * 2 * HEAD])
            dvs, dks = [], []
            for h in range(2):
                here = left if h == 0 else jnp.logical_not(left)
                qh = jnp.where(here, q, 0)
                e = jnp.exp2(nt(k, qh) * SCALE)
                if mask is not None:
                    e = jnp.where(mask, e, 0.0)
                dod = aug[2 * j + h]
                ds = (e * nt(jnp.where(here, v * 0.125, 0.125).astype(jnp.bfloat16), dod)).astype(
                    jnp.bfloat16
                )
                dvs.append(mm(e.astype(jnp.bfloat16), dod))
                dks.append(mm(ds, qh))
                at = j * 2 * HEAD + h * HEAD
                dqt[at : at + HEAD] += mm(keyed(mask, lambda i: kt[at : at + HEAD, i]), ds)
            add(mask, lanes, dks[0] + dks[1], jnp.where(left, dvs[0], dvs[1]))

    closes = causal | leaf
    shift = jnp.where(causal, 0, block)

    @pl.when(jnp.logical_not(closes))
    def _():
        step(None)

    @pl.when(closes)
    def _():
        col = lax.broadcasted_iota(jnp.int32, (block, block), 0)
        row = lax.broadcasted_iota(jnp.int32, (block, block), 1)
        step((col <= row + shift) & (col < reach))

    @pl.when(last)
    def _():
        out[qrow, 0:width] = dqt[...].T.astype(jnp.bfloat16)

    @pl.when(p == pl.num_programs(0) - 1)
    def _():
        out[:, width : 2 * width] = dk[...].astype(jnp.bfloat16)
        out[:, 2 * width :] = dv[...].astype(jnp.bfloat16)
        for t in range(3):
            lanes = slice(t * width, (t + 1) * width)
            sums[:, lanes] = jnp.sum(out[:, lanes].astype(jnp.float32), 0, keepdims=True)
        for r, made in zip(riders, parts):
            r.finish()
            r.store(made)


def attend_back(values, pairs, qkv, kt, datt, att, tot, block, trunk, nf, riders, ident):
    rows, width = qkv.shape[0], qkv.shape[1] // 3
    by_q = lambda p: (block_fields(p, rows // block, trunk)[0], 0)
    heads = width // HEAD
    branches = (rows // block - trunk) // 3
    made = [(k, z.shape[1] - at, z.shape[2] // k) for z, at, k in riders]
    once = lambda s: pl.BlockSpec(s, lambda p: (0,) * len(s), pipeline_mode=pl.Buffered(1))
    hbm = pl.BlockSpec(memory_space=pl.ANY)
    out = pl.pallas_call(
        functools.partial(
            attend_back_kernel, width, block, rows // block, trunk, branches, nf, [r[1] for r in riders]
        ),
        grid=(len(pairs),),
        out_shape=[
            jax.ShapeDtypeStruct((rows, 3 * width), jnp.bfloat16),
            jax.ShapeDtypeStruct((1, 3 * width), jnp.float32),
        ]
        + [jax.ShapeDtypeStruct(s, jnp.bfloat16) for s in made],
        in_specs=[pl.BlockSpec(memory_space=pltpu.SMEM), once((rows, 3 * width)), once((width, rows))]
        + [pl.BlockSpec((block, width), by_q)] * 3
        + [hbm] * len(riders),
        out_specs=[once((rows, 3 * width)), once((1, 3 * width))] + [once(s) for s in made],
        scratch_shapes=[
            pltpu.VMEM((rows, width), jnp.float32),
            pltpu.VMEM((rows, width), jnp.float32),
            pltpu.VMEM((width, block), jnp.float32),
            pltpu.VMEM((heads, block, 2 * HEAD), jnp.bfloat16),
        ]
        + sum([PlaneSum.scratch(nf, z.shape[1] - at, z.shape[2]) for z, at, k in riders], []),
        compiler_params=pltpu.CompilerParams(
            dimension_semantics=("arbitrary",),
            vmem_limit_bytes=60 << 20,
            collective_id=ident,
            has_side_effects=True,
        ),
        cost_estimate=SMALL,
        name="attend_back",
    )(values, qkv, kt, datt, att, tot, *[r[0] for r in riders])
    return out[0], out[1], out[2:]


def layer_norm(values, gain, shift):
    centred = values - jnp.mean(values, -1, keepdims=True)
    spread = jnp.mean(centred * centred, -1, keepdims=True)
    return centred * lax.rsqrt(spread + 1e-05) * gain + shift


def contract_rows(left, right):
    return lax.dot_general(
        left, right, (((0,), (0,)), ((), ())), preferred_element_type=jnp.float32
    )


def contract_cols(left, right):
    return lax.dot_general(
        left, right, (((1,), (1,)), ((), ())), preferred_element_type=jnp.float32
    )


def after(value, other):
    return value + (other[(0,) * other.ndim] * 0).astype(value.dtype)


def row_major(x):
    return with_layout_constraint(x, Layout(major_to_minor=tuple(range(x.ndim))))


def local(
    tokens,
    ln1_gain,
    ln1_bias,
    qkv_weight,
    qv_bias,
    out_weight,
    out_bias,
    ln2_gain,
    ln2_bias,
    fc_weight,
    fc_bias,
    proj_weight,
    proj_bias,
    seg_lengths,
    parents,
    cotangent,
):
    n = lax.axis_size("seq")
    nf = lax.axis_size("fsdp")
    s = lax.axis_index("seq")
    f = lax.axis_index("fsdp")
    trunk = n // 4
    block, width = tokens.shape[1], tokens.shape[2]
    rows = width // nf
    hidden = fc_weight.shape[1] * n
    piece = hidden // (n * nf)
    group = n // nf
    wide = 2 * HEAD * (-(-HEADS // (2 * n)))
    low = jnp.bfloat16
    wider = jnp.float32

    vectors = [ln1_gain, ln1_bias, qv_bias, out_bias, ln2_gain, ln2_bias, fc_bias, proj_bias]
    sizes = [v.shape[0] for v in vectors]
    qkv_cols = qkv_weight.shape[1]
    even = qkv_cols % 8 == 0
    forth = Rows(n, qkv_cols, width, wide, False) if even else None
    back = Rows(n, qkv_cols, width, wide, True) if even else None
    turned, proj_blocks, fc_blocks, out_blocks, gathered = exchange(
        qkv_weight.T,
        proj_weight.reshape(n, piece, width // n),
        fc_weight.reshape(rows, nf, piece).transpose(1, 0, 2),
        out_weight,
        [jnp.stack([v for v in vectors if v.shape == ln1_gain.shape])]
        + [v.reshape(1, -1) for v in vectors if v.shape != ln1_gain.shape],
        n,
        nf,
        forth,
        wide,
        0,
    )
    short = iter(jnp.unstack(gathered[0], axis=1))
    long = iter(gathered[1:])
    whole = [next(short) if v.shape == ln1_gain.shape else next(long) for v in vectors]
    whole = [v.reshape(-1).astype(wider) for v in whole]
    gain_one, shift_one, bias_qv, bias_out, gain_two, shift_two, bias_fc, bias_proj = whole
    bias_three = jnp.stack([bias_qv[:width], jnp.zeros((width,), wider), bias_qv[width:]])
    bias_three = jnp.pad(bias_three, ((0, 0), (0, n * wide - width)))
    bias_mine = lax.dynamic_slice_in_dim(bias_three, s * wide, wide, 1).reshape(1, -1)
    bias_hidden = lax.dynamic_index_in_dim(bias_fc.reshape(nf, n, piece), s, 1, False)
    bias_hidden = bias_hidden.reshape(1, -1)

    if even:
        turned = turned.reshape(3, wide, rows)
        kept = lax.broadcasted_iota(jnp.int32, turned.shape, 1) + s * wide < width
        turned = jnp.where(kept, turned, 0).reshape(3 * wide, rows)
    else:
        turned = lax.all_gather(qkv_weight.T, "seq", axis=0, tiled=True).reshape(3, width, rows)
        turned = jnp.pad(turned, ((0, 0), (0, n * wide - width), (0, 0)))
        turned = lax.dynamic_slice_in_dim(turned, s * wide, wide, 1).reshape(3 * wide, rows)
    pairs = block_pairs(n, trunk)
    table = block_values(seg_lengths[0], parents[0], pairs, block)

    resid = tokens[0].astype(wider)
    out_turned = out_blocks.reshape(width, width // n).T
    normed_one, out_turned, qkv_mine = seq_gather(
        layer_norm(resid, gain_one, shift_one).astype(low),
        n,
        1,
        "gather_one",
        rider=(turned.T, True, nf),
        second=out_turned,
    )
    out_turned = out_turned.reshape(width, width)
    qkv_mine = qkv_mine.reshape(width, 3 * wide)
    fc_rows = fc_blocks.transpose(1, 0, 2).reshape(rows, nf * piece)
    fc_mine = lax.all_gather(after(fc_rows, normed_one), "fsdp", axis=0, tiled=True)

    upstream = cotangent[0].astype(wider)
    proj_rows = proj_blocks.transpose(1, 0, 2).reshape(piece, width)
    proj_mine = lax.all_gather(after(proj_rows, normed_one), "fsdp", axis=0, tiled=True)
    projected, attended_low, attended, totals, keys_turned, upstream_all = attend(
        table, pairs, normed_one, qkv_mine, bias_mine, block, trunk, cotangent[0], n, 8
    )
    attended_mine = to_tokens(attended_low.reshape(n, block, wide), n, wide, 2)[:, :width]
    middle = resid + contract_cols(attended_mine, out_turned) + bias_out
    normed_two = layer_norm(middle, gain_two, shift_two).astype(low)
    ff = nf * piece

    def expand(value, fc, bias, proj):
        pre = mm(value, fc[...]) + bias[...]
        bend = math.sqrt(2 / math.pi)
        square = pre * pre
        inner = jnp.tanh(pre * (bend + bend * 0.044715 * square))
        half = 0.5 + 0.5 * inner
        act = (pre * half).astype(low)
        slope = half + 0.5 * pre * (1 - inner * inner) * (bend + 3 * bend * 0.044715 * square)
        return act, slope.astype(low), mm(act, proj[...]).astype(low)

    normed_two, hidden_act, hidden_slope, mixed = seq_gather(
        normed_two,
        n,
        3,
        "gather_two",
        expand,
        (fc_mine, bias_hidden, proj_mine),
        ((ff, low), (ff, low), (width, low)),
        modes=(0, 0, 0),
    )

    def shrink(up, slope, proj, fc):
        grad = (nt(up, proj[...]) * slope.astype(wider)).astype(low)
        return nt(grad, fc[...]), grad

    grad_normed_two, grad_pre, grad_proj, unused_sums, mixed = seq_scatter(
        n,
        width,
        4,
        "scatter_two",
        shrink,
        (upstream_all, hidden_slope),
        (proj_mine, fc_mine),
        ((ff, low),),
        side=(hidden_act, upstream_all),
        carry=mixed,
    )
    mixed = lax.psum_scatter(mixed, "seq", scatter_dimension=0, tiled=True)
    grad_proj = grad_proj.reshape(nf, piece, width)
    cut = piece * 3 // 32 * 8
    unused_two, norm_two_back = jax.vjp(layer_norm, middle, gain_two, shift_two)
    grad_middle_norm, grad_gain_two, grad_shift_two = norm_two_back(grad_normed_two)
    grad_middle = upstream + grad_middle_norm
    grad_branch = grad_middle.astype(low)
    grad_attended, grad_fc, hidden_sums, proj_first, grad_out = to_heads(
        grad_branch,
        out_turned,
        attended_mine,
        n,
        nf,
        wide,
        5,
        normed_two,
        grad_pre,
        grad_proj,
        cut,
    )
    grad_attended = grad_attended.reshape(n * block, wide)
    grad_projected, column_sums, (fc_part, proj_second) = attend_back(
        table,
        pairs,
        projected,
        keys_turned,
        grad_attended,
        attended,
        totals,
        block,
        trunk,
        nf,
        ((grad_fc.reshape(nf, rows, ff), 0, nf), (grad_proj, cut, n)),
        9,
    )
    grad_qkv, output, proj_first, proj_second, fc_out = contract(
        normed_one,
        grad_projected,
        middle,
        mixed,
        bias_proj.reshape(1, -1),
        proj_first,
        proj_second,
        fc_part,
        n,
        nf,
        block,
        10,
    )
    output = output[None]
    input_grad, grad_gain_one, grad_shift_one, qkv_parts = seq_scatter(
        n,
        width,
        6,
        "scatter_one",
        lambda g, w: (nt(g, w[...]),),
        (grad_projected,),
        (qkv_mine,),
        rider=(grad_qkv.reshape(nf, rows, 3 * wide), False, nf),
        norm=(tokens[0], gain_one.reshape(1, -1), grad_middle, low),
    )
    input_grad = input_grad[None]

    out_part = lax.psum_scatter(grad_out, "seq", scatter_dimension=0, tiled=True).T
    out_part = after(out_part, qkv_parts).reshape(nf, rows, width // n)
    qkv_part = jnp.sum(qkv_parts.astype(wider), 0).astype(low).T

    column_sums = column_sums.reshape(3, wide)
    placed = lax.dynamic_update_slice_in_dim(
        jnp.zeros((3, n * wide), wider), column_sums, s * wide, 1
    )[:, :width]
    grad_qv = jnp.concatenate([placed[0], placed[2]])
    hidden_sums = hidden_sums.reshape(nf, 1, piece)
    grad_fc_bias = lax.dynamic_update_slice_in_dim(
        jnp.zeros((nf, n, piece), wider), hidden_sums, s, 1
    )
    parts = [
        grad_gain_one,
        grad_shift_one,
        grad_qv,
        jnp.sum(grad_branch.astype(wider), 0),
        grad_gain_two,
        grad_shift_two,
        grad_fc_bias,
        jnp.sum(upstream, 0),
    ]
    summed, qkv_out, out_out = give_back(
        jnp.concatenate([p.reshape(nf, -1) for p in parts], 1),
        qkv_part,
        qkv_cols,
        out_part,
        n,
        nf,
        back,
        7,
    )
    if not even:
        qkv_part = qkv_part.reshape(3, wide, rows)
        qkv_out = lax.all_gather(qkv_part, "seq", axis=1, tiled=True)[:, :width]
        qkv_out = qkv_out.reshape(3 * width, rows)
        qkv_out = lax.dynamic_slice_in_dim(qkv_out, s * qkv_cols, qkv_cols, 0)
    out_out = jnp.sum(out_out.astype(wider), 0)
    qkv_out = qkv_out.T.astype(wider)
    proj_out = jnp.concatenate([proj_first, proj_second], 1)
    proj_out = proj_out.reshape(n * piece, width // n).astype(wider)
    fc_out = fc_out.transpose(1, 0, 2).reshape(rows, nf * piece).astype(wider)
    vector_out = []
    at = 0
    for size in sizes:
        vector_out.append(summed[at : at + size])
        at += size
    return (
        output,
        input_grad,
        vector_out[0],
        vector_out[1],
        qkv_out,
        vector_out[2],
        out_out,
        vector_out[3],
        vector_out[4],
        vector_out[5],
        fc_out,
        vector_out[6],
        proj_out,
        vector_out[7],
    )


def solution(mesh):
    in_specs = (
        P("fsdp", "seq", None),
        P("fsdp"),
        P("fsdp"),
        P("fsdp", "seq"),
        P("fsdp"),
        P("fsdp", "seq"),
        P("fsdp"),
        P("fsdp"),
        P("fsdp"),
        P("fsdp", "seq"),
        P("fsdp"),
        P("fsdp", "seq"),
        P("fsdp"),
        P("fsdp", None),
        P("fsdp", None),
        P("fsdp", "seq", None),
    )
    out_specs = (
        P("fsdp", "seq", None),
        P("fsdp", "seq", None),
        P("fsdp"),
        P("fsdp"),
        P("fsdp", "seq"),
        P("fsdp"),
        P("fsdp", "seq"),
        P("fsdp"),
        P("fsdp"),
        P("fsdp"),
        P("fsdp", "seq"),
        P("fsdp"),
        P("fsdp", "seq"),
        P("fsdp"),
    )
    return jax.shard_map(local, mesh=mesh, in_specs=in_specs, out_specs=out_specs, check_vma=False)
```
